32 devices in a mesh: dp: 8 (over y, x, core), mp: 4 (over z).
Axes of the slice: x: 2, y: 2, z: 4, core: 2. Of those that a mesh axis runs over, the one named last changes fastest.
Arguments:
- tokens: bfloat16 [8, 2048, 512], P('dp', 'mp'), may hold values from -6 to 6
- cotangent: bfloat16 [8, 2048, 512], P('dp', 'mp'), may hold values from -6 to 6
- lengths: int32 [8], P('dp'), may hold values from 512 to 2048, as said below
- owners: int32 [96], replicated, may hold values from 0 to 7, as said below
- w_qkv: bfloat16 [512, 1536], P(None, 'mp'), may hold values from -0.25 to 0.25
- w_out: bfloat16 [512, 512], P('mp'), may hold values from -0.75 to 0.75
- w_in: bfloat16 [512, 2048], P(None, 'mp'), may hold values from -0.25 to 0.25
- w_down: bfloat16 [2048, 512], P('mp'), may hold values from -0.125 to 0.125
- master: float32 [192, 256, 128], P('dp', 'mp'), may hold values from -0.75 to 0.75
- first_moment: float32 [192, 256, 128], P('dp', 'mp'), may hold values from -28 to 28
- second_moment: float32 [192, 256, 128], P('dp', 'mp'), may hold values from 49.152 to 409.6
- norm_gains: float32 [2, 512], replicated, may hold values from 0.25 to 1.75
- norm_biases: float32 [2, 512], replicated, may hold values from -1.5 to 1.5
- norm_first: float32 [4, 512], replicated, may hold values from -64 to 64
- norm_second: float32 [4, 512], replicated, may hold values from 262.144 to 2064.384
Outputs:
- outputs: bfloat16 [8, 2048, 512], P('dp', 'mp')
- tokens_grad: float32 [8, 2048, 512], P('dp', 'mp')
- first_new: float32 [192, 256, 128], P('dp', 'mp')
- second_new: float32 [192, 256, 128], P('dp', 'mp')
- master_new: float32 [192, 256, 128], P('dp', 'mp')
- new_qkv: bfloat16 [512, 1536], P(None, 'mp')
- new_out: bfloat16 [512, 512], P('mp')
- new_in: bfloat16 [512, 2048], P(None, 'mp')
- new_down: bfloat16 [2048, 512], P('mp')
- norm_first_new: float32 [4, 512], replicated
- norm_second_new: float32 [4, 512], replicated
- norm_new: float32 [4, 512], replicated
The draws below stay inside these ranges and needn't reach their ends.
Inputs may be any that keep to these rules, and one draw needn't show every extreme that they name: `lengths`: one sequence in every draw has all 2048 positions valid. `owners`: no owner holds more than 24 blocks and one owner holds exactly 24.
All inputs are finite; a program needn't handle non-finite values.
Results may differ from the reference program's by a relative error of at most 0.0097.
Values may be sent and summed in bfloat16 or wider, within the bound.
No kernel may reach another device: no remote copies, remote signals or barrier semaphores. Data moves between devices by JAX's collectives and lax.ppermute only.
A program may use at most 128 MiB of HBM per device.

```python
import math
import jax
import jax.numpy as jnp
from jax import lax

D = 512
HEADS = 8
HEAD = 64
FF = 2048
BAND = 30
MARGIN = 32
QBLOCK = 512
SEQ_LEN = 2048
BR = 64
STEP = 10
SEQS = 8
HEADS_DEV = 2
NBLK = 96
CAP = 24
N_MP = 4


def draw_lengths(key, part):
    key_vals, key_pick = jax.random.split(jax.random.fold_in(key, 11))
    drawn = jax.random.randint(key_vals, (SEQS,), SEQ_LEN // 4, SEQ_LEN + 1)
    chosen = jax.random.randint(key_pick, (), 0, SEQS)
    return jnp.where(jnp.arange(SEQS) == chosen, SEQ_LEN, drawn).astype(jnp.int32)


def draw_owners(key, part):
    key_order, key_rest, key_mix = jax.random.split(jax.random.fold_in(key, 23), 3)
    order = jax.random.permutation(key_order, SEQS)
    others = order[1 + jnp.arange((SEQS - 1) * CAP) // CAP]
    others = jax.random.permutation(key_rest, others)[:NBLK - CAP]
    merged = jnp.concatenate([jnp.full((CAP,), order[0]), others])
    return jax.random.permutation(key_mix, merged).astype(jnp.int32)


def block_levels(stream_key, dims, cuts, least, high):
    level, own = 1.0, jax.random.fold_in(stream_key, 6)
    for dim, shards_of in cuts:
        heights = jnp.exp(jax.random.uniform(jax.random.fold_in(own, dim), (shards_of,), jnp.float32, least / len(cuts), high / len(cuts)))
        level = level * jnp.repeat(heights, dims[dim] // shards_of).reshape([-1 if axis == dim else 1 for axis in range(len(dims))])
    return level


def bell_draw(rng, extent, scale, most, cuts=(), kind=jnp.bfloat16):
    entries = jax.random.normal(rng, extent, jnp.float32) * scale
    if len(cuts) > 0:
        entries = block_levels(rng, extent, cuts, -0.22, 0.18) * entries
    return jnp.clip(entries, min=-most, max=most).astype(kind)


def setup_inputs(seed: int = 0) -> dict:
    splits = jax.random.split(jax.random.key(seed), 16)
    tokens = bell_draw(splits[0], (SEQS, SEQ_LEN, D), 1.0, 6.0, ((0, 8), (1, 4)))
    cotangent = bell_draw(splits[1], (SEQS, SEQ_LEN, D), 1.0, 6.0, ((0, 8), (1, 4)))
    lengths = draw_lengths(jax.random.fold_in(splits[15], 71), 0)
    owners = draw_owners(jax.random.fold_in(splits[15], 71), 0)
    w_qkv = bell_draw(splits[4], (D, 3 * D), D ** -0.5, 0.25, ((1, 4),))
    w_out = bell_draw(splits[5], (D, D), (D // 8) ** -0.5, 0.75, ((0, 4),))
    w_in = bell_draw(splits[6], (D, FF), D ** -0.5, 0.25, ((1, 4),))
    w_down = bell_draw(splits[7], (FF, D), FF ** -0.5, 0.125, ((0, 4),))
    master = bell_draw(splits[8], (SEQS * CAP, N_MP * BR, 128), 0.05, 0.75, ((0, 8), (1, 4)), jnp.float32)
    first_moment = bell_draw(splits[9], (SEQS * CAP, N_MP * BR, 128), (0.038 * (SEQS * SEQ_LEN) ** 0.5), 28.0, ((0, 8), (1, 4)), jnp.float32)
    second_moment = jnp.clip(jnp.exp(math.log(409.6) - 2.1202635 * jax.random.uniform(splits[10], (SEQS * CAP, N_MP * BR, 128), jnp.float32) ** block_levels(splits[10], (SEQS * CAP, N_MP * BR, 128), ((0, 8), (1, 4)), -0.2, 0.2)), 49.152, 409.6)
    norm_gains = jnp.clip(1.0 + 0.15 * jax.random.normal(splits[11], (2, D), jnp.float32), 0.25, 1.75)
    norm_biases = bell_draw(splits[12], (2, D), 0.3, 1.5, (), jnp.float32)
    norm_first = bell_draw(splits[13], (4, D), (0.086 * (SEQS * SEQ_LEN) ** 0.5), 64.0, (), jnp.float32)
    norm_second = jnp.clip(jnp.exp(jax.random.uniform(splits[14], (4, D), jnp.float32, math.log(262.144), math.log(2064.384))), 262.144, 2064.384)
    return {"tokens": tokens, "cotangent": cotangent, "lengths": lengths, "owners": owners, "w_qkv": w_qkv, "w_out": w_out, "w_in": w_in, "w_down": w_down, "master": master, "first_moment": first_moment, "second_moment": second_moment, "norm_gains": norm_gains, "norm_biases": norm_biases, "norm_first": norm_first, "norm_second": norm_second}


@jax.custom_vjp
def low(v):
    return lax.optimization_barrier(v.astype(jnp.bfloat16)).astype(jnp.float32)

@jax.custom_vjp
def low_back(v):
    return v

def low_keep(v):
    return (low(v), None)

def low_pass(kept, grad):
    return (grad,)

def back_keep(v):
    return (v, None)

def back_low(kept, grad):
    return (low(grad),)
low.defvjp(low_keep, low_pass)
low_back.defvjp(back_keep, back_low)
highest = lax.Precision.HIGHEST
learn_rate = 0.1
norm_rate = 0.3
decay_rate = 0.1
beta_one = 0.9
beta_two = 0.95
adam_epsilon = 1e-08
norm_epsilon = 1e-05

def layer_norm(values, scale_gain, shift_bias):
    row_mean = lax.optimization_barrier(jnp.mean(values, axis=-1, keepdims=True))
    centered = values - row_mean
    variance = lax.optimization_barrier(jnp.mean(centered * centered, axis=-1, keepdims=True))
    return centered * lax.rsqrt(variance + norm_epsilon) * scale_gain + shift_bias

def far_field(query, keys, values, key_mask, valid_count):
    masked = key_mask[:, None, None]
    feat_keys = (jax.nn.elu(keys) + 1.0) * masked
    tanh_keys = jnp.tanh(keys) * masked
    feat_query = jax.nn.elu(query) + 1.0
    tanh_query = jnp.tanh(query)
    state_one = jnp.einsum('lhe,lhf->hef', feat_keys, values, precision=highest)
    normaliser = lax.optimization_barrier(jnp.sum(feat_keys, axis=0))
    denominator = jnp.einsum('lhe,he->lh', feat_query, normaliser, precision=highest)
    first_part = jnp.einsum('lhe,hef->lhf', feat_query, state_one, precision=highest) / denominator[:, :, None]
    state_two = jnp.einsum('lhe,lhf->hef', tanh_keys, values, precision=highest) / valid_count
    return first_part + jnp.einsum('lhe,hef->lhf', tanh_query, state_two, precision=highest)

def band_mask(anchor, length, seq_len):
    query_pos = anchor + jnp.arange(QBLOCK, dtype=jnp.int32)
    key_pos = anchor - MARGIN + jnp.arange(QBLOCK + 2 * MARGIN, dtype=jnp.int32)
    offsets = query_pos[:, None] - key_pos[None, :]
    inside = (key_pos >= 0) & (key_pos < seq_len)
    return (jnp.abs(offsets) <= BAND) & inside[None, :] & ((key_pos < length)[None, :] | (offsets == 0))

def near_field(query, keys, values, length):
    seq_len = query.shape[0]
    key_pad = jnp.pad(keys, ((MARGIN, MARGIN), (0, 0), (0, 0)))
    value_pad = jnp.pad(values, ((MARGIN, MARGIN), (0, 0), (0, 0)))
    span = QBLOCK + 2 * MARGIN

    def window(anchor):
        query_blk = lax.dynamic_slice_in_dim(query, anchor, QBLOCK, 0)
        key_blk = lax.dynamic_slice_in_dim(key_pad, anchor, span, 0)
        value_blk = lax.dynamic_slice_in_dim(value_pad, anchor, span, 0)
        scores = jnp.einsum('qhe,khe->hqk', query_blk, key_blk, precision=highest) * 0.125
        scores = low_back(scores)
        scores = jnp.where(band_mask(anchor, length, seq_len)[None], scores, -1e+30)
        row_max = lax.optimization_barrier(jnp.max(scores, axis=-1, keepdims=True))
        exponent = jnp.exp(scores - row_max)
        attn_probs = exponent / lax.optimization_barrier(jnp.sum(exponent, axis=-1, keepdims=True))
        return jnp.einsum('hqk,khe->qhe', low(attn_probs), value_blk, precision=highest)
    anchors = jnp.arange(seq_len // QBLOCK, dtype=jnp.int32) * QBLOCK
    results = lax.map(jax.checkpoint(window), anchors)
    return results.reshape(seq_len, query.shape[1], query.shape[2])

def block_forward(inputs, mat_qkv, mat_out, mat_in, mat_down, gains, biases, length):
    seq_len = inputs.shape[0]
    first_norm = low(layer_norm(inputs, gains[0], biases[0]))
    projected = jnp.dot(first_norm, mat_qkv, precision=highest).reshape(seq_len, N_MP, 3, HEADS_DEV, HEAD)
    query = low_back(low(projected[:, :, 0].reshape(seq_len, HEADS, HEAD)))
    keys = low_back(low(projected[:, :, 1].reshape(seq_len, HEADS, HEAD)))
    values = low_back(low(projected[:, :, 2].reshape(seq_len, HEADS, HEAD)))
    key_mask = (jnp.arange(seq_len, dtype=jnp.int32) < length).astype(inputs.dtype)
    valid_count = length.astype(inputs.dtype)
    mixed = near_field(query, keys, values, length) + far_field(query, keys, values, key_mask, valid_count)
    context = low_back(low(mixed.reshape(seq_len, D)))
    second_in = inputs + low_back(jnp.dot(context, mat_out, precision=highest))
    second_norm = low(layer_norm(second_in, gains[1], biases[1]))
    pre_act = low_back(jnp.dot(second_norm, mat_in, precision=highest))
    hidden = low(jax.nn.gelu(pre_act))
    return second_in + low_back(jnp.dot(hidden, mat_down, precision=highest))

def flat_group(group, grad_qkv, grad_out, grad_in, grad_down):
    cols_q = grad_qkv.shape[1] // N_MP
    rows_o = grad_out.shape[0] // N_MP
    cols_i = grad_in.shape[1] // N_MP
    rows_d = grad_down.shape[0] // N_MP
    pieces = [grad_qkv[:, group * cols_q:(group + 1) * cols_q].reshape(-1, 128), grad_out[group * rows_o:(group + 1) * rows_o].reshape(-1, 128), grad_in[:, group * cols_i:(group + 1) * cols_i].reshape(-1, 128), grad_down[group * rows_d:(group + 1) * rows_d].reshape(-1, 128)]
    return jnp.concatenate(pieces, axis=0).reshape(NBLK, BR, 128)

def reference(tokens, cotangent, lengths, owners, w_qkv, w_out, w_in, w_down, master, first_moment, second_moment, norm_gains, norm_biases, norm_first, norm_second):
    mat_qkv = w_qkv.astype(jnp.float32)
    mat_out = w_out.astype(jnp.float32)
    mat_in = w_in.astype(jnp.float32)
    mat_down = w_down.astype(jnp.float32)

    def one_sequence(running, inputs):
        seq_tokens, seq_cot, length = inputs
        valid = (jnp.arange(SEQ_LEN, dtype=jnp.int32) < length).astype(jnp.float32)
        grad_seq = seq_cot.astype(jnp.float32) * valid[:, None]

        def forward(a_in, a_qkv, a_out, a_inw, a_down, a_gain, a_bias):
            return block_forward(a_in, a_qkv, a_out, a_inw, a_down, a_gain, a_bias, length)
        result, backward = jax.vjp(forward, seq_tokens.astype(jnp.float32), mat_qkv, mat_out, mat_in, mat_down, norm_gains, norm_biases)
        grads = backward(grad_seq)
        running = tuple((old + new for old, new in zip(running, grads[1:])))
        return (running, (result.astype(jnp.bfloat16), grads[0]))
    zeros = tuple((jnp.zeros_like(item) for item in (mat_qkv, mat_out, mat_in, mat_down, norm_gains, norm_biases)))
    sums, (outputs, tokens_grad) = lax.scan(one_sequence, zeros, (tokens, cotangent, lengths))
    corr_one = 1.0 - beta_one ** STEP
    corr_two = 1.0 - beta_two ** STEP
    norm_grad = jnp.stack([sums[4][0], sums[5][0], sums[4][1], sums[5][1]])
    norm_params = jnp.stack([norm_gains[0], norm_biases[0], norm_gains[1], norm_biases[1]])
    norm_first_new = beta_one * norm_first + (1.0 - beta_one) * norm_grad
    norm_second_new = beta_two * norm_second + (1.0 - beta_two) * norm_grad * norm_grad
    norm_new = norm_params - norm_rate * (norm_first_new / corr_one / (jnp.sqrt(norm_second_new / corr_two) + adam_epsilon))
    grad_blocks = jnp.concatenate([flat_group(group, sums[0], sums[1], sums[2], sums[3]) for group in range(N_MP)], axis=1)
    onehot = (owners[:, None] == jnp.arange(SEQS, dtype=jnp.int32)[None, :]).astype(jnp.int32)
    slot_index = lax.optimization_barrier(jnp.sum(jnp.cumsum(onehot, axis=0) * onehot, axis=1)) - 1
    slot_rows = (owners * CAP + slot_index).astype(jnp.int32)
    first_old = first_moment[slot_rows]
    second_old = second_moment[slot_rows]
    master_old = master[slot_rows]
    first_blk = beta_one * first_old + (1.0 - beta_one) * grad_blocks
    second_blk = beta_two * second_old + (1.0 - beta_two) * grad_blocks * grad_blocks
    master_blk = master_old - learn_rate * (first_blk / corr_one / (jnp.sqrt(second_blk / corr_two) + adam_epsilon) + decay_rate * master_old)
    first_new = first_moment.at[slot_rows].set(first_blk)
    second_new = second_moment.at[slot_rows].set(second_blk)
    master_new = master.at[slot_rows].set(master_blk)
    rows_q = D * (3 * D // N_MP) // 128
    rows_o = D // N_MP * D // 128
    rows_i = D * (FF // N_MP) // 128
    parts_q, parts_o, parts_i, parts_d = ([], [], [], [])
    for group in range(N_MP):
        flat = master_blk[:, group * BR:(group + 1) * BR].reshape(NBLK * BR, 128)
        parts_q.append(flat[:rows_q].reshape(D, 3 * D // N_MP))
        parts_o.append(flat[rows_q:rows_q + rows_o].reshape(D // N_MP, D))
        parts_i.append(flat[rows_q + rows_o:rows_q + rows_o + rows_i].reshape(D, FF // N_MP))
        parts_d.append(flat[rows_q + rows_o + rows_i:].reshape(FF // N_MP, D))
    new_qkv = jnp.concatenate(parts_q, axis=1).astype(jnp.bfloat16)
    new_out = jnp.concatenate(parts_o, axis=0).astype(jnp.bfloat16)
    new_in = jnp.concatenate(parts_i, axis=1).astype(jnp.bfloat16)
    new_down = jnp.concatenate(parts_d, axis=0).astype(jnp.bfloat16)
    return (outputs, tokens_grad, first_new, second_new, master_new, new_qkv, new_out, new_in, new_down, norm_first_new, norm_second_new, norm_new)
```

```python
import functools

import jax
import jax.numpy as jnp
from jax import lax
from jax.experimental import pallas as pl
from jax.experimental.pallas import tpu as pltpu
from jax.sharding import PartitionSpec as P

HEAD = 64
BAND = 30
STEP = 10
HALO = 64
EDGE = 32
QB = 64
WIN = 128
PAIR = 128
STATE = 144

learn_rate = 0.1
norm_rate = 0.3
decay_rate = 0.1
beta_one = 0.9
beta_two = 0.95
adam_epsilon = 1e-08
norm_epsilon = 1e-05
GELU_C = 0.7978845608028654
GELU_A = 0.044715

f32 = jnp.float32
bf16 = jnp.bfloat16

VM = pl.BlockSpec(memory_space=pltpu.VMEM)
SM = pl.BlockSpec(memory_space=pltpu.SMEM)
ANY = pl.BlockSpec(memory_space=pl.ANY)


def call(body, outs, in_specs, scratch, flops, moved, vmem=48):
    return pl.pallas_call(
        body,
        out_shape=tuple(jax.ShapeDtypeStruct(s, d) for s, d in outs),
        in_specs=in_specs,
        out_specs=tuple(VM for _ in outs),
        scratch_shapes=scratch,
        compiler_params=pltpu.CompilerParams(vmem_limit_bytes=vmem << 20),
        cost_estimate=pl.CostEstimate(flops=flops, bytes_accessed=moved, transcendentals=0),
    )


def dot(a, b):
    return jnp.dot(a, b, preferred_element_type=f32)


def dot_nt(a, b):
    return lax.dot_general(a, b, (((1,), (1,)), ((), ())), preferred_element_type=f32)


def dot_tn(a, b):
    return lax.dot_general(a, b, (((0,), (0,)), ((), ())), preferred_element_type=f32)


def normalize(x):
    mean = jnp.mean(x, axis=-1, keepdims=True)
    cen = x - mean
    var = jnp.mean(cen * cen, axis=-1, keepdims=True)
    rstd = lax.rsqrt(var + norm_epsilon)
    return cen * rstd, rstd


def same_head(n=PAIR):
    r = lax.broadcasted_iota(jnp.int32, (n, n), 0)
    c = lax.broadcasted_iota(jnp.int32, (n, n), 1)
    return (r < HEAD) == (c < HEAD)


def pack_state(s1, s2, z):
    both = jnp.where(same_head(), s1, pltpu.roll(s2, HEAD, 1))
    hi = z.astype(bf16).astype(f32)
    row = lax.broadcasted_iota(jnp.int32, (16, PAIR), 0)
    tail = jnp.where(row == 0, hi, jnp.where(row == 1, z - hi, 0.0))
    return both.astype(bf16), tail.astype(bf16)


def unpack_state(refs, g):
    tot = refs[0][g].astype(f32)
    for r in refs[1:]:
        tot = tot + r[g].astype(f32)
    both = tot[:PAIR]
    diag = same_head()
    s1 = jnp.where(diag, both, 0.0)
    s2 = jnp.where(diag, pltpu.roll(both, HEAD, 1), 0.0)
    z = tot[PAIR : PAIR + 1] + tot[PAIR + 1 : PAIR + 2]
    return s1, s2, z


def split_dot(a, ones):
    hi, lo = two(a)
    return dot(hi, ones) + dot(lo, ones)


def two(a):
    hi = a.astype(bf16)
    return hi, (a - hi.astype(f32)).astype(bf16)


def phi(v):
    low = jnp.exp(jnp.minimum(v, 0.0))
    return jnp.where(v > 0, v + 1.0, low), jnp.where(v > 0, 1.0, low)


def band_parts():
    r = lax.broadcasted_iota(jnp.int32, (2 * QB, WIN), 0) % QB
    c = lax.broadcasted_iota(jnp.int32, (2 * QB, WIN), 1)
    off = r + EDGE - c
    return (jnp.abs(off) <= BAND), off == 0, c[:1]


def stacked(rows):
    lane = lax.broadcasted_iota(jnp.int32, (1, PAIR), 1)
    first = (lane < HEAD).astype(f32).astype(bf16)
    second = (lane >= HEAD).astype(f32).astype(bf16)
    return jnp.concatenate([rows * first, rows * second], axis=0)


def unstack(both):
    lane = lax.broadcasted_iota(jnp.int32, (QB, PAIR), 1)
    return jnp.where(lane < HEAD, both[:QB], both[QB:])


def softmax_block(qs, kw, mask):
    scores = jnp.where(mask, dot_nt(qs, kw) * 0.125, -1e30)
    top = jnp.max(scores, axis=-1, keepdims=True)
    ex = jnp.exp(scores - top)
    return ex / jnp.sum(ex, axis=-1, keepdims=True)


def fetch_pieces(meta, own, oth, lo, rows, place, sem):
    groups = own.shape[1]
    core = meta[2]
    copies = []
    for pq in range(4):
        for buf, row, half in ((own, meta[3 + pq], core), (oth, meta[7 + pq], 1 - core)):
            for g in range(groups):
                src = buf.at[row, g, pl.ds(lo, rows), :]
                copies.append(pltpu.make_async_copy(src, place(g, half * 4 + pq), sem))
    for c in copies:
        c.start()
    return copies


def qkv_body(meta, tok, left, right, gains, biases, own, oth, qkv_o, a1_o, st_o, w_o, a1e, sem):
    rows = tok.shape[0]
    groups = own.shape[1]
    pr = own.shape[2]
    copies = fetch_pieces(
        meta, own, oth, 0, pr,
        lambda g, p: w_o.at[g, pl.ds(pl.multiple_of(p * pr, pr), pr), :], sem,
    )
    gain, bias = gains[0:1, :], biases[0:1, :]

    def ln(x):
        return (normalize(x.astype(f32))[0] * gain + bias).astype(bf16)

    a1e[0:HALO, :] = ln(left[...])
    a1e[HALO + rows :, :] = ln(right[...])

    def chunk(i, _):
        at = pl.ds(pl.multiple_of(i * 64, 64), 64)
        val = ln(tok[at, :])
        a1_o[at, :] = val
        a1e[pl.ds(pl.multiple_of(i * 64 + HALO, 64), 64), :] = val
        return 0

    lax.fori_loop(0, rows // 64, chunk, 0)
    for c in copies:
        c.wait()
    length, base = meta[0], meta[1]
    pos = base + lax.broadcasted_iota(jnp.int32, (rows, 1), 0)
    valid = (pos < length).astype(f32)
    for g in range(groups):
        qkv_o[g] = dot(a1e[...], w_o[g]).astype(bf16)
        keys = qkv_o[g, HALO : HALO + rows, PAIR : 2 * PAIR].astype(f32)
        vals = qkv_o[g, HALO : HALO + rows, 2 * PAIR :]
        feat = phi(keys)[0] * valid
        z = jnp.sum(feat, axis=0, keepdims=True)
        fhi, flo = two(feat)
        thi, tlo = two(jnp.tanh(keys) * valid)
        s1 = dot_tn(fhi, vals) + dot_tn(flo, vals)
        s2 = dot_tn(thi, vals) + dot_tn(tlo, vals)
        st_o[g, :PAIR, :], st_o[g, PAIR:, :] = pack_state(s1, s2, z)


def near_body(meta, qkv, near_o):
    groups = qkv.shape[0]
    rows = near_o.shape[0]
    length, base = meta[0], meta[1]
    band, diag, lane = band_parts()

    def block(b, _):
        at = b * QB
        kpos = base + at - EDGE + lane
        mask = band & (((kpos >= 0) & (kpos < length)) | diag)
        q_at = pl.ds(pl.multiple_of(at + HALO, QB), QB)
        w_at = pl.ds(pl.multiple_of(at + HALO - EDGE, EDGE), WIN)
        for g in range(groups):
            qs = stacked(qkv[g, q_at, 0:PAIR])
            p = softmax_block(qs, qkv[g, w_at, PAIR : 2 * PAIR], mask)
            res = dot(p.astype(bf16), qkv[g, w_at, 2 * PAIR :])
            near_o[pl.ds(pl.multiple_of(at, QB), QB), g * PAIR : (g + 1) * PAIR] = unstack(res)
        return 0

    lax.fori_loop(0, rows // QB, block, 0)


def main_body(
    meta, near, qkv, s0, s1, s2, s3, tok, cot, gains, biases, own, oth,
    out_o, do_o, dx2_o, ctx_o, a2_o, dm_o, hid_o, du_o, dctx_o, dqf_o, dst_o, ng_o, wout_o,
    w_in, w_down, x2, u, dh, acc, da2, far1, inv, dnum, phq, thq, sem,
):
    groups = own.shape[1]
    rows, width = tok.shape
    pr, orow = 64 * own.shape[2] // 144, own.shape[2] // 9
    length, base = meta[0], meta[1]
    copies = fetch_pieces(
        meta, own, oth, 2 * pr, orow,
        lambda g, p: wout_o.at[pl.ds(pl.multiple_of(g * 8 * orow + p * orow, orow), orow), :], sem.at[0],
    )
    later = fetch_pieces(
        meta, own, oth, 0, pr,
        lambda g, p: w_in.at[g, pl.ds(pl.multiple_of(p * pr, pr), pr), :], sem.at[1],
    )
    later += fetch_pieces(
        meta, own, oth, pr, pr,
        lambda g, p: w_down.at[g, pl.ds(pl.multiple_of(p * pr, pr), pr), :], sem.at[2],
    )
    rlen = 1.0 / length.astype(f32)
    gain, bias = gains[1:2, :], biases[1:2, :]
    ones = same_head().astype(f32).astype(bf16)
    states = [unpack_state((s0, s1, s2, s3), g) for g in range(groups)]
    cr = 128

    def far_chunk(i, _):
        at = pl.ds(pl.multiple_of(i * cr, cr), cr)
        q_at = pl.ds(pl.multiple_of(i * cr + HALO, HALO), cr)
        for g in range(groups):
            cols = slice(g * PAIR, (g + 1) * PAIR)
            st1, st2, z = states[g]
            q = qkv[g, q_at, 0:PAIR].astype(f32)
            ph = phi(q)[0]
            phi_hi, phi_lo = two(ph)
            th_hi, th_lo = two(jnp.tanh(q))
            s1_hi, s1_lo = two(st1)
            s2_hi, s2_lo = two(st2)
            phq[at, cols] = phi_hi
            thq[at, cols] = th_hi
            rec = 1.0 / split_dot(ph * z, ones)
            part = (dot(phi_hi, s1_hi) + dot(phi_hi, s1_lo) + dot(phi_lo, s1_hi)) * rec
            part2 = dot(th_hi, s2_hi) + dot(th_hi, s2_lo) + dot(th_lo, s2_hi)
            inv[at, cols] = rec
            far1[at, cols] = part
            full = near[at, cols] + (part + part2 * rlen)
            ctx_o[at, cols] = full.astype(bf16)
        pos = base + i * cr + lax.broadcasted_iota(jnp.int32, (cr, 1), 0)
        dm_o[at, :] = (cot[at, :].astype(f32) * (pos < length).astype(f32)).astype(bf16)
        return 0

    lax.fori_loop(0, rows // cr, far_chunk, 0)
    for c in copies:
        c.wait()
    x2[...] = dot(ctx_o[...], wout_o[...])

    def norm_chunk(i, _):
        at = pl.ds(pl.multiple_of(i * 32, 32), 32)
        val = x2[at, :] + tok[at, :].astype(f32)
        x2[at, :] = val
        a2_o[at, :] = (normalize(val)[0] * gain + bias).astype(bf16)
        return 0

    lax.fori_loop(0, rows // 32, norm_chunk, 0)
    for c in later:
        c.wait()
    for g in range(groups):
        u[...] = dot(a2_o[...], w_in[g])
        dh[...] = dot_nt(dm_o[...], w_down[g])

        def act(i, _, g=g):
            at = pl.ds(pl.multiple_of(i * 16, 16), 16)
            v = u[at, :]
            sq = v * v
            t = jnp.tanh(GELU_C * v * (1.0 + GELU_A * sq))
            half = 0.5 * (1.0 + t)
            hid_o[g, at, :] = (v * half).astype(bf16)
            slope = half + 0.5 * v * (1.0 - t * t) * (GELU_C * (1.0 + 3.0 * GELU_A * sq))
            du_o[g, at, :] = (dh[at, :] * slope).astype(bf16)
            return 0

        lax.fori_loop(0, rows // 16, act, 0)
        if g == 0:
            acc[...] = dot(hid_o[g], w_down[g])
            da2[...] = dot_nt(du_o[g], w_in[g])
        else:
            acc[...] += dot(hid_o[g], w_down[g])
            da2[...] += dot_nt(du_o[g], w_in[g])

    def back_chunk(i, carry):
        dg, db = carry
        at = pl.ds(pl.multiple_of(i * 32, 32), 32)
        val = x2[at, :]
        out_o[at, :] = (val + acc[at, :]).astype(bf16)
        xh, rstd = normalize(val)
        d = da2[at, :]
        dg = dg + jnp.sum(d * xh, axis=0, keepdims=True)
        db = db + jnp.sum(d, axis=0, keepdims=True)
        e = d * gain
        m1 = jnp.mean(e, axis=-1, keepdims=True)
        m2 = jnp.mean(e * xh, axis=-1, keepdims=True)
        dx = dm_o[at, :].astype(f32) + rstd * (e - m1 - xh * m2)
        dx2_o[at, :] = dx
        do_o[at, :] = dx.astype(bf16)
        return dg, db

    zero = jnp.zeros((1, width), f32)
    dg, db = lax.fori_loop(0, rows // 32, back_chunk, (zero, zero))
    ng_o[0:1, :] = dg
    ng_o[1:2, :] = db
    dctx_o[...] = dot_nt(do_o[...], wout_o[...]).astype(bf16)

    def far_back(i, carry):
        at = pl.ds(pl.multiple_of(i * cr, cr), cr)
        q_at = pl.ds(pl.multiple_of(i * cr + HALO, HALO), cr)
        out = []
        for g in range(groups):
            cols = slice(g * PAIR, (g + 1) * PAIR)
            st1, st2, z = states[g]
            q = qkv[g, q_at, 0:PAIR].astype(f32)
            slope = phi(q)[1]
            th = thq[at, cols].astype(f32)
            dc = dctx_o[at, cols]
            dcf = dc.astype(f32)
            rec = inv[at, cols]
            dn = (dcf * rec).astype(bf16)
            dnum[at, cols] = dn
            dden = -split_dot(dcf * far1[at, cols], ones) * rec
            out.append(carry[g] + jnp.sum(phq[at, cols].astype(f32) * dden, axis=0, keepdims=True))
            dphi = dot_nt(dn, st1.astype(bf16)) + dden * z
            dth = dot_nt(dc, st2.astype(bf16)) * rlen
            dqf_o[at, cols] = dphi * slope + dth * (1.0 - th * th)
        return tuple(out)

    none = jnp.zeros((1, PAIR), f32)
    dz = lax.fori_loop(0, rows // cr, far_back, (none,) * groups)
    for g in range(groups):
        cols = slice(g * PAIR, (g + 1) * PAIR)
        d1 = dot_tn(phq[:, cols], dnum[:, cols])
        d2 = dot_tn(thq[:, cols], dctx_o[:, cols]) * rlen
        dst_o[g, :PAIR, :], dst_o[g, PAIR:, :] = pack_state(d1, d2, dz[g])


def put_halves(core, ref, g, lo, grad):
    n, width = grad.shape
    tiles = grad.reshape(n // 16, 2, 8, width)
    for h in range(2):
        half = tiles[:, h].reshape(n // 2, width).astype(ref.dtype)
        ref[h ^ core, g, lo : lo + n // 2, :] = half


def grads_body(meta, ctx, do, a2, dm, hid, du, g_o):
    core = meta[2]
    groups, rows, width = hid.shape
    n_out = ctx.shape[1] // groups
    for g in range(groups):
        put_halves(core, g_o, g, 0, dot_tn(ctx[:, g * n_out : (g + 1) * n_out], do[...]))
        put_halves(core, g_o, g, n_out // 2, dot_tn(a2[...], du[g]))
        put_halves(core, g_o, g, n_out // 2 + width // 2, dot_tn(hid[g], dm[...]))


def near_back_body(meta, qkv, dctx, do_l, do_r, wout, dqf, dq_o, dk_o, dv_o, dce, dqe, dke, dve):
    groups = qkv.shape[0]
    rows = dctx.shape[0]
    length, base = meta[0], meta[1]
    band, diag, lane = band_parts()
    dce[0:EDGE, :] = dot_nt(do_l[...], wout[...]).astype(bf16)
    dce[EDGE : EDGE + rows, :] = dctx[...]
    dce[EDGE + rows :, :] = dot_nt(do_r[...], wout[...]).astype(bf16)
    dke[...] = jnp.zeros(dke.shape, f32)
    dve[...] = jnp.zeros(dve.shape, f32)

    def block(b, _):
        at = b * QB
        kpos = base + at - HALO + lane
        mask = band & (((kpos >= 0) & (kpos < length)) | diag)
        c_at = pl.ds(pl.multiple_of(at, QB), QB)
        q_at = pl.ds(pl.multiple_of(at + EDGE, EDGE), QB)
        w_at = pl.ds(pl.multiple_of(at, QB), WIN)
        for g in range(groups):
            cols = slice(g * PAIR, (g + 1) * PAIR)
            qs = stacked(qkv[g, q_at, 0:PAIR])
            kw = qkv[g, w_at, PAIR : 2 * PAIR]
            p = softmax_block(qs, kw, mask)
            ds_ = stacked(dce[c_at, cols])
            dp = dot_nt(ds_, qkv[g, w_at, 2 * PAIR :])
            row = jnp.sum(p * dp, axis=-1, keepdims=True)
            dsc = (p * (dp - row)).astype(bf16)
            dqe[c_at, cols] = unstack(dot(dsc, kw))
            dke[w_at, cols] += dot_tn(dsc, qs)
            dve[w_at, cols] += dot_tn(p.astype(bf16), ds_)
        return 0

    lax.fori_loop(0, rows // QB + 1, block, 0)
    dq_o[...] = (dqe[EDGE : EDGE + rows, :] * 0.125 + dqf[...]).astype(bf16)
    dk_o[...] = dke[HALO : HALO + rows, :] * 0.125
    dv_o[...] = dve[HALO : HALO + rows, :]


def last_body(
    meta, qkv, dq, dkn, dvn, s0, s1, s2, s3, wqkv, a1, tok, dx2, gains, ng2,
    tg_o, gq_o, ng_o, dproj, da1, flat, pseudo, ngs,
):
    groups = qkv.shape[0]
    rows, width = tok.shape
    length, base, core = meta[0], meta[1], meta[2]
    gain = gains[0:1, :]
    cr = 128
    states = [unpack_state((s0, s1, s2, s3), g) for g in range(groups)]

    def far_chunk(i, _):
        at = pl.ds(pl.multiple_of(i * cr, cr), cr)
        e_at = pl.ds(pl.multiple_of(i * cr + HALO, HALO), cr)
        pos = base + i * cr + lax.broadcasted_iota(jnp.int32, (cr, 1), 0)
        valid = (pos < length).astype(f32)
        for g in range(groups):
            cols = slice(g * PAIR, (g + 1) * PAIR)
            d1, d2, dz = states[g]
            d1, d2 = d1.astype(bf16), d2.astype(bf16)
            k = qkv[g, e_at, PAIR : 2 * PAIR].astype(f32)
            v = qkv[g, e_at, 2 * PAIR :]
            ph, slope = phi(k)
            th = jnp.tanh(k)
            dk = (dot_nt(v, d1) + dz) * slope + dot_nt(v, d2) * (1.0 - th * th)
            dv = dot((ph * valid).astype(bf16), d1) + dot((th * valid).astype(bf16), d2)
            dproj[g, at, 0:PAIR] = dq[at, cols]
            dproj[g, at, PAIR : 2 * PAIR] = (dkn[at, cols] + dk * valid).astype(bf16)
            dproj[g, at, 2 * PAIR :] = (dvn[at, cols] + dv).astype(bf16)
        return 0

    lax.fori_loop(0, rows // cr, far_chunk, 0)
    n_flat = 3 * width
    for g in range(groups):
        grad = dot_tn(a1[...], dproj[g])
        for part in range(3):
            flat[pl.ds(part, width, stride=3), :] = grad[:, part * PAIR : (part + 1) * PAIR]
        for j in range(4):
            pseudo[:, j * 128 : (j + 1) * 128] = flat[pl.ds(j, n_flat // 4, stride=4), :]
        put_halves(core, gq_o, g, 0, pseudo[...])
        if g == 0:
            da1[...] = dot_nt(dproj[g], wqkv[g])
        else:
            da1[...] += dot_nt(dproj[g], wqkv[g])

    def back_chunk(i, carry):
        dg, db = carry
        at = pl.ds(pl.multiple_of(i * 32, 32), 32)
        xh, rstd = normalize(tok[at, :].astype(f32))
        d = da1[at, :]
        dg = dg + jnp.sum(d * xh, axis=0, keepdims=True)
        db = db + jnp.sum(d, axis=0, keepdims=True)
        e = d * gain
        m1 = jnp.mean(e, axis=-1, keepdims=True)
        m2 = jnp.mean(e * xh, axis=-1, keepdims=True)
        tg_o[at, :] = dx2[at, :] + rstd * (e - m1 - xh * m2)
        return dg, db

    zero = jnp.zeros((1, width), f32)
    dg, db = lax.fori_loop(0, rows // 32, back_chunk, (zero, zero))
    for k, val in enumerate((dg, db, ng2[0:1, :], ng2[1:2, :])):
        for j in range(width // 128):
            at = k * (width // 128) + j
            ngs[at : at + 1, :] = val[:, j * 128 : (j + 1) * 128]
    n = ngs.shape[0]
    hi = ngs[...].astype(bf16)
    ng_o[0:n, :] = hi
    ng_o[n:, :] = (ngs[...] - hi.astype(f32)).astype(bf16)


def route_body(blocks, zq, zm, send_o, piece, ngs):
    n_ng = 2 * ngs.shape[0]
    nq = zq.shape[1] - n_ng
    nm = zm.shape[1]
    dests, per, _ = send_o.shape
    caps = (per - n_ng) // 8
    src = range(zq.shape[0])
    piece[0:nq, :] = sum(zq[s, 0:nq, :].astype(f32) for s in src)
    piece[nq:, :] = sum(zm[s].astype(f32) for s in src)
    half = n_ng // 2
    ngs[...] = sum(zq[s, nq : nq + half, :].astype(f32) + zq[s, nq + half :, :].astype(f32) for s in src)
    hi = ngs[...].astype(bf16)
    lo = (ngs[...] - hi.astype(f32)).astype(bf16)

    def dest(d, _):
        for r in range(0, caps, 2):
            pair = [
                piece[pl.ds(pl.multiple_of(blocks[d * caps + r + k] * 8, 8), 8), :] for k in range(2)
            ]
            send_o[d, r * 8 : r * 8 + 16, :] = jnp.concatenate(pair, axis=0)
        send_o[d, caps * 8 : caps * 8 + half, :] = hi.astype(f32)
        send_o[d, caps * 8 + half :, :] = lo.astype(f32)
        return 0

    lax.fori_loop(0, dests, dest, 0)


def adam_body(filled, sources, recv, master, first, second, f_o, s_o, m_o, w_o, ng_o, two, grad):
    caps, br, _ = master.shape
    n_ng = recv.shape[1] - caps * 8
    corr_one = 1.0 - beta_one**STEP
    corr_two = 1.0 - beta_two**STEP
    for j in range(4):
        for c in range(2):
            two[:, c] = recv[sources[c * 4 + j], 0 : caps * 8, :].astype(f32).reshape(caps, 8, 128)
        grad[pl.ds(j, caps * 16, stride=4), :] = two[...].reshape(caps * 16, 128)
    half = n_ng // 2

    def add(s, tot):
        part = recv[s, caps * 8 :, :].astype(f32)
        return tot + (part[:half] + part[half:])

    ng_o[...] = lax.fori_loop(0, recv.shape[0], add, jnp.zeros(ng_o.shape, f32))

    def slot(r, _):
        g = grad[pl.ds(pl.multiple_of(r * br, br), br), :]
        m_old, f_old, s_old = master[r], first[r], second[r]
        fn = beta_one * f_old + (1.0 - beta_one) * g
        sn = beta_two * s_old + (1.0 - beta_two) * g * g
        step = fn / corr_one / (jnp.sqrt(sn / corr_two) + adam_epsilon)
        mn = m_old - learn_rate * (step + decay_rate * m_old)
        keep = jnp.full(g.shape, filled[r], jnp.int32) > 0
        f_o[r] = jnp.where(keep, fn, f_old)
        s_o[r] = jnp.where(keep, sn, s_old)
        m_o[r] = jnp.where(keep, mn, m_old)
        grad[pl.ds(pl.multiple_of(r * br, br), br), :] = mn
        return 0

    lax.fori_loop(0, caps, slot, 0)
    for j in range(4):
        val = grad[pl.ds(j, caps * 16, stride=4), :].astype(bf16)
        w_o[:, :, j * 128 : (j + 1) * 128] = val.reshape(caps, 16, 128)


def place_body(other, index, own, oth, q_o, out_o, in_o, down_o, pseudo, flat):
    def block(b):
        take = jnp.full((16, 512), other[b], jnp.int32) > 0
        return jnp.where(take, oth[index[b]].astype(f32), own[index[b]].astype(f32))

    first = 0
    for ref in (pseudo, out_o, in_o, down_o):
        n = ref.shape[0] // 16

        def move(b, _, ref=ref, first=first):
            ref[pl.ds(pl.multiple_of(b * 16, 16), 16), :] = block(first + b).astype(ref.dtype)
            return 0

        lax.fori_loop(0, n, move, 0)
        first += n
    rows = q_o.shape[0]
    for j in range(4):
        flat[pl.ds(j, 3 * rows // 4, stride=4), :] = pseudo[:, j * 128 : (j + 1) * 128]
    for part in range(3):
        q_o[:, part * 128 : (part + 1) * 128] = flat[pl.ds(part, rows, stride=3), :].astype(bf16)


def per_device(
    tokens, cotangent, lengths, owners, w_qkv, w_out, w_in, w_down,
    master, first_moment, second_moment, norm_gains, norm_biases, norm_first, norm_second,
):
    rows, width = tokens.shape[1], tokens.shape[2]
    groups = lax.axis_size("mp")
    ndp = lax.axis_size("dp")
    nbits = ndp.bit_length() - 1
    rest = list(range(1, nbits))
    order = (rest, rest[:2][::-1] + rest[2:][::-1])
    me, zi = lax.axis_index("dp"), lax.axis_index("mp")
    core = me & 1

    def bit_of(who, at, s):
        return (who >> jnp.where(at == 0, order[0][s], order[1][s])) & 1

    def swap(x, s):
        return lax.ppermute(x, "dp", [(i, i ^ (1 << order[i & 1][s])) for i in range(ndp)])

    def swap_core(x):
        return lax.ppermute(x, "dp", [(i, i ^ 1) for i in range(ndp)])

    def from_mp(x, step):
        return lax.ppermute(x, "mp", [(i, i + step) for i in range(groups) if 0 <= i + step < groups])

    def swap_mp(x, mask):
        return lax.ppermute(x, "mp", [(i, i ^ mask) for i in range(groups)])

    def exchange(x, axis):
        return lax.all_to_all(x, axis, 0, 0, tiled=True)

    def all_states(x):
        return [x] + [swap_mp(x, m) for m in range(1, groups)]

    q0, q1 = bit_of(me, core, 0), bit_of(me, core, 1)
    o0, o1 = bit_of(me, 1 - core, 0), bit_of(me, 1 - core, 1)
    length = lengths[0]
    base = zi * rows
    ids = [length, base, core]
    ids += [((t >> 1) ^ q0) + 2 * ((t & 1) ^ q1) for t in range(4)]
    ids += [((t >> 1) ^ o0) + 2 * ((t & 1) ^ o1) for t in range(4)]
    meta = jnp.stack(ids).astype(jnp.int32)

    def gather(piece):
        buf = exchange(jnp.broadcast_to(piece, (groups,) + piece.shape), "mp")[None]
        for s in range(2):
            buf = jnp.concatenate([buf, swap(buf, s)], axis=0)
        return buf, swap_core(buf)

    mine = core * 4 + q0 * 2 + q1

    def part_of(w):
        n = w.shape[0] // 8
        return lax.dynamic_slice_in_dim(w, mine * n, n, 0)

    tok, cot = tokens[0], cotangent[0]
    left, right = from_mp(tok[rows - HALO :], 1), from_mp(tok[:HALO], -1)
    qkv_own, qkv_oth = gather(part_of(w_qkv))
    ffn_own, ffn_oth = gather(jnp.concatenate([part_of(w_in), part_of(w_down), part_of(w_out)], axis=0))

    ext = rows + 2 * HALO
    mm = 2 * rows * width
    qkv, a1, state, wqkv = call(
        qkv_body,
        [
            ((groups, ext, 3 * PAIR), bf16), ((rows, width), bf16),
            ((groups, STATE, PAIR), bf16), ((groups, width, 3 * PAIR), bf16),
        ],
        [SM] + [VM] * 5 + [ANY] * 2,
        [pltpu.VMEM((ext, width), bf16), pltpu.SemaphoreType.DMA],
        2 * ext * width * 3 * width, 6 << 20,
    )(meta, tok, left, right, norm_gains, norm_biases, qkv_own, qkv_oth)
    states = all_states(state)
    [near] = call(
        near_body, [((rows, width), f32)], [SM, VM], [], mm * 1024, 12 << 20,
    )(meta, qkv)

    hid_w = w_in.shape[1]
    big = pltpu.VMEM((rows, width), f32)
    low = pltpu.VMEM((rows, width), bf16)
    (outputs, do, dx2, ctx, a2, dm, hid, du, dctx, dqf, dstate, ng2, wout) = call(
        main_body,
        [
            ((rows, width), bf16), ((rows, width), bf16), ((rows, width), f32), ((rows, width), bf16),
            ((rows, width), bf16), ((rows, width), bf16), ((groups, rows, hid_w), bf16),
            ((groups, rows, hid_w), bf16), ((rows, width), bf16), ((rows, width), f32),
            ((groups, STATE, PAIR), bf16), ((2, width), f32), ((width, width), bf16),
        ],
        [SM] + [VM] * 10 + [ANY] * 2,
        [
            pltpu.VMEM((groups, width, hid_w), bf16), pltpu.VMEM((groups, hid_w, width), bf16),
            big, pltpu.VMEM((rows, hid_w), f32), pltpu.VMEM((rows, hid_w), f32), big, big, big, big,
            low, low, low, pltpu.SemaphoreType.DMA((3,)),
        ],
        mm * hid_w * groups * 4, 24 << 20,
    )(meta, near, qkv, *states, tok, cot, norm_gains, norm_biases, ffn_own, ffn_oth)

    dstates = all_states(dstate)
    do_l, do_r = from_mp(do[rows - EDGE :], 1), from_mp(do[:EDGE], -1)
    n_m = (w_out.shape[0] + w_in.shape[0] + w_down.shape[0]) // 2
    [grad_m] = call(
        grads_body, [((2, groups, n_m, width), bf16)], [SM] + [VM] * 6, [],
        mm * (2 * hid_w * groups + width), 12 << 20,
    )(meta, ctx, do, a2, dm, hid, du)

    def reduce(both, extra=None):
        tot = both[0].astype(f32) + swap_core(both[1]).astype(f32)
        for s in range(nbits - 1):
            if s < 2:
                n = tot.shape[-1] // 2
                bit = bit_of(me, core, s)
                give = lax.dynamic_slice_in_dim(tot, (1 - bit) * n, n, 2).astype(bf16)
                tot = lax.dynamic_slice_in_dim(tot, bit * n, n, 2) + swap(give, s).astype(f32)
            else:
                tot = tot.astype(bf16).astype(f32) + swap(tot.astype(bf16), s).astype(f32)
        msg = tot.astype(bf16)
        if extra is not None:
            more = jnp.broadcast_to(extra, (groups,) + extra.shape)
            msg = jnp.concatenate([msg, more], axis=1)
        return exchange(msg, "mp")

    z_m = reduce(grad_m)
    dq, dkn, dvn = call(
        near_back_body,
        [((rows, width), bf16), ((rows, width), f32), ((rows, width), f32)],
        [SM] + [VM] * 6,
        [
            pltpu.VMEM((rows + 2 * EDGE, width), bf16), pltpu.VMEM((rows + 2 * EDGE, width), f32),
            pltpu.VMEM((ext, width), f32), pltpu.VMEM((ext, width), f32),
        ],
        mm * 2048, 24 << 20,
    )(meta, qkv, dctx, do_l, do_r, wout, dqf)
    n_q = w_qkv.size // width // 2
    n_ng = 4 * width // 128
    tokens_grad, grad_q, ng = call(
        last_body,
        [((rows, width), f32), ((2, groups, n_q, width), f32), ((2 * n_ng, 128), bf16)],
        [SM] + [VM] * 14,
        [
            pltpu.VMEM((groups, rows, 3 * PAIR), bf16), big, pltpu.VMEM((3 * width, 128), f32),
            pltpu.VMEM((2 * n_q, width), f32), pltpu.VMEM((n_ng, 128), f32),
        ],
        mm * 6 * width, 24 << 20,
    )(meta, qkv, dq, dkn, dvn, *dstates, wqkv, a1, tok, dx2, norm_gains, ng2)
    z_q = reduce(grad_q, ng)

    capacity, block_rows = master.shape[0], master.shape[1]
    blocks = owners.shape[0]
    earlier = jnp.arange(blocks)[None, :] < jnp.arange(blocks)[:, None]
    alike = owners[None, :] == owners[:, None]
    slot = jnp.sum((earlier & alike).astype(jnp.int32), axis=1)
    slot_rows = owners * capacity + slot
    hit = slot_rows[None, :] == jnp.arange(ndp * capacity, dtype=jnp.int32)[:, None]
    held = jnp.sum(jnp.where(hit, jnp.arange(blocks, dtype=jnp.int32)[None, :], 0), axis=1)
    filled = lax.dynamic_slice_in_dim(
        jnp.sum(hit.astype(jnp.int32), axis=1), me * capacity, capacity, 0
    )
    per = capacity * 8 + 2 * n_ng
    [send] = call(
        route_body, [((ndp, per, 128), f32)], [SM, VM, VM],
        [pltpu.VMEM((blocks * 8, 128), f32), pltpu.VMEM((n_ng, 128), f32)],
        1 << 20, 4 << 20,
    )(held, z_q, z_m)
    recv = exchange(send, "dp")
    high = me - (me & 7)
    sources = jnp.stack(
        [
            high + c + ((j >> 1) << order[c][0]) + ((j & 1) << order[c][1])
            for c in range(2)
            for j in range(4)
        ]
    ).astype(jnp.int32)
    state_shape = (capacity, block_rows, 128)
    first_new, second_new, master_new, fresh, norm_sum = call(
        adam_body,
        [(state_shape, f32)] * 3 + [((capacity, 16, 512), bf16), ((n_ng, 128), f32)],
        [SM, SM] + [VM] * 4,
        [pltpu.VMEM((capacity, 2, 8, 128), f32), pltpu.VMEM((capacity * block_rows, 128), f32)],
        1 << 20, 8 << 20,
    )(filled, sources, recv, master, first_moment, second_moment)

    buf = fresh[None]
    for s in range(nbits - 1):
        buf = jnp.concatenate([buf, swap(buf, s)], axis=0)
    oth = swap_core(buf)
    owner_core = owners & 1
    far_core = owner_core ^ core
    start = jnp.where(far_core == 1, me ^ 1, me)
    rel = start ^ owners
    at = sum(
        ((rel >> jnp.where(owner_core == 0, order[0][s], order[1][s])) & 1) << s for s in range(nbits - 1)
    )
    index = (at * capacity + slot).astype(jnp.int32)
    flat_shape = (buf.shape[0] * capacity, 16, 512)
    new_qkv, new_out, new_in, new_down = call(
        place_body,
        [(w_qkv.shape, bf16), (w_out.shape, bf16), (w_in.shape, bf16), (w_down.shape, bf16)],
        [SM, SM, VM, VM],
        [pltpu.VMEM((w_qkv.size // 512, 512), f32), pltpu.VMEM((w_qkv.size // 128, 128), f32)],
        1 << 20, 6 << 20,
    )(far_core, index, buf.reshape(flat_shape), oth.reshape(flat_shape))

    corr_one = 1.0 - beta_one**STEP
    corr_two = 1.0 - beta_two**STEP
    norm_grad = norm_sum.reshape(4, width)
    norm_params = jnp.stack([norm_gains[0], norm_biases[0], norm_gains[1], norm_biases[1]])
    norm_first_new = beta_one * norm_first + (1.0 - beta_one) * norm_grad
    norm_second_new = beta_two * norm_second + (1.0 - beta_two) * norm_grad * norm_grad
    norm_new = norm_params - norm_rate * (
        norm_first_new / corr_one / (jnp.sqrt(norm_second_new / corr_two) + adam_epsilon)
    )
    return (
        outputs[None], tokens_grad[None], first_new, second_new, master_new,
        new_qkv, new_out, new_in, new_down, norm_first_new, norm_second_new, norm_new,
    )


def solution(mesh):
    sharded = P("dp", "mp", None)
    return jax.shard_map(
        per_device,
        mesh=mesh,
        in_specs=(
            sharded, sharded, P("dp"), P(), P(None, "mp"), P("mp", None), P(None, "mp"), P("mp", None),
            sharded, sharded, sharded, P(), P(), P(), P(),
        ),
        out_specs=(
            sharded, sharded, sharded, sharded, sharded,
            P(None, "mp"), P("mp", None), P(None, "mp"), P("mp", None), P(), P(), P(),
        ),
        check_vma=False,
    )
```

```python
import functools

import jax
import jax.numpy as jnp
from jax import lax
from jax.experimental import pallas as pl
from jax.experimental.pallas import tpu as pltpu
from jax.sharding import PartitionSpec as P

HEAD = 64
BAND = 30
STEP = 10
HALO = 64
EDGE = 32
QB = 64
WIN = 128
PAIR = 128
COST = 1
STATE = 144

learn_rate = 0.1
norm_rate = 0.3
decay_rate = 0.1
beta_one = 0.9
beta_two = 0.95
adam_epsilon = 1e-08
norm_epsilon = 1e-05
GELU_C = 0.7978845608028654
GELU_A = 0.044715

f32 = jnp.float32
bf16 = jnp.bfloat16

VM = pl.BlockSpec(memory_space=pltpu.VMEM)
HB = pl.BlockSpec(memory_space=pltpu.HBM)
SM = pl.BlockSpec(memory_space=pltpu.SMEM)


def call(body, outs, in_specs, scratch, flops, moved, vmem=48, out_specs=None):
    specs = out_specs or tuple(VM for _ in outs)
    run = pl.pallas_call(
        body,
        out_shape=tuple(
            pltpu.HBM(s, d) if spec is HB else jax.ShapeDtypeStruct(s, d) for (s, d), spec in zip(outs, specs)
        ),
        in_specs=in_specs,
        out_specs=specs,
        scratch_shapes=scratch,
        compiler_params=pltpu.CompilerParams(vmem_limit_bytes=vmem << 20),
        cost_estimate=pl.CostEstimate(flops=flops // COST, bytes_accessed=moved // COST, transcendentals=0),
    )

    def fixed(*args):
        return run(
            *[
                pltpu.with_memory_space_constraint(x, pltpu.HBM) if spec is HB else x
                for x, spec in zip(args, in_specs)
            ]
        )

    return fixed


def dot(a, b):
    return jnp.dot(a, b, preferred_element_type=f32)


def turned(a):
    return a.astype(f32).T.astype(bf16)


def dot_nt(a, b):
    return dot(a, turned(b))


def dot_tn(a, b):
    return lax.dot_general(a, b, (((0,), (0,)), ((), ())), preferred_element_type=f32)


def normalize(x):
    mean = jnp.mean(x, axis=-1, keepdims=True)
    cen = x - mean
    var = jnp.mean(cen * cen, axis=-1, keepdims=True)
    rstd = lax.rsqrt(var + norm_epsilon)
    return cen * rstd, rstd


def same_head(n=PAIR):
    r = lax.broadcasted_iota(jnp.int32, (n, n), 0)
    c = lax.broadcasted_iota(jnp.int32, (n, n), 1)
    return (r < HEAD) == (c < HEAD)


def pack_state(s1, s2, z):
    both = jnp.where(same_head(), s1, pltpu.roll(s2, HEAD, 1))
    hi = z.astype(bf16).astype(f32)
    row = lax.broadcasted_iota(jnp.int32, (16, PAIR), 0)
    tail = jnp.where(row == 0, hi, jnp.where(row == 1, z - hi, 0.0))
    return both.astype(bf16), tail.astype(bf16)


def unpack_state(refs, g):
    tot = refs[0][g].astype(f32)
    for r in refs[1:]:
        tot = tot + r[g].astype(f32)
    both = tot[:PAIR]
    diag = same_head()
    s1 = jnp.where(diag, both, 0.0)
    s2 = jnp.where(diag, pltpu.roll(both, HEAD, 1), 0.0)
    z = tot[PAIR : PAIR + 1] + tot[PAIR + 1 : PAIR + 2]
    return s1, s2, z


def split_dot(a, ones):
    hi, lo = two(a)
    return dot(hi, ones) + dot(lo, ones)


def two(a):
    hi = a.astype(bf16)
    return hi, (a - hi.astype(f32)).astype(bf16)


def phi(v):
    low = jnp.exp(jnp.minimum(v, 0.0))
    return jnp.where(v > 0, v + 1.0, low), jnp.where(v > 0, 1.0, low)


def band_parts():
    c = lax.broadcasted_iota(jnp.int32, (WIN, 2 * QB), 0)
    r = lax.broadcasted_iota(jnp.int32, (WIN, 2 * QB), 1) % QB
    off = r + EDGE - c
    return (jnp.abs(off) <= BAND), off == 0, c


def stacked(rows):
    lane = lax.broadcasted_iota(jnp.int32, (1, PAIR), 1)
    first = (lane < HEAD).astype(f32).astype(bf16)
    second = (lane >= HEAD).astype(f32).astype(bf16)
    return jnp.concatenate([rows * first, rows * second], axis=0)


def unstack(both):
    lane = lax.broadcasted_iota(jnp.int32, (QB, PAIR), 1)
    return jnp.where(lane < HEAD, both[:QB], both[QB:])


def softmax_of(raw, mask):
    scores = jnp.where(mask, raw * 0.125, -1e30)
    ex = jnp.exp(scores - jnp.max(scores, axis=0, keepdims=True))
    return ex * (1.0 / jnp.sum(ex, axis=0, keepdims=True))


def fetch_pieces(meta, first, own, oth, lo, rows, weight, sem):
    n = own.shape[0]
    core = meta[2]
    copies = []
    for pq in range(n):
        for buf, row, half in ((own, meta[first + pq], core), (oth, meta[first + n + pq], 1 - core)):
            at = pl.ds(pl.multiple_of((half * n + pq) * rows, rows), rows)
            for m in range(buf.shape[1]):
                src = buf.at[row, m, pl.ds(lo, rows), :]
                copies.append(pltpu.make_async_copy(src, weight.at[meta[15] ^ m, at, :], sem))
    for c in copies:
        c.start()
    return copies


def norm_body(tok, left, right, gains, biases, a1e_o):
    rows = tok.shape[0]
    gain, bias = gains[0:1, :], biases[0:1, :]

    def ln(x):
        return (normalize(x.astype(f32))[0] * gain + bias).astype(bf16)

    a1e_o[0:HALO, :] = ln(left[...])
    a1e_o[HALO + rows :, :] = ln(right[...])

    def chunk(i, _):
        at = pl.ds(pl.multiple_of(i * 128, 128), 128)
        a1e_o[pl.ds(pl.multiple_of(i * 128 + HALO, 64), 128), :] = ln(tok[at, :])
        return 0

    lax.fori_loop(0, rows // 128, chunk, 0)


def qkv_body(meta, a1e, own, oth, qkv_o, st_o, w, sem):
    ext = a1e.shape[0]
    rows = ext - 2 * HALO
    groups = own.shape[1]
    for c in fetch_pieces(meta, 11, own, oth, 0, own.shape[2], w, sem):
        c.wait()
    length, base = meta[0], meta[1]
    pos = base + lax.broadcasted_iota(jnp.int32, (rows, 1), 0)
    valid = (pos < length).astype(f32)
    gs = range(groups)
    for g in gs:
        qkv_o[g] = dot(a1e[...], w[g]).astype(bf16)
    own_rows = slice(HALO, HALO + rows)
    parts = []
    for g in gs:
        keys = qkv_o[g, own_rows, PAIR : 2 * PAIR].astype(f32)
        feat = phi(keys)[0] * valid
        parts.append((jnp.sum(feat, axis=0, keepdims=True), two(feat), two(jnp.tanh(keys) * valid)))
    for g in gs:
        z, (fhi, flo), (thi, tlo) = parts[g]
        vals = qkv_o[g, own_rows, 2 * PAIR :]
        s1 = dot_tn(fhi, vals) + dot_tn(flo, vals)
        s2 = dot_tn(thi, vals) + dot_tn(tlo, vals)
        st_o[g, :PAIR, :], st_o[g, PAIR:, :] = pack_state(s1, s2, z)


def near_body(meta, qkv, near_o):
    groups = qkv.shape[0]
    rows = near_o.shape[0]
    length, base = meta[0], meta[1]
    band, diag, lane = band_parts()

    def block(b, _):
        at = b * QB
        kpos = base + at - EDGE + lane
        mask = band & (((kpos >= 0) & (kpos < length)) | diag)
        q_at = pl.ds(pl.multiple_of(at + HALO, QB), QB)
        w_at = pl.ds(pl.multiple_of(at + HALO - EDGE, EDGE), WIN)
        gs = range(groups)
        sc = [dot_nt(qkv[g, w_at, PAIR : 2 * PAIR], stacked(qkv[g, q_at, 0:PAIR])) for g in gs]
        p = [softmax_of(sc[g], mask).astype(bf16) for g in gs]
        res = [dot_tn(p[g], qkv[g, w_at, 2 * PAIR :]) for g in gs]
        for g in gs:
            near_o[pl.ds(pl.multiple_of(at, QB), QB), g * PAIR : (g + 1) * PAIR] = unstack(res[g])
        return 0

    lax.fori_loop(0, rows // QB, block, 0, unroll=4)


def put_halves(core, keep, give, g, lo, grad):
    n, width = grad.shape
    tiles = grad.reshape(n // 16, 2, 8, width)
    even, odd = tiles[:, 0].reshape(n // 2, width), tiles[:, 1].reshape(n // 2, width)
    first = jnp.full(even.shape, core, jnp.int32) == 0
    at = slice(lo, lo + n // 2)
    keep[g, at, :] = jnp.where(first, even, odd).astype(keep.dtype)
    give[g, at, :] = jnp.where(first, odd, even).astype(give.dtype)


def main_body(
    meta, near, qkv, s0, s1, s2, s3, tok, cot, gains, biases, io_own, io_oth, dn_own, dn_oth,
    out_h, do_o, dx2_h, dctx_o, dqf_h, dst_o, ng_o, wout_o, keep_h, give_h,
    w_in, w_down, x2, xhat, rs, u, dh, acc, da2, far1, inv, dnum, phq, thq,
    ctx_o, a2_o, dm_o, hid_o, du_o, out_o, give, sem, out_sem,
):
    rows, width = tok.shape
    groups = dn_own.shape[1]
    pr = dn_own.shape[2]
    orow = io_own.shape[2] - pr
    core = meta[2]
    sent = []

    def send(src, dst):
        sent.append(pltpu.make_async_copy(src, dst, out_sem))
        sent[-1].start()

    length, base = meta[0], meta[1]
    copies = fetch_pieces(meta, 3, io_own, io_oth, pr, orow, wout_o, sem.at[0])
    later = fetch_pieces(meta, 3, io_own, io_oth, 0, pr, w_in, sem.at[1])
    last = fetch_pieces(meta, 3, dn_own, dn_oth, 0, pr, w_down, sem.at[2])
    rlen = 1.0 / length.astype(f32)
    gain, bias = gains[1:2, :], biases[1:2, :]
    ones = same_head().astype(f32).astype(bf16)
    gs = range(groups)
    cols = [slice(g * PAIR, (g + 1) * PAIR) for g in gs]
    states = [unpack_state((s0, s1, s2, s3), g) for g in gs]
    s1b, s2b = [two(st[0]) for st in states], [two(st[1]) for st in states]
    cr = 128

    def far_chunk(i, _):
        at = pl.ds(pl.multiple_of(i * cr, cr), cr)
        q_at = pl.ds(pl.multiple_of(i * cr + HALO, HALO), cr)
        q = [qkv[g, q_at, 0:PAIR].astype(f32) for g in gs]
        ph = [phi(q[g])[0] for g in gs]
        ph2 = [two(ph[g]) for g in gs]
        th2 = [two(jnp.tanh(q[g])) for g in gs]
        den = [split_dot(ph[g] * states[g][2], ones) for g in gs]
        num = [dot(ph2[g][0], s1b[g][0]) + dot(ph2[g][0], s1b[g][1]) + dot(ph2[g][1], s1b[g][0]) for g in gs]
        sec = [dot(th2[g][0], s2b[g][0]) + dot(th2[g][0], s2b[g][1]) + dot(th2[g][1], s2b[g][0]) for g in gs]
        for g in gs:
            phq[at, cols[g]] = ph2[g][0]
            thq[at, cols[g]] = th2[g][0]
        rec = [1.0 / den[g] for g in gs]
        for g in gs:
            part = num[g] * rec[g]
            inv[at, cols[g]] = rec[g]
            far1[at, cols[g]] = part
            ctx_o[at, cols[g]] = (near[at, cols[g]] + (part + sec[g] * rlen)).astype(bf16)
        pos = base + i * cr + lax.broadcasted_iota(jnp.int32, (cr, 1), 0)
        dm_o[at, :] = (cot[at, :].astype(f32) * (pos < length).astype(f32)).astype(bf16)
        return 0

    lax.fori_loop(0, rows // cr, far_chunk, 0)
    for c in copies:
        c.wait()
    wout = wout_o[...].reshape(width, width)
    x2[...] = dot(ctx_o[...], wout)

    def norm_chunk(i, _):
        at = pl.ds(pl.multiple_of(i * 64, 64), 64)
        val = x2[at, :] + tok[at, :].astype(f32)
        x2[at, :] = val
        xh, rstd = normalize(val)
        xhat[at, :] = xh
        rs[at, :] = jnp.broadcast_to(rstd, (64, 128))
        a2_o[at, :] = (xh * gain + bias).astype(bf16)
        return 0

    lax.fori_loop(0, rows // 64, norm_chunk, 0)
    for c in later + last:
        c.wait()
    for g in gs:
        u[g, 0:rows, :] = dot(a2_o[...], w_in[g])
        dh[g, 0:rows, :] = dot_nt(dm_o[...], w_down[g])

    def act(i, _):
        at = pl.ds(pl.multiple_of(i * 16, 16), 16)
        for g in gs:
            v = u[g, at, :]
            sq = v * v
            half = 0.5 + 0.5 * jnp.tanh(v * (GELU_C + GELU_C * GELU_A * sq))
            hid = v * half
            hid_o[g, at, :] = hid.astype(bf16)
            slope = half + (hid * (1.0 - half)) * (2.0 * GELU_C + 6.0 * GELU_C * GELU_A * sq)
            du_o[g, at, :] = (dh[g, at, :] * slope).astype(bf16)
        return 0

    lax.fori_loop(0, rows // 16, act, 0)
    acc[...] = sum(dot(hid_o[g], w_down[g]) for g in gs)
    da2[...] = sum(dot_nt(du_o[g], w_in[g]) for g in gs)

    def back_chunk(i, carry):
        dg, db = carry
        at = pl.ds(pl.multiple_of(i * 64, 64), 64)
        out_o[at, :] = (x2[at, :] + acc[at, :]).astype(bf16)
        xh = xhat[at, :]
        rstd = rs[at, 0:1]
        d = da2[at, :]
        dg = dg + jnp.sum(d * xh, axis=0, keepdims=True)
        db = db + jnp.sum(d, axis=0, keepdims=True)
        e = d * gain
        m1 = jnp.mean(e, axis=-1, keepdims=True)
        m2 = jnp.mean(e * xh, axis=-1, keepdims=True)
        dx = dm_o[at, :].astype(f32) + rstd * (e - m1 - xh * m2)
        acc[at, :] = dx
        do_o[at, :] = dx.astype(bf16)
        return dg, db

    zero = jnp.zeros((1, width), f32)
    dg, db = lax.fori_loop(0, rows // 64, back_chunk, (zero, zero))
    send(out_o, out_h)
    send(acc, dx2_h)
    ng_o[0:1, :] = dg
    ng_o[1:2, :] = db
    dctx_o[...] = dot_nt(do_o[...], wout).astype(bf16)

    def far_back(i, carry):
        at = pl.ds(pl.multiple_of(i * cr, cr), cr)
        q_at = pl.ds(pl.multiple_of(i * cr + HALO, HALO), cr)
        dc = [dctx_o[at, cols[g]] for g in gs]
        dcf = [dc[g].astype(f32) for g in gs]
        rec = [inv[at, cols[g]] for g in gs]
        dn = [(dcf[g] * rec[g]).astype(bf16) for g in gs]
        dots = [split_dot(dcf[g] * far1[at, cols[g]], ones) for g in gs]
        dph = [dot_nt(dn[g], s1b[g][0]) for g in gs]
        dth = [dot_nt(dc[g], s2b[g][0]) for g in gs]
        out = []
        for g in gs:
            dnum[at, cols[g]] = dn[g]
            dden = -dots[g] * rec[g]
            out.append(carry[g] + jnp.sum(phq[at, cols[g]].astype(f32) * dden, axis=0, keepdims=True))
            slope = phi(qkv[g, q_at, 0:PAIR].astype(f32))[1]
            th = thq[at, cols[g]].astype(f32)
            da2[at, cols[g]] = (dph[g] + dden * states[g][2]) * slope + dth[g] * rlen * (1.0 - th * th)
        return tuple(out)

    none = jnp.zeros((1, PAIR), f32)
    dz = lax.fori_loop(0, rows // cr, far_back, (none,) * groups)
    for g in gs:
        d1 = dot_tn(phq[:, cols[g]], dnum[:, cols[g]])
        d2 = dot_tn(thq[:, cols[g]], dctx_o[:, cols[g]]) * rlen
        dst_o[g, :PAIR, :], dst_o[g, PAIR:, :] = pack_state(d1, d2, dz[g])
    send(da2, dqf_h)
    n_out = ctx_o.shape[1] // groups
    hw = hid_o.shape[2]
    keep = u

    def finish(g, lo, n, grad):
        put_halves(core, keep, give, g, lo, grad)
        part = pl.ds(lo, n)
        send(keep.at[g, part, :], keep_h.at[g, part, :])
        send(give.at[g, part, :], give_h.at[g, part, :])

    for g in gs:
        finish(g, n_out // 2, width // 2, dot_tn(a2_o[...], du_o[g]))
    for g in gs:
        finish(g, 0, n_out // 2, dot_tn(ctx_o[:, g * n_out : (g + 1) * n_out], do_o[...]))
    for g in gs:
        finish(g, n_out // 2 + width // 2, hw // 2, dot_tn(hid_o[g], dm_o[...]))
    for c in sent:
        c.wait()


def near_back_body(
    meta, qkv, dctx, do_l, do_r, wout_h, dqf_h, dq_o, dk_o, dv_o, dce, dqe, dke, dve, wout, dqf, sem,
):
    groups = qkv.shape[0]
    rows = dctx.shape[0]
    length, base = meta[0], meta[1]
    band, diag, lane = band_parts()
    first = pltpu.make_async_copy(wout_h, wout, sem.at[0])
    first.start()
    second = pltpu.make_async_copy(dqf_h, dqf, sem.at[1])
    second.start()
    first.wait()
    w = wout[...].reshape(dctx.shape[1], -1)
    dce[0:EDGE, :] = dot_nt(do_l[...], w).astype(bf16)
    dce[EDGE : EDGE + rows, :] = dctx[...]
    dce[EDGE + rows :, :] = dot_nt(do_r[...], w).astype(bf16)
    dke[...] = jnp.zeros(dke.shape, f32)
    dve[...] = jnp.zeros(dve.shape, f32)

    def block(b, _):
        at = b * QB
        kpos = base + at - HALO + lane
        mask = band & (((kpos >= 0) & (kpos < length)) | diag)
        c_at = pl.ds(pl.multiple_of(at, QB), QB)
        q_at = pl.ds(pl.multiple_of(at + EDGE, EDGE), QB)
        w_at = pl.ds(pl.multiple_of(at, QB), WIN)
        gs = range(groups)
        cols = [slice(g * PAIR, (g + 1) * PAIR) for g in gs]
        qs = [stacked(qkv[g, q_at, 0:PAIR]) for g in gs]
        cs = [stacked(dce[c_at, cols[g]]) for g in gs]
        kw = [qkv[g, w_at, PAIR : 2 * PAIR] for g in gs]
        sc = [dot_nt(kw[g], qs[g]) for g in gs]
        dp = [dot_nt(qkv[g, w_at, 2 * PAIR :], cs[g]) for g in gs]
        p = [softmax_of(sc[g], mask) for g in gs]
        row = [jnp.sum(p[g] * dp[g], axis=0, keepdims=True) for g in gs]
        ds = [(p[g] * (dp[g] - row[g])).astype(bf16) for g in gs]
        pb = [p[g].astype(bf16) for g in gs]
        for g in gs:
            dke[w_at, cols[g]] += dot(ds[g], qs[g])
            dve[w_at, cols[g]] += dot(pb[g], cs[g])
        dq = [dot_tn(ds[g], kw[g]) for g in gs]
        for g in gs:
            dqe[c_at, cols[g]] = unstack(dq[g])
        return 0

    lax.fori_loop(0, rows // QB + 1, block, 0, unroll=3)
    second.wait()
    dq_o[...] = (dqe[EDGE : EDGE + rows, :] * 0.125 + dqf[...]).astype(bf16)
    dk_o[...] = dke[HALO : HALO + rows, :] * 0.125
    dv_o[...] = dve[HALO : HALO + rows, :]


def proj_body(meta, qkv, dq, dkn, dvn, s0, s1, s2, s3, a1e, dproj_h, keep_o, give_o, dproj, flat, pseudo, sem):
    groups = qkv.shape[0]
    rows, width = dq.shape
    length, base, core = meta[0], meta[1], meta[2]
    cr = 128
    gs = range(groups)
    cols = [slice(g * PAIR, (g + 1) * PAIR) for g in gs]
    states = [unpack_state((s0, s1, s2, s3), g) for g in gs]
    s1b, s2b = [st[0].astype(bf16) for st in states], [st[1].astype(bf16) for st in states]

    def far_chunk(i, _):
        at = pl.ds(pl.multiple_of(i * cr, cr), cr)
        e_at = pl.ds(pl.multiple_of(i * cr + HALO, HALO), cr)
        pos = base + i * cr + lax.broadcasted_iota(jnp.int32, (cr, 1), 0)
        valid = (pos < length).astype(f32)
        k = [qkv[g, e_at, PAIR : 2 * PAIR].astype(f32) for g in gs]
        v = [qkv[g, e_at, 2 * PAIR :] for g in gs]
        feat = [phi(k[g]) for g in gs]
        th = [jnp.tanh(k[g]) for g in gs]
        vd1 = [dot_nt(v[g], s1b[g]) for g in gs]
        vd2 = [dot_nt(v[g], s2b[g]) for g in gs]
        dv = [
            dot((feat[g][0] * valid).astype(bf16), s1b[g]) + dot((th[g] * valid).astype(bf16), s2b[g]) for g in gs
        ]
        for g in gs:
            dk = (vd1[g] + states[g][2]) * feat[g][1] + vd2[g] * (1.0 - th[g] * th[g])
            dproj[g, at, 0:PAIR] = dq[at, cols[g]]
            dproj[g, at, PAIR : 2 * PAIR] = (dkn[at, cols[g]] + dk * valid).astype(bf16)
            dproj[g, at, 2 * PAIR :] = (dvn[at, cols[g]] + dv[g]).astype(bf16)
        return 0

    lax.fori_loop(0, rows // cr, far_chunk, 0)
    out = pltpu.make_async_copy(dproj, dproj_h, sem)
    out.start()
    n_flat = 3 * width
    for g in gs:
        grad = dot_tn(a1e[HALO : HALO + rows, :], dproj[g])
        for part in range(3):
            flat[pl.ds(part, width, stride=3), :] = grad[:, part * PAIR : (part + 1) * PAIR]
        for j in range(4):
            pseudo[:, j * 128 : (j + 1) * 128] = flat[pl.ds(j, n_flat // 4, stride=4), :]
        put_halves(core, keep_o, give_o, g, 0, pseudo[...])
    out.wait()


def last_body(
    meta, dproj_h, own, oth, tok, dx2_h, gains, ng2, tg_o, ng_o, da1, ngs, wqkv, dproj, dx2, sem, sems,
):
    groups = dproj.shape[0]
    rows, width = tok.shape
    gain = gains[0:1, :]
    copies = fetch_pieces(meta, 11, own, oth, 0, own.shape[2], wqkv, sem)
    copies.append(pltpu.make_async_copy(dproj_h, dproj, sems.at[0]))
    copies[-1].start()
    late = pltpu.make_async_copy(dx2_h, dx2, sems.at[1])
    late.start()
    for c in copies:
        c.wait()
    da1[...] = sum(dot_nt(dproj[g], wqkv[g]) for g in range(groups))

    late.wait()

    def back_chunk(i, carry):
        dg, db = carry
        at = pl.ds(pl.multiple_of(i * 64, 64), 64)
        xh, rstd = normalize(tok[at, :].astype(f32))
        d = da1[at, :]
        dg = dg + jnp.sum(d * xh, axis=0, keepdims=True)
        db = db + jnp.sum(d, axis=0, keepdims=True)
        e = d * gain
        m1 = jnp.mean(e, axis=-1, keepdims=True)
        m2 = jnp.mean(e * xh, axis=-1, keepdims=True)
        tg_o[at, :] = dx2[at, :] + rstd * (e - m1 - xh * m2)
        return dg, db

    zero = jnp.zeros((1, width), f32)
    dg, db = lax.fori_loop(0, rows // 64, back_chunk, (zero, zero))
    for k, val in enumerate((dg, db, ng2[0:1, :], ng2[1:2, :])):
        for j in range(width // 128):
            at = k * (width // 128) + j
            ngs[at : at + 1, :] = val[:, j * 128 : (j + 1) * 128]
    n = ngs.shape[0]
    hi = ngs[...].astype(bf16)
    ng_o[0:n, :] = hi
    ng_o[n:, :] = (ngs[...] - hi.astype(f32)).astype(bf16)


def slices_body(where, master, first, second, out_h, held, parts, sem, out_sem):
    caps = held.shape[1] // 64
    copies = [pltpu.make_async_copy(ref, held.at[t], sem.at[t]) for t, ref in enumerate((master, first, second))]
    for c in copies:
        c.start()
    sent = []
    for t in range(3):
        copies[t].wait()
        for j in range(4):
            val = held[t, pl.ds(j, caps * 16, stride=4), :].reshape(caps, 2, 8, 128)
            for c in range(2):
                parts[t, c, j] = val[:, c].reshape(caps * 8, 128)
                for d in where[c][j]:
                    sent.append(pltpu.make_async_copy(parts.at[t, c, j], out_h.at[d, t], out_sem))
                    sent[-1].start()
    for c in sent:
        c.wait()


def adam(g, m_old, f_old, s_old):
    corr_one = 1.0 - beta_one**STEP
    corr_two = 1.0 - beta_two**STEP
    fn = beta_one * f_old + (1.0 - beta_one) * g
    sn = beta_two * s_old + (1.0 - beta_two) * g * g
    step = fn / corr_one / (jnp.sqrt(sn / corr_two) + adam_epsilon)
    return fn, sn, m_old - learn_rate * (step + decay_rate * m_old)


def pieces_body(first, count, owners, slots, *refs):
    parts, st, piece_o, w_o, norms = refs[:count], refs[count], refs[count + 1], refs[count + 2], refs[count + 3 :]
    n = piece_o.shape[0]
    src = [(r, s) for r in parts for s in range(r.shape[0])]
    piece_o[...] = sum(r[s, 0:n, :].astype(f32) for r, s in src)
    if norms:
        k = (parts[0].shape[1] - n) // 2
        norms[0][...] = sum(r[s, n : n + k, :].astype(f32) + r[s, n + k :, :].astype(f32) for r, s in src)

    def pair(i, _):
        new = []
        for k in range(2):
            b = i * 2 + k
            at = pl.ds(pl.multiple_of(slots[first + b] * 8, 8), 8)
            own = owners[first + b]
            g = piece_o[pl.ds(pl.multiple_of(b * 8, 8), 8), :]
            new.append(adam(g, st[own, 0, at, :], st[own, 1, at, :], st[own, 2, at, :])[2])
        w_o[pl.ds(pl.multiple_of(i * 16, 16), 16), :] = jnp.concatenate(new, axis=0).astype(bf16)
        return 0

    lax.fori_loop(0, n // 16, pair, 0, unroll=4)


def route_body(blocks, pq, pm, ng, send_o):
    nq = pq.shape[0] // 8
    dests, per, _ = send_o.shape
    caps = (per - ng.shape[0]) // 8

    def dest(d, _):
        for r in range(caps):
            b = blocks[d * caps + r]
            one = pq[pl.ds(pl.multiple_of(jnp.minimum(b, nq - 1) * 8, 8), 8), :]
            two_ = pm[pl.ds(pl.multiple_of(jnp.maximum(b - nq, 0) * 8, 8), 8), :]
            send_o[d, r * 8 : r * 8 + 8, :] = jnp.where(jnp.full((8, 128), b, jnp.int32) < nq, one, two_)
        send_o[d, caps * 8 :, :] = ng[...]
        return 0

    lax.fori_loop(0, dests, dest, 0)


def adam_body(filled, sources, recv, master, first, second, f_o, s_o, m_o, ng_o, two, grad):
    caps, br, _ = master.shape
    for j in range(4):
        for c in range(2):
            two[:, c] = recv[sources[c * 4 + j], 0 : caps * 8, :].reshape(caps, 8, 128)
        grad[pl.ds(j, caps * 16, stride=4), :] = two[...].reshape(caps * 16, 128)

    def add(s, tot):
        return tot + recv[s, caps * 8 :, :]

    ng_o[...] = lax.fori_loop(0, recv.shape[0], add, jnp.zeros(ng_o.shape, f32))

    def slot(r, _):
        g = grad[pl.ds(pl.multiple_of(r * br, br), br), :]
        m_old, f_old, s_old = master[r], first[r], second[r]
        fn, sn, mn = adam(g, m_old, f_old, s_old)
        keep = jnp.full(g.shape, filled[r], jnp.int32) > 0
        f_o[r] = jnp.where(keep, fn, f_old)
        s_o[r] = jnp.where(keep, sn, s_old)
        m_o[r] = jnp.where(keep, mn, m_old)
        return 0

    lax.fori_loop(0, caps, slot, 0, unroll=2)


def columns(meta, own, oth, j, lo, n):
    core = meta[2]
    a = own[meta[3 + j], lo : lo + n, :].astype(f32)
    b = oth[meta[7 + j], lo : lo + n, :].astype(f32)
    first = jnp.full(a.shape, core, jnp.int32) == 0
    even, odd = jnp.where(first, a, b), jnp.where(first, b, a)
    both = jnp.concatenate([even.reshape(n // 8, 1, 8, 128), odd.reshape(n // 8, 1, 8, 128)], axis=1)
    return both.reshape(2 * n, 128)


def place_body(meta, own, oth, out_o, in_o, down_o):
    lo = 0
    for ref in (out_o, in_o, down_o):
        n = ref.shape[0] // 2
        for j in range(4):
            ref[:, j * 128 : (j + 1) * 128] = columns(meta, own, oth, j, lo, n).astype(bf16)
        lo += n


def place_qkv_body(meta, own, oth, q_o, flat):
    n = own.shape[1]
    rows = q_o.shape[0]
    for j in range(4):
        flat[pl.ds(j, 2 * n, stride=4), :] = columns(meta, own, oth, j, 0, n)
    for part in range(3):
        q_o[:, part * 128 : (part + 1) * 128] = flat[pl.ds(part, rows, stride=3), :].astype(bf16)


def per_device(
    tokens, cotangent, lengths, owners, w_qkv, w_out, w_in, w_down,
    master, first_moment, second_moment, norm_gains, norm_biases, norm_first, norm_second,
):
    rows, width = tokens.shape[1], tokens.shape[2]
    groups = lax.axis_size("mp")
    ndp = lax.axis_size("dp")
    nbits = ndp.bit_length() - 1
    rest = list(range(1, nbits))
    order = (rest, rest[:2][::-1] + rest[2:][::-1])
    me, zi = lax.axis_index("dp"), lax.axis_index("mp")
    core = me & 1

    def bit_of(who, at, s):
        return (who >> jnp.where(at == 0, order[0][s], order[1][s])) & 1

    def swap(x, s):
        return lax.ppermute(x, "dp", [(i, i ^ (1 << order[i & 1][s])) for i in range(ndp)])

    def swap_core(x):
        return lax.ppermute(x, "dp", [(i, i ^ 1) for i in range(ndp)])

    def from_mp(x, step):
        return lax.ppermute(x, "mp", [(i, i + step) for i in range(groups) if 0 <= i + step < groups])

    def swap_mp(x, mask):
        return lax.ppermute(x, "mp", [(i, i ^ mask) for i in range(groups)])

    def exchange(x, axis):
        return lax.all_to_all(x, axis, 0, 0, tiled=True)

    def all_states(x):
        return [x] + [swap_mp(x, m) for m in range(1, groups)]

    q0, q1 = bit_of(me, core, 0), bit_of(me, core, 1)
    o0, o1 = bit_of(me, 1 - core, 0), bit_of(me, 1 - core, 1)
    length = lengths[0]
    base = zi * rows
    ids = [length, base, core]
    ids += [((t >> 1) ^ q0) + 2 * ((t & 1) ^ q1) for t in range(4)]
    ids += [((t >> 1) ^ o0) + 2 * ((t & 1) ^ o1) for t in range(4)]
    ids += [q0, 1 - q0, o0, 1 - o0, zi]
    meta = jnp.stack(ids).astype(jnp.int32)

    def after(x, *deps):
        return lax.optimization_barrier((x,) + deps)[0]

    def over_mp(piece):
        return jnp.stack([piece] + [swap_mp(piece, m) for m in range(1, groups)])[None]

    def grow(buf, s):
        return jnp.concatenate([buf, swap(buf, s)], axis=0)

    def part_of(w, n, at):
        return lax.dynamic_slice_in_dim(w, at * (w.shape[0] // n), w.shape[0] // n, 0)

    mine = core * 4 + q0 * 2 + q1
    tok, cot = tokens[0], cotangent[0]
    ext = rows + 2 * HALO
    mm = 2 * rows * width
    qkv_z = over_mp(part_of(w_qkv, 4, core * 2 + q0))
    left, right = from_mp(tok[rows - HALO :], 1), from_mp(tok[:HALO], -1)
    io_piece = jnp.concatenate([part_of(w_in, 8, mine), part_of(w_out, 8, mine)], axis=0)
    io_z = over_mp(io_piece)
    dn_z = over_mp(part_of(w_down, 8, mine))
    [a1e] = call(norm_body, [((ext, width), bf16)], [VM] * 5, [], 4 * mm, 1 << 20, 16)(
        tok, left, right, norm_gains, norm_biases
    )
    qkv_own = grow(after(qkv_z, a1e), 0)
    io_z = after(io_z, qkv_own)
    qkv_oth = swap_core(after(qkv_own, io_z))
    io_one = grow(io_z, 0)
    proj_w = pltpu.VMEM((groups, width, 3 * PAIR), bf16)
    qkv, state = call(
        qkv_body,
        [((groups, ext, 3 * PAIR), bf16), ((groups, STATE, PAIR), bf16)],
        [SM, VM, HB, HB],
        [proj_w, pltpu.SemaphoreType.DMA],
        2 * ext * width * 3 * width, 6 << 20, 20,
    )(meta, after(a1e, dn_z), qkv_own, qkv_oth)
    states = all_states(state)
    io_one = after(io_one, qkv)
    dn_one = grow(after(dn_z, io_one), 0)
    io_own = grow(io_one, 1)
    capacity, block_rows = master.shape[0], master.shape[1]
    where = [[[] for _ in range(4)] for _ in range(2)]
    for d in range(ndp):
        b = order[d & 1]
        where[d & 1][2 * ((d >> b[0]) & 1) + ((d >> b[1]) & 1)].append(d)
    flat_state = [x.reshape(capacity * block_rows, 128) for x in (master, first_moment, second_moment)]
    [parts] = call(
        functools.partial(slices_body, where), [((ndp, 3, capacity * 8, 128), f32)], [HB] * 3,
        [
            pltpu.VMEM((3, capacity * block_rows, 128), f32), pltpu.VMEM((3, 2, 4, capacity * 8, 128), f32),
            pltpu.SemaphoreType.DMA((3,)), pltpu.SemaphoreType.DMA,
        ],
        1 << 20, 4 << 20, 12, (HB,),
    )(*flat_state)
    [near] = call(
        near_body, [((rows, width), f32)], [SM, VM], [], mm * 1024, 12 << 20, 16,
    )(meta, after(qkv, dn_one, parts, *states))
    io_oth = swap_core(after(io_own, near))
    dn_own = grow(after(dn_one, *states), 1)
    dn_oth = swap_core(after(dn_own, near))

    held_state = exchange(after(parts, dn_own), "dp")

    hid_w = w_in.shape[1]
    big = pltpu.VMEM((rows, width), f32)
    low = pltpu.VMEM((rows, width), bf16)
    n_m = (w_out.shape[0] + w_in.shape[0] + w_down.shape[0]) // 2
    wide = pltpu.VMEM((groups, max(rows, n_m), hid_w), f32)
    four = pltpu.VMEM((groups, rows, hid_w), bf16)
    (outputs, do, dx2, dctx, dqf, dstate, ng2, wout, grad_m, give_m) = call(
        main_body,
        [
            ((rows, width), bf16), ((rows, width), bf16), ((rows, width), f32), ((rows, width), bf16),
            ((rows, width), f32), ((groups, STATE, PAIR), bf16), ((2, width), f32),
            ((groups,) + w_out.shape, bf16), ((groups, n_m, width), f32), ((groups, n_m, width), bf16),
        ],
        [SM] + [VM] * 10 + [HB] * 4,
        [
            pltpu.VMEM((groups, width, hid_w), bf16), pltpu.VMEM((groups, hid_w, width), bf16),
            big, big, pltpu.VMEM((rows, 128), f32), wide, wide, big, big, big, big,
            low, low, low, low, low, low, four, four, low, pltpu.VMEM((groups, n_m, width), bf16),
            pltpu.SemaphoreType.DMA((3,)), pltpu.SemaphoreType.DMA,
        ],
        mm * hid_w * groups * 6, 24 << 20, 44,
        (HB, VM, HB, VM, HB, VM, VM, VM, HB, HB),
    )(meta, near, qkv, *states, tok, cot, norm_gains, norm_biases, io_own, io_oth, dn_own, dn_oth)

    do, dstate, give_m, grad_m, _ = lax.optimization_barrier((do, dstate, give_m, grad_m, held_state))
    dstates = all_states(dstate)
    do_l, do_r = from_mp(do[rows - EDGE :], 1), from_mp(do[:EDGE], -1)

    def halve(own, got, s):
        n = own.shape[-1] // 2
        bit = bit_of(me, core, s)

        def half(at, own, got):
            a = lax.dynamic_slice_in_dim(own, at * n, n, own.ndim - 1).astype(f32)
            return a + lax.dynamic_slice_in_dim(got, at * n, n, own.ndim - 1).astype(f32)

        give = half(1 - bit, own, got).astype(bf16)
        own, got = after(own, give), after(got, give)
        return give, half(bit, own, got)

    def finish(keep, got, extra=None):
        tot = keep + got.astype(f32)
        for s in range(2, nbits - 1):
            tot = tot.astype(bf16).astype(f32) + swap(tot.astype(bf16), s).astype(f32)
        msg = tot.astype(bf16)
        if extra is None:
            return [exchange(msg, "mp")]
        more = jnp.broadcast_to(extra, (groups,) + extra.shape)
        msg = jnp.concatenate([msg, more], axis=1)
        part = [lax.dynamic_slice_in_dim(msg, zi ^ m, 1, 0) for m in range(groups)]
        return part[:1] + [swap_mp(part[m], m) for m in range(1, groups)]

    give_m, keep_m = halve(grad_m, swap_core(give_m), 0)
    got_m = swap(give_m, 0)
    dq, dkn, dvn = call(
        near_back_body,
        [((rows, width), bf16), ((rows, width), f32), ((rows, width), f32)],
        [SM] + [VM] * 4 + [HB] * 2,
        [
            pltpu.VMEM((rows + 2 * EDGE, width), bf16), pltpu.VMEM((rows + 2 * EDGE, width), f32),
            pltpu.VMEM((ext, width), f32), pltpu.VMEM((ext, width), f32),
            pltpu.VMEM(wout.shape, bf16), big, pltpu.SemaphoreType.DMA((2,)),
        ],
        mm * 2048, 24 << 20, 20,
    )(meta, qkv, after(dctx, give_m, *dstates), do_l, do_r, wout, dqf)
    give_m, keep_m = halve(keep_m, after(got_m, dq), 1)
    got_m = swap(give_m, 1)
    n_q = w_qkv.size // width // 2
    n_ng = 4 * width // 128
    dproj, grad_q, give_q = call(
        proj_body,
        [((groups, rows, 3 * PAIR), bf16), ((groups, n_q, width), f32), ((groups, n_q, width), f32)],
        [SM] + [VM] * 9,
        [
            pltpu.VMEM((groups, rows, 3 * PAIR), bf16), pltpu.VMEM((3 * width, 128), f32),
            pltpu.VMEM((2 * n_q, width), f32), pltpu.SemaphoreType.DMA,
        ],
        mm * 3 * width, 24 << 20, 20, (HB, VM, VM),
    )(meta, qkv, after(dq, give_m), dkn, dvn, *dstates, a1e)
    got_q = swap_core(after(give_q, got_m))
    tokens_grad, ng = call(
        last_body,
        [((rows, width), f32), ((2 * n_ng, 128), bf16)],
        [SM, HB, HB, HB, VM, HB, VM, VM],
        [
            big, pltpu.VMEM((n_ng, 128), f32), proj_w, pltpu.VMEM((groups, rows, 3 * PAIR), bf16), big,
            pltpu.SemaphoreType.DMA, pltpu.SemaphoreType.DMA((2,)),
        ],
        mm * 3 * width, 8 << 20, 16,
    )(meta, dproj, qkv_own, qkv_oth, tok, dx2, norm_gains, ng2)
    give_q, keep_q = halve(grad_q, got_q, 0)
    got_q = swap(give_q, 0)
    z_m = finish(keep_m, got_m)
    give_q, keep_q = halve(keep_q, got_q, 1)
    got_q = swap(give_q, 1)
    z_q = finish(keep_q, got_q, ng)

    blocks = owners.shape[0]
    earlier = jnp.arange(blocks)[None, :] < jnp.arange(blocks)[:, None]
    alike = owners[None, :] == owners[:, None]
    slot = jnp.sum((earlier & alike).astype(jnp.int32), axis=1)
    slot_rows = owners * capacity + slot
    hit = slot_rows[None, :] == jnp.arange(ndp * capacity, dtype=jnp.int32)[:, None]
    held = jnp.sum(jnp.where(hit, jnp.arange(blocks, dtype=jnp.int32)[None, :], 0), axis=1)
    filled = lax.dynamic_slice_in_dim(
        jnp.sum(hit.astype(jnp.int32), axis=1), me * capacity, capacity, 0
    )
    nb_q = n_q * 2 // 16

    def updated(z, n, first, extra=()):
        return call(
            functools.partial(pieces_body, first, len(z)),
            [((n, 128), f32), ((n, 128), bf16)] + list(extra),
            [SM, SM] + [VM] * (len(z) + 1), [], 1 << 20, 4 << 20, 20,
        )(owners, slot, *z, held_state)

    def everywhere(piece):
        buf = piece[None]
        for s in range(2):
            buf = grow(buf, s)
        return buf, swap_core(buf)

    piece_m, fresh_m = updated(z_m, n_m, nb_q)
    m_own, m_oth = everywhere(fresh_m)
    piece_q, fresh_q, ng_z = updated(z_q, n_q, 0, [((n_ng, 128), f32)])
    q_own, q_oth = everywhere(fresh_q)
    [send] = call(
        route_body, [((ndp, capacity * 8 + n_ng, 128), f32)], [SM, VM, VM, VM], [], 1 << 20, 4 << 20, 16,
    )(held, piece_q, piece_m, ng_z)
    recv = exchange(send, "dp")
    high = me - (me & 7)
    sources = jnp.stack(
        [
            high + c + ((j >> 1) << order[c][0]) + ((j & 1) << order[c][1])
            for c in range(2)
            for j in range(4)
        ]
    ).astype(jnp.int32)
    state_shape = (capacity, block_rows, 128)
    first_new, second_new, master_new, norm_sum = call(
        adam_body,
        [(state_shape, f32)] * 3 + [((n_ng, 128), f32)],
        [SM, SM] + [VM] * 4,
        [pltpu.VMEM((capacity, 2, 8, 128), f32), pltpu.VMEM((capacity * block_rows, 128), f32)],
        1 << 20, 8 << 20, 20,
    )(filled, sources, recv, master, first_moment, second_moment)
    new_out, new_in, new_down = call(
        place_body, [(w_out.shape, bf16), (w_in.shape, bf16), (w_down.shape, bf16)],
        [SM, VM, VM], [], 1 << 20, 4 << 20, 16,
    )(meta, m_own, m_oth)
    [new_qkv] = call(
        place_qkv_body, [(w_qkv.shape, bf16)], [SM, VM, VM],
        [pltpu.VMEM((w_qkv.size // 128, 128), f32)], 1 << 20, 2 << 20, 16,
    )(meta, q_own, q_oth)

    corr_one = 1.0 - beta_one**STEP
    corr_two = 1.0 - beta_two**STEP
    norm_grad = norm_sum.reshape(4, width)
    norm_params = jnp.stack([norm_gains[0], norm_biases[0], norm_gains[1], norm_biases[1]])
    norm_first_new = beta_one * norm_first + (1.0 - beta_one) * norm_grad
    norm_second_new = beta_two * norm_second + (1.0 - beta_two) * norm_grad * norm_grad
    norm_new = norm_params - norm_rate * (
        norm_first_new / corr_one / (jnp.sqrt(norm_second_new / corr_two) + adam_epsilon)
    )
    return (
        outputs[None], tokens_grad[None], first_new, second_new, master_new,
        new_qkv, new_out, new_in, new_down, norm_first_new, norm_second_new, norm_new,
    )


def solution(mesh):
    sharded = P("dp", "mp", None)
    return jax.shard_map(
        per_device,
        mesh=mesh,
        in_specs=(
            sharded, sharded, P("dp"), P(), P(None, "mp"), P("mp", None), P(None, "mp"), P("mp", None),
            sharded, sharded, sharded, P(), P(), P(), P(),
        ),
        out_specs=(
            sharded, sharded, sharded, sharded, sharded,
            P(None, "mp"), P("mp", None), P(None, "mp"), P("mp", None), P(), P(), P(),
        ),
        check_vma=False,
    )
```

```python
import functools

import jax
import jax.numpy as jnp
from jax import lax
from jax.experimental import pallas as pl
from jax.experimental.pallas import tpu as pltpu
from jax.sharding import PartitionSpec as P

HEAD = 64
BAND = 30
STEP = 10
HALO = 64
EDGE = 32
QB = 64
WIN = 128
PAIR = 128
COST = 1
STATE = 144

learn_rate = 0.1
norm_rate = 0.3
decay_rate = 0.1
beta_one = 0.9
beta_two = 0.95
adam_epsilon = 1e-08
norm_epsilon = 1e-05
GELU_C = 0.7978845608028654
GELU_A = 0.044715

f32 = jnp.float32
bf16 = jnp.bfloat16

VM = pl.BlockSpec(memory_space=pltpu.VMEM)
HB = pl.BlockSpec(memory_space=pltpu.HBM)
SM = pl.BlockSpec(memory_space=pltpu.SMEM)


def call(body, outs, in_specs, scratch, flops, moved, vmem=48, out_specs=None):
    specs = out_specs or tuple(VM for _ in outs)
    run = pl.pallas_call(
        body,
        out_shape=tuple(
            pltpu.HBM(s, d) if spec is HB else jax.ShapeDtypeStruct(s, d) for (s, d), spec in zip(outs, specs)
        ),
        in_specs=in_specs,
        out_specs=specs,
        scratch_shapes=scratch,
        compiler_params=pltpu.CompilerParams(vmem_limit_bytes=vmem << 20),
        cost_estimate=pl.CostEstimate(flops=flops // COST, bytes_accessed=moved // COST, transcendentals=0),
    )

    def fixed(*args):
        return run(
            *[
                pltpu.with_memory_space_constraint(x, pltpu.HBM) if spec is HB else x
                for x, spec in zip(args, in_specs)
            ]
        )

    return fixed


def dot(a, b):
    return jnp.dot(a, b, preferred_element_type=f32)


def turned(a):
    return a.astype(f32).T.astype(bf16)


def dot_nt(a, b):
    return dot(a, turned(b))


def dot_tn(a, b):
    return lax.dot_general(a, b, (((0,), (0,)), ((), ())), preferred_element_type=f32)


def normalize(x):
    mean = jnp.mean(x, axis=-1, keepdims=True)
    cen = x - mean
    var = jnp.mean(cen * cen, axis=-1, keepdims=True)
    rstd = lax.rsqrt(var + norm_epsilon)
    return cen * rstd, rstd


def same_head(n=PAIR):
    r = lax.broadcasted_iota(jnp.int32, (n, n), 0)
    c = lax.broadcasted_iota(jnp.int32, (n, n), 1)
    return (r < HEAD) == (c < HEAD)


def pack_state(s1, s2, z):
    both = jnp.where(same_head(), s1, pltpu.roll(s2, HEAD, 1))
    hi = z.astype(bf16).astype(f32)
    row = lax.broadcasted_iota(jnp.int32, (16, PAIR), 0)
    tail = jnp.where(row == 0, hi, jnp.where(row == 1, z - hi, 0.0))
    return both.astype(bf16), tail.astype(bf16)


def unpack_state(refs, g):
    tot = refs[0][g].astype(f32)
    for r in refs[1:]:
        tot = tot + r[g].astype(f32)
    both = tot[:PAIR]
    diag = same_head()
    s1 = jnp.where(diag, both, 0.0)
    s2 = jnp.where(diag, pltpu.roll(both, HEAD, 1), 0.0)
    z = tot[PAIR : PAIR + 1] + tot[PAIR + 1 : PAIR + 2]
    return s1, s2, z


def split_dot(a, ones):
    hi, lo = two(a)
    return dot(hi, ones) + dot(lo, ones)


def two(a):
    hi = a.astype(bf16)
    return hi, (a - hi.astype(f32)).astype(bf16)


def phi(v):
    low = jnp.exp(jnp.minimum(v, 0.0))
    return jnp.where(v > 0, v + 1.0, low), jnp.where(v > 0, 1.0, low)


def band_parts():
    c = lax.broadcasted_iota(jnp.int32, (WIN, 2 * QB), 0)
    r = lax.broadcasted_iota(jnp.int32, (WIN, 2 * QB), 1) % QB
    off = r + EDGE - c
    return (jnp.abs(off) <= BAND), off == 0, c


def stacked(rows):
    lane = lax.broadcasted_iota(jnp.int32, (1, PAIR), 1)
    first = (lane < HEAD).astype(f32).astype(bf16)
    second = (lane >= HEAD).astype(f32).astype(bf16)
    return jnp.concatenate([rows * first, rows * second], axis=0)


def unstack(both):
    lane = lax.broadcasted_iota(jnp.int32, (QB, PAIR), 1)
    return jnp.where(lane < HEAD, both[:QB], both[QB:])


def softmax_of(raw, mask):
    scores = jnp.where(mask, raw * 0.125, -1e30)
    ex = jnp.exp(scores - jnp.max(scores, axis=0, keepdims=True))
    return ex * (1.0 / jnp.sum(ex, axis=0, keepdims=True))


def piece_at(meta, r, bits, other):
    b0, b1 = (meta[6], meta[7]) if other else (meta[4], meta[5])
    core = 1 - meta[2] if other else meta[2]
    if bits == 1:
        return core * 2 + (b0 ^ r)
    return core * 4 + (b0 ^ (r & 1)) * 2 + (b1 ^ (r >> 1))


def fetch_pieces(meta, bufs, lo, rows, weight, sem):
    n = len(bufs) // 2
    copies = []
    for k, buf in enumerate(bufs):
        p = piece_at(meta, k % n, n // 2, k >= n)
        at = pl.ds(pl.multiple_of(p * rows, rows), rows)
        for m in range(buf.shape[0]):
            src = buf.at[m, pl.ds(lo, rows), :]
            copies.append(pltpu.make_async_copy(src, weight.at[meta[3] ^ m, at, :], sem))
    for c in copies:
        c.start()
    return copies


def norm_body(tok, left, right, gains, biases, a1e_o):
    rows = tok.shape[0]
    gain, bias = gains[0:1, :], biases[0:1, :]

    def ln(x):
        return (normalize(x.astype(f32))[0] * gain + bias).astype(bf16)

    a1e_o[0:HALO, :] = ln(left[...])
    a1e_o[HALO + rows :, :] = ln(right[...])

    def chunk(i, _):
        at = pl.ds(pl.multiple_of(i * 128, 128), 128)
        a1e_o[pl.ds(pl.multiple_of(i * 128 + HALO, 64), 128), :] = ln(tok[at, :])
        return 0

    lax.fori_loop(0, rows // 128, chunk, 0)


def qkv_body(meta, a1e, *refs):
    bufs, (qkv_o, st_o, w, sem) = refs[:4], refs[4:]
    ext = a1e.shape[0]
    rows = ext - 2 * HALO
    groups = bufs[0].shape[0]
    for c in fetch_pieces(meta, bufs, 0, bufs[0].shape[1], w, sem):
        c.wait()
    length, base = meta[0], meta[1]
    pos = base + lax.broadcasted_iota(jnp.int32, (rows, 1), 0)
    valid = (pos < length).astype(f32)
    gs = range(groups)
    for g in gs:
        qkv_o[g] = dot(a1e[...], w[g]).astype(bf16)
    own_rows = slice(HALO, HALO + rows)
    parts = []
    for g in gs:
        keys = qkv_o[g, own_rows, PAIR : 2 * PAIR].astype(f32)
        feat = phi(keys)[0] * valid
        parts.append((jnp.sum(feat, axis=0, keepdims=True), two(feat), two(jnp.tanh(keys) * valid)))
    for g in gs:
        z, (fhi, flo), (thi, tlo) = parts[g]
        vals = qkv_o[g, own_rows, 2 * PAIR :]
        s1 = dot_tn(fhi, vals) + dot_tn(flo, vals)
        s2 = dot_tn(thi, vals) + dot_tn(tlo, vals)
        st_o[g, :PAIR, :], st_o[g, PAIR:, :] = pack_state(s1, s2, z)


def near_body(meta, qkv, near_o):
    groups = qkv.shape[0]
    rows = near_o.shape[0]
    length, base = meta[0], meta[1]
    band, diag, lane = band_parts()

    def block(b, _):
        at = b * QB
        kpos = base + at - EDGE + lane
        mask = band & (((kpos >= 0) & (kpos < length)) | diag)
        q_at = pl.ds(pl.multiple_of(at + HALO, QB), QB)
        w_at = pl.ds(pl.multiple_of(at + HALO - EDGE, EDGE), WIN)
        gs = range(groups)
        sc = [dot_nt(qkv[g, w_at, PAIR : 2 * PAIR], stacked(qkv[g, q_at, 0:PAIR])) for g in gs]
        p = [softmax_of(sc[g], mask).astype(bf16) for g in gs]
        res = [dot_tn(p[g], qkv[g, w_at, 2 * PAIR :]) for g in gs]
        for g in gs:
            near_o[pl.ds(pl.multiple_of(at, QB), QB), g * PAIR : (g + 1) * PAIR] = unstack(res[g])
        return 0

    lax.fori_loop(0, rows // QB, block, 0, unroll=4)


def put_halves(core, keep, give, g, lo, grad):
    n, width = grad.shape
    tiles = grad.reshape(n // 16, 2, 8, width)
    even, odd = tiles[:, 0].reshape(n // 2, width), tiles[:, 1].reshape(n // 2, width)
    first = jnp.full(even.shape, core, jnp.int32) == 0
    at = slice(lo, lo + n // 2)
    keep[g, at, :] = jnp.where(first, even, odd).astype(keep.dtype)
    give[g, at, :] = jnp.where(first, odd, even).astype(give.dtype)


def main_body(meta, near, qkv, s0, s1, s2, s3, tok, cot, gains, biases, *refs):
    bufs, refs = refs[:8], refs[8:]
    out_h, do_o, head_o, tail_o, dx2_h, dctx_o, dqf_h, dst_o, ng_o, wout_o, keep_h, give_h = refs[:12]
    w_in, w_down, x2, xhat, rs, u, dh, acc, da2, far1, inv, dnum, phq, thq = refs[12:26]
    ctx_o, a2_o, dm_o, hid_o, du_o, out_o, keep, give, sem, out_sem = refs[26:]
    rows, width = tok.shape
    groups, hw = hid_o.shape[0], hid_o.shape[2]
    pr = hw // 8
    orow = bufs[0].shape[1] - 2 * pr
    core = meta[2]
    sent = []

    def send(src, dst):
        sent.append(pltpu.make_async_copy(src, dst, out_sem))
        sent[-1].start()

    length, base = meta[0], meta[1]
    copies = fetch_pieces(meta, bufs, 2 * pr, orow, wout_o, sem.at[0])
    later = fetch_pieces(meta, bufs, 0, pr, w_in, sem.at[1])
    last = fetch_pieces(meta, bufs, pr, pr, w_down, sem.at[2])
    rlen = 1.0 / length.astype(f32)
    gain, bias = gains[1:2, :], biases[1:2, :]
    ones = same_head().astype(f32).astype(bf16)
    gs = range(groups)
    cols = [slice(g * PAIR, (g + 1) * PAIR) for g in gs]
    states = [unpack_state((s0, s1, s2, s3), g) for g in gs]
    s1b, s2b = [two(st[0]) for st in states], [two(st[1]) for st in states]
    cr = 128

    def far_chunk(i, _):
        at = pl.ds(pl.multiple_of(i * cr, cr), cr)
        q_at = pl.ds(pl.multiple_of(i * cr + HALO, HALO), cr)
        q = [qkv[g, q_at, 0:PAIR].astype(f32) for g in gs]
        ph = [phi(q[g])[0] for g in gs]
        ph2 = [two(ph[g]) for g in gs]
        th2 = [two(jnp.tanh(q[g])) for g in gs]
        den = [split_dot(ph[g] * states[g][2], ones) for g in gs]
        num = [dot(ph2[g][0], s1b[g][0]) + dot(ph2[g][0], s1b[g][1]) + dot(ph2[g][1], s1b[g][0]) for g in gs]
        sec = [dot(th2[g][0], s2b[g][0]) + dot(th2[g][0], s2b[g][1]) + dot(th2[g][1], s2b[g][0]) for g in gs]
        for g in gs:
            phq[at, cols[g]] = ph2[g][0]
            thq[at, cols[g]] = th2[g][0]
        rec = [1.0 / den[g] for g in gs]
        for g in gs:
            part = num[g] * rec[g]
            inv[at, cols[g]] = rec[g]
            far1[at, cols[g]] = part
            ctx_o[at, cols[g]] = (near[at, cols[g]] + (part + sec[g] * rlen)).astype(bf16)
        pos = base + i * cr + lax.broadcasted_iota(jnp.int32, (cr, 1), 0)
        dm_o[at, :] = (cot[at, :].astype(f32) * (pos < length).astype(f32)).astype(bf16)
        return 0

    lax.fori_loop(0, rows // cr, far_chunk, 0)
    for c in copies:
        c.wait()
    wout = wout_o[...].reshape(width, width)
    x2[...] = dot(ctx_o[...], wout)

    def norm_chunk(i, _):
        at = pl.ds(pl.multiple_of(i * 64, 64), 64)
        val = x2[at, :] + tok[at, :].astype(f32)
        x2[at, :] = val
        xh, rstd = normalize(val)
        xhat[at, :] = xh
        rs[at, :] = jnp.broadcast_to(rstd, (64, 128))
        a2_o[at, :] = (xh * gain + bias).astype(bf16)
        return 0

    lax.fori_loop(0, rows // 64, norm_chunk, 0)
    for c in later + last:
        c.wait()
    for g in gs:
        u[g] = dot(a2_o[...], w_in[g])
        dh[g] = dot_nt(dm_o[...], w_down[g])

    def act(i, _):
        at = pl.ds(pl.multiple_of(i * 16, 16), 16)
        for g in gs:
            v = u[g, at, :]
            sq = v * v
            half = 0.5 + 0.5 * jnp.tanh(v * (GELU_C + GELU_C * GELU_A * sq))
            hid = v * half
            hid_o[g, at, :] = hid.astype(bf16)
            slope = half + (hid * (1.0 - half)) * (2.0 * GELU_C + 6.0 * GELU_C * GELU_A * sq)
            du_o[g, at, :] = (dh[g, at, :] * slope).astype(bf16)
        return 0

    lax.fori_loop(0, rows // 16, act, 0)
    acc[...] = sum(dot(hid_o[g], w_down[g]) for g in gs)
    da2[...] = sum(dot_nt(du_o[g], w_in[g]) for g in gs)

    def back_chunk(i, carry):
        dg, db = carry
        at = pl.ds(pl.multiple_of(i * 64, 64), 64)
        out_o[at, :] = (x2[at, :] + acc[at, :]).astype(bf16)
        xh = xhat[at, :]
        rstd = rs[at, 0:1]
        d = da2[at, :]
        dg = dg + jnp.sum(d * xh, axis=0, keepdims=True)
        db = db + jnp.sum(d, axis=0, keepdims=True)
        e = d * gain
        m1 = jnp.mean(e, axis=-1, keepdims=True)
        m2 = jnp.mean(e * xh, axis=-1, keepdims=True)
        dx = dm_o[at, :].astype(f32) + rstd * (e - m1 - xh * m2)
        acc[at, :] = dx
        do_o[at, :] = dx.astype(bf16)
        return dg, db

    zero = jnp.zeros((1, width), f32)
    dg, db = lax.fori_loop(0, rows // 64, back_chunk, (zero, zero))
    head_o[...] = do_o[0:EDGE, :]
    tail_o[...] = do_o[rows - EDGE :, :]
    send(out_o, out_h)
    send(acc, dx2_h)
    ng_o[0:1, :] = dg
    ng_o[1:2, :] = db
    dctx_o[...] = dot_nt(do_o[...], wout).astype(bf16)

    def far_back(i, carry):
        at = pl.ds(pl.multiple_of(i * cr, cr), cr)
        q_at = pl.ds(pl.multiple_of(i * cr + HALO, HALO), cr)
        dc = [dctx_o[at, cols[g]] for g in gs]
        dcf = [dc[g].astype(f32) for g in gs]
        rec = [inv[at, cols[g]] for g in gs]
        dn = [(dcf[g] * rec[g]).astype(bf16) for g in gs]
        dots = [split_dot(dcf[g] * far1[at, cols[g]], ones) for g in gs]
        dph = [dot_nt(dn[g], s1b[g][0]) for g in gs]
        dth = [dot_nt(dc[g], s2b[g][0]) for g in gs]
        out = []
        for g in gs:
            dnum[at, cols[g]] = dn[g]
            dden = -dots[g] * rec[g]
            out.append(carry[g] + jnp.sum(phq[at, cols[g]].astype(f32) * dden, axis=0, keepdims=True))
            slope = phi(qkv[g, q_at, 0:PAIR].astype(f32))[1]
            th = thq[at, cols[g]].astype(f32)
            da2[at, cols[g]] = (dph[g] + dden * states[g][2]) * slope + dth[g] * rlen * (1.0 - th * th)
        return tuple(out)

    none = jnp.zeros((1, PAIR), f32)
    dz = lax.fori_loop(0, rows // cr, far_back, (none,) * groups)
    for g in gs:
        d1 = dot_tn(phq[:, cols[g]], dnum[:, cols[g]])
        d2 = dot_tn(thq[:, cols[g]], dctx_o[:, cols[g]]) * rlen
        dst_o[g, :PAIR, :], dst_o[g, PAIR:, :] = pack_state(d1, d2, dz[g])
    send(da2, dqf_h)
    n_out = ctx_o.shape[1] // groups

    def finish(g, lo, n, grad):
        put_halves(core, keep, give, g, lo, grad)
        part = pl.ds(lo, n)
        send(keep.at[g, part, :], keep_h.at[g, part, :])
        send(give.at[g, part, :], give_h.at[g, part, :])

    for g in gs:
        finish(g, n_out // 2, width // 2, dot_tn(a2_o[...], du_o[g]))
    for g in gs:
        finish(g, 0, n_out // 2, dot_tn(ctx_o[:, g * n_out : (g + 1) * n_out], do_o[...]))
    for g in gs:
        finish(g, n_out // 2 + width // 2, hw // 2, dot_tn(hid_o[g], dm_o[...]))
    for c in sent:
        c.wait()


def near_back_body(
    meta, qkv, dctx, do_l, do_r, wout_h, dqf_h, dq_o, dk_o, dv_o, dce, dqe, dke, dve, wout, dqf, sem,
):
    groups = qkv.shape[0]
    rows = dctx.shape[0]
    length, base = meta[0], meta[1]
    band, diag, lane = band_parts()
    first = pltpu.make_async_copy(wout_h, wout, sem.at[0])
    first.start()
    second = pltpu.make_async_copy(dqf_h, dqf, sem.at[1])
    second.start()
    first.wait()
    w = wout[...].reshape(dctx.shape[1], -1)
    dce[0:EDGE, :] = dot_nt(do_l[...], w).astype(bf16)
    dce[EDGE : EDGE + rows, :] = dctx[...]
    dce[EDGE + rows :, :] = dot_nt(do_r[...], w).astype(bf16)
    dke[...] = jnp.zeros(dke.shape, f32)
    dve[...] = jnp.zeros(dve.shape, f32)

    def block(b, _):
        at = b * QB
        kpos = base + at - HALO + lane
        mask = band & (((kpos >= 0) & (kpos < length)) | diag)
        c_at = pl.ds(pl.multiple_of(at, QB), QB)
        q_at = pl.ds(pl.multiple_of(at + EDGE, EDGE), QB)
        w_at = pl.ds(pl.multiple_of(at, QB), WIN)
        gs = range(groups)
        cols = [slice(g * PAIR, (g + 1) * PAIR) for g in gs]
        qs = [stacked(qkv[g, q_at, 0:PAIR]) for g in gs]
        cs = [stacked(dce[c_at, cols[g]]) for g in gs]
        kw = [qkv[g, w_at, PAIR : 2 * PAIR] for g in gs]
        sc = [dot_nt(kw[g], qs[g]) for g in gs]
        dp = [dot_nt(qkv[g, w_at, 2 * PAIR :], cs[g]) for g in gs]
        p = [softmax_of(sc[g], mask) for g in gs]
        row = [jnp.sum(p[g] * dp[g], axis=0, keepdims=True) for g in gs]
        ds = [(p[g] * (dp[g] - row[g])).astype(bf16) for g in gs]
        pb = [p[g].astype(bf16) for g in gs]
        for g in gs:
            dke[w_at, cols[g]] += dot(ds[g], qs[g])
            dve[w_at, cols[g]] += dot(pb[g], cs[g])
        dq = [dot_tn(ds[g], kw[g]) for g in gs]
        for g in gs:
            dqe[c_at, cols[g]] = unstack(dq[g])
        return 0

    lax.fori_loop(0, rows // QB + 1, block, 0, unroll=9)
    second.wait()
    dq_o[...] = (dqe[EDGE : EDGE + rows, :] * 0.125 + dqf[...]).astype(bf16)
    dk_o[...] = dke[HALO : HALO + rows, :] * 0.125
    dv_o[...] = dve[HALO : HALO + rows, :]


def proj_body(meta, qkv, dq, dkn, dvn, s0, s1, s2, s3, a1e, dproj_h, keep_o, give_o, dproj, flat, pseudo, sem):
    groups = qkv.shape[0]
    rows, width = dq.shape
    length, base, core = meta[0], meta[1], meta[2]
    cr = 128
    gs = range(groups)
    cols = [slice(g * PAIR, (g + 1) * PAIR) for g in gs]
    states = [unpack_state((s0, s1, s2, s3), g) for g in gs]
    s1b, s2b = [st[0].astype(bf16) for st in states], [st[1].astype(bf16) for st in states]

    def far_chunk(i, _):
        at = pl.ds(pl.multiple_of(i * cr, cr), cr)
        e_at = pl.ds(pl.multiple_of(i * cr + HALO, HALO), cr)
        pos = base + i * cr + lax.broadcasted_iota(jnp.int32, (cr, 1), 0)
        valid = (pos < length).astype(f32)
        k = [qkv[g, e_at, PAIR : 2 * PAIR].astype(f32) for g in gs]
        v = [qkv[g, e_at, 2 * PAIR :] for g in gs]
        feat = [phi(k[g]) for g in gs]
        th = [jnp.tanh(k[g]) for g in gs]
        vd1 = [dot_nt(v[g], s1b[g]) for g in gs]
        vd2 = [dot_nt(v[g], s2b[g]) for g in gs]
        dv = [
            dot((feat[g][0] * valid).astype(bf16), s1b[g]) + dot((th[g] * valid).astype(bf16), s2b[g]) for g in gs
        ]
        for g in gs:
            dk = (vd1[g] + states[g][2]) * feat[g][1] + vd2[g] * (1.0 - th[g] * th[g])
            dproj[g, at, 0:PAIR] = dq[at, cols[g]]
            dproj[g, at, PAIR : 2 * PAIR] = (dkn[at, cols[g]] + dk * valid).astype(bf16)
            dproj[g, at, 2 * PAIR :] = (dvn[at, cols[g]] + dv[g]).astype(bf16)
        return 0

    lax.fori_loop(0, rows // cr, far_chunk, 0)
    out = pltpu.make_async_copy(dproj, dproj_h, sem)
    out.start()
    n_flat = 3 * width
    for g in gs:
        grad = dot_tn(a1e[HALO : HALO + rows, :], dproj[g])
        for part in range(3):
            flat[pl.ds(part, width, stride=3), :] = grad[:, part * PAIR : (part + 1) * PAIR]
        for j in range(4):
            pseudo[:, j * 128 : (j + 1) * 128] = flat[pl.ds(j, n_flat // 4, stride=4), :]
        put_halves(core, keep_o, give_o, g, 0, pseudo[...])
    out.wait()


def last_body(meta, dproj_h, tok, dx2_h, gains, ng2, *refs):
    bufs, (tg_o, ng_o, da1, ngs, wqkv, dproj, dx2, sem, sems) = refs[:4], refs[4:]
    groups = dproj.shape[0]
    rows, width = tok.shape
    gain = gains[0:1, :]
    copies = fetch_pieces(meta, bufs, 0, bufs[0].shape[1], wqkv, sem)
    copies.append(pltpu.make_async_copy(dproj_h, dproj, sems.at[0]))
    copies[-1].start()
    late = pltpu.make_async_copy(dx2_h, dx2, sems.at[1])
    late.start()
    for c in copies:
        c.wait()
    da1[...] = sum(dot_nt(dproj[g], wqkv[g]) for g in range(groups))

    late.wait()

    def back_chunk(i, carry):
        dg, db = carry
        at = pl.ds(pl.multiple_of(i * 64, 64), 64)
        xh, rstd = normalize(tok[at, :].astype(f32))
        d = da1[at, :]
        dg = dg + jnp.sum(d * xh, axis=0, keepdims=True)
        db = db + jnp.sum(d, axis=0, keepdims=True)
        e = d * gain
        m1 = jnp.mean(e, axis=-1, keepdims=True)
        m2 = jnp.mean(e * xh, axis=-1, keepdims=True)
        tg_o[at, :] = dx2[at, :] + rstd * (e - m1 - xh * m2)
        return dg, db

    zero = jnp.zeros((1, width), f32)
    dg, db = lax.fori_loop(0, rows // 64, back_chunk, (zero, zero))
    for k, val in enumerate((dg, db, ng2[0:1, :], ng2[1:2, :])):
        for j in range(width // 128):
            at = k * (width // 128) + j
            ngs[at : at + 1, :] = val[:, j * 128 : (j + 1) * 128]
    ng_o[...] = ngs[...]


def slices_body(where, master, first, second, out_h, held, parts, sem, out_sem):
    caps = held.shape[1] // 64
    copies = [pltpu.make_async_copy(ref, held.at[t], sem.at[t]) for t, ref in enumerate((master, first, second))]
    for c in copies:
        c.start()
    sent = []
    for t in range(3):
        copies[t].wait()
        for j in range(4):
            val = held[t, pl.ds(j, caps * 16, stride=4), :].reshape(caps, 2, 8, 128)
            for c in range(2):
                parts[t, c, j] = val[:, c].reshape(caps * 8, 128)
                for d in where[c][j]:
                    sent.append(pltpu.make_async_copy(parts.at[t, c, j], out_h.at[d, t], out_sem))
                    sent[-1].start()
    for c in sent:
        c.wait()


def adam(g, m_old, f_old, s_old):
    corr_one = 1.0 - beta_one**STEP
    corr_two = 1.0 - beta_two**STEP
    fn = beta_one * f_old + (1.0 - beta_one) * g
    sn = beta_two * s_old + (1.0 - beta_two) * g * g
    step = fn / corr_one / (jnp.sqrt(sn / corr_two) + adam_epsilon)
    return fn, sn, m_old - learn_rate * (step + decay_rate * m_old)


def pieces_body(first, count, owners, slots, *refs):
    parts, st, piece_o, w_o, norms = refs[:count], refs[count], refs[count + 1], refs[count + 2], refs[count + 3 :]
    n = piece_o.shape[0]
    src = [(r, s) for r in parts for s in range(r.shape[0])]
    piece_o[...] = sum(r[s, 0:n, :].astype(f32) for r, s in src)
    if norms:
        norms[0][...] = sum(r[s, n:, :] for r, s in src)

    def pair(i, _):
        new = []
        for k in range(2):
            b = i * 2 + k
            at = pl.ds(pl.multiple_of(slots[first + b] * 8, 8), 8)
            own = owners[first + b]
            g = piece_o[pl.ds(pl.multiple_of(b * 8, 8), 8), :]
            new.append(adam(g, st[own, 0, at, :], st[own, 1, at, :], st[own, 2, at, :])[2])
        w_o[pl.ds(pl.multiple_of(i * 16, 16), 16), :] = jnp.concatenate(new, axis=0).astype(bf16)
        return 0

    lax.fori_loop(0, n // 16, pair, 0, unroll=4)


def route_body(blocks, pq, pm, ng, send_o):
    nq = pq.shape[0] // 8
    dests, per, _ = send_o.shape
    k_ng = ng.shape[0]
    caps = (per - 2 * k_ng) // 8
    hi, lo = two(ng[...])

    def dest(d, _):
        for r in range(0, caps, 2):
            both = []
            for k in range(2):
                b = blocks[d * caps + r + k]
                x = pq[pl.ds(pl.multiple_of(jnp.minimum(b, nq - 1) * 8, 8), 8), :]
                y = pm[pl.ds(pl.multiple_of(jnp.maximum(b - nq, 0) * 8, 8), 8), :]
                both.append(jnp.where(jnp.full((8, 128), b, jnp.int32) < nq, x, y))
            send_o[d, r * 8 : r * 8 + 16, :] = jnp.concatenate(both, axis=0).astype(bf16)
        send_o[d, caps * 8 : caps * 8 + k_ng, :], send_o[d, caps * 8 + k_ng :, :] = hi, lo
        return 0

    lax.fori_loop(0, dests, dest, 0)


def adam_body(filled, sources, recv, master, first, second, f_o, s_o, m_o, ng_o, two, grad):
    caps, br, _ = master.shape
    for j in range(4):
        for c in range(2):
            two[:, c] = recv[sources[c * 4 + j], 0 : caps * 8, :].astype(f32).reshape(caps, 8, 128)
        grad[pl.ds(j, caps * 16, stride=4), :] = two[...].reshape(caps * 16, 128)

    def add(s, tot):
        part = recv[s, caps * 8 :, :].astype(f32)
        return tot + (part[: part.shape[0] // 2] + part[part.shape[0] // 2 :])

    ng_o[...] = lax.fori_loop(0, recv.shape[0], add, jnp.zeros(ng_o.shape, f32))

    def slot(r, _):
        g = grad[pl.ds(pl.multiple_of(r * br, br), br), :]
        m_old, f_old, s_old = master[r], first[r], second[r]
        fn, sn, mn = adam(g, m_old, f_old, s_old)
        keep = jnp.full(g.shape, filled[r], jnp.int32) > 0
        f_o[r] = jnp.where(keep, fn, f_old)
        s_o[r] = jnp.where(keep, sn, s_old)
        m_o[r] = jnp.where(keep, mn, m_old)
        return 0

    lax.fori_loop(0, caps, slot, 0, unroll=2)


def collect(meta, bufs, held, sem):
    copies = []
    for k, buf in enumerate(bufs):
        copies.append(pltpu.make_async_copy(buf, held.at[piece_at(meta, k % 4, 2, k >= 4)], sem))
        copies[-1].start()
    for c in copies:
        c.wait()


def columns(held, j, lo, n):
    even, odd = [held[c * 4 + j, lo : lo + n, :].astype(f32).reshape(n // 8, 1, 8, 128) for c in range(2)]
    return jnp.concatenate([even, odd], axis=1).reshape(2 * n, 128)


def place_body(meta, *refs):
    bufs, outs, (held, sem) = refs[:8], refs[8:11], refs[11:]
    collect(meta, bufs, held, sem)
    lo = 0
    for ref in outs:
        n = ref.shape[0] // 2
        for j in range(4):
            ref[:, j * 128 : (j + 1) * 128] = columns(held, j, lo, n).astype(bf16)
        lo += n


def place_qkv_body(meta, *refs):
    bufs, (q_o, held, flat, sem) = refs[:8], refs[8:]
    collect(meta, bufs, held, sem)
    n = held.shape[1]
    rows = q_o.shape[0]
    for j in range(4):
        flat[pl.ds(j, 2 * n, stride=4), :] = columns(held, j, 0, n)
    for part in range(3):
        q_o[:, part * 128 : (part + 1) * 128] = flat[pl.ds(part, rows, stride=3), :].astype(bf16)


def per_device(
    tokens, cotangent, lengths, owners, w_qkv, w_out, w_in, w_down,
    master, first_moment, second_moment, norm_gains, norm_biases, norm_first, norm_second,
):
    rows, width = tokens.shape[1], tokens.shape[2]
    groups = lax.axis_size("mp")
    ndp = lax.axis_size("dp")
    nbits = ndp.bit_length() - 1
    rest = list(range(1, nbits))
    order = (rest, rest[:2][::-1] + rest[2:][::-1])
    me, zi = lax.axis_index("dp"), lax.axis_index("mp")
    core = me & 1

    def bit_of(who, at, s):
        return (who >> jnp.where(at == 0, order[0][s], order[1][s])) & 1

    def swap(x, s):
        return lax.ppermute(x, "dp", [(i, i ^ (1 << order[i & 1][s])) for i in range(ndp)])

    def swap_core(x):
        return lax.ppermute(x, "dp", [(i, i ^ 1) for i in range(ndp)])

    def from_mp(x, step):
        return lax.ppermute(x, "mp", [(i, i + step) for i in range(groups) if 0 <= i + step < groups])

    def swap_mp(x, mask):
        return lax.ppermute(x, "mp", [(i, i ^ mask) for i in range(groups)])

    def exchange(x, axis):
        return lax.all_to_all(x, axis, 0, 0, tiled=True)

    def all_states(x):
        return [x] + [swap_mp(x, m) for m in range(1, groups)]

    q0, q1 = bit_of(me, core, 0), bit_of(me, core, 1)
    o0, o1 = bit_of(me, 1 - core, 0), bit_of(me, 1 - core, 1)
    length = lengths[0]
    base = zi * rows
    ids = [length, base, core, zi, q0, q1, o0, o1]
    meta = jnp.stack(ids).astype(jnp.int32)

    def after(x, *deps):
        return lax.optimization_barrier((x,) + deps)[0]

    def over_mp(piece):
        return jnp.stack([piece] + [swap_mp(piece, m) for m in range(1, groups)])

    def both_cores(bufs):
        return bufs + [swap_core(b) for b in bufs]

    def part_of(w, n, at):
        return lax.dynamic_slice_in_dim(w, at * (w.shape[0] // n), w.shape[0] // n, 0)

    mine = core * 4 + q0 * 2 + q1
    tok, cot = tokens[0], cotangent[0]
    ext = rows + 2 * HALO
    mm = 2 * rows * width
    qkv_z = over_mp(part_of(w_qkv, 4, core * 2 + q0))
    left, right = from_mp(tok[rows - HALO :], 1), from_mp(tok[:HALO], -1)
    qkv_bufs = [qkv_z, swap(qkv_z, 0)]
    ffn_piece = jnp.concatenate([part_of(w, 8, mine) for w in (w_in, w_down, w_out)], axis=0)
    ffn_z = over_mp(after(ffn_piece, qkv_z))
    [a1e] = call(norm_body, [((ext, width), bf16)], [VM] * 5, [], 4 * mm, 1 << 20, 16)(
        tok, left, right, norm_gains, norm_biases
    )
    qkv_bufs = both_cores([qkv_bufs[0], after(qkv_bufs[1], a1e)])
    proj_w = pltpu.VMEM((groups, width, 3 * PAIR), bf16)
    qkv, state = call(
        qkv_body,
        [((groups, ext, 3 * PAIR), bf16), ((groups, STATE, PAIR), bf16)],
        [SM, VM] + [HB] * 4,
        [proj_w, pltpu.SemaphoreType.DMA],
        2 * ext * width * 3 * width, 6 << 20, 20,
    )(meta, after(a1e, ffn_z), *qkv_bufs)
    states = all_states(state)
    ffn_z = after(ffn_z, a1e, qkv_bufs[1])
    ffn_x, ffn_y = swap(ffn_z, 0), swap(ffn_z, 1)
    ffn_bufs = [ffn_z, ffn_x, ffn_y, swap(after(ffn_x, ffn_y, *states), 1)]
    capacity, block_rows = master.shape[0], master.shape[1]
    where = [[[] for _ in range(4)] for _ in range(2)]
    for d in range(ndp):
        b = order[d & 1]
        where[d & 1][2 * ((d >> b[0]) & 1) + ((d >> b[1]) & 1)].append(d)
    flat_state = [x.reshape(capacity * block_rows, 128) for x in (master, first_moment, second_moment)]
    [parts] = call(
        functools.partial(slices_body, where), [((ndp, 3, capacity * 8, 128), f32)], [HB] * 3,
        [
            pltpu.VMEM((3, capacity * block_rows, 128), f32), pltpu.VMEM((3, 2, 4, capacity * 8, 128), f32),
            pltpu.SemaphoreType.DMA((3,)), pltpu.SemaphoreType.DMA,
        ],
        1 << 20, 4 << 20, 12, (HB,),
    )(*flat_state)
    [near] = call(
        near_body, [((rows, width), f32)], [SM, VM], [], mm * 1024, 12 << 20, 16,
    )(meta, after(qkv, parts, ffn_bufs[1], ffn_bufs[2], *states))
    ffn_bufs = both_cores(ffn_bufs)
    held_state = exchange(after(parts, ffn_bufs[3]), "dp")

    hid_w = w_in.shape[1]
    big = pltpu.VMEM((rows, width), f32)
    low = pltpu.VMEM((rows, width), bf16)
    n_m = (w_out.shape[0] + w_in.shape[0] + w_down.shape[0]) // 2
    wide = pltpu.VMEM((groups, rows, hid_w), f32)
    half = pltpu.VMEM((groups, n_m, width), bf16)
    four = pltpu.VMEM((groups, rows, hid_w), bf16)
    (outputs, do, head, tail, dx2, dctx, dqf, dstate, ng2, wout, grad_m, give_m) = call(
        main_body,
        [
            ((rows, width), bf16), ((rows, width), bf16), ((EDGE, width), bf16), ((EDGE, width), bf16),
            ((rows, width), f32), ((rows, width), bf16), ((rows, width), f32), ((groups, STATE, PAIR), bf16), ((2, width), f32),
            ((groups,) + w_out.shape, bf16), ((groups, n_m, width), bf16), ((groups, n_m, width), bf16),
        ],
        [SM] + [VM] * 10 + [HB] * 8,
        [
            pltpu.VMEM((groups, width, hid_w), bf16), pltpu.VMEM((groups, hid_w, width), bf16),
            big, big, pltpu.VMEM((rows, 128), f32), wide, wide, big, big, big, big,
            low, low, low, low, low, low, four, four, low, half, half,
            pltpu.SemaphoreType.DMA((3,)), pltpu.SemaphoreType.DMA,
        ],
        mm * hid_w * groups * 6, 24 << 20, 44,
        (HB, VM, VM, VM, HB, VM, HB, VM, VM, VM, HB, HB),
    )(meta, near, qkv, *states, tok, cot, norm_gains, norm_biases, *ffn_bufs)

    head, tail, dstate, give_m, _ = lax.optimization_barrier((head, tail, dstate, give_m, held_state))
    dstates = all_states(dstate)
    do_l, do_r = from_mp(tail, 1), from_mp(head, -1)

    def halve(own, got, s):
        n = own.shape[-1] // 2
        bit = bit_of(me, core, s)

        def half(at, own, got):
            a = lax.dynamic_slice_in_dim(own, at * n, n, own.ndim - 1).astype(f32)
            return a + lax.dynamic_slice_in_dim(got, at * n, n, own.ndim - 1).astype(f32)

        give = half(1 - bit, own, got).astype(bf16)
        own, got = after(own, give), after(got, give)
        return give, half(bit, own, got)

    def finish(keep, got, extra=None):
        tot = keep + got.astype(f32)
        for s in range(2, nbits - 1):
            tot = tot.astype(bf16).astype(f32) + swap(tot.astype(bf16), s).astype(f32)
        if extra is None:
            return [exchange(tot.astype(bf16), "mp")]
        msg = jnp.concatenate([tot, jnp.broadcast_to(extra, (groups,) + extra.shape)], axis=1)
        part = [lax.dynamic_slice_in_dim(msg, zi ^ m, 1, 0) for m in range(groups)]
        return part[:1] + [swap_mp(part[m], m) for m in range(1, groups)]

    give_m, keep_m = halve(grad_m, after(swap_core(give_m), do_l, do_r, dstates[1]), 0)
    got_m = swap(give_m, 0)
    dq, dkn, dvn = call(
        near_back_body,
        [((rows, width), bf16), ((rows, width), f32), ((rows, width), f32)],
        [SM] + [VM] * 4 + [HB] * 2,
        [
            pltpu.VMEM((rows + 2 * EDGE, width), bf16), pltpu.VMEM((rows + 2 * EDGE, width), f32),
            pltpu.VMEM((ext, width), f32), pltpu.VMEM((ext, width), f32),
            pltpu.VMEM(wout.shape, bf16), big, pltpu.SemaphoreType.DMA((2,)),
        ],
        mm * 2048, 24 << 20, 20,
    )(meta, qkv, after(dctx, give_m), do_l, do_r, wout, dqf)
    n_q = w_qkv.size // width // 2
    n_ng = 4 * width // 128
    dproj, grad_q, give_q = call(
        proj_body,
        [((groups, rows, 3 * PAIR), bf16), ((groups, n_q, width), f32), ((groups, n_q, width), f32)],
        [SM] + [VM] * 9,
        [
            pltpu.VMEM((groups, rows, 3 * PAIR), bf16), pltpu.VMEM((3 * width, 128), f32),
            pltpu.VMEM((2 * n_q, width), f32), pltpu.SemaphoreType.DMA,
        ],
        mm * 3 * width, 24 << 20, 20, (HB, VM, VM),
    )(meta, qkv, dq, dkn, dvn, *dstates, a1e)
    got_q = swap_core(give_q)
    give_m, keep_m = halve(keep_m, after(got_m, give_q), 1)
    got_m = swap(give_m, 1)
    give_q, keep_q = halve(grad_q, got_q, 0)
    got_q = swap(give_q, 0)
    tokens_grad, ng = call(
        last_body,
        [((rows, width), f32), ((n_ng, 128), f32)],
        [SM, HB, VM, HB, VM, VM] + [HB] * 4,
        [
            big, pltpu.VMEM((n_ng, 128), f32), proj_w, pltpu.VMEM((groups, rows, 3 * PAIR), bf16), big,
            pltpu.SemaphoreType.DMA, pltpu.SemaphoreType.DMA((2,)),
        ],
        mm * 3 * width, 8 << 20, 16,
    )(meta, after(dproj, give_q), tok, dx2, norm_gains, ng2, *qkv_bufs)
    z_m = finish(keep_m, after(got_m, give_q))
    give_q, keep_q = halve(keep_q, after(got_q, ng), 1)
    got_q = swap(give_q, 1)
    z_m = [after(z_m[0], give_q)]


    blocks = owners.shape[0]
    earlier = jnp.arange(blocks)[None, :] < jnp.arange(blocks)[:, None]
    alike = owners[None, :] == owners[:, None]
    slot = jnp.sum((earlier & alike).astype(jnp.int32), axis=1)
    slot_rows = owners * capacity + slot
    hit = slot_rows[None, :] == jnp.arange(ndp * capacity, dtype=jnp.int32)[:, None]
    held = jnp.sum(jnp.where(hit, jnp.arange(blocks, dtype=jnp.int32)[None, :], 0), axis=1)
    filled = lax.dynamic_slice_in_dim(
        jnp.sum(hit.astype(jnp.int32), axis=1), me * capacity, capacity, 0
    )
    nb_q = n_q * 2 // 16

    def updated(z, n, first, extra=()):
        return call(
            functools.partial(pieces_body, first, len(z)),
            [((n, 128), f32), ((n, 128), bf16)] + list(extra),
            [SM, SM] + [VM] * (len(z) + 1), [], 1 << 20, 4 << 20, 20,
        )(owners, slot, *z, held_state)

    def everywhere(piece):
        x, y = swap(piece, 0), swap(piece, 1)
        return both_cores([piece, x, y, swap(x, 1)])

    piece_m, fresh_m = updated(z_m, n_m, nb_q)
    m_bufs = everywhere(fresh_m)
    z_q = finish(keep_q, after(got_q, fresh_m), ng)
    z_q[0] = after(z_q[0], m_bufs[1], m_bufs[2])
    piece_q, fresh_q, ng_z = updated(z_q, n_q, 0, [((n_ng, 128), f32)])
    q_bufs = everywhere(fresh_q)
    [send] = call(
        route_body, [((ndp, capacity * 8 + 2 * n_ng, 128), bf16)], [SM, VM, VM, VM], [], 1 << 20, 4 << 20, 16,
    )(held, piece_q, piece_m, ng_z)
    recv = exchange(send, "dp")
    high = me - (me & 7)
    sources = jnp.stack(
        [
            high + c + ((j >> 1) << order[c][0]) + ((j & 1) << order[c][1])
            for c in range(2)
            for j in range(4)
        ]
    ).astype(jnp.int32)
    state_shape = (capacity, block_rows, 128)
    first_new, second_new, master_new, norm_sum = call(
        adam_body,
        [(state_shape, f32)] * 3 + [((n_ng, 128), f32)],
        [SM, SM] + [VM] * 4,
        [pltpu.VMEM((capacity, 2, 8, 128), f32), pltpu.VMEM((capacity * block_rows, 128), f32)],
        1 << 20, 8 << 20, 20,
    )(filled, sources, recv, master, first_moment, second_moment)
    new_out, new_in, new_down = call(
        place_body, [(w_out.shape, bf16), (w_in.shape, bf16), (w_down.shape, bf16)],
        [SM] + [HB] * 8, [pltpu.VMEM((8, n_m, 128), bf16), pltpu.SemaphoreType.DMA],
        1 << 20, 4 << 20, 16,
    )(meta, *m_bufs)
    [new_qkv] = call(
        place_qkv_body, [(w_qkv.shape, bf16)], [SM] + [HB] * 8,
        [
            pltpu.VMEM((8, n_q, 128), bf16), pltpu.VMEM((w_qkv.size // 128, 128), f32),
            pltpu.SemaphoreType.DMA,
        ],
        1 << 20, 2 << 20, 16,
    )(meta, *q_bufs)

    corr_one = 1.0 - beta_one**STEP
    corr_two = 1.0 - beta_two**STEP
    norm_grad = norm_sum.reshape(4, width)
    norm_params = jnp.stack([norm_gains[0], norm_biases[0], norm_gains[1], norm_biases[1]])
    norm_first_new = beta_one * norm_first + (1.0 - beta_one) * norm_grad
    norm_second_new = beta_two * norm_second + (1.0 - beta_two) * norm_grad * norm_grad
    norm_new = norm_params - norm_rate * (
        norm_first_new / corr_one / (jnp.sqrt(norm_second_new / corr_two) + adam_epsilon)
    )
    return (
        outputs[None], tokens_grad[None], first_new, second_new, master_new,
        new_qkv, new_out, new_in, new_down, norm_first_new, norm_second_new, norm_new,
    )


def solution(mesh):
    sharded = P("dp", "mp", None)
    return jax.shard_map(
        per_device,
        mesh=mesh,
        in_specs=(
            sharded, sharded, P("dp"), P(), P(None, "mp"), P("mp", None), P(None, "mp"), P("mp", None),
            sharded, sharded, sharded, P(), P(), P(), P(),
        ),
        out_specs=(
            sharded, sharded, sharded, sharded, sharded,
            P(None, "mp"), P("mp", None), P(None, "mp"), P("mp", None), P(), P(), P(),
        ),
        check_vma=False,
    )
```

```python
import functools

import jax
import jax.numpy as jnp
from jax import lax
from jax.experimental import pallas as pl
from jax.experimental.pallas import tpu as pltpu
from jax.sharding import PartitionSpec as P

HEAD = 64
BAND = 30
STEP = 10
HALO = 64
EDGE = 32
QB = 64
WIN = 128
PAIR = 128
COST = 1
STATE = 144

learn_rate = 0.1
norm_rate = 0.3
decay_rate = 0.1
beta_one = 0.9
beta_two = 0.95
adam_epsilon = 1e-08
norm_epsilon = 1e-05
GELU_C = 0.7978845608028654
GELU_A = 0.044715

f32 = jnp.float32
bf16 = jnp.bfloat16

VM = pl.BlockSpec(memory_space=pltpu.VMEM)
HB = pl.BlockSpec(memory_space=pltpu.HBM)
SM = pl.BlockSpec(memory_space=pltpu.SMEM)


def call(body, outs, in_specs, scratch, flops, moved, vmem=48, out_specs=None):
    specs = out_specs or tuple(VM for _ in outs)
    run = pl.pallas_call(
        body,
        out_shape=tuple(
            pltpu.HBM(s, d) if spec is HB else jax.ShapeDtypeStruct(s, d) for (s, d), spec in zip(outs, specs)
        ),
        in_specs=in_specs,
        out_specs=specs,
        scratch_shapes=scratch,
        compiler_params=pltpu.CompilerParams(vmem_limit_bytes=vmem << 20),
        cost_estimate=pl.CostEstimate(flops=flops // COST, bytes_accessed=moved // COST, transcendentals=0),
    )

    def fixed(*args):
        return run(
            *[
                pltpu.with_memory_space_constraint(x, pltpu.HBM) if spec is HB else x
                for x, spec in zip(args, in_specs)
            ]
        )

    return fixed


def load(pairs, sem):
    copies = [pltpu.make_async_copy(a, b, sem) for a, b in pairs]
    for c in copies:
        c.start()
    return copies


def dot(a, b):
    return jnp.dot(a, b, preferred_element_type=f32)


def turned(a):
    return a.astype(f32).T.astype(bf16)


def dot_nt(a, b):
    return dot(a, turned(b))


def dot_tn(a, b):
    return lax.dot_general(a, b, (((0,), (0,)), ((), ())), preferred_element_type=f32)


def normalize(x):
    mean = jnp.mean(x, axis=-1, keepdims=True)
    cen = x - mean
    var = jnp.mean(cen * cen, axis=-1, keepdims=True)
    rstd = lax.rsqrt(var + norm_epsilon)
    return cen * rstd, rstd


def same_head(n=PAIR):
    r = lax.broadcasted_iota(jnp.int32, (n, n), 0)
    c = lax.broadcasted_iota(jnp.int32, (n, n), 1)
    return (r < HEAD) == (c < HEAD)


def pack_state(s1, s2, z):
    both = jnp.where(same_head(), s1, pltpu.roll(s2, HEAD, 1))
    hi = z.astype(bf16).astype(f32)
    row = lax.broadcasted_iota(jnp.int32, (16, PAIR), 0)
    tail = jnp.where(row == 0, hi, jnp.where(row == 1, z - hi, 0.0))
    return both.astype(bf16), tail.astype(bf16)


def unpack_state(refs, g):
    tot = refs[0][g].astype(f32)
    for r in refs[1:]:
        tot = tot + r[g].astype(f32)
    both = tot[:PAIR]
    diag = same_head()
    s1 = jnp.where(diag, both, 0.0)
    s2 = jnp.where(diag, pltpu.roll(both, HEAD, 1), 0.0)
    z = tot[PAIR : PAIR + 1] + tot[PAIR + 1 : PAIR + 2]
    return s1, s2, z


def split_dot(a, ones):
    hi, lo = two(a)
    return dot(hi, ones) + dot(lo, ones)


def two(a):
    hi = a.astype(bf16)
    return hi, (a - hi.astype(f32)).astype(bf16)


def phi(v):
    low = jnp.exp(jnp.minimum(v, 0.0))
    return jnp.where(v > 0, v + 1.0, low), jnp.where(v > 0, 1.0, low)


def band_parts():
    c = lax.broadcasted_iota(jnp.int32, (WIN, 2 * QB), 0)
    r = lax.broadcasted_iota(jnp.int32, (WIN, 2 * QB), 1) % QB
    off = r + EDGE - c
    return (jnp.abs(off) <= BAND), off == 0, c


def stacked(rows):
    lane = lax.broadcasted_iota(jnp.int32, (1, PAIR), 1)
    first = (lane < HEAD).astype(f32).astype(bf16)
    second = (lane >= HEAD).astype(f32).astype(bf16)
    return jnp.concatenate([rows * first, rows * second], axis=0)


def unstack(both):
    lane = lax.broadcasted_iota(jnp.int32, (QB, PAIR), 1)
    return jnp.where(lane < HEAD, both[:QB], both[QB:])


def softmax_of(raw, mask):
    scores = jnp.where(mask, raw * 0.125, -1e30)
    ex = jnp.exp(scores - jnp.max(scores, axis=0, keepdims=True))
    return ex * (1.0 / jnp.sum(ex, axis=0, keepdims=True))


def piece_at(meta, r, bits, other):
    b0, b1 = (meta[6], meta[7]) if other else (meta[4], meta[5])
    core = 1 - meta[2] if other else meta[2]
    if bits == 1:
        return core * 2 + (b0 ^ r)
    return core * 4 + (b0 ^ (r & 1)) * 2 + (b1 ^ (r >> 1))


def fetch_pieces(meta, bufs, lo, rows, weight, sem):
    n = len(bufs) // 2
    copies = []
    for k, buf in enumerate(bufs):
        p = piece_at(meta, k % n, n // 2, k >= n)
        at = pl.ds(pl.multiple_of(p * rows, rows), rows)
        for m in range(buf.shape[0]):
            src = buf.at[m, pl.ds(lo, rows), :]
            copies.append(pltpu.make_async_copy(src, weight.at[meta[3] ^ m, at, :], sem))
    for c in copies:
        c.start()
    return copies


def norm_body(tok, left, right, gains, biases, a1e_h, a1e_o, sem):
    rows = tok.shape[0]
    gain, bias = gains[0:1, :], biases[0:1, :]

    def ln(x):
        return (normalize(x.astype(f32))[0] * gain + bias).astype(bf16)

    a1e_o[0:HALO, :] = ln(left[...])
    a1e_o[HALO + rows :, :] = ln(right[...])

    def chunk(i, _):
        at = pl.ds(pl.multiple_of(i * 128, 128), 128)
        a1e_o[pl.ds(pl.multiple_of(i * 128 + HALO, 64), 128), :] = ln(tok[at, :])
        return 0

    lax.fori_loop(0, rows // 128, chunk, 0)
    out = pltpu.make_async_copy(a1e_o, a1e_h, sem)
    out.start()
    out.wait()


def qkv_body(meta, a1e_h, *refs):
    bufs, (qkv_h, st_o, w, qkv_o, a1e, sem, out_sem) = refs[:4], refs[4:]
    pull = pltpu.make_async_copy(a1e_h, a1e, out_sem)
    pull.start()
    ext = a1e.shape[0]
    rows = ext - 2 * HALO
    groups = bufs[0].shape[0]
    for c in fetch_pieces(meta, bufs, 0, bufs[0].shape[1], w, sem):
        c.wait()
    pull.wait()
    length, base = meta[0], meta[1]
    pos = base + lax.broadcasted_iota(jnp.int32, (rows, 1), 0)
    valid = (pos < length).astype(f32)
    gs = range(groups)
    for g in gs:
        qkv_o[g] = dot(a1e[...], w[g]).astype(bf16)
    own_rows = slice(HALO, HALO + rows)
    out = pltpu.make_async_copy(qkv_o, qkv_h, out_sem)
    out.start()
    parts = []
    for g in gs:
        keys = qkv_o[g, own_rows, PAIR : 2 * PAIR].astype(f32)
        feat = phi(keys)[0] * valid
        parts.append((jnp.sum(feat, axis=0, keepdims=True), two(feat), two(jnp.tanh(keys) * valid)))
    for g in gs:
        z, (fhi, flo), (thi, tlo) = parts[g]
        vals = qkv_o[g, own_rows, 2 * PAIR :]
        s1 = dot_tn(fhi, vals) + dot_tn(flo, vals)
        s2 = dot_tn(thi, vals) + dot_tn(tlo, vals)
        st_o[g, :PAIR, :], st_o[g, PAIR:, :] = pack_state(s1, s2, z)
    out.wait()


def near_body(meta, qkv_h, near_h, qkv, near_o, sem):
    pull = pltpu.make_async_copy(qkv_h, qkv, sem)
    pull.start()
    groups = qkv.shape[0]
    rows = near_o.shape[0]
    length, base = meta[0], meta[1]
    band, diag, lane = band_parts()
    pull.wait()

    def block(b, _):
        at = b * QB
        kpos = base + at - EDGE + lane
        mask = band & (((kpos >= 0) & (kpos < length)) | diag)
        q_at = pl.ds(pl.multiple_of(at + HALO, QB), QB)
        w_at = pl.ds(pl.multiple_of(at + HALO - EDGE, EDGE), WIN)
        gs = range(groups)
        sc = [dot_nt(qkv[g, w_at, PAIR : 2 * PAIR], stacked(qkv[g, q_at, 0:PAIR])) for g in gs]
        p = [softmax_of(sc[g], mask).astype(bf16) for g in gs]
        res = [dot_tn(p[g], qkv[g, w_at, 2 * PAIR :]) for g in gs]
        for g in gs:
            near_o[pl.ds(pl.multiple_of(at, QB), QB), g * PAIR : (g + 1) * PAIR] = unstack(res[g])
        return 0

    lax.fori_loop(0, rows // QB, block, 0, unroll=4)
    out = pltpu.make_async_copy(near_o, near_h, sem)
    out.start()
    out.wait()


def put_halves(core, keep, give, g, lo, grad):
    n, width = grad.shape
    tiles = grad.reshape(n // 16, 2, 8, width)
    even, odd = tiles[:, 0].reshape(n // 2, width), tiles[:, 1].reshape(n // 2, width)
    first = jnp.full(even.shape, core, jnp.int32) == 0
    at = slice(lo, lo + n // 2)
    keep[g, at, :] = jnp.where(first, even, odd).astype(keep.dtype)
    give[g, at, :] = jnp.where(first, odd, even).astype(give.dtype)


def main_body(meta, near_h, qkv_h, h0, h1, h2, h3, tok_h, cot_h, gains, biases, *refs):
    bufs, refs = refs[:8], refs[8:]
    out_h, head_o, tail_o, dx2_h, dctx_h, dqf_h, dst_o, ng_o, wout_h, keep_h, give_h = refs[:11]
    refs = refs[11:]
    do_o, dctx_o, wout_o, near, tok, cot, st = refs[:7]
    refs = (None,) * 5 + refs
    w_in, w_down, x2, xhat, rs, u, dh, acc, da2, far1, inv, dnum, phq, thq = refs[12:26]
    ctx_o, a2_o, dm_o, hid_o, du_o, out_o, keep, give, query, sem, out_sem = refs[26:]
    rows, width = tok.shape
    groups, hw = hid_o.shape[0], hid_o.shape[2]
    s0, s1, s2, s3 = [st.at[k] for k in range(4)]
    moved = load([(near_h, near), (tok_h, tok), (cot_h, cot)] + [(h, st.at[k]) for k, h in enumerate((h0, h1, h2, h3))], sem.at[4])
    pr = hw // 8
    orow = bufs[0].shape[1] - 2 * pr
    core = meta[2]
    sent = []

    def send(src, dst):
        sent.append(pltpu.make_async_copy(src, dst, out_sem))
        sent[-1].start()

    length, base = meta[0], meta[1]
    pull = pltpu.make_async_copy(qkv_h.at[:, pl.ds(HALO, rows), pl.ds(0, PAIR)], query, sem.at[3])
    pull.start()
    copies = fetch_pieces(meta, bufs, 2 * pr, orow, wout_o, sem.at[0])
    later = fetch_pieces(meta, bufs, 0, pr, w_in, sem.at[1])
    last = fetch_pieces(meta, bufs, pr, pr, w_down, sem.at[2])
    rlen = 1.0 / length.astype(f32)
    gain, bias = gains[1:2, :], biases[1:2, :]
    ones = same_head().astype(f32).astype(bf16)
    gs = range(groups)
    cols = [slice(g * PAIR, (g + 1) * PAIR) for g in gs]
    for c in moved:
        c.wait()
    states = [unpack_state((s0, s1, s2, s3), g) for g in gs]
    s1b, s2b = [two(st[0]) for st in states], [two(st[1]) for st in states]
    cr = 128

    def far_chunk(i, _):
        at = pl.ds(pl.multiple_of(i * cr, cr), cr)
        q = [query[g, at, :].astype(f32) for g in gs]
        ph = [phi(q[g])[0] for g in gs]
        ph2 = [two(ph[g]) for g in gs]
        th2 = [two(jnp.tanh(q[g])) for g in gs]
        den = [split_dot(ph[g] * states[g][2], ones) for g in gs]
        num = [dot(ph2[g][0], s1b[g][0]) + dot(ph2[g][0], s1b[g][1]) + dot(ph2[g][1], s1b[g][0]) for g in gs]
        sec = [dot(th2[g][0], s2b[g][0]) + dot(th2[g][0], s2b[g][1]) + dot(th2[g][1], s2b[g][0]) for g in gs]
        for g in gs:
            phq[at, cols[g]] = ph2[g][0]
            thq[at, cols[g]] = th2[g][0]
        rec = [1.0 / den[g] for g in gs]
        for g in gs:
            part = num[g] * rec[g]
            inv[at, cols[g]] = rec[g]
            far1[at, cols[g]] = part
            ctx_o[at, cols[g]] = (near[at, cols[g]] + (part + sec[g] * rlen)).astype(bf16)
        pos = base + i * cr + lax.broadcasted_iota(jnp.int32, (cr, 1), 0)
        dm_o[at, :] = (cot[at, :].astype(f32) * (pos < length).astype(f32)).astype(bf16)
        return 0

    pull.wait()
    lax.fori_loop(0, rows // cr, far_chunk, 0)
    for c in copies:
        c.wait()
    wout = wout_o[...].reshape(width, width)
    x2[...] = dot(ctx_o[...], wout)

    def norm_chunk(i, _):
        at = pl.ds(pl.multiple_of(i * 64, 64), 64)
        val = x2[at, :] + tok[at, :].astype(f32)
        x2[at, :] = val
        xh, rstd = normalize(val)
        xhat[at, :] = xh
        rs[at, :] = jnp.broadcast_to(rstd, (64, 128))
        a2_o[at, :] = (xh * gain + bias).astype(bf16)
        return 0

    lax.fori_loop(0, rows // 64, norm_chunk, 0)
    for c in later + last:
        c.wait()
    for g in gs:
        u[g] = dot(a2_o[...], w_in[g])
        dh[g] = dot_nt(dm_o[...], w_down[g])

    def act(i, _):
        at = pl.ds(pl.multiple_of(i * 16, 16), 16)
        for g in gs:
            v = u[g, at, :]
            sq = v * v
            half = 0.5 + 0.5 * jnp.tanh(v * (GELU_C + GELU_C * GELU_A * sq))
            hid = v * half
            hid_o[g, at, :] = hid.astype(bf16)
            slope = half + (hid * (1.0 - half)) * (2.0 * GELU_C + 6.0 * GELU_C * GELU_A * sq)
            du_o[g, at, :] = (dh[g, at, :] * slope).astype(bf16)
        return 0

    lax.fori_loop(0, rows // 16, act, 0)
    acc[...] = sum(dot(hid_o[g], w_down[g]) for g in gs)
    da2[...] = sum(dot_nt(du_o[g], w_in[g]) for g in gs)

    def back_chunk(i, carry):
        dg, db = carry
        at = pl.ds(pl.multiple_of(i * 64, 64), 64)
        out_o[at, :] = (x2[at, :] + acc[at, :]).astype(bf16)
        xh = xhat[at, :]
        rstd = rs[at, 0:1]
        d = da2[at, :]
        dg = dg + jnp.sum(d * xh, axis=0, keepdims=True)
        db = db + jnp.sum(d, axis=0, keepdims=True)
        e = d * gain
        m1 = jnp.mean(e, axis=-1, keepdims=True)
        m2 = jnp.mean(e * xh, axis=-1, keepdims=True)
        dx = dm_o[at, :].astype(f32) + rstd * (e - m1 - xh * m2)
        acc[at, :] = dx
        do_o[at, :] = dx.astype(bf16)
        return dg, db

    zero = jnp.zeros((1, width), f32)
    dg, db = lax.fori_loop(0, rows // 64, back_chunk, (zero, zero))
    head_o[...] = do_o[0:EDGE, :]
    tail_o[...] = do_o[rows - EDGE :, :]
    send(out_o, out_h)
    send(wout_o, wout_h)
    send(acc, dx2_h)
    ng_o[0:1, :] = dg
    ng_o[1:2, :] = db
    dctx_o[...] = dot_nt(do_o[...], wout).astype(bf16)
    send(dctx_o, dctx_h)

    def far_back(i, carry):
        at = pl.ds(pl.multiple_of(i * cr, cr), cr)
        dc = [dctx_o[at, cols[g]] for g in gs]
        dcf = [dc[g].astype(f32) for g in gs]
        rec = [inv[at, cols[g]] for g in gs]
        dn = [(dcf[g] * rec[g]).astype(bf16) for g in gs]
        dots = [split_dot(dcf[g] * far1[at, cols[g]], ones) for g in gs]
        dph = [dot_nt(dn[g], s1b[g][0]) for g in gs]
        dth = [dot_nt(dc[g], s2b[g][0]) for g in gs]
        out = []
        for g in gs:
            dnum[at, cols[g]] = dn[g]
            dden = -dots[g] * rec[g]
            out.append(carry[g] + jnp.sum(phq[at, cols[g]].astype(f32) * dden, axis=0, keepdims=True))
            slope = phi(query[g, at, :].astype(f32))[1]
            th = thq[at, cols[g]].astype(f32)
            da2[at, cols[g]] = (dph[g] + dden * states[g][2]) * slope + dth[g] * rlen * (1.0 - th * th)
        return tuple(out)

    none = jnp.zeros((1, PAIR), f32)
    dz = lax.fori_loop(0, rows // cr, far_back, (none,) * groups)
    for g in gs:
        d1 = dot_tn(phq[:, cols[g]], dnum[:, cols[g]])
        d2 = dot_tn(thq[:, cols[g]], dctx_o[:, cols[g]]) * rlen
        dst_o[g, :PAIR, :], dst_o[g, PAIR:, :] = pack_state(d1, d2, dz[g])
    send(da2, dqf_h)
    n_out = ctx_o.shape[1] // groups

    def finish(g, lo, n, grad):
        put_halves(core, keep, give, g, lo, grad)
        part = pl.ds(lo, n)
        send(keep.at[g, part, :], keep_h.at[g, part, :])
        send(give.at[g, part, :], give_h.at[g, part, :])

    for g in gs:
        finish(g, n_out // 2, width // 2, dot_tn(a2_o[...], du_o[g]))
    for g in gs:
        finish(g, 0, n_out // 2, dot_tn(ctx_o[:, g * n_out : (g + 1) * n_out], do_o[...]))
    for g in gs:
        finish(g, n_out // 2 + width // 2, hw // 2, dot_tn(hid_o[g], dm_o[...]))
    for c in sent:
        c.wait()


def near_back_body(
    meta, qkv_h, dctx_h, do_l, do_r, wout_h, dqf_h, dq_o, dk_o, dv_o, dce, dqe, dke, dve, wout, dqf, qkv, sem,
):
    pull = pltpu.make_async_copy(qkv_h, qkv, sem.at[2])
    pull.start()
    groups = qkv.shape[0]
    rows, width = dctx_h.shape
    third = pltpu.make_async_copy(dctx_h, dce.at[pl.ds(EDGE, rows), :], sem.at[3])
    third.start()
    length, base = meta[0], meta[1]
    band, diag, lane = band_parts()
    first = pltpu.make_async_copy(wout_h, wout, sem.at[0])
    first.start()
    second = pltpu.make_async_copy(dqf_h, dqf, sem.at[1])
    second.start()
    first.wait()
    w = wout[...].reshape(width, -1)
    dce[0:EDGE, :] = dot_nt(do_l[...], w).astype(bf16)
    dce[EDGE + rows :, :] = dot_nt(do_r[...], w).astype(bf16)
    dke[...] = jnp.zeros(dke.shape, f32)
    dve[...] = jnp.zeros(dve.shape, f32)
    pull.wait()
    third.wait()

    def block(b, _):
        at = b * QB
        kpos = base + at - HALO + lane
        mask = band & (((kpos >= 0) & (kpos < length)) | diag)
        c_at = pl.ds(pl.multiple_of(at, QB), QB)
        q_at = pl.ds(pl.multiple_of(at + EDGE, EDGE), QB)
        w_at = pl.ds(pl.multiple_of(at, QB), WIN)
        gs = range(groups)
        cols = [slice(g * PAIR, (g + 1) * PAIR) for g in gs]
        qs = [stacked(qkv[g, q_at, 0:PAIR]) for g in gs]
        cs = [stacked(dce[c_at, cols[g]]) for g in gs]
        kw = [qkv[g, w_at, PAIR : 2 * PAIR] for g in gs]
        sc = [dot_nt(kw[g], qs[g]) for g in gs]
        dp = [dot_nt(qkv[g, w_at, 2 * PAIR :], cs[g]) for g in gs]
        p = [softmax_of(sc[g], mask) for g in gs]
        row = [jnp.sum(p[g] * dp[g], axis=0, keepdims=True) for g in gs]
        ds = [(p[g] * (dp[g] - row[g])).astype(bf16) for g in gs]
        pb = [p[g].astype(bf16) for g in gs]
        for g in gs:
            dke[w_at, cols[g]] += dot(ds[g], qs[g])
            dve[w_at, cols[g]] += dot(pb[g], cs[g])
        dq = [dot_tn(ds[g], kw[g]) for g in gs]
        for g in gs:
            dqe[c_at, cols[g]] = unstack(dq[g])
        return 0

    lax.fori_loop(0, rows // QB + 1, block, 0, unroll=9)
    second.wait()
    dq_o[...] = (dqe[EDGE : EDGE + rows, :] * 0.125 + dqf[...]).astype(bf16)
    dk_o[...] = dke[HALO : HALO + rows, :] * 0.125
    dv_o[...] = dve[HALO : HALO + rows, :]


def proj_body(
    meta, qkv_h, dq, dkn, dvn, s0, s1, s2, s3, a1e_h, dproj_h, keep_o, give_o, dproj, flat, pseudo, qkv, a1e, sem, in_sem,
):
    rows = dq.shape[0]
    other = pltpu.make_async_copy(a1e_h.at[pl.ds(HALO, rows), :], a1e, in_sem.at[1])
    other.start()
    pull = pltpu.make_async_copy(qkv_h, qkv, in_sem.at[0])
    pull.start()
    groups = qkv.shape[0]
    rows, width = dq.shape
    length, base, core = meta[0], meta[1], meta[2]
    cr = 128
    gs = range(groups)
    cols = [slice(g * PAIR, (g + 1) * PAIR) for g in gs]
    states = [unpack_state((s0, s1, s2, s3), g) for g in gs]
    s1b, s2b = [st[0].astype(bf16) for st in states], [st[1].astype(bf16) for st in states]

    def far_chunk(i, _):
        at = pl.ds(pl.multiple_of(i * cr, cr), cr)
        e_at = pl.ds(pl.multiple_of(i * cr + HALO, HALO), cr)
        pos = base + i * cr + lax.broadcasted_iota(jnp.int32, (cr, 1), 0)
        valid = (pos < length).astype(f32)
        k = [qkv[g, e_at, PAIR : 2 * PAIR].astype(f32) for g in gs]
        v = [qkv[g, e_at, 2 * PAIR :] for g in gs]
        feat = [phi(k[g]) for g in gs]
        th = [jnp.tanh(k[g]) for g in gs]
        vd1 = [dot_nt(v[g], s1b[g]) for g in gs]
        vd2 = [dot_nt(v[g], s2b[g]) for g in gs]
        dv = [
            dot((feat[g][0] * valid).astype(bf16), s1b[g]) + dot((th[g] * valid).astype(bf16), s2b[g]) for g in gs
        ]
        for g in gs:
            dk = (vd1[g] + states[g][2]) * feat[g][1] + vd2[g] * (1.0 - th[g] * th[g])
            dproj[g, at, 0:PAIR] = dq[at, cols[g]]
            dproj[g, at, PAIR : 2 * PAIR] = (dkn[at, cols[g]] + dk * valid).astype(bf16)
            dproj[g, at, 2 * PAIR :] = (dvn[at, cols[g]] + dv[g]).astype(bf16)
        return 0

    pull.wait()
    lax.fori_loop(0, rows // cr, far_chunk, 0)
    out = pltpu.make_async_copy(dproj, dproj_h, sem)
    out.start()
    other.wait()
    n_flat = 3 * width
    for g in gs:
        grad = dot_tn(a1e[...], dproj[g])
        for part in range(3):
            flat[pl.ds(part, width, stride=3), :] = grad[:, part * PAIR : (part + 1) * PAIR]
        for j in range(4):
            pseudo[:, j * 128 : (j + 1) * 128] = flat[pl.ds(j, n_flat // 4, stride=4), :]
        put_halves(core, keep_o, give_o, g, 0, pseudo[...])
    out.wait()


def last_body(meta, dproj_h, tok, dx2_h, gains, ng2, *refs):
    bufs, (tg_o, ng_o, da1, ngs, wqkv, dproj, dx2, sem, sems) = refs[:4], refs[4:]
    groups = dproj.shape[0]
    rows, width = tok.shape
    gain = gains[0:1, :]
    copies = fetch_pieces(meta, bufs, 0, bufs[0].shape[1], wqkv, sem)
    copies.append(pltpu.make_async_copy(dproj_h, dproj, sems.at[0]))
    copies[-1].start()
    late = pltpu.make_async_copy(dx2_h, dx2, sems.at[1])
    late.start()
    for c in copies:
        c.wait()
    da1[...] = sum(dot_nt(dproj[g], wqkv[g]) for g in range(groups))

    late.wait()

    def back_chunk(i, carry):
        dg, db = carry
        at = pl.ds(pl.multiple_of(i * 64, 64), 64)
        xh, rstd = normalize(tok[at, :].astype(f32))
        d = da1[at, :]
        dg = dg + jnp.sum(d * xh, axis=0, keepdims=True)
        db = db + jnp.sum(d, axis=0, keepdims=True)
        e = d * gain
        m1 = jnp.mean(e, axis=-1, keepdims=True)
        m2 = jnp.mean(e * xh, axis=-1, keepdims=True)
        tg_o[at, :] = dx2[at, :] + rstd * (e - m1 - xh * m2)
        return dg, db

    zero = jnp.zeros((1, width), f32)
    dg, db = lax.fori_loop(0, rows // 64, back_chunk, (zero, zero))
    for k, val in enumerate((dg, db, ng2[0:1, :], ng2[1:2, :])):
        for j in range(width // 128):
            at = k * (width // 128) + j
            ngs[at : at + 1, :] = val[:, j * 128 : (j + 1) * 128]
    ng_o[...] = ngs[...]


def halve_body(bit, own, got, give_o, keep_o):
    groups, _, n = give_o.shape
    out = pl.ds(pl.multiple_of((1 - bit[0]) * n, 128), n)
    stay = pl.ds(pl.multiple_of(bit[0] * n, 128), n)
    for g in range(groups):
        give_o[g] = (own[g, :, out].astype(f32) + got[g, :, out].astype(f32)).astype(bf16)
    for g in range(groups):
        keep_o[g] = own[g, :, stay].astype(f32) + got[g, :, stay].astype(f32)


def total_body(meta, keep, got, *outs):
    for m, out in enumerate(outs):
        g = meta[3] ^ m
        out[0] = (keep[g] + got[g].astype(f32)).astype(bf16)


def total_q_body(meta, keep, got, ng, *outs):
    n = keep.shape[1]
    for m, out in enumerate(outs):
        g = meta[3] ^ m
        out[0, 0:n, :] = keep[g] + got[g].astype(f32)
        out[0, n:, :] = ng[...]


def slices_body(where, master, first, second, out_h, held, parts, sem, out_sem):
    caps = held.shape[1] // 64
    copies = [pltpu.make_async_copy(ref, held.at[t], sem.at[t]) for t, ref in enumerate((master, first, second))]
    for c in copies:
        c.start()
    sent = []
    for t in range(3):
        copies[t].wait()
        for j in range(4):
            val = held[t, pl.ds(j, caps * 16, stride=4), :].reshape(caps, 2, 8, 128)
            for c in range(2):
                parts[t, c, j] = val[:, c].reshape(caps * 8, 128)
                for d in where[c][j]:
                    sent.append(pltpu.make_async_copy(parts.at[t, c, j], out_h.at[d, t], out_sem))
                    sent[-1].start()
    for c in sent:
        c.wait()


def adam(g, m_old, f_old, s_old):
    corr_one = 1.0 - beta_one**STEP
    corr_two = 1.0 - beta_two**STEP
    fn = beta_one * f_old + (1.0 - beta_one) * g
    sn = beta_two * s_old + (1.0 - beta_two) * g * g
    step = fn / corr_one / (jnp.sqrt(sn / corr_two) + adam_epsilon)
    return fn, sn, m_old - learn_rate * (step + decay_rate * m_old)


def pieces_body(first, count, owners, slots, *refs):
    parts, (st, piece_o, w_o) = refs[:count], refs[count:]
    n = piece_o.shape[0]
    src = [(r, s) for r in parts for s in range(r.shape[0])]
    piece_o[...] = sum(r[s, 0:n, :].astype(f32) for r, s in src)
    if w_o.shape[0] > n:
        hi, lo = two(sum(r[s, n:, :] for r, s in src))
        k = hi.shape[0]
        w_o[n : 2 * n, :] = piece_o[...].astype(bf16)
        w_o[2 * n : 2 * n + k, :], w_o[2 * n + k :, :] = hi, lo

    def pair(i, _):
        new = []
        for k in range(2):
            b = i * 2 + k
            at = pl.ds(pl.multiple_of(slots[first + b] * 8, 8), 8)
            own = owners[first + b]
            g = piece_o[pl.ds(pl.multiple_of(b * 8, 8), 8), :]
            new.append(adam(g, st[own, 0, at, :], st[own, 1, at, :], st[own, 2, at, :])[2])
        w_o[pl.ds(pl.multiple_of(i * 16, 16), 16), :] = jnp.concatenate(new, axis=0).astype(bf16)
        return 0

    lax.fori_loop(0, n // 16, pair, 0, unroll=4)


def route_body(first, blocks, piece, send_o):
    dests, per, _ = send_o.shape
    caps = per // 8

    def dest(d, _):
        for r in range(0, caps, 2):
            at = [jnp.maximum(blocks[d * caps + r + k] - first, 0) * 8 for k in range(2)]
            both = [piece[pl.ds(pl.multiple_of(a, 8), 8), :] for a in at]
            send_o[d, r * 8 : r * 8 + 16, :] = jnp.concatenate(both, axis=0).astype(bf16)
        return 0

    lax.fori_loop(0, dests, dest, 0)


def owner_body(
    meta, counts, blocks, recv_h, master_h, first_h, second_h, gains, biases, n_first, n_second, *refs
):
    bufs, (f_o, s_o, m_o, q_o, nf_o, ns_o, np_o) = refs[:8], refs[8:15]
    held, later, early, parts, grad, flat, total, recv, master, first, second, sem, sems = refs[15:]
    moved = load([(recv_h, recv), (master_h, master), (first_h, first), (second_h, second)], sems)
    collect(meta, bufs, held, sem)
    for c in moved:
        c.wait()
    caps, br, _ = master.shape
    n = q_o.shape[0] * q_o.shape[1] // (128 * 64)
    k_ng = total.shape[0]
    for p in range(8):
        later[p] = recv[meta[9 + p]].astype(f32)
        early[p] = held[p, n * 8 : n * 16, :].astype(f32)
    total[...] = sum(
        held[p, n * 16 : n * 16 + k_ng, :].astype(f32) + held[p, n * 16 + k_ng :, :].astype(f32) for p in range(8)
    )
    start = meta[8] * caps

    def pick(r, _):
        b = blocks[start + r]
        old = pl.ds(pl.multiple_of(jnp.minimum(b, n - 1) * 8, 8), 8)
        new = pl.ds(pl.multiple_of(r * 8, 8), 8)
        is_q = jnp.full((8, 128), b, jnp.int32) < n
        for p in range(8):
            parts[p % 4, r, p // 4] = jnp.where(is_q, early[p, old, :], later[p, new, :])
        return 0

    lax.fori_loop(0, caps, pick, 0, unroll=2)
    for j in range(4):
        grad[pl.ds(j, caps * 16, stride=4), :] = parts[j].reshape(caps * 16, 128)

    def slot(r, _):
        g = grad[pl.ds(pl.multiple_of(r * br, br), br), :]
        m_old, f_old, s_old = master[r], first[r], second[r]
        fn, sn, mn = adam(g, m_old, f_old, s_old)
        keep = jnp.full(g.shape, counts[start + r], jnp.int32) > 0
        f_o[r] = jnp.where(keep, fn, f_old)
        s_o[r] = jnp.where(keep, sn, s_old)
        m_o[r] = jnp.where(keep, mn, m_old)
        return 0

    lax.fori_loop(0, caps, slot, 0, unroll=2)
    rows = q_o.shape[0]
    for j in range(4):
        flat[pl.ds(j, n * 16, stride=4), :] = columns(held, j, 0, n * 8)
    for part in range(3):
        q_o[:, part * 128 : (part + 1) * 128] = flat[pl.ds(part, rows, stride=3), :].astype(bf16)
    corr_one = 1.0 - beta_one**STEP
    corr_two = 1.0 - beta_two**STEP
    per = n_first.shape[1] // 128
    for k in range(4):
        old = (biases if k % 2 else gains)[k // 2 : k // 2 + 1, :]
        g = jnp.concatenate([total[k * per + j : k * per + j + 1, :] for j in range(per)], axis=1)
        fn = beta_one * n_first[k : k + 1, :] + (1.0 - beta_one) * g
        sn = beta_two * n_second[k : k + 1, :] + (1.0 - beta_two) * g * g
        nf_o[k : k + 1, :] = fn
        ns_o[k : k + 1, :] = sn
        np_o[k : k + 1, :] = old - norm_rate * (fn / corr_one / (jnp.sqrt(sn / corr_two) + adam_epsilon))


def collect(meta, bufs, held, sem):
    copies = []
    for k, buf in enumerate(bufs):
        copies.append(pltpu.make_async_copy(buf, held.at[piece_at(meta, k % 4, 2, k >= 4)], sem))
        copies[-1].start()
    for c in copies:
        c.wait()


def columns(held, j, lo, n):
    even, odd = [held[c * 4 + j, lo : lo + n, :].astype(f32).reshape(n // 8, 1, 8, 128) for c in range(2)]
    return jnp.concatenate([even, odd], axis=1).reshape(2 * n, 128)


def place_body(meta, *refs):
    bufs, outs, (held, sem) = refs[:8], refs[8:11], refs[11:]
    collect(meta, bufs, held, sem)
    lo = 0
    for ref in outs:
        n = ref.shape[0] // 2
        for j in range(4):
            ref[:, j * 128 : (j + 1) * 128] = columns(held, j, lo, n).astype(bf16)
        lo += n


def per_device(
    tokens, cotangent, lengths, owners, w_qkv, w_out, w_in, w_down,
    master, first_moment, second_moment, norm_gains, norm_biases, norm_first, norm_second,
):
    rows, width = tokens.shape[1], tokens.shape[2]
    groups = lax.axis_size("mp")
    ndp = lax.axis_size("dp")
    nbits = ndp.bit_length() - 1
    rest = list(range(1, nbits))
    order = (rest, rest[:2][::-1] + rest[2:][::-1])
    me, zi = lax.axis_index("dp"), lax.axis_index("mp")
    core = me & 1

    def bit_of(who, at, s):
        return (who >> jnp.where(at == 0, order[0][s], order[1][s])) & 1

    def swap(x, s):
        return lax.ppermute(x, "dp", [(i, i ^ (1 << order[i & 1][s])) for i in range(ndp)])

    def swap_core(x):
        return lax.ppermute(x, "dp", [(i, i ^ 1) for i in range(ndp)])

    def from_mp(x, step):
        return lax.ppermute(x, "mp", [(i, i + step) for i in range(groups) if 0 <= i + step < groups])

    def swap_mp(x, mask):
        return lax.ppermute(x, "mp", [(i, i ^ mask) for i in range(groups)])

    def exchange(x, axis):
        return lax.all_to_all(x, axis, 0, 0, tiled=True)

    def all_states(x):
        return [x] + [swap_mp(x, m) for m in range(1, groups)]

    q0, q1 = bit_of(me, core, 0), bit_of(me, core, 1)
    o0, o1 = bit_of(me, 1 - core, 0), bit_of(me, 1 - core, 1)
    length = lengths[0]
    base = zi * rows
    ids = [length, base, core, zi, q0, q1, o0, o1, me]
    ids += [
        me - (me & 7) + c + ((j >> 1) << order[c][0]) + ((j & 1) << order[c][1]) for c in range(2) for j in range(4)
    ]
    meta = jnp.stack(ids).astype(jnp.int32)

    def after(x, *deps):
        return lax.optimization_barrier((x,) + deps)[0]

    def over_mp(piece):
        return jnp.stack([piece] + [swap_mp(piece, m) for m in range(1, groups)])

    def both_cores(bufs):
        return bufs + [swap_core(b) for b in bufs]

    def part_of(w, n, at):
        return lax.dynamic_slice_in_dim(w, at * (w.shape[0] // n), w.shape[0] // n, 0)

    mine = core * 4 + q0 * 2 + q1
    tok, cot = tokens[0], cotangent[0]
    ext = rows + 2 * HALO
    mm = 2 * rows * width
    qkv_z = over_mp(part_of(w_qkv, 4, core * 2 + q0))
    left, right = from_mp(tok[rows - HALO :], 1), from_mp(tok[:HALO], -1)
    ffn_piece = jnp.concatenate([part_of(w, 8, mine) for w in (w_in, w_down, w_out)], axis=0)
    qkv_z = after(qkv_z, left, right, ffn_piece)
    qkv_bufs = [qkv_z, swap(qkv_z, 0)]
    ffn_z = over_mp(after(ffn_piece, qkv_z))
    [a1e] = call(norm_body, [((ext, width), bf16)], [VM] * 5,
        [pltpu.VMEM((ext, width), bf16), pltpu.SemaphoreType.DMA], 4 * mm, 1 << 20, 16, (HB,),
    )(
        tok, left, right, norm_gains, norm_biases
    )
    qkv_bufs = both_cores([qkv_bufs[0], after(qkv_bufs[1], a1e)])
    all_qkv = pltpu.VMEM((groups, ext, 3 * PAIR), bf16)
    proj_w = pltpu.VMEM((groups, width, 3 * PAIR), bf16)
    qkv, state = call(
        qkv_body,
        [((groups, ext, 3 * PAIR), bf16), ((groups, STATE, PAIR), bf16)],
        [SM] + [HB] * 5,
        [proj_w, all_qkv, pltpu.VMEM((ext, width), bf16), pltpu.SemaphoreType.DMA, pltpu.SemaphoreType.DMA],
        2 * ext * width * 3 * width, 6 << 20, 20, (HB, VM),
    )(meta, after(a1e, ffn_z), *qkv_bufs)
    states = all_states(state)
    ffn_z = after(ffn_z, a1e, qkv_bufs[1])
    ffn_x, ffn_y = swap(ffn_z, 0), swap(ffn_z, 1)
    ffn_bufs = [ffn_z, ffn_x, ffn_y, swap(after(ffn_x, ffn_y, *states), 1)]
    capacity, block_rows = master.shape[0], master.shape[1]
    where = [[[] for _ in range(4)] for _ in range(2)]
    for d in range(ndp):
        b = order[d & 1]
        where[d & 1][2 * ((d >> b[0]) & 1) + ((d >> b[1]) & 1)].append(d)
    flat_state = [x.reshape(capacity * block_rows, 128) for x in (master, first_moment, second_moment)]
    [parts] = call(
        functools.partial(slices_body, where), [((ndp, 3, capacity * 8, 128), f32)], [HB] * 3,
        [
            pltpu.VMEM((3, capacity * block_rows, 128), f32), pltpu.VMEM((3, 2, 4, capacity * 8, 128), f32),
            pltpu.SemaphoreType.DMA((3,)), pltpu.SemaphoreType.DMA,
        ],
        1 << 20, 4 << 20, 12, (HB,),
    )(*flat_state)
    blocks = owners.shape[0]
    earlier = jnp.arange(blocks)[None, :] < jnp.arange(blocks)[:, None]
    alike = owners[None, :] == owners[:, None]
    slot = jnp.sum((earlier & alike).astype(jnp.int32), axis=1)
    slot_rows = owners * capacity + slot
    hit = slot_rows[None, :] == jnp.arange(ndp * capacity, dtype=jnp.int32)[:, None]
    held = jnp.sum(jnp.where(hit, jnp.arange(blocks, dtype=jnp.int32)[None, :], 0), axis=1)
    counts = jnp.sum(hit.astype(jnp.int32), axis=1)
    [near] = call(
        near_body, [((rows, width), f32)], [SM, HB],
        [all_qkv, pltpu.VMEM((rows, width), f32), pltpu.SemaphoreType.DMA], mm * 1024, 12 << 20, 16, (HB,),
    )(meta, after(qkv, parts, slot, held, counts, ffn_bufs[1], ffn_bufs[2], *states))
    ffn_bufs = both_cores(ffn_bufs)
    held_state = exchange(after(parts, ffn_bufs[3], near), "dp")

    hid_w = w_in.shape[1]
    big = pltpu.VMEM((rows, width), f32)
    low = pltpu.VMEM((rows, width), bf16)
    n_m = (w_out.shape[0] + w_in.shape[0] + w_down.shape[0]) // 2
    wide = pltpu.VMEM((groups, rows, hid_w), f32)
    half = pltpu.VMEM((groups, n_m, width), bf16)
    four = pltpu.VMEM((groups, rows, hid_w), bf16)
    (outputs, head, tail, dx2, dctx, dqf, dstate, ng2, wout, grad_m, give_m) = call(
        main_body,
        [
            ((rows, width), bf16), ((EDGE, width), bf16), ((EDGE, width), bf16),
            ((rows, width), f32), ((rows, width), bf16), ((rows, width), f32), ((groups, STATE, PAIR), bf16), ((2, width), f32),
            ((groups,) + w_out.shape, bf16), ((groups, n_m, width), bf16), ((groups, n_m, width), bf16),
        ],
        [SM] + [HB] * 8 + [VM] * 2 + [HB] * 8,
        [
            low, low, pltpu.VMEM((groups,) + w_out.shape, bf16), big, low, low,
            pltpu.VMEM((4, groups, STATE, PAIR), bf16),
            pltpu.VMEM((groups, width, hid_w), bf16), pltpu.VMEM((groups, hid_w, width), bf16),
            big, big, pltpu.VMEM((rows, 128), f32), wide, wide, big, big, big, big,
            low, low, low, low, low, low, four, four, low, half, half,
            pltpu.VMEM((groups, rows, PAIR), bf16), pltpu.SemaphoreType.DMA((5,)), pltpu.SemaphoreType.DMA,
        ],
        mm * hid_w * groups * 6, 24 << 20, 44,
        (HB, VM, VM, HB, HB, HB, VM, VM, HB, HB, HB),
    )(meta, near, qkv, *states, tok, cot, norm_gains, norm_biases, *ffn_bufs)

    head, tail, dstate, give_m, _ = lax.optimization_barrier((head, tail, dstate, give_m, held_state))
    do_l, do_r = from_mp(tail, 1), from_mp(head, -1)
    late = after(dstate, do_l, do_r)
    dstates = [dstate, swap_mp(dstate, 1)] + [swap_mp(late, m) for m in range(2, groups)]

    bits = [bit_of(me, core, s).astype(jnp.int32).reshape(1) for s in range(2)]

    def halve(own, got, s):
        shape = own.shape[:-1] + (own.shape[-1] // 2,)
        return call(
            halve_body, [(shape, bf16), (shape, f32)], [SM, VM, VM], [], 1 << 20, 4 << 20, 16,
        )(bits[s], own, got)

    def rest_of(keep, got):
        for s in range(2, nbits - 1):
            tot = (keep + got.astype(f32)).astype(bf16)
            keep, got = tot.astype(f32), swap(tot, s)
        return keep, got

    def finish_m(keep, got):
        part = call(
            total_body, [((1,) + keep.shape[1:], bf16)] * groups, [SM, VM, VM], [], 1 << 20, 2 << 20, 12,
        )(meta, *rest_of(keep, got))
        return [part[0]] + [swap_mp(part[m], m) for m in range(1, groups)]

    def finish_q(keep, got, extra):
        keep, got = rest_of(keep, got)
        for s in range(2, nbits - 1):
            extra = extra + swap(extra, s)
        shape = (1, keep.shape[1] + extra.shape[0], keep.shape[2])
        part = call(
            total_q_body, [(shape, f32)] * groups, [SM, VM, VM, VM], [], 1 << 20, 2 << 20, 12,
        )(meta, keep, got, extra)
        return [part[0]] + [swap_mp(part[m], m) for m in range(1, groups)]

    give_m, keep_m = halve(grad_m, after(swap_core(give_m), do_l, do_r, dstates[1]), 0)
    got_m = swap(give_m, 0)
    dq, dkn, dvn = call(
        near_back_body,
        [((rows, width), bf16), ((rows, width), f32), ((rows, width), f32)],
        [SM, HB, HB] + [VM] * 2 + [HB] * 2,
        [
            pltpu.VMEM((rows + 2 * EDGE, width), bf16), pltpu.VMEM((rows + 2 * EDGE, width), f32),
            pltpu.VMEM((ext, width), f32), pltpu.VMEM((ext, width), f32),
            pltpu.VMEM(wout.shape, bf16), big, all_qkv, pltpu.SemaphoreType.DMA((4,)),
        ],
        mm * 2048, 24 << 20, 20,
    )(meta, qkv, after(dctx, give_m), do_l, do_r, wout, dqf)
    n_q = w_qkv.size // width // 2
    n_ng = 4 * width // 128
    dproj, grad_q, give_q = call(
        proj_body,
        [((groups, rows, 3 * PAIR), bf16), ((groups, n_q, width), f32), ((groups, n_q, width), f32)],
        [SM, HB] + [VM] * 7 + [HB],
        [
            pltpu.VMEM((groups, rows, 3 * PAIR), bf16), pltpu.VMEM((3 * width, 128), f32),
            pltpu.VMEM((2 * n_q, width), f32), all_qkv, low,
            pltpu.SemaphoreType.DMA, pltpu.SemaphoreType.DMA((2,)),
        ],
        mm * 3 * width, 24 << 20, 20, (HB, VM, VM),
    )(meta, qkv, dq, dkn, dvn, *dstates, a1e)
    got_q = swap_core(after(give_q, got_m))
    give_m, keep_m = halve(keep_m, after(got_m, give_q), 1)
    got_m = swap(give_m, 1)
    give_q, keep_q = halve(grad_q, got_q, 0)
    got_q = swap(give_q, 0)
    tokens_grad, ng = call(
        last_body,
        [((rows, width), f32), ((n_ng, 128), f32)],
        [SM, HB, VM, HB, VM, VM] + [HB] * 4,
        [
            big, pltpu.VMEM((n_ng, 128), f32), proj_w, pltpu.VMEM((groups, rows, 3 * PAIR), bf16), big,
            pltpu.SemaphoreType.DMA, pltpu.SemaphoreType.DMA((2,)),
        ],
        mm * 3 * width, 8 << 20, 16,
    )(meta, after(dproj, give_q), tok, dx2, norm_gains, ng2, *qkv_bufs)
    z_m = finish_m(keep_m, after(got_m, give_q, ng, got_q))
    give_q, keep_q = halve(keep_q, after(got_q, ng), 1)
    got_q = swap(give_q, 1)
    z_m[0] = after(z_m[0], give_q)

    nb_q = n_q * 2 // 16

    def updated(z, n, first, extra):
        return call(
            functools.partial(pieces_body, first, len(z)),
            [((n, 128), f32), ((n + extra, 128), bf16)],
            [SM, SM] + [VM] * (len(z) + 1), [], 1 << 20, 4 << 20, 20,
        )(owners, slot, *z, held_state)

    def everywhere(piece, *first):
        x, y = swap(piece, 0), swap(piece, 1)
        return both_cores([piece, x, y, swap(after(x, *first), 1)])

    piece_m, fresh_m = updated(z_m, n_m, nb_q, 0)
    [send] = call(
        functools.partial(route_body, nb_q), [((ndp, capacity * 8, 128), bf16)], [SM, VM], [],
        1 << 20, 4 << 20, 16,
    )(held, piece_m)
    recv = exchange(send, "dp")
    m_bufs = everywhere(fresh_m)
    z_q = finish_q(keep_q, after(got_q, fresh_m), ng)
    z_q[0] = after(z_q[0], *m_bufs[1:4])
    _, fresh_q = updated(z_q, n_q, 0, n_q + 2 * n_ng)
    new_out, new_in, new_down = call(
        place_body, [(w_out.shape, bf16), (w_in.shape, bf16), (w_down.shape, bf16)],
        [SM] + [HB] * 8, [pltpu.VMEM((8, n_m, 128), bf16), pltpu.SemaphoreType.DMA],
        1 << 20, 4 << 20, 16,
    )(meta, *m_bufs)
    q_bufs = everywhere(fresh_q, new_down)
    state_shape = (capacity, block_rows, 128)
    norm_shape = (4, width)
    n_held = fresh_q.shape[0]
    (first_new, second_new, master_new, new_qkv, norm_first_new, norm_second_new, norm_new) = call(
        owner_body,
        [(state_shape, f32)] * 3 + [(w_qkv.shape, bf16)] + [(norm_shape, f32)] * 3,
        [SM] * 3 + [HB] * 4 + [VM] * 4 + [HB] * 8,
        [
            pltpu.VMEM((8, n_held, 128), bf16), pltpu.VMEM((8, capacity * 8, 128), f32),
            pltpu.VMEM((8, n_q, 128), f32), pltpu.VMEM((4, capacity, 2, 8, 128), f32),
            pltpu.VMEM((capacity * block_rows, 128), f32), pltpu.VMEM((w_qkv.size // 128, 128), f32),
            pltpu.VMEM((n_ng, 128), f32), pltpu.VMEM((ndp, capacity * 8, 128), bf16),
            pltpu.VMEM(state_shape, f32), pltpu.VMEM(state_shape, f32), pltpu.VMEM(state_shape, f32),
            pltpu.SemaphoreType.DMA, pltpu.SemaphoreType.DMA,
        ],
        1 << 20, 8 << 20, 24,
    )(
        meta, counts, held, recv, master, first_moment, second_moment,
        norm_gains, norm_biases, norm_first, norm_second, *q_bufs,
    )
    return (
        outputs[None], tokens_grad[None], first_new, second_new, master_new,
        new_qkv, new_out, new_in, new_down, norm_first_new, norm_second_new, norm_new,
    )


def solution(mesh):
    sharded = P("dp", "mp", None)
    return jax.shard_map(
        per_device,
        mesh=mesh,
        in_specs=(
            sharded, sharded, P("dp"), P(), P(None, "mp"), P("mp", None), P(None, "mp"), P("mp", None),
            sharded, sharded, sharded, P(), P(), P(), P(),
        ),
        out_specs=(
            sharded, sharded, sharded, sharded, sharded,
            P(None, "mp"), P("mp", None), P(None, "mp"), P("mp", None), P(), P(), P(),
        ),
        check_vma=False,
    )
```

```python
import functools

import jax
import jax.numpy as jnp
from jax import lax
from jax.experimental import pallas as pl
from jax.experimental.pallas import tpu as pltpu
from jax.sharding import PartitionSpec as P

HEAD = 64
BAND = 30
STEP = 10
HALO = 64
EDGE = 32
QB = 64
WIN = 128
PAIR = 128
COST = 1
STATE = 144

learn_rate = 0.1
norm_rate = 0.3
decay_rate = 0.1
beta_one = 0.9
beta_two = 0.95
adam_epsilon = 1e-08
norm_epsilon = 1e-05
GELU_C = 0.7978845608028654
GELU_A = 0.044715

f32 = jnp.float32
bf16 = jnp.bfloat16

VM = pl.BlockSpec(memory_space=pltpu.VMEM)
HB = pl.BlockSpec(memory_space=pltpu.HBM)
SM = pl.BlockSpec(memory_space=pltpu.SMEM)


def call(body, outs, in_specs, scratch, flops, moved, vmem=48, out_specs=None):
    specs = out_specs or tuple(VM for _ in outs)
    run = pl.pallas_call(
        body,
        out_shape=tuple(
            pltpu.HBM(s, d) if spec is HB else jax.ShapeDtypeStruct(s, d) for (s, d), spec in zip(outs, specs)
        ),
        in_specs=in_specs,
        out_specs=specs,
        scratch_shapes=scratch,
        compiler_params=pltpu.CompilerParams(vmem_limit_bytes=vmem << 20),
        cost_estimate=pl.CostEstimate(flops=flops // COST, bytes_accessed=moved // COST, transcendentals=0),
    )

    def fixed(*args):
        return run(
            *[
                pltpu.with_memory_space_constraint(x, pltpu.HBM) if spec is HB else x
                for x, spec in zip(args, in_specs)
            ]
        )

    return fixed


def load(pairs, sem):
    copies = [pltpu.make_async_copy(a, b, sem) for a, b in pairs]
    for c in copies:
        c.start()
    return copies


def dot(a, b):
    return jnp.dot(a, b, preferred_element_type=f32)


def turned(a):
    return a.astype(f32).T.astype(bf16)


def dot_nt(a, b):
    return dot(a, turned(b))


def dot_tn(a, b):
    return lax.dot_general(a, b, (((0,), (0,)), ((), ())), preferred_element_type=f32)


def normalize(x):
    mean = jnp.mean(x, axis=-1, keepdims=True)
    cen = x - mean
    var = jnp.mean(cen * cen, axis=-1, keepdims=True)
    rstd = lax.rsqrt(var + norm_epsilon)
    return cen * rstd, rstd


def same_head(n=PAIR):
    r = lax.broadcasted_iota(jnp.int32, (n, n), 0)
    c = lax.broadcasted_iota(jnp.int32, (n, n), 1)
    return (r < HEAD) == (c < HEAD)


def pack_state(s1, s2, z):
    both = jnp.where(same_head(), s1, pltpu.roll(s2, HEAD, 1))
    hi = z.astype(bf16).astype(f32)
    row = lax.broadcasted_iota(jnp.int32, (16, PAIR), 0)
    tail = jnp.where(row == 0, hi, jnp.where(row == 1, z - hi, 0.0))
    return both.astype(bf16), tail.astype(bf16)


def unpack_state(refs, g):
    tot = refs[0][g].astype(f32)
    for r in refs[1:]:
        tot = tot + r[g].astype(f32)
    both = tot[:PAIR]
    diag = same_head()
    s1 = jnp.where(diag, both, 0.0)
    s2 = jnp.where(diag, pltpu.roll(both, HEAD, 1), 0.0)
    z = tot[PAIR : PAIR + 1] + tot[PAIR + 1 : PAIR + 2]
    return s1, s2, z


def split_dot(a, ones):
    hi, lo = two(a)
    return dot(hi, ones) + dot(lo, ones)


def two(a):
    hi = a.astype(bf16)
    return hi, (a - hi.astype(f32)).astype(bf16)


def phi(v):
    low = jnp.exp(jnp.minimum(v, 0.0))
    return jnp.where(v > 0, v + 1.0, low), jnp.where(v > 0, 1.0, low)


def band_parts():
    c = lax.broadcasted_iota(jnp.int32, (WIN, 2 * QB), 0)
    r = lax.broadcasted_iota(jnp.int32, (WIN, 2 * QB), 1) % QB
    off = r + EDGE - c
    return (jnp.abs(off) <= BAND), off == 0, c


def stacked(rows):
    lane = lax.broadcasted_iota(jnp.int32, (1, PAIR), 1)
    first = (lane < HEAD).astype(f32).astype(bf16)
    second = (lane >= HEAD).astype(f32).astype(bf16)
    return jnp.concatenate([rows * first, rows * second], axis=0)


def unstack(both):
    lane = lax.broadcasted_iota(jnp.int32, (QB, PAIR), 1)
    return jnp.where(lane < HEAD, both[:QB], both[QB:])


def softmax_of(raw, mask):
    scores = jnp.where(mask, raw * 0.125, -1e30)
    ex = jnp.exp(scores - jnp.max(scores, axis=0, keepdims=True))
    return ex * (1.0 / jnp.sum(ex, axis=0, keepdims=True))


def piece_at(meta, r, bits, other):
    b0, b1 = (meta[6], meta[7]) if other else (meta[4], meta[5])
    core = 1 - meta[2] if other else meta[2]
    if bits == 1:
        return core * 2 + (b0 ^ r)
    return core * 4 + (b0 ^ (r & 1)) * 2 + (b1 ^ (r >> 1))


def fetch_pieces(meta, bufs, lo, rows, weight, sem):
    n = len(bufs) // 2
    copies = []
    for k, buf in enumerate(bufs):
        p = piece_at(meta, k % n, n // 2, k >= n)
        at = pl.ds(pl.multiple_of(p * rows, rows), rows)
        for m in range(buf.shape[0]):
            src = buf.at[m, pl.ds(lo, rows), :]
            copies.append(pltpu.make_async_copy(src, weight.at[meta[3] ^ m, at, :], sem))
    for c in copies:
        c.start()
    return copies


def norm_body(tok, left, right, gains, biases, a1e_h, a1e_o, sem):
    rows = tok.shape[0]
    gain, bias = gains[0:1, :], biases[0:1, :]

    def ln(x):
        return (normalize(x.astype(f32))[0] * gain + bias).astype(bf16)

    a1e_o[0:HALO, :] = ln(left[...])
    a1e_o[HALO + rows :, :] = ln(right[...])

    def chunk(i, _):
        at = pl.ds(pl.multiple_of(i * 128, 128), 128)
        a1e_o[pl.ds(pl.multiple_of(i * 128 + HALO, 64), 128), :] = ln(tok[at, :])
        return 0

    lax.fori_loop(0, rows // 128, chunk, 0)
    out = pltpu.make_async_copy(a1e_o, a1e_h, sem)
    out.start()
    out.wait()


def qkv_body(meta, a1e_h, *refs):
    bufs, (qkv_h, st_o, w, qkv_o, a1e, sem, out_sem) = refs[:4], refs[4:]
    pull = pltpu.make_async_copy(a1e_h, a1e, out_sem)
    pull.start()
    ext = a1e.shape[0]
    rows = ext - 2 * HALO
    groups = bufs[0].shape[0]
    for c in fetch_pieces(meta, bufs, 0, bufs[0].shape[1], w, sem):
        c.wait()
    pull.wait()
    length, base = meta[0], meta[1]
    pos = base + lax.broadcasted_iota(jnp.int32, (rows, 1), 0)
    valid = (pos < length).astype(f32)
    gs = range(groups)
    for g in gs:
        qkv_o[g] = dot(a1e[...], w[g]).astype(bf16)
    own_rows = slice(HALO, HALO + rows)
    out = pltpu.make_async_copy(qkv_o, qkv_h, out_sem)
    out.start()
    parts = []
    for g in gs:
        keys = qkv_o[g, own_rows, PAIR : 2 * PAIR].astype(f32)
        feat = phi(keys)[0] * valid
        parts.append((jnp.sum(feat, axis=0, keepdims=True), two(feat), two(jnp.tanh(keys) * valid)))
    for g in gs:
        z, (fhi, flo), (thi, tlo) = parts[g]
        vals = qkv_o[g, own_rows, 2 * PAIR :]
        s1 = dot_tn(fhi, vals) + dot_tn(flo, vals)
        s2 = dot_tn(thi, vals) + dot_tn(tlo, vals)
        st_o[g, :PAIR, :], st_o[g, PAIR:, :] = pack_state(s1, s2, z)
    out.wait()


def near_body(meta, qkv_h, near_h, qkv, near_o, sem):
    pull = pltpu.make_async_copy(qkv_h, qkv, sem)
    pull.start()
    groups = qkv.shape[0]
    rows = near_o.shape[0]
    length, base = meta[0], meta[1]
    band, diag, lane = band_parts()
    pull.wait()

    def block(b, _):
        at = b * QB
        kpos = base + at - EDGE + lane
        mask = band & (((kpos >= 0) & (kpos < length)) | diag)
        q_at = pl.ds(pl.multiple_of(at + HALO, QB), QB)
        w_at = pl.ds(pl.multiple_of(at + HALO - EDGE, EDGE), WIN)
        gs = range(groups)
        sc = [dot_nt(qkv[g, w_at, PAIR : 2 * PAIR], stacked(qkv[g, q_at, 0:PAIR])) for g in gs]
        p = [softmax_of(sc[g], mask).astype(bf16) for g in gs]
        res = [dot_tn(p[g], qkv[g, w_at, 2 * PAIR :]) for g in gs]
        for g in gs:
            near_o[pl.ds(pl.multiple_of(at, QB), QB), g * PAIR : (g + 1) * PAIR] = unstack(res[g])
        return 0

    lax.fori_loop(0, rows // QB, block, 0, unroll=4)
    out = pltpu.make_async_copy(near_o, near_h, sem)
    out.start()
    out.wait()


def put_halves(core, keep, give, g, lo, grad):
    n, width = grad.shape
    tiles = grad.reshape(n // 16, 2, 8, width)
    even, odd = tiles[:, 0].reshape(n // 2, width), tiles[:, 1].reshape(n // 2, width)
    first = jnp.full(even.shape, core, jnp.int32) == 0
    at = slice(lo, lo + n // 2)
    keep[g, at, :] = jnp.where(first, even, odd).astype(keep.dtype)
    give[g, at, :] = jnp.where(first, odd, even).astype(give.dtype)


def main_body(meta, near_h, qkv_h, h0, h1, h2, h3, tok_h, cot_h, gains, biases, *refs):
    bufs, refs = refs[:8], refs[8:]
    out_h, dst_o, far_o, dx2_h, dctx_h, dqf_h, ng_o, wout_h, keep_h, give_h = refs[:10]
    refs = refs[10:]
    do_o, dctx_o, wout_o, near, tok, cot, st = refs[:7]
    refs = (None,) * 5 + refs
    w_in, w_down, x2, xhat, rs, u, dh, acc, da2, far1, inv, dnum, phq, thq = refs[12:26]
    ctx_o, a2_o, dm_o, hid_o, du_o, out_o, keep, give, query, sem, out_sem = refs[26:]
    rows, width = tok.shape
    groups, hw = hid_o.shape[0], hid_o.shape[2]
    s0, s1, s2, s3 = [st.at[k] for k in range(4)]
    moved = load([(near_h, near), (tok_h, tok), (cot_h, cot)] + [(h, st.at[k]) for k, h in enumerate((h0, h1, h2, h3))], sem.at[4])
    pr = hw // 8
    orow = bufs[0].shape[1] - 2 * pr
    core = meta[2]
    sent = []

    def send(src, dst):
        sent.append(pltpu.make_async_copy(src, dst, out_sem))
        sent[-1].start()

    length, base = meta[0], meta[1]
    pull = pltpu.make_async_copy(qkv_h.at[:, pl.ds(HALO, rows), pl.ds(0, PAIR)], query, sem.at[3])
    pull.start()
    copies = fetch_pieces(meta, bufs, 2 * pr, orow, wout_o, sem.at[0])
    later = fetch_pieces(meta, bufs, 0, pr, w_in, sem.at[1])
    last = fetch_pieces(meta, bufs, pr, pr, w_down, sem.at[2])
    rlen = 1.0 / length.astype(f32)
    gain, bias = gains[1:2, :], biases[1:2, :]
    ones = same_head().astype(f32).astype(bf16)
    gs = range(groups)
    cols = [slice(g * PAIR, (g + 1) * PAIR) for g in gs]
    for c in moved:
        c.wait()
    states = [unpack_state((s0, s1, s2, s3), g) for g in gs]
    s1b, s2b = [two(st[0]) for st in states], [two(st[1]) for st in states]
    cr = 128

    def far_chunk(i, _):
        at = pl.ds(pl.multiple_of(i * cr, cr), cr)
        q = [query[g, at, :].astype(f32) for g in gs]
        ph = [phi(q[g])[0] for g in gs]
        ph2 = [two(ph[g]) for g in gs]
        th2 = [two(jnp.tanh(q[g])) for g in gs]
        den = [split_dot(ph[g] * states[g][2], ones) for g in gs]
        num = [dot(ph2[g][0], s1b[g][0]) + dot(ph2[g][0], s1b[g][1]) + dot(ph2[g][1], s1b[g][0]) for g in gs]
        sec = [dot(th2[g][0], s2b[g][0]) + dot(th2[g][0], s2b[g][1]) + dot(th2[g][1], s2b[g][0]) for g in gs]
        for g in gs:
            phq[at, cols[g]] = ph2[g][0]
            thq[at, cols[g]] = th2[g][0]
        rec = [1.0 / den[g] for g in gs]
        for g in gs:
            part = num[g] * rec[g]
            inv[at, cols[g]] = rec[g]
            far1[at, cols[g]] = part
            ctx_o[at, cols[g]] = (near[at, cols[g]] + (part + sec[g] * rlen)).astype(bf16)
        pos = base + i * cr + lax.broadcasted_iota(jnp.int32, (cr, 1), 0)
        dm_o[at, :] = (cot[at, :].astype(f32) * (pos < length).astype(f32)).astype(bf16)
        return 0

    pull.wait()
    lax.fori_loop(0, rows // cr, far_chunk, 0)
    for c in copies:
        c.wait()
    wout = wout_o[...].reshape(width, width)
    x2[...] = dot(ctx_o[...], wout)

    def norm_chunk(i, _):
        at = pl.ds(pl.multiple_of(i * 64, 64), 64)
        val = x2[at, :] + tok[at, :].astype(f32)
        x2[at, :] = val
        xh, rstd = normalize(val)
        xhat[at, :] = xh
        rs[at, :] = jnp.broadcast_to(rstd, (64, 128))
        a2_o[at, :] = (xh * gain + bias).astype(bf16)
        return 0

    lax.fori_loop(0, rows // 64, norm_chunk, 0)
    for c in later + last:
        c.wait()
    for g in gs:
        u[g] = dot(a2_o[...], w_in[g])
        dh[g] = dot_nt(dm_o[...], w_down[g])

    def act(i, _):
        at = pl.ds(pl.multiple_of(i * 16, 16), 16)
        for g in gs:
            v = u[g, at, :]
            sq = v * v
            half = 0.5 + 0.5 * jnp.tanh(v * (GELU_C + GELU_C * GELU_A * sq))
            hid = v * half
            hid_o[g, at, :] = hid.astype(bf16)
            slope = half + (hid * (1.0 - half)) * (2.0 * GELU_C + 6.0 * GELU_C * GELU_A * sq)
            du_o[g, at, :] = (dh[g, at, :] * slope).astype(bf16)
        return 0

    lax.fori_loop(0, rows // 16, act, 0)
    acc[...] = sum(dot(hid_o[g], w_down[g]) for g in gs)
    da2[...] = sum(dot_nt(du_o[g], w_in[g]) for g in gs)

    def back_chunk(i, carry):
        dg, db = carry
        at = pl.ds(pl.multiple_of(i * 64, 64), 64)
        out_o[at, :] = (x2[at, :] + acc[at, :]).astype(bf16)
        xh = xhat[at, :]
        rstd = rs[at, 0:1]
        d = da2[at, :]
        dg = dg + jnp.sum(d * xh, axis=0, keepdims=True)
        db = db + jnp.sum(d, axis=0, keepdims=True)
        e = d * gain
        m1 = jnp.mean(e, axis=-1, keepdims=True)
        m2 = jnp.mean(e * xh, axis=-1, keepdims=True)
        dx = dm_o[at, :].astype(f32) + rstd * (e - m1 - xh * m2)
        acc[at, :] = dx
        do_o[at, :] = dx.astype(bf16)
        return dg, db

    zero = jnp.zeros((1, width), f32)
    dg, db = lax.fori_loop(0, rows // 64, back_chunk, (zero, zero))
    even = jnp.full((EDGE, width), meta[3] & 1, jnp.int32) == 0
    head, tail = do_o[0:EDGE, :].astype(f32), do_o[rows - EDGE :, :].astype(f32)
    near_edge, far_edge = jnp.where(even, tail, head).astype(bf16), jnp.where(even, head, tail).astype(bf16)
    for g in gs:
        dst_o[g, STATE:, :] = near_edge[:, cols[g]]
        far_o[g, STATE:, :] = far_edge[:, cols[g]]
    send(out_o, out_h)
    send(wout_o, wout_h)
    send(acc, dx2_h)
    ng_o[0:1, :] = dg
    ng_o[1:2, :] = db
    dctx_o[...] = dot_nt(do_o[...], wout).astype(bf16)
    send(dctx_o, dctx_h)

    def far_back(i, carry):
        at = pl.ds(pl.multiple_of(i * cr, cr), cr)
        dc = [dctx_o[at, cols[g]] for g in gs]
        dcf = [dc[g].astype(f32) for g in gs]
        rec = [inv[at, cols[g]] for g in gs]
        dn = [(dcf[g] * rec[g]).astype(bf16) for g in gs]
        dots = [split_dot(dcf[g] * far1[at, cols[g]], ones) for g in gs]
        dph = [dot_nt(dn[g], s1b[g][0]) for g in gs]
        dth = [dot_nt(dc[g], s2b[g][0]) for g in gs]
        out = []
        for g in gs:
            dnum[at, cols[g]] = dn[g]
            dden = -dots[g] * rec[g]
            out.append(carry[g] + jnp.sum(phq[at, cols[g]].astype(f32) * dden, axis=0, keepdims=True))
            slope = phi(query[g, at, :].astype(f32))[1]
            th = thq[at, cols[g]].astype(f32)
            da2[at, cols[g]] = (dph[g] + dden * states[g][2]) * slope + dth[g] * rlen * (1.0 - th * th)
        return tuple(out)

    none = jnp.zeros((1, PAIR), f32)
    dz = lax.fori_loop(0, rows // cr, far_back, (none,) * groups)
    for g in gs:
        d1 = dot_tn(phq[:, cols[g]], dnum[:, cols[g]])
        d2 = dot_tn(thq[:, cols[g]], dctx_o[:, cols[g]]) * rlen
        both, low = pack_state(d1, d2, dz[g])
        for ref in (dst_o, far_o):
            ref[g, :PAIR, :] = both
            ref[g, PAIR:STATE, :] = low
    send(da2, dqf_h)
    n_out = ctx_o.shape[1] // groups

    def finish(g, lo, n, grad):
        put_halves(core, keep, give, g, lo, grad)
        part = pl.ds(lo, n)
        send(keep.at[g, part, :], keep_h.at[g, part, :])
        send(give.at[g, part, :], give_h.at[g, part, :])

    for g in gs:
        finish(g, n_out // 2, width // 2, dot_tn(a2_o[...], du_o[g]))
    for g in gs:
        finish(g, 0, n_out // 2, dot_tn(ctx_o[:, g * n_out : (g + 1) * n_out], do_o[...]))
    for g in gs:
        finish(g, n_out // 2 + width // 2, hw // 2, dot_tn(hid_o[g], dm_o[...]))
    for c in sent:
        c.wait()


def near_back_body(
    meta, qkv_h, dctx_h, one, three, wout_h, dqf_h, dq_o, dk_o, dv_o, dce, dqe, dke, dve, wout, dqf, qkv, sem,
):
    pull = pltpu.make_async_copy(qkv_h, qkv, sem.at[2])
    pull.start()
    groups = qkv.shape[0]
    rows, width = dctx_h.shape
    third = pltpu.make_async_copy(dctx_h, dce.at[pl.ds(EDGE, rows), :], sem.at[3])
    third.start()
    length, base = meta[0], meta[1]
    band, diag, lane = band_parts()
    first = pltpu.make_async_copy(wout_h, wout, sem.at[0])
    first.start()
    second = pltpu.make_async_copy(dqf_h, dqf, sem.at[1])
    second.start()
    first.wait()
    w = wout[...].reshape(width, -1)
    z = meta[3]
    odd = jnp.full((EDGE, width), z & 1, jnp.int32) == 1
    side = [
        jnp.concatenate([ref[g, STATE:, :] for g in range(groups)], axis=1).astype(f32) for ref in (one, three)
    ]
    last_z = meta[17] - 1
    do_l = jnp.where(odd, side[0], side[1]) * (z > 0).astype(f32)
    do_r = jnp.where(odd, side[1], side[0]) * (z < last_z).astype(f32)
    dce[0:EDGE, :] = dot_nt(do_l.astype(bf16), w).astype(bf16)
    dce[EDGE + rows :, :] = dot_nt(do_r.astype(bf16), w).astype(bf16)
    dke[...] = jnp.zeros(dke.shape, f32)
    dve[...] = jnp.zeros(dve.shape, f32)
    pull.wait()
    third.wait()

    def block(b, _):
        at = b * QB
        kpos = base + at - HALO + lane
        mask = band & (((kpos >= 0) & (kpos < length)) | diag)
        c_at = pl.ds(pl.multiple_of(at, QB), QB)
        q_at = pl.ds(pl.multiple_of(at + EDGE, EDGE), QB)
        w_at = pl.ds(pl.multiple_of(at, QB), WIN)
        gs = range(groups)
        cols = [slice(g * PAIR, (g + 1) * PAIR) for g in gs]
        qs = [stacked(qkv[g, q_at, 0:PAIR]) for g in gs]
        cs = [stacked(dce[c_at, cols[g]]) for g in gs]
        kw = [qkv[g, w_at, PAIR : 2 * PAIR] for g in gs]
        sc = [dot_nt(kw[g], qs[g]) for g in gs]
        dp = [dot_nt(qkv[g, w_at, 2 * PAIR :], cs[g]) for g in gs]
        p = [softmax_of(sc[g], mask) for g in gs]
        row = [jnp.sum(p[g] * dp[g], axis=0, keepdims=True) for g in gs]
        ds = [(p[g] * (dp[g] - row[g])).astype(bf16) for g in gs]
        pb = [p[g].astype(bf16) for g in gs]
        for g in gs:
            dke[w_at, cols[g]] += dot(ds[g], qs[g])
            dve[w_at, cols[g]] += dot(pb[g], cs[g])
        dq = [dot_tn(ds[g], kw[g]) for g in gs]
        for g in gs:
            dqe[c_at, cols[g]] = unstack(dq[g])
        return 0

    lax.fori_loop(0, rows // QB + 1, block, 0, unroll=9)
    second.wait()
    dq_o[...] = (dqe[EDGE : EDGE + rows, :] * 0.125 + dqf[...]).astype(bf16)
    dk_o[...] = dke[HALO : HALO + rows, :] * 0.125
    dv_o[...] = dve[HALO : HALO + rows, :]


def proj_body(
    meta, qkv_h, dq, dkn, dvn, s0, s1, s2, s3, a1e_h, dproj_h, keep_o, give_o, dproj, flat, pseudo, qkv, a1e, sem, in_sem,
):
    rows = dq.shape[0]
    other = pltpu.make_async_copy(a1e_h.at[pl.ds(HALO, rows), :], a1e, in_sem.at[1])
    other.start()
    pull = pltpu.make_async_copy(qkv_h, qkv, in_sem.at[0])
    pull.start()
    groups = qkv.shape[0]
    rows, width = dq.shape
    length, base, core = meta[0], meta[1], meta[2]
    cr = 128
    gs = range(groups)
    cols = [slice(g * PAIR, (g + 1) * PAIR) for g in gs]
    states = [unpack_state((s0, s1, s2, s3), g) for g in gs]
    s1b, s2b = [st[0].astype(bf16) for st in states], [st[1].astype(bf16) for st in states]

    def far_chunk(i, _):
        at = pl.ds(pl.multiple_of(i * cr, cr), cr)
        e_at = pl.ds(pl.multiple_of(i * cr + HALO, HALO), cr)
        pos = base + i * cr + lax.broadcasted_iota(jnp.int32, (cr, 1), 0)
        valid = (pos < length).astype(f32)
        k = [qkv[g, e_at, PAIR : 2 * PAIR].astype(f32) for g in gs]
        v = [qkv[g, e_at, 2 * PAIR :] for g in gs]
        feat = [phi(k[g]) for g in gs]
        th = [jnp.tanh(k[g]) for g in gs]
        vd1 = [dot_nt(v[g], s1b[g]) for g in gs]
        vd2 = [dot_nt(v[g], s2b[g]) for g in gs]
        dv = [
            dot((feat[g][0] * valid).astype(bf16), s1b[g]) + dot((th[g] * valid).astype(bf16), s2b[g]) for g in gs
        ]
        for g in gs:
            dk = (vd1[g] + states[g][2]) * feat[g][1] + vd2[g] * (1.0 - th[g] * th[g])
            dproj[g, at, 0:PAIR] = dq[at, cols[g]]
            dproj[g, at, PAIR : 2 * PAIR] = (dkn[at, cols[g]] + dk * valid).astype(bf16)
            dproj[g, at, 2 * PAIR :] = (dvn[at, cols[g]] + dv[g]).astype(bf16)
        return 0

    pull.wait()
    lax.fori_loop(0, rows // cr, far_chunk, 0)
    out = pltpu.make_async_copy(dproj, dproj_h, sem)
    out.start()
    other.wait()
    n_flat = 3 * width
    for g in gs:
        grad = dot_tn(a1e[...], dproj[g])
        for part in range(3):
            flat[pl.ds(part, width, stride=3), :] = grad[:, part * PAIR : (part + 1) * PAIR]
        for j in range(4):
            pseudo[:, j * 128 : (j + 1) * 128] = flat[pl.ds(j, n_flat // 4, stride=4), :]
        put_halves(core, keep_o, give_o, g, 0, pseudo[...])
    out.wait()


def last_body(meta, dproj_h, tok, dx2_h, gains, ng2, *refs):
    bufs, (tg_o, ng_o, da1, ngs, wqkv, dproj, dx2, sem, sems) = refs[:4], refs[4:]
    groups = dproj.shape[0]
    rows, width = tok.shape
    gain = gains[0:1, :]
    copies = fetch_pieces(meta, bufs, 0, bufs[0].shape[1], wqkv, sem)
    copies.append(pltpu.make_async_copy(dproj_h, dproj, sems.at[0]))
    copies[-1].start()
    late = pltpu.make_async_copy(dx2_h, dx2, sems.at[1])
    late.start()
    for c in copies:
        c.wait()
    da1[...] = sum(dot_nt(dproj[g], wqkv[g]) for g in range(groups))

    late.wait()

    def back_chunk(i, carry):
        dg, db = carry
        at = pl.ds(pl.multiple_of(i * 64, 64), 64)
        xh, rstd = normalize(tok[at, :].astype(f32))
        d = da1[at, :]
        dg = dg + jnp.sum(d * xh, axis=0, keepdims=True)
        db = db + jnp.sum(d, axis=0, keepdims=True)
        e = d * gain
        m1 = jnp.mean(e, axis=-1, keepdims=True)
        m2 = jnp.mean(e * xh, axis=-1, keepdims=True)
        tg_o[at, :] = dx2[at, :] + rstd * (e - m1 - xh * m2)
        return dg, db

    zero = jnp.zeros((1, width), f32)
    dg, db = lax.fori_loop(0, rows // 64, back_chunk, (zero, zero))
    for k, val in enumerate((dg, db, ng2[0:1, :], ng2[1:2, :])):
        for j in range(width // 128):
            at = k * (width // 128) + j
            ngs[at : at + 1, :] = val[:, j * 128 : (j + 1) * 128]
    ng_o[...] = ngs[...]


def halve_body(bit, own, got, give_o, keep_o):
    groups, _, n = give_o.shape
    out = pl.ds(pl.multiple_of((1 - bit[0]) * n, 128), n)
    stay = pl.ds(pl.multiple_of(bit[0] * n, 128), n)
    for g in range(groups):
        give_o[g] = (own[g, :, out].astype(f32) + got[g, :, out].astype(f32)).astype(bf16)
    for g in range(groups):
        keep_o[g] = own[g, :, stay].astype(f32) + got[g, :, stay].astype(f32)


def total_body(meta, keep, got, *outs):
    for m, out in enumerate(outs):
        g = meta[3] ^ m
        out[0] = (keep[g] + got[g].astype(f32)).astype(bf16)


def total_q_body(meta, keep, got, ng, *outs):
    n, k = keep.shape[1], ng.shape[0]
    hi, lo = two(ng[...])
    for m, out in enumerate(outs):
        g = meta[3] ^ m
        out[0, 0:n, :] = (keep[g] + got[g].astype(f32)).astype(bf16)
        out[0, n : n + k, :], out[0, n + k :, :] = hi, lo


def slices_body(where, master, first, second, out_h, held, parts, sem, out_sem):
    caps = held.shape[1] // 64
    copies = [pltpu.make_async_copy(ref, held.at[t], sem.at[t]) for t, ref in enumerate((master, first, second))]
    for c in copies:
        c.start()
    sent = []
    for t in range(3):
        copies[t].wait()
        for j in range(4):
            val = held[t, pl.ds(j, caps * 16, stride=4), :].reshape(caps, 2, 8, 128)
            for c in range(2):
                parts[t, c, j] = val[:, c].reshape(caps * 8, 128)
                for d in where[c][j]:
                    sent.append(pltpu.make_async_copy(parts.at[t, c, j], out_h.at[d, t], out_sem))
                    sent[-1].start()
    for c in sent:
        c.wait()


def adam(g, m_old, f_old, s_old):
    corr_one = 1.0 - beta_one**STEP
    corr_two = 1.0 - beta_two**STEP
    fn = beta_one * f_old + (1.0 - beta_one) * g
    sn = beta_two * s_old + (1.0 - beta_two) * g * g
    step = fn / corr_one / (jnp.sqrt(sn / corr_two) + adam_epsilon)
    return fn, sn, m_old - learn_rate * (step + decay_rate * m_old)


def pieces_body(first, count, owners, slots, *refs):
    parts, (st, w_o, piece_o) = refs[:count], refs[count:]
    n = piece_o.shape[0]
    src = [(r, s) for r in parts for s in range(r.shape[0])]
    piece_o[...] = sum(r[s, 0:n, :].astype(f32) for r, s in src)
    w_o[n : 2 * n, :] = piece_o[...].astype(bf16)
    if w_o.shape[0] > 2 * n:
        k = (parts[0].shape[1] - n) // 2
        w_o[2 * n : 3 * n, :] = two(piece_o[...])[1]
        norms = sum(r[s, n : n + k, :].astype(f32) + r[s, n + k :, :].astype(f32) for r, s in src)
        w_o[3 * n : 3 * n + k, :], w_o[3 * n + k :, :] = two(norms)

    def pair(i, _):
        new = []
        for k in range(2):
            b = i * 2 + k
            at = pl.ds(pl.multiple_of(slots[first + b] * 8, 8), 8)
            own = owners[first + b]
            g = piece_o[pl.ds(pl.multiple_of(b * 8, 8), 8), :]
            new.append(adam(g, st[own, 0, at, :], st[own, 1, at, :], st[own, 2, at, :])[2])
        w_o[pl.ds(pl.multiple_of(i * 16, 16), 16), :] = jnp.concatenate(new, axis=0).astype(bf16)
        return 0

    lax.fori_loop(0, n // 16, pair, 0, unroll=4)


def owner_body(
    meta, counts, blocks, later_h, master_h, first_h, second_h, gains, biases, n_first, n_second, *refs
):
    bufs, (f_o, s_o, m_o, q_o, nf_o, ns_o, np_o) = refs[:8], refs[8:15]
    held, early, parts, grad, flat, total, master, first, second, sem, sems = refs[15:]
    moved = load([(later_h, parts), (master_h, master), (first_h, first), (second_h, second)], sems)
    collect(meta, bufs, held, sem)
    for c in moved:
        c.wait()
    caps, br, _ = master.shape
    n = q_o.shape[0] * q_o.shape[1] // (128 * 64)
    k_ng = total.shape[0]
    for p in range(8):
        early[p] = held[p, n * 8 : n * 16, :].astype(f32) + held[p, n * 16 : n * 24, :].astype(f32)
    total[...] = sum(
        held[p, n * 24 : n * 24 + k_ng, :].astype(f32) + held[p, n * 24 + k_ng :, :].astype(f32) for p in range(8)
    )
    start = meta[8] * caps

    def pick(r, _):
        b = blocks[start + r]
        old = pl.ds(pl.multiple_of(jnp.minimum(b, n - 1) * 8, 8), 8)
        is_q = jnp.full((8, 128), b, jnp.int32) < n
        for p in range(8):
            parts[p % 4, r, p // 4] = jnp.where(is_q, early[p, old, :], parts[p % 4, r, p // 4])
        return 0

    lax.fori_loop(0, caps, pick, 0, unroll=2)
    for j in range(4):
        grad[pl.ds(j, caps * 16, stride=4), :] = parts[j].reshape(caps * 16, 128)

    def slot(r, _):
        g = grad[pl.ds(pl.multiple_of(r * br, br), br), :]
        m_old, f_old, s_old = master[r], first[r], second[r]
        fn, sn, mn = adam(g, m_old, f_old, s_old)
        keep = jnp.full(g.shape, counts[start + r], jnp.int32) > 0
        f_o[r] = jnp.where(keep, fn, f_old)
        s_o[r] = jnp.where(keep, sn, s_old)
        m_o[r] = jnp.where(keep, mn, m_old)
        return 0

    lax.fori_loop(0, caps, slot, 0, unroll=2)
    rows = q_o.shape[0]
    for j in range(4):
        flat[pl.ds(j, n * 16, stride=4), :] = columns(held, j, 0, n * 8)
    for part in range(3):
        q_o[:, part * 128 : (part + 1) * 128] = flat[pl.ds(part, rows, stride=3), :].astype(bf16)
    corr_one = 1.0 - beta_one**STEP
    corr_two = 1.0 - beta_two**STEP
    per = n_first.shape[1] // 128
    for k in range(4):
        old = (biases if k % 2 else gains)[k // 2 : k // 2 + 1, :]
        g = jnp.concatenate([total[k * per + j : k * per + j + 1, :] for j in range(per)], axis=1)
        fn = beta_one * n_first[k : k + 1, :] + (1.0 - beta_one) * g
        sn = beta_two * n_second[k : k + 1, :] + (1.0 - beta_two) * g * g
        nf_o[k : k + 1, :] = fn
        ns_o[k : k + 1, :] = sn
        np_o[k : k + 1, :] = old - norm_rate * (fn / corr_one / (jnp.sqrt(sn / corr_two) + adam_epsilon))


def collect(meta, bufs, held, sem):
    copies = []
    for k, buf in enumerate(bufs):
        copies.append(pltpu.make_async_copy(buf, held.at[piece_at(meta, k % 4, 2, k >= 4)], sem))
        copies[-1].start()
    for c in copies:
        c.wait()


def columns(held, j, lo, n):
    even, odd = [held[c * 4 + j, lo : lo + n, :].astype(f32).reshape(n // 8, 1, 8, 128) for c in range(2)]
    return jnp.concatenate([even, odd], axis=1).reshape(2 * n, 128)


def place_body(first, meta, blocks, *refs):
    bufs, outs, (parts_h, held, grads, parts, sem) = refs[:8], refs[8:11], refs[11:]
    collect(meta, bufs, held, sem)
    half = held.shape[1] // 2
    for p in range(8):
        grads[p] = held[p, half:, :].astype(f32)
    caps = parts.shape[1]

    def pick(r, _):
        b = jnp.maximum(blocks[meta[8] * caps + r] - first, 0)
        at = pl.ds(pl.multiple_of(b * 8, 8), 8)
        for p in range(8):
            parts[p % 4, r, p // 4] = grads[p, at, :]
        return 0

    lax.fori_loop(0, caps, pick, 0, unroll=2)
    out = pltpu.make_async_copy(parts, parts_h, sem)
    out.start()
    lo = 0
    for ref in outs:
        n = ref.shape[0] // 2
        for j in range(4):
            ref[:, j * 128 : (j + 1) * 128] = columns(held, j, lo, n).astype(bf16)
        lo += n
    out.wait()


def per_device(
    tokens, cotangent, lengths, owners, w_qkv, w_out, w_in, w_down,
    master, first_moment, second_moment, norm_gains, norm_biases, norm_first, norm_second,
):
    rows, width = tokens.shape[1], tokens.shape[2]
    groups = lax.axis_size("mp")
    ndp = lax.axis_size("dp")
    nbits = ndp.bit_length() - 1
    rest = list(range(1, nbits))
    order = (rest, rest[:2][::-1] + rest[2:][::-1])
    me, zi = lax.axis_index("dp"), lax.axis_index("mp")
    core = me & 1

    def bit_of(who, at, s):
        return (who >> jnp.where(at == 0, order[0][s], order[1][s])) & 1

    def swap(x, s):
        return lax.ppermute(x, "dp", [(i, i ^ (1 << order[i & 1][s])) for i in range(ndp)])

    def swap_core(x):
        return lax.ppermute(x, "dp", [(i, i ^ 1) for i in range(ndp)])

    def from_mp(x, step):
        return lax.ppermute(x, "mp", [(i, i + step) for i in range(groups) if 0 <= i + step < groups])

    def swap_mp(x, mask):
        return lax.ppermute(x, "mp", [(i, i ^ mask) for i in range(groups)])

    def exchange(x, axis):
        return lax.all_to_all(x, axis, 0, 0, tiled=True)

    def all_states(x):
        return [x] + [swap_mp(x, m) for m in range(1, groups)]

    q0, q1 = bit_of(me, core, 0), bit_of(me, core, 1)
    o0, o1 = bit_of(me, 1 - core, 0), bit_of(me, 1 - core, 1)
    length = lengths[0]
    base = zi * rows
    ids = [length, base, core, zi, q0, q1, o0, o1, me]
    ids += [
        me - (me & 7) + c + ((j >> 1) << order[c][0]) + ((j & 1) << order[c][1]) for c in range(2) for j in range(4)
    ]
    ids.append(jnp.int32(groups))
    meta = jnp.stack(ids).astype(jnp.int32)

    def after(x, *deps):
        return lax.optimization_barrier((x,) + deps)[0]

    def over_mp(piece):
        return [piece] + [swap_mp(piece, m) for m in range(1, groups)]

    def both_cores(bufs):
        return bufs + [swap_core(b) for b in bufs]

    def part_of(w, n, at):
        return lax.dynamic_slice_in_dim(w, at * (w.shape[0] // n), w.shape[0] // n, 0)

    mine = core * 4 + q0 * 2 + q1
    tok, cot = tokens[0], cotangent[0]
    ext = rows + 2 * HALO
    mm = 2 * rows * width
    qkv_z = over_mp(part_of(w_qkv, 4, core * 2 + q0))
    left, right = from_mp(tok[rows - HALO :], 1), from_mp(tok[:HALO], -1)
    ffn_piece = jnp.concatenate([part_of(w, 8, mine) for w in (w_in, w_down, w_out)], axis=0)
    qkv_z = after(jnp.stack(qkv_z), left, right, ffn_piece)
    ffn_z = jnp.stack(over_mp(after(ffn_piece, qkv_z)))
    qkv_bufs = [qkv_z, swap(qkv_z, 0)]
    capacity, block_rows = master.shape[0], master.shape[1]
    where = [[[] for _ in range(4)] for _ in range(2)]
    for d in range(ndp):
        b = order[d & 1]
        where[d & 1][2 * ((d >> b[0]) & 1) + ((d >> b[1]) & 1)].append(d)
    flat_state = [x.reshape(capacity * block_rows, 128) for x in (master, first_moment, second_moment)]
    [parts] = call(
        functools.partial(slices_body, where), [((ndp, 3, capacity * 8, 128), f32)], [HB] * 3,
        [
            pltpu.VMEM((3, capacity * block_rows, 128), f32), pltpu.VMEM((3, 2, 4, capacity * 8, 128), f32),
            pltpu.SemaphoreType.DMA((3,)), pltpu.SemaphoreType.DMA,
        ],
        1 << 20, 4 << 20, 12, (HB,),
    )(*flat_state)
    [a1e] = call(norm_body, [((ext, width), bf16)], [VM] * 5,
        [pltpu.VMEM((ext, width), bf16), pltpu.SemaphoreType.DMA], 4 * mm, 1 << 20, 16, (HB,),
    )(
        after(tok, parts), left, right, norm_gains, norm_biases
    )
    qkv_bufs = both_cores([qkv_bufs[0], after(qkv_bufs[1], a1e)])
    all_qkv = pltpu.VMEM((groups, ext, 3 * PAIR), bf16)
    proj_w = pltpu.VMEM((groups, width, 3 * PAIR), bf16)
    qkv, state = call(
        qkv_body,
        [((groups, ext, 3 * PAIR), bf16), ((groups, STATE, PAIR), bf16)],
        [SM] + [HB] * 5,
        [proj_w, all_qkv, pltpu.VMEM((ext, width), bf16), pltpu.SemaphoreType.DMA, pltpu.SemaphoreType.DMA],
        2 * ext * width * 3 * width, 6 << 20, 20, (HB, VM),
    )(meta, after(a1e, ffn_z), *qkv_bufs)
    states = all_states(state)
    ffn_z = after(ffn_z, a1e, qkv_bufs[1])
    ffn_x, ffn_y = swap(ffn_z, 0), swap(ffn_z, 1)
    ffn_bufs = [ffn_z, ffn_x, ffn_y, swap(after(ffn_x, ffn_y, *states), 1)]
    blocks = owners.shape[0]
    earlier = jnp.arange(blocks)[None, :] < jnp.arange(blocks)[:, None]
    alike = owners[None, :] == owners[:, None]
    slot = jnp.sum((earlier & alike).astype(jnp.int32), axis=1)
    slot_rows = owners * capacity + slot
    hit = slot_rows[None, :] == jnp.arange(ndp * capacity, dtype=jnp.int32)[:, None]
    held = jnp.sum(jnp.where(hit, jnp.arange(blocks, dtype=jnp.int32)[None, :], 0), axis=1)
    counts = jnp.sum(hit.astype(jnp.int32), axis=1)
    [near] = call(
        near_body, [((rows, width), f32)], [SM, HB],
        [all_qkv, pltpu.VMEM((rows, width), f32), pltpu.SemaphoreType.DMA], mm * 1024, 12 << 20, 16, (HB,),
    )(meta, after(qkv, slot, held, counts, ffn_bufs[1], ffn_bufs[2], *states))
    ffn_bufs = both_cores(ffn_bufs)
    held_state = exchange(after(parts, ffn_bufs[3], near), "dp")

    hid_w = w_in.shape[1]
    big = pltpu.VMEM((rows, width), f32)
    low = pltpu.VMEM((rows, width), bf16)
    n_m = (w_out.shape[0] + w_in.shape[0] + w_down.shape[0]) // 2
    wide = pltpu.VMEM((groups, rows, hid_w), f32)
    half = pltpu.VMEM((groups, n_m, width), bf16)
    four = pltpu.VMEM((groups, rows, hid_w), bf16)
    (outputs, dstate, dfar, dx2, dctx, dqf, ng2, wout, grad_m, give_m) = call(
        main_body,
        [
            ((rows, width), bf16), ((groups, STATE + EDGE, PAIR), bf16), ((groups, STATE + EDGE, PAIR), bf16),
            ((rows, width), f32), ((rows, width), bf16), ((rows, width), f32), ((2, width), f32),
            ((groups,) + w_out.shape, bf16), ((groups, n_m, width), bf16), ((groups, n_m, width), bf16),
        ],
        [SM] + [HB] * 8 + [VM] * 2 + [HB] * 8,
        [
            low, low, pltpu.VMEM((groups,) + w_out.shape, bf16), big, low, low,
            pltpu.VMEM((4, groups, STATE, PAIR), bf16),
            pltpu.VMEM((groups, width, hid_w), bf16), pltpu.VMEM((groups, hid_w, width), bf16),
            big, big, pltpu.VMEM((rows, 128), f32), wide, wide, big, big, big, big,
            low, low, low, low, low, low, four, four, low, half, half,
            pltpu.VMEM((groups, rows, PAIR), bf16), pltpu.SemaphoreType.DMA((5,)), pltpu.SemaphoreType.DMA,
        ],
        mm * hid_w * groups * 6, 24 << 20, 44,
        (HB, VM, VM, HB, HB, HB, VM, HB, HB, HB),
    )(meta, near, qkv, *states, tok, cot, norm_gains, norm_biases, *ffn_bufs)

    dstate, dfar, give_m, _ = lax.optimization_barrier((dstate, dfar, give_m, held_state))
    dstates = [dstate, swap_mp(dstate, 1), swap_mp(dstate, 2), swap_mp(dfar, 3)]

    bits = [bit_of(me, core, s).astype(jnp.int32).reshape(1) for s in range(2)]

    def halve(own, got, s):
        shape = own.shape[:-1] + (own.shape[-1] // 2,)
        return call(
            halve_body, [(shape, bf16), (shape, f32)], [SM, VM, VM], [], 1 << 20, 4 << 20, 16,
        )(bits[s], own, got)

    def rest_of(keep, got):
        for s in range(2, nbits - 1):
            tot = (keep + got.astype(f32)).astype(bf16)
            keep, got = tot.astype(f32), swap(tot, s)
        return keep, got

    def to_groups(part):
        return [part[0]] + [swap_mp(part[m], m) for m in range(1, groups)]

    def total_m(keep, got):
        return call(
            total_body, [((1,) + keep.shape[1:], bf16)] * groups, [SM, VM, VM], [], 1 << 20, 2 << 20, 12,
        )(meta, *rest_of(keep, got))

    def total_q(keep, got, extra):
        keep, got = rest_of(keep, got)
        for s in range(2, nbits - 1):
            extra = extra + swap(extra, s)
        shape = (1, keep.shape[1] + 2 * extra.shape[0], keep.shape[2])
        return call(
            total_q_body, [(shape, bf16)] * groups, [SM, VM, VM, VM], [], 1 << 20, 2 << 20, 12,
        )(meta, keep, got, extra)

    give_m, keep_m = halve(grad_m, after(swap_core(give_m), dstates[1], dstates[3]), 0)
    got_m = swap(give_m, 0)
    dq, dkn, dvn = call(
        near_back_body,
        [((rows, width), bf16), ((rows, width), f32), ((rows, width), f32)],
        [SM, HB, HB] + [VM] * 2 + [HB] * 2,
        [
            pltpu.VMEM((rows + 2 * EDGE, width), bf16), pltpu.VMEM((rows + 2 * EDGE, width), f32),
            pltpu.VMEM((ext, width), f32), pltpu.VMEM((ext, width), f32),
            pltpu.VMEM(wout.shape, bf16), big, all_qkv, pltpu.SemaphoreType.DMA((4,)),
        ],
        mm * 2048, 24 << 20, 20,
    )(meta, qkv, after(dctx, give_m), dstates[1], dstates[3], wout, dqf)
    n_q = w_qkv.size // width // 2
    n_ng = 4 * width // 128
    dproj, grad_q, give_q = call(
        proj_body,
        [((groups, rows, 3 * PAIR), bf16), ((groups, n_q, width), f32), ((groups, n_q, width), f32)],
        [SM, HB] + [VM] * 7 + [HB],
        [
            pltpu.VMEM((groups, rows, 3 * PAIR), bf16), pltpu.VMEM((3 * width, 128), f32),
            pltpu.VMEM((2 * n_q, width), f32), all_qkv, low,
            pltpu.SemaphoreType.DMA, pltpu.SemaphoreType.DMA((2,)),
        ],
        mm * 3 * width, 24 << 20, 20, (HB, VM, VM),
    )(meta, qkv, dq, dkn, dvn, *dstates, a1e)
    got_q = swap_core(after(give_q, got_m))
    give_m, keep_m = halve(keep_m, after(got_m, give_q), 1)
    got_m = swap(give_m, 1)
    give_q, keep_q = halve(grad_q, got_q, 0)
    got_q = swap(give_q, 0)
    tokens_grad, ng = call(
        last_body,
        [((rows, width), f32), ((n_ng, 128), f32)],
        [SM, HB, VM, HB, VM, VM] + [HB] * 4,
        [
            big, pltpu.VMEM((n_ng, 128), f32), proj_w, pltpu.VMEM((groups, rows, 3 * PAIR), bf16), big,
            pltpu.SemaphoreType.DMA, pltpu.SemaphoreType.DMA((2,)),
        ],
        mm * 3 * width, 8 << 20, 16,
    )(meta, after(dproj, give_q), tok, dx2, norm_gains, ng2, *qkv_bufs)
    give_q, keep_q = halve(keep_q, after(got_q, ng), 1)
    z_m = to_groups(total_m(keep_m, after(got_m, give_q)))
    got_q = swap(give_q, 1)
    nb_q = n_q * 2 // 16

    def updated(z, n, first, extra):
        return call(
            functools.partial(pieces_body, first, len(z)),
            [((2 * n + extra, 128), bf16)],
            [SM, SM] + [VM] * (len(z) + 1), [pltpu.VMEM((n, 128), f32)], 1 << 20, 4 << 20, 20,
        )(owners, slot, *z, held_state)[0]

    def everywhere(piece, *first):
        x, y = swap(piece, 0), swap(piece, 1)
        return both_cores([piece, x, y, swap(after(x, *first), 1)])

    part_q = total_q(keep_q, got_q, ng)
    z_q = to_groups(part_q)
    z_m[0] = after(z_m[0], part_q[0])
    fresh_m = updated(z_m, n_m, nb_q, 0)
    m_x, m_y = swap(fresh_m, 0), swap(fresh_m, 1)
    z_q[0] = after(z_q[0], m_x, m_y)
    fresh_q = updated(z_q, n_q, 0, n_q + 2 * n_ng)
    q_x, q_y = swap(fresh_q, 0), swap(fresh_q, 1)
    m_bufs = both_cores([fresh_m, m_x, m_y, swap(after(m_x, fresh_q), 1)])
    part_shape = (4, capacity, 2, 8, 128)
    new_out, new_in, new_down, later = call(
        functools.partial(place_body, nb_q),
        [(w_out.shape, bf16), (w_in.shape, bf16), (w_down.shape, bf16), (part_shape, f32)],
        [SM, SM] + [HB] * 8,
        [
            pltpu.VMEM((8, 2 * n_m, 128), bf16), pltpu.VMEM((8, n_m, 128), f32), pltpu.VMEM(part_shape, f32),
            pltpu.SemaphoreType.DMA,
        ],
        1 << 20, 4 << 20, 16, (VM, VM, VM, HB),
    )(meta, held, *m_bufs)
    q_z = swap(after(q_x, q_y, m_bufs[3]), 1)
    q_bufs = [fresh_q, q_x, q_y, q_z]
    q_bufs += [swap_core(b) for b in q_bufs[:3]] + [swap_core(after(q_z, new_down))]
    state_shape = (capacity, block_rows, 128)
    norm_shape = (4, width)
    n_held = fresh_q.shape[0]
    (first_new, second_new, master_new, new_qkv, norm_first_new, norm_second_new, norm_new) = call(
        owner_body,
        [(state_shape, f32)] * 3 + [(w_qkv.shape, bf16)] + [(norm_shape, f32)] * 3,
        [SM] * 3 + [HB] * 4 + [VM] * 4 + [HB] * 8,
        [
            pltpu.VMEM((8, n_held, 128), bf16), pltpu.VMEM((8, n_q, 128), f32), pltpu.VMEM(part_shape, f32),
            pltpu.VMEM((capacity * block_rows, 128), f32), pltpu.VMEM((w_qkv.size // 128, 128), f32),
            pltpu.VMEM((n_ng, 128), f32),
            pltpu.VMEM(state_shape, f32), pltpu.VMEM(state_shape, f32), pltpu.VMEM(state_shape, f32),
            pltpu.SemaphoreType.DMA, pltpu.SemaphoreType.DMA,
        ],
        1 << 20, 8 << 20, 24,
    )(
        meta, counts, held, later, master, first_moment, second_moment,
        norm_gains, norm_biases, norm_first, norm_second, *q_bufs,
    )
    return (
        outputs[None], tokens_grad[None], first_new, second_new, master_new,
        new_qkv, new_out, new_in, new_down, norm_first_new, norm_second_new, norm_new,
    )


def solution(mesh):
    sharded = P("dp", "mp", None)
    return jax.shard_map(
        per_device,
        mesh=mesh,
        in_specs=(
            sharded, sharded, P("dp"), P(), P(None, "mp"), P("mp", None), P(None, "mp"), P("mp", None),
            sharded, sharded, sharded, P(), P(), P(), P(),
        ),
        out_specs=(
            sharded, sharded, sharded, sharded, sharded,
            P(None, "mp"), P("mp", None), P(None, "mp"), P("mp", None), P(), P(), P(),
        ),
        check_vma=False,
    )
```

```python
import functools

import jax
import jax.numpy as jnp
from jax import lax
from jax.experimental import pallas as pl
from jax.experimental.pallas import tpu as pltpu
from jax.sharding import PartitionSpec as P

HEAD = 64
BAND = 30
STEP = 10
HALO = 64
EDGE = 32
QB = 64
WIN = 128
PAIR = 128
COST = 1
STATE = 144

learn_rate = 0.1
norm_rate = 0.3
decay_rate = 0.1
beta_one = 0.9
beta_two = 0.95
adam_epsilon = 1e-08
norm_epsilon = 1e-05
GELU_C = 0.7978845608028654
GELU_A = 0.044715

f32 = jnp.float32
bf16 = jnp.bfloat16

VM = pl.BlockSpec(memory_space=pltpu.VMEM)
HB = pl.BlockSpec(memory_space=pltpu.HBM)
SM = pl.BlockSpec(memory_space=pltpu.SMEM)


def call(body, outs, in_specs, scratch, flops, moved, vmem=48, out_specs=None):
    specs = out_specs or tuple(VM for _ in outs)
    run = pl.pallas_call(
        body,
        out_shape=tuple(
            pltpu.HBM(s, d) if spec is HB else jax.ShapeDtypeStruct(s, d) for (s, d), spec in zip(outs, specs)
        ),
        in_specs=in_specs,
        out_specs=specs,
        scratch_shapes=scratch,
        compiler_params=pltpu.CompilerParams(vmem_limit_bytes=vmem << 20),
        cost_estimate=pl.CostEstimate(flops=flops // COST, bytes_accessed=moved // COST, transcendentals=0),
    )

    def fixed(*args):
        return run(
            *[
                pltpu.with_memory_space_constraint(x, pltpu.HBM) if spec is HB else x
                for x, spec in zip(args, in_specs)
            ]
        )

    return fixed


def load(pairs, sem):
    copies = [pltpu.make_async_copy(a, b, sem) for a, b in pairs]
    for c in copies:
        c.start()
    return copies


def dot(a, b):
    return jnp.dot(a, b, preferred_element_type=f32)


def turned(a):
    return a.astype(f32).T.astype(bf16)


def dot_nt(a, b):
    return dot(a, turned(b))


def dot_tn(a, b):
    return lax.dot_general(a, b, (((0,), (0,)), ((), ())), preferred_element_type=f32)


def normalize(x):
    mean = jnp.mean(x, axis=-1, keepdims=True)
    cen = x - mean
    var = jnp.mean(cen * cen, axis=-1, keepdims=True)
    rstd = lax.rsqrt(var + norm_epsilon)
    return cen * rstd, rstd


def same_head(n=PAIR):
    r = lax.broadcasted_iota(jnp.int32, (n, n), 0)
    c = lax.broadcasted_iota(jnp.int32, (n, n), 1)
    return (r < HEAD) == (c < HEAD)


def pack_state(s1, s2, z):
    both = jnp.where(same_head(), s1, pltpu.roll(s2, HEAD, 1))
    hi = z.astype(bf16).astype(f32)
    row = lax.broadcasted_iota(jnp.int32, (16, PAIR), 0)
    tail = jnp.where(row == 0, hi, jnp.where(row == 1, z - hi, 0.0))
    return both.astype(bf16), tail.astype(bf16)


def unpack_state(refs, g):
    tot = refs[0][g].astype(f32)
    for r in refs[1:]:
        tot = tot + r[g].astype(f32)
    both = tot[:PAIR]
    diag = same_head()
    s1 = jnp.where(diag, both, 0.0)
    s2 = jnp.where(diag, pltpu.roll(both, HEAD, 1), 0.0)
    z = tot[PAIR : PAIR + 1] + tot[PAIR + 1 : PAIR + 2]
    return s1, s2, z


def split_dot(a, ones):
    hi, lo = two(a)
    return dot(hi, ones) + dot(lo, ones)


def two(a):
    hi = a.astype(bf16)
    return hi, (a - hi.astype(f32)).astype(bf16)


def phi(v):
    low = jnp.exp(jnp.minimum(v, 0.0))
    return jnp.where(v > 0, v + 1.0, low), jnp.where(v > 0, 1.0, low)


def band_parts():
    c = lax.broadcasted_iota(jnp.int32, (WIN, 2 * QB), 0)
    r = lax.broadcasted_iota(jnp.int32, (WIN, 2 * QB), 1) % QB
    off = r + EDGE - c
    return (jnp.abs(off) <= BAND), off == 0, c


def stacked(rows):
    lane = lax.broadcasted_iota(jnp.int32, (1, PAIR), 1)
    first = (lane < HEAD).astype(f32).astype(bf16)
    second = (lane >= HEAD).astype(f32).astype(bf16)
    return jnp.concatenate([rows * first, rows * second], axis=0)


def unstack(both):
    lane = lax.broadcasted_iota(jnp.int32, (QB, PAIR), 1)
    return jnp.where(lane < HEAD, both[:QB], both[QB:])


def softmax_of(raw, mask):
    scores = jnp.where(mask, raw * 0.125, -1e30)
    ex = jnp.exp(scores - jnp.max(scores, axis=0, keepdims=True))
    return ex * (1.0 / jnp.sum(ex, axis=0, keepdims=True))


def piece_at(meta, r, bits, other):
    b0, b1 = (meta[6], meta[7]) if other else (meta[4], meta[5])
    core = 1 - meta[2] if other else meta[2]
    if bits == 1:
        return core * 2 + (b0 ^ r)
    return core * 4 + (b0 ^ (r & 1)) * 2 + (b1 ^ (r >> 1))


def fetch_pieces(meta, bufs, lo, rows, weight, sem):
    n = len(bufs) // 2
    copies = []
    for k, buf in enumerate(bufs):
        p = piece_at(meta, k % n, n // 2, k >= n)
        at = pl.ds(pl.multiple_of(p * rows, rows), rows)
        for m in range(buf.shape[0]):
            src = buf.at[m, pl.ds(lo, rows), :]
            copies.append(pltpu.make_async_copy(src, weight.at[meta[3] ^ m, at, :], sem))
    for c in copies:
        c.start()
    return copies


def norm_body(tok, left, right, gains, biases, a1e_h, a1e_o, sem):
    rows = tok.shape[0]
    gain, bias = gains[0:1, :], biases[0:1, :]

    def ln(x):
        return (normalize(x.astype(f32))[0] * gain + bias).astype(bf16)

    a1e_o[0:HALO, :] = ln(left[...])
    a1e_o[HALO + rows :, :] = ln(right[...])

    def chunk(i, _):
        at = pl.ds(pl.multiple_of(i * 128, 128), 128)
        a1e_o[pl.ds(pl.multiple_of(i * 128 + HALO, 64), 128), :] = ln(tok[at, :])
        return 0

    lax.fori_loop(0, rows // 128, chunk, 0)
    out = pltpu.make_async_copy(a1e_o, a1e_h, sem)
    out.start()
    out.wait()


def qkv_body(meta, a1e_h, *refs):
    bufs, (qkv_h, st_o, w, qkv_o, a1e, sem, out_sem) = refs[:4], refs[4:]
    pull = pltpu.make_async_copy(a1e_h, a1e, out_sem)
    pull.start()
    ext = a1e.shape[0]
    rows = ext - 2 * HALO
    groups = bufs[0].shape[0]
    for c in fetch_pieces(meta, bufs, 0, bufs[0].shape[1], w, sem):
        c.wait()
    pull.wait()
    length, base = meta[0], meta[1]
    pos = base + lax.broadcasted_iota(jnp.int32, (rows, 1), 0)
    valid = (pos < length).astype(f32)
    gs = range(groups)
    for g in gs:
        qkv_o[g] = dot(a1e[...], w[g]).astype(bf16)
    own_rows = slice(HALO, HALO + rows)
    out = pltpu.make_async_copy(qkv_o, qkv_h, out_sem)
    out.start()
    parts = []
    for g in gs:
        keys = qkv_o[g, own_rows, PAIR : 2 * PAIR].astype(f32)
        feat = phi(keys)[0] * valid
        parts.append((jnp.sum(feat, axis=0, keepdims=True), two(feat), two(jnp.tanh(keys) * valid)))
    for g in gs:
        z, (fhi, flo), (thi, tlo) = parts[g]
        vals = qkv_o[g, own_rows, 2 * PAIR :]
        s1 = dot_tn(fhi, vals) + dot_tn(flo, vals)
        s2 = dot_tn(thi, vals) + dot_tn(tlo, vals)
        st_o[g, :PAIR, :], st_o[g, PAIR:, :] = pack_state(s1, s2, z)
    out.wait()


def near_body(meta, qkv_h, near_h, qkv, near_o, sem):
    pull = pltpu.make_async_copy(qkv_h, qkv, sem)
    pull.start()
    groups = qkv.shape[0]
    rows = near_o.shape[0]
    length, base = meta[0], meta[1]
    band, diag, lane = band_parts()
    pull.wait()

    def block(b, _):
        at = b * QB
        kpos = base + at - EDGE + lane
        mask = band & (((kpos >= 0) & (kpos < length)) | diag)
        q_at = pl.ds(pl.multiple_of(at + HALO, QB), QB)
        w_at = pl.ds(pl.multiple_of(at + HALO - EDGE, EDGE), WIN)
        gs = range(groups)
        sc = [dot_nt(qkv[g, w_at, PAIR : 2 * PAIR], stacked(qkv[g, q_at, 0:PAIR])) for g in gs]
        p = [softmax_of(sc[g], mask).astype(bf16) for g in gs]
        res = [dot_tn(p[g], qkv[g, w_at, 2 * PAIR :]) for g in gs]
        for g in gs:
            near_o[pl.ds(pl.multiple_of(at, QB), QB), g * PAIR : (g + 1) * PAIR] = unstack(res[g])
        return 0

    lax.fori_loop(0, rows // QB, block, 0, unroll=4)
    out = pltpu.make_async_copy(near_o, near_h, sem)
    out.start()
    out.wait()


def put_halves(core, keep, give, g, lo, grad):
    n, width = grad.shape
    tiles = grad.reshape(n // 16, 2, 8, width)
    even, odd = tiles[:, 0].reshape(n // 2, width), tiles[:, 1].reshape(n // 2, width)
    first = jnp.full(even.shape, core, jnp.int32) == 0
    at = slice(lo, lo + n // 2)
    keep[g, at, :] = jnp.where(first, even, odd).astype(keep.dtype)
    give[g, at, :] = jnp.where(first, odd, even).astype(give.dtype)


def main_body(meta, near_h, qkv_h, h0, h1, h2, h3, tok_h, cot_h, gains, biases, *refs):
    bufs, refs = refs[:8], refs[8:]
    out_h, dst_o, far_o, dx2_h, dctx_h, dqf_h, ng_o, wout_h, keep_h, give_h = refs[:10]
    refs = refs[10:]
    do_o, dctx_o, wout_o, near, tok, cot, st = refs[:7]
    refs = (None,) * 5 + refs
    w_in, w_down, x2, xhat, rs, u, dh, acc, da2, far1, inv, dnum, phq, thq = refs[12:26]
    ctx_o, a2_o, dm_o, hid_o, du_o, out_o, keep, give, query, sem, out_sem = refs[26:]
    rows, width = tok.shape
    groups, hw = hid_o.shape[0], hid_o.shape[2]
    s0, s1, s2, s3 = [st.at[k] for k in range(4)]
    moved = load([(near_h, near), (tok_h, tok), (cot_h, cot)] + [(h, st.at[k]) for k, h in enumerate((h0, h1, h2, h3))], sem.at[4])
    pr = hw // 8
    orow = bufs[0].shape[1] - 2 * pr
    core = meta[2]
    sent = []

    def send(src, dst):
        sent.append(pltpu.make_async_copy(src, dst, out_sem))
        sent[-1].start()

    length, base = meta[0], meta[1]
    pull = pltpu.make_async_copy(qkv_h.at[:, pl.ds(HALO, rows), pl.ds(0, PAIR)], query, sem.at[3])
    pull.start()
    copies = fetch_pieces(meta, bufs, 2 * pr, orow, wout_o, sem.at[0])
    later = fetch_pieces(meta, bufs, 0, pr, w_in, sem.at[1])
    last = fetch_pieces(meta, bufs, pr, pr, w_down, sem.at[2])
    rlen = 1.0 / length.astype(f32)
    gain, bias = gains[1:2, :], biases[1:2, :]
    ones = same_head().astype(f32).astype(bf16)
    gs = range(groups)
    cols = [slice(g * PAIR, (g + 1) * PAIR) for g in gs]
    for c in moved:
        c.wait()
    states = [unpack_state((s0, s1, s2, s3), g) for g in gs]
    s1b, s2b = [two(st[0]) for st in states], [two(st[1]) for st in states]
    cr = 128

    def far_chunk(i, _):
        at = pl.ds(pl.multiple_of(i * cr, cr), cr)
        q = [query[g, at, :].astype(f32) for g in gs]
        ph = [phi(q[g])[0] for g in gs]
        ph2 = [two(ph[g]) for g in gs]
        th2 = [two(jnp.tanh(q[g])) for g in gs]
        den = [split_dot(ph[g] * states[g][2], ones) for g in gs]
        num = [dot(ph2[g][0], s1b[g][0]) + dot(ph2[g][0], s1b[g][1]) + dot(ph2[g][1], s1b[g][0]) for g in gs]
        sec = [dot(th2[g][0], s2b[g][0]) + dot(th2[g][0], s2b[g][1]) + dot(th2[g][1], s2b[g][0]) for g in gs]
        for g in gs:
            phq[at, cols[g]] = ph2[g][0]
            thq[at, cols[g]] = th2[g][0]
        rec = [1.0 / den[g] for g in gs]
        for g in gs:
            part = num[g] * rec[g]
            inv[at, cols[g]] = rec[g]
            far1[at, cols[g]] = part
            ctx_o[at, cols[g]] = (near[at, cols[g]] + (part + sec[g] * rlen)).astype(bf16)
        pos = base + i * cr + lax.broadcasted_iota(jnp.int32, (cr, 1), 0)
        dm_o[at, :] = (cot[at, :].astype(f32) * (pos < length).astype(f32)).astype(bf16)
        return 0

    pull.wait()
    lax.fori_loop(0, rows // cr, far_chunk, 0)
    for c in copies:
        c.wait()
    wout = wout_o[...].reshape(width, width)
    x2[...] = dot(ctx_o[...], wout)

    def norm_chunk(i, _):
        at = pl.ds(pl.multiple_of(i * 128, 128), 128)
        val = x2[at, :] + tok[at, :].astype(f32)
        x2[at, :] = val
        xh, rstd = normalize(val)
        xhat[at, :] = xh
        rs[at, :] = jnp.broadcast_to(rstd, (128, 128))
        a2_o[at, :] = (xh * gain + bias).astype(bf16)
        return 0

    lax.fori_loop(0, rows // 128, norm_chunk, 0)
    for c in later + last:
        c.wait()
    for g in gs:
        u[g] = dot(a2_o[...], w_in[g])
        dh[g] = dot_nt(dm_o[...], w_down[g])

    def act(i, _):
        at = pl.ds(pl.multiple_of(i * 16, 16), 16)
        for g in gs:
            v = u[g, at, :]
            sq = v * v
            half = 0.5 + 0.5 * jnp.tanh(v * (GELU_C + GELU_C * GELU_A * sq))
            hid = v * half
            hid_o[g, at, :] = hid.astype(bf16)
            slope = half + (hid * (1.0 - half)) * (2.0 * GELU_C + 6.0 * GELU_C * GELU_A * sq)
            du_o[g, at, :] = (dh[g, at, :] * slope).astype(bf16)
        return 0

    lax.fori_loop(0, rows // 16, act, 0)
    acc[...] = sum(dot(hid_o[g], w_down[g]) for g in gs)
    da2[...] = sum(dot_nt(du_o[g], w_in[g]) for g in gs)

    def back_chunk(i, carry):
        dg, db = carry
        at = pl.ds(pl.multiple_of(i * 128, 128), 128)
        out_o[at, :] = (x2[at, :] + acc[at, :]).astype(bf16)
        xh = xhat[at, :]
        rstd = rs[at, 0:1]
        d = da2[at, :]
        dg = dg + jnp.sum(d * xh, axis=0, keepdims=True)
        db = db + jnp.sum(d, axis=0, keepdims=True)
        e = d * gain
        m1 = jnp.mean(e, axis=-1, keepdims=True)
        m2 = jnp.mean(e * xh, axis=-1, keepdims=True)
        dx = dm_o[at, :].astype(f32) + rstd * (e - m1 - xh * m2)
        acc[at, :] = dx
        do_o[at, :] = dx.astype(bf16)
        return dg, db

    zero = jnp.zeros((1, width), f32)
    dg, db = lax.fori_loop(0, rows // 128, back_chunk, (zero, zero))
    even = jnp.full((EDGE, width), meta[3] & 1, jnp.int32) == 0
    head, tail = do_o[0:EDGE, :].astype(f32), do_o[rows - EDGE :, :].astype(f32)
    near_edge, far_edge = jnp.where(even, tail, head).astype(bf16), jnp.where(even, head, tail).astype(bf16)
    for g in gs:
        dst_o[g, STATE:, :] = near_edge[:, cols[g]]
        far_o[g, STATE:, :] = far_edge[:, cols[g]]
    send(out_o, out_h)
    send(wout_o, wout_h)
    send(acc, dx2_h)
    ng_o[0:1, :] = dg
    ng_o[1:2, :] = db
    dctx_o[...] = dot_nt(do_o[...], wout).astype(bf16)
    send(dctx_o, dctx_h)

    def far_back(i, carry):
        at = pl.ds(pl.multiple_of(i * cr, cr), cr)
        dc = [dctx_o[at, cols[g]] for g in gs]
        dcf = [dc[g].astype(f32) for g in gs]
        rec = [inv[at, cols[g]] for g in gs]
        dn = [(dcf[g] * rec[g]).astype(bf16) for g in gs]
        dots = [split_dot(dcf[g] * far1[at, cols[g]], ones) for g in gs]
        dph = [dot_nt(dn[g], s1b[g][0]) for g in gs]
        dth = [dot_nt(dc[g], s2b[g][0]) for g in gs]
        out = []
        for g in gs:
            dnum[at, cols[g]] = dn[g]
            dden = -dots[g] * rec[g]
            out.append(carry[g] + jnp.sum(phq[at, cols[g]].astype(f32) * dden, axis=0, keepdims=True))
            slope = phi(query[g, at, :].astype(f32))[1]
            th = thq[at, cols[g]].astype(f32)
            da2[at, cols[g]] = (dph[g] + dden * states[g][2]) * slope + dth[g] * rlen * (1.0 - th * th)
        return tuple(out)

    none = jnp.zeros((1, PAIR), f32)
    dz = lax.fori_loop(0, rows // cr, far_back, (none,) * groups)
    for g in gs:
        d1 = dot_tn(phq[:, cols[g]], dnum[:, cols[g]])
        d2 = dot_tn(thq[:, cols[g]], dctx_o[:, cols[g]]) * rlen
        both, low = pack_state(d1, d2, dz[g])
        for ref in (dst_o, far_o):
            ref[g, :PAIR, :] = both
            ref[g, PAIR:STATE, :] = low
    send(da2, dqf_h)
    n_out = ctx_o.shape[1] // groups

    def finish(g, lo, n, grad):
        put_halves(core, keep, give, g, lo, grad)
        part = pl.ds(lo, n)
        send(keep.at[g, part, :], keep_h.at[g, part, :])
        send(give.at[g, part, :], give_h.at[g, part, :])

    for g in gs:
        finish(g, n_out // 2, width // 2, dot_tn(a2_o[...], du_o[g]))
    for g in gs:
        finish(g, 0, n_out // 2, dot_tn(ctx_o[:, g * n_out : (g + 1) * n_out], do_o[...]))
    for g in gs:
        finish(g, n_out // 2 + width // 2, hw // 2, dot_tn(hid_o[g], dm_o[...]))
    for c in sent:
        c.wait()


def near_back_body(
    meta, qkv_h, dctx_h, one, three, wout_h, dqf_h, dq_o, dk_o, dv_o, dce, dqe, dke, dve, wout, dqf, qkv, sem,
):
    pull = pltpu.make_async_copy(qkv_h, qkv, sem.at[2])
    pull.start()
    groups = qkv.shape[0]
    rows, width = dctx_h.shape
    third = pltpu.make_async_copy(dctx_h, dce.at[pl.ds(EDGE, rows), :], sem.at[3])
    third.start()
    length, base = meta[0], meta[1]
    band, diag, lane = band_parts()
    first = pltpu.make_async_copy(wout_h, wout, sem.at[0])
    first.start()
    second = pltpu.make_async_copy(dqf_h, dqf, sem.at[1])
    second.start()
    first.wait()
    w = wout[...].reshape(width, -1)
    z = meta[3]
    odd = jnp.full((EDGE, width), z & 1, jnp.int32) == 1
    side = [
        jnp.concatenate([ref[g, STATE:, :] for g in range(groups)], axis=1).astype(f32) for ref in (one, three)
    ]
    last_z = meta[17] - 1
    do_l = jnp.where(odd, side[0], side[1]) * (z > 0).astype(f32)
    do_r = jnp.where(odd, side[1], side[0]) * (z < last_z).astype(f32)
    dce[0:EDGE, :] = dot_nt(do_l.astype(bf16), w).astype(bf16)
    dce[EDGE + rows :, :] = dot_nt(do_r.astype(bf16), w).astype(bf16)
    dke[...] = jnp.zeros(dke.shape, f32)
    dve[...] = jnp.zeros(dve.shape, f32)
    pull.wait()
    third.wait()

    def block(b, _):
        at = b * QB
        kpos = base + at - HALO + lane
        mask = band & (((kpos >= 0) & (kpos < length)) | diag)
        c_at = pl.ds(pl.multiple_of(at, QB), QB)
        q_at = pl.ds(pl.multiple_of(at + EDGE, EDGE), QB)
        w_at = pl.ds(pl.multiple_of(at, QB), WIN)
        gs = range(groups)
        cols = [slice(g * PAIR, (g + 1) * PAIR) for g in gs]
        qs = [stacked(qkv[g, q_at, 0:PAIR]) for g in gs]
        cs = [stacked(dce[c_at, cols[g]]) for g in gs]
        kw = [qkv[g, w_at, PAIR : 2 * PAIR] for g in gs]
        sc = [dot_nt(kw[g], qs[g]) for g in gs]
        dp = [dot_nt(qkv[g, w_at, 2 * PAIR :], cs[g]) for g in gs]
        p = [softmax_of(sc[g], mask) for g in gs]
        row = [jnp.sum(p[g] * dp[g], axis=0, keepdims=True) for g in gs]
        ds = [(p[g] * (dp[g] - row[g])).astype(bf16) for g in gs]
        pb = [p[g].astype(bf16) for g in gs]
        for g in gs:
            dke[w_at, cols[g]] += dot(ds[g], qs[g])
            dve[w_at, cols[g]] += dot(pb[g], cs[g])
        dq = [dot_tn(ds[g], kw[g]) for g in gs]
        for g in gs:
            dqe[c_at, cols[g]] = unstack(dq[g])
        return 0

    lax.fori_loop(0, rows // QB + 1, block, 0, unroll=9)
    second.wait()
    dq_o[...] = (dqe[EDGE : EDGE + rows, :] * 0.125 + dqf[...]).astype(bf16)
    dk_o[...] = dke[HALO : HALO + rows, :] * 0.125
    dv_o[...] = dve[HALO : HALO + rows, :]


def proj_body(
    meta, qkv_h, dq, dkn, dvn, s0, s1, s2, s3, a1e_h, dproj_h, keep_o, give_o, dproj, flat, pseudo, qkv, a1e, sem, in_sem,
):
    rows = dq.shape[0]
    other = pltpu.make_async_copy(a1e_h.at[pl.ds(HALO, rows), :], a1e, in_sem.at[1])
    other.start()
    pull = pltpu.make_async_copy(qkv_h, qkv, in_sem.at[0])
    pull.start()
    groups = qkv.shape[0]
    rows, width = dq.shape
    length, base, core = meta[0], meta[1], meta[2]
    cr = 128
    gs = range(groups)
    cols = [slice(g * PAIR, (g + 1) * PAIR) for g in gs]
    states = [unpack_state((s0, s1, s2, s3), g) for g in gs]
    s1b, s2b = [st[0].astype(bf16) for st in states], [st[1].astype(bf16) for st in states]

    def far_chunk(i, _):
        at = pl.ds(pl.multiple_of(i * cr, cr), cr)
        e_at = pl.ds(pl.multiple_of(i * cr + HALO, HALO), cr)
        pos = base + i * cr + lax.broadcasted_iota(jnp.int32, (cr, 1), 0)
        valid = (pos < length).astype(f32)
        k = [qkv[g, e_at, PAIR : 2 * PAIR].astype(f32) for g in gs]
        v = [qkv[g, e_at, 2 * PAIR :] for g in gs]
        feat = [phi(k[g]) for g in gs]
        th = [jnp.tanh(k[g]) for g in gs]
        vd1 = [dot_nt(v[g], s1b[g]) for g in gs]
        vd2 = [dot_nt(v[g], s2b[g]) for g in gs]
        dv = [
            dot((feat[g][0] * valid).astype(bf16), s1b[g]) + dot((th[g] * valid).astype(bf16), s2b[g]) for g in gs
        ]
        for g in gs:
            dk = (vd1[g] + states[g][2]) * feat[g][1] + vd2[g] * (1.0 - th[g] * th[g])
            dproj[g, at, 0:PAIR] = dq[at, cols[g]]
            dproj[g, at, PAIR : 2 * PAIR] = (dkn[at, cols[g]] + dk * valid).astype(bf16)
            dproj[g, at, 2 * PAIR :] = (dvn[at, cols[g]] + dv[g]).astype(bf16)
        return 0

    pull.wait()
    lax.fori_loop(0, rows // cr, far_chunk, 0)
    out = pltpu.make_async_copy(dproj, dproj_h, sem)
    out.start()
    other.wait()
    n_flat = 3 * width
    for g in gs:
        grad = dot_tn(a1e[...], dproj[g])
        for part in range(3):
            flat[pl.ds(part, width, stride=3), :] = grad[:, part * PAIR : (part + 1) * PAIR]
        for j in range(4):
            pseudo[:, j * 128 : (j + 1) * 128] = flat[pl.ds(j, n_flat // 4, stride=4), :]
        put_halves(core, keep_o, give_o, g, 0, pseudo[...])
    out.wait()


def last_body(meta, dproj_h, tok, dx2_h, gains, ng2, *refs):
    bufs, (tg_o, ng_o, da1, ngs, wqkv, dproj, dx2, sem, sems) = refs[:4], refs[4:]
    groups = dproj.shape[0]
    rows, width = tok.shape
    gain = gains[0:1, :]
    copies = fetch_pieces(meta, bufs, 0, bufs[0].shape[1], wqkv, sem)
    copies.append(pltpu.make_async_copy(dproj_h, dproj, sems.at[0]))
    copies[-1].start()
    late = pltpu.make_async_copy(dx2_h, dx2, sems.at[1])
    late.start()
    for c in copies:
        c.wait()
    da1[...] = sum(dot_nt(dproj[g], wqkv[g]) for g in range(groups))

    late.wait()

    def back_chunk(i, carry):
        dg, db = carry
        at = pl.ds(pl.multiple_of(i * 64, 64), 64)
        xh, rstd = normalize(tok[at, :].astype(f32))
        d = da1[at, :]
        dg = dg + jnp.sum(d * xh, axis=0, keepdims=True)
        db = db + jnp.sum(d, axis=0, keepdims=True)
        e = d * gain
        m1 = jnp.mean(e, axis=-1, keepdims=True)
        m2 = jnp.mean(e * xh, axis=-1, keepdims=True)
        tg_o[at, :] = dx2[at, :] + rstd * (e - m1 - xh * m2)
        return dg, db

    zero = jnp.zeros((1, width), f32)
    dg, db = lax.fori_loop(0, rows // 64, back_chunk, (zero, zero))
    for k, val in enumerate((dg, db, ng2[0:1, :], ng2[1:2, :])):
        for j in range(width // 128):
            at = k * (width // 128) + j
            ngs[at : at + 1, :] = val[:, j * 128 : (j + 1) * 128]
    ng_o[...] = ngs[...]


def halve_body(bit, own, got, give_o, keep_o):
    groups, _, n = give_o.shape
    out = pl.ds(pl.multiple_of((1 - bit[0]) * n, 128), n)
    stay = pl.ds(pl.multiple_of(bit[0] * n, 128), n)
    for g in range(groups):
        give_o[g] = (own[g, :, out].astype(f32) + got[g, :, out].astype(f32)).astype(bf16)
    for g in range(groups):
        keep_o[g] = own[g, :, stay].astype(f32) + got[g, :, stay].astype(f32)


def total_body(meta, keep, got, *outs):
    for m, out in enumerate(outs):
        g = meta[3] ^ m
        out[0] = (keep[g] + got[g].astype(f32)).astype(bf16)


def total_q_body(meta, keep, got, ng, *outs):
    n, k = keep.shape[1], ng.shape[0]
    hi, lo = two(ng[...])
    for m, out in enumerate(outs):
        g = meta[3] ^ m
        out[0, 0:n, :] = (keep[g] + got[g].astype(f32)).astype(bf16)
        out[0, n : n + k, :], out[0, n + k :, :] = hi, lo


def slices_body(where, master, first, second, out_h, held, parts, sem, out_sem):
    caps = held.shape[1] // 64
    copies = [pltpu.make_async_copy(ref, held.at[t], sem.at[t]) for t, ref in enumerate((master, first, second))]
    for c in copies:
        c.start()
    sent = []
    for t in range(3):
        copies[t].wait()
        for j in range(4):
            val = held[t, pl.ds(j, caps * 16, stride=4), :].reshape(caps, 2, 8, 128)
            for c in range(2):
                hi, lo = two(val[:, c].reshape(caps * 8, 128))
                for k, part in ((0, hi), (1, lo)) if t == 0 else ((t + 1, hi),):
                    parts[k, c, j] = part
                    for d in where[c][j]:
                        sent.append(pltpu.make_async_copy(parts.at[k, c, j], out_h.at[d, k], out_sem))
                        sent[-1].start()
    for c in sent:
        c.wait()


def widen_body(recv_h, st_o, recv, sem):
    copies = load([(recv_h.at[d], recv.at[d]) for d in range(recv.shape[0])], sem)
    for c in copies:
        c.wait()

    def owner(d, _):
        st_o[d, 0] = recv[d, 0].astype(f32) + recv[d, 1].astype(f32)
        st_o[d, 1] = recv[d, 2].astype(f32)
        st_o[d, 2] = recv[d, 3].astype(f32)
        return 0

    lax.fori_loop(0, recv.shape[0], owner, 0)


def adam(g, m_old, f_old, s_old):
    corr_one = 1.0 - beta_one**STEP
    corr_two = 1.0 - beta_two**STEP
    fn = beta_one * f_old + (1.0 - beta_one) * g
    sn = beta_two * s_old + (1.0 - beta_two) * g * g
    step = fn / corr_one / (jnp.sqrt(sn / corr_two) + adam_epsilon)
    return fn, sn, m_old - learn_rate * (step + decay_rate * m_old)


def pieces_body(first, count, owners, slots, *refs):
    parts, (st, w_o, piece_o) = refs[:count], refs[count:]
    n = piece_o.shape[0]
    src = [(r, s) for r in parts for s in range(r.shape[0])]
    piece_o[...] = sum(r[s, 0:n, :].astype(f32) for r, s in src)
    w_o[n : 2 * n, :] = piece_o[...].astype(bf16)
    if w_o.shape[0] > 2 * n:
        k = (parts[0].shape[1] - n) // 2
        w_o[2 * n : 3 * n, :] = two(piece_o[...])[1]
        norms = sum(r[s, n : n + k, :].astype(f32) + r[s, n + k :, :].astype(f32) for r, s in src)
        w_o[3 * n : 3 * n + k, :], w_o[3 * n + k :, :] = two(norms)

    def pair(i, _):
        new = []
        for k in range(2):
            b = i * 2 + k
            at = pl.ds(pl.multiple_of(slots[first + b] * 8, 8), 8)
            own = owners[first + b]
            g = piece_o[pl.ds(pl.multiple_of(b * 8, 8), 8), :]
            new.append(adam(g, st[own, 0, at, :], st[own, 1, at, :], st[own, 2, at, :])[2])
        w_o[pl.ds(pl.multiple_of(i * 16, 16), 16), :] = jnp.concatenate(new, axis=0).astype(bf16)
        return 0

    lax.fori_loop(0, n // 16, pair, 0, unroll=4)


def owner_body(
    meta, counts, blocks, later_h, master_h, first_h, second_h, gains, biases, n_first, n_second, *refs
):
    bufs, (f_o, s_o, m_o, q_o, nf_o, ns_o, np_o) = refs[:8], refs[8:15]
    held, early, parts, grad, flat, total, master, first, second, sem, sems = refs[15:]
    moved = load([(later_h, parts), (master_h, master), (first_h, first), (second_h, second)], sems)
    collect(meta, bufs, held, sem)
    for c in moved:
        c.wait()
    caps, br, _ = master.shape
    n = q_o.shape[0] * q_o.shape[1] // (128 * 64)
    k_ng = total.shape[0]
    for p in range(8):
        early[p] = held[p, n * 8 : n * 16, :].astype(f32) + held[p, n * 16 : n * 24, :].astype(f32)
    total[...] = sum(
        held[p, n * 24 : n * 24 + k_ng, :].astype(f32) + held[p, n * 24 + k_ng :, :].astype(f32) for p in range(8)
    )
    start = meta[8] * caps

    def pick(r, _):
        b = blocks[start + r]
        old = pl.ds(pl.multiple_of(jnp.minimum(b, n - 1) * 8, 8), 8)
        is_q = jnp.full((8, 128), b, jnp.int32) < n
        for p in range(8):
            parts[p % 4, r, p // 4] = jnp.where(is_q, early[p, old, :], parts[p % 4, r, p // 4])
        return 0

    lax.fori_loop(0, caps, pick, 0, unroll=2)
    for j in range(4):
        grad[pl.ds(j, caps * 16, stride=4), :] = parts[j].reshape(caps * 16, 128)

    def slot(r, _):
        g = grad[pl.ds(pl.multiple_of(r * br, br), br), :]
        m_old, f_old, s_old = master[r], first[r], second[r]
        fn, sn, mn = adam(g, m_old, f_old, s_old)
        keep = jnp.full(g.shape, counts[start + r], jnp.int32) > 0
        f_o[r] = jnp.where(keep, fn, f_old)
        s_o[r] = jnp.where(keep, sn, s_old)
        m_o[r] = jnp.where(keep, mn, m_old)
        return 0

    lax.fori_loop(0, caps, slot, 0, unroll=2)
    rows = q_o.shape[0]
    for j in range(4):
        flat[pl.ds(j, n * 16, stride=4), :] = columns(held, j, 0, n * 8)
    for part in range(3):
        q_o[:, part * 128 : (part + 1) * 128] = flat[pl.ds(part, rows, stride=3), :].astype(bf16)
    corr_one = 1.0 - beta_one**STEP
    corr_two = 1.0 - beta_two**STEP
    per = n_first.shape[1] // 128
    for k in range(4):
        old = (biases if k % 2 else gains)[k // 2 : k // 2 + 1, :]
        g = jnp.concatenate([total[k * per + j : k * per + j + 1, :] for j in range(per)], axis=1)
        fn = beta_one * n_first[k : k + 1, :] + (1.0 - beta_one) * g
        sn = beta_two * n_second[k : k + 1, :] + (1.0 - beta_two) * g * g
        nf_o[k : k + 1, :] = fn
        ns_o[k : k + 1, :] = sn
        np_o[k : k + 1, :] = old - norm_rate * (fn / corr_one / (jnp.sqrt(sn / corr_two) + adam_epsilon))


def collect(meta, bufs, held, sem):
    copies = []
    for k, buf in enumerate(bufs):
        copies.append(pltpu.make_async_copy(buf, held.at[piece_at(meta, k % 4, 2, k >= 4)], sem))
        copies[-1].start()
    for c in copies:
        c.wait()


def columns(held, j, lo, n):
    even, odd = [held[c * 4 + j, lo : lo + n, :].astype(f32).reshape(n // 8, 1, 8, 128) for c in range(2)]
    return jnp.concatenate([even, odd], axis=1).reshape(2 * n, 128)


def place_body(first, meta, blocks, *refs):
    bufs, outs, (parts_h, held, grads, parts, sem) = refs[:8], refs[8:11], refs[11:]
    collect(meta, bufs, held, sem)
    half = held.shape[1] // 2
    for p in range(8):
        grads[p] = held[p, half:, :].astype(f32)
    caps = parts.shape[1]

    def pick(r, _):
        b = jnp.maximum(blocks[meta[8] * caps + r] - first, 0)
        at = pl.ds(pl.multiple_of(b * 8, 8), 8)
        for p in range(8):
            parts[p % 4, r, p // 4] = grads[p, at, :]
        return 0

    lax.fori_loop(0, caps, pick, 0, unroll=2)
    out = pltpu.make_async_copy(parts, parts_h, sem)
    out.start()
    lo = 0
    for ref in outs:
        n = ref.shape[0] // 2
        for j in range(4):
            ref[:, j * 128 : (j + 1) * 128] = columns(held, j, lo, n).astype(bf16)
        lo += n
    out.wait()


def per_device(
    tokens, cotangent, lengths, owners, w_qkv, w_out, w_in, w_down,
    master, first_moment, second_moment, norm_gains, norm_biases, norm_first, norm_second,
):
    rows, width = tokens.shape[1], tokens.shape[2]
    groups = lax.axis_size("mp")
    ndp = lax.axis_size("dp")
    nbits = ndp.bit_length() - 1
    rest = list(range(1, nbits))
    order = (rest, rest[:2][::-1] + rest[2:][::-1])
    me, zi = lax.axis_index("dp"), lax.axis_index("mp")
    core = me & 1

    def bit_of(who, at, s):
        return (who >> jnp.where(at == 0, order[0][s], order[1][s])) & 1

    def swap(x, s):
        return lax.ppermute(x, "dp", [(i, i ^ (1 << order[i & 1][s])) for i in range(ndp)])

    def swap_core(x):
        return lax.ppermute(x, "dp", [(i, i ^ 1) for i in range(ndp)])

    def from_mp(x, step):
        return lax.ppermute(x, "mp", [(i, i + step) for i in range(groups) if 0 <= i + step < groups])

    def swap_mp(x, mask):
        return lax.ppermute(x, "mp", [(i, i ^ mask) for i in range(groups)])

    def exchange(x, axis):
        return lax.all_to_all(x, axis, 0, 0, tiled=True)

    def all_states(x):
        return [x] + [swap_mp(x, m) for m in range(1, groups)]

    q0, q1 = bit_of(me, core, 0), bit_of(me, core, 1)
    o0, o1 = bit_of(me, 1 - core, 0), bit_of(me, 1 - core, 1)
    length = lengths[0]
    base = zi * rows
    ids = [length, base, core, zi, q0, q1, o0, o1, me]
    ids += [
        me - (me & 7) + c + ((j >> 1) << order[c][0]) + ((j & 1) << order[c][1]) for c in range(2) for j in range(4)
    ]
    ids.append(jnp.int32(groups))
    meta = jnp.stack(ids).astype(jnp.int32)

    def after(x, *deps):
        return lax.optimization_barrier((x,) + deps)[0]

    def over_mp(piece):
        return [piece] + [swap_mp(piece, m) for m in range(1, groups)]

    def both_cores(bufs):
        return bufs + [swap_core(b) for b in bufs]

    def part_of(w, n, at):
        return lax.dynamic_slice_in_dim(w, at * (w.shape[0] // n), w.shape[0] // n, 0)

    mine = core * 4 + q0 * 2 + q1
    tok, cot = tokens[0], cotangent[0]
    ext = rows + 2 * HALO
    mm = 2 * rows * width
    qkv_z = over_mp(part_of(w_qkv, 4, core * 2 + q0))
    left, right = from_mp(tok[rows - HALO :], 1), from_mp(tok[:HALO], -1)
    ffn_piece = jnp.concatenate([part_of(w, 8, mine) for w in (w_in, w_down, w_out)], axis=0)
    qkv_z = after(jnp.stack(qkv_z), left, right, ffn_piece)
    ffn_z = jnp.stack(over_mp(after(ffn_piece, qkv_z)))
    qkv_bufs = [qkv_z, swap(qkv_z, 0)]
    capacity, block_rows = master.shape[0], master.shape[1]
    where = [[[] for _ in range(4)] for _ in range(2)]
    for d in range(ndp):
        b = order[d & 1]
        where[d & 1][2 * ((d >> b[0]) & 1) + ((d >> b[1]) & 1)].append(d)
    flat_state = [x.reshape(capacity * block_rows, 128) for x in (master, first_moment, second_moment)]
    [parts] = call(
        functools.partial(slices_body, where), [((ndp, 4, capacity * 8, 128), bf16)], [HB] * 3,
        [
            pltpu.VMEM((3, capacity * block_rows, 128), f32), pltpu.VMEM((4, 2, 4, capacity * 8, 128), bf16),
            pltpu.SemaphoreType.DMA((3,)), pltpu.SemaphoreType.DMA,
        ],
        1 << 20, 4 << 20, 12, (HB,),
    )(*flat_state)
    [a1e] = call(norm_body, [((ext, width), bf16)], [VM] * 5,
        [pltpu.VMEM((ext, width), bf16), pltpu.SemaphoreType.DMA], 4 * mm, 1 << 20, 16, (HB,),
    )(
        after(tok, parts), left, right, norm_gains, norm_biases
    )
    qkv_bufs = both_cores([qkv_bufs[0], after(qkv_bufs[1], a1e)])
    all_qkv = pltpu.VMEM((groups, ext, 3 * PAIR), bf16)
    proj_w = pltpu.VMEM((groups, width, 3 * PAIR), bf16)
    qkv, state = call(
        qkv_body,
        [((groups, ext, 3 * PAIR), bf16), ((groups, STATE, PAIR), bf16)],
        [SM] + [HB] * 5,
        [proj_w, all_qkv, pltpu.VMEM((ext, width), bf16), pltpu.SemaphoreType.DMA, pltpu.SemaphoreType.DMA],
        2 * ext * width * 3 * width, 6 << 20, 20, (HB, VM),
    )(meta, after(a1e, ffn_z), *qkv_bufs)
    states = all_states(state)
    ffn_z = after(ffn_z, a1e, qkv_bufs[1])
    ffn_x, ffn_y = swap(ffn_z, 0), swap(ffn_z, 1)
    ffn_oth = [swap_core(b) for b in (ffn_z, ffn_x, ffn_y)]
    ffn_bufs = [ffn_z, ffn_x, ffn_y, swap(after(ffn_x, ffn_y, *states), 1)]
    blocks = owners.shape[0]
    earlier = jnp.arange(blocks)[None, :] < jnp.arange(blocks)[:, None]
    alike = owners[None, :] == owners[:, None]
    slot = jnp.sum((earlier & alike).astype(jnp.int32), axis=1)
    slot_rows = owners * capacity + slot
    hit = slot_rows[None, :] == jnp.arange(ndp * capacity, dtype=jnp.int32)[:, None]
    held = jnp.sum(jnp.where(hit, jnp.arange(blocks, dtype=jnp.int32)[None, :], 0), axis=1)
    counts = jnp.sum(hit.astype(jnp.int32), axis=1)
    [near] = call(
        near_body, [((rows, width), f32)], [SM, HB],
        [all_qkv, pltpu.VMEM((rows, width), f32), pltpu.SemaphoreType.DMA], mm * 1024, 12 << 20, 16, (HB,),
    )(meta, after(qkv, slot, held, counts, *ffn_oth, *states))
    ffn_bufs = ffn_bufs + ffn_oth + [swap_core(ffn_bufs[3])]
    held_state = exchange(after(parts, ffn_bufs[3], near), "dp")

    hid_w = w_in.shape[1]
    big = pltpu.VMEM((rows, width), f32)
    low = pltpu.VMEM((rows, width), bf16)
    n_m = (w_out.shape[0] + w_in.shape[0] + w_down.shape[0]) // 2
    wide = pltpu.VMEM((groups, rows, hid_w), f32)
    half = pltpu.VMEM((groups, n_m, width), bf16)
    four = pltpu.VMEM((groups, rows, hid_w), bf16)
    (outputs, dstate, dfar, dx2, dctx, dqf, ng2, wout, grad_m, give_m) = call(
        main_body,
        [
            ((rows, width), bf16), ((groups, STATE + EDGE, PAIR), bf16), ((groups, STATE + EDGE, PAIR), bf16),
            ((rows, width), f32), ((rows, width), bf16), ((rows, width), f32), ((2, width), f32),
            ((groups,) + w_out.shape, bf16), ((groups, n_m, width), bf16), ((groups, n_m, width), bf16),
        ],
        [SM] + [HB] * 8 + [VM] * 2 + [HB] * 8,
        [
            low, low, pltpu.VMEM((groups,) + w_out.shape, bf16), big, low, low,
            pltpu.VMEM((4, groups, STATE, PAIR), bf16),
            pltpu.VMEM((groups, width, hid_w), bf16), pltpu.VMEM((groups, hid_w, width), bf16),
            big, big, pltpu.VMEM((rows, 128), f32), wide, wide, big, big, big, big,
            low, low, low, low, low, low, four, four, low, half, half,
            pltpu.VMEM((groups, rows, PAIR), bf16), pltpu.SemaphoreType.DMA((5,)), pltpu.SemaphoreType.DMA,
        ],
        mm * hid_w * groups * 6, 24 << 20, 44,
        (HB, VM, VM, HB, HB, HB, VM, HB, HB, HB),
    )(meta, near, qkv, *states, tok, cot, norm_gains, norm_biases, *ffn_bufs)

    dstate, dfar, give_m, _ = lax.optimization_barrier((dstate, dfar, give_m, held_state))
    dstates = [dstate, swap_mp(dstate, 1), swap_mp(dstate, 2), swap_mp(dfar, 3)]

    [slot_state] = call(
        widen_body, [((ndp, 3, capacity * 8, 128), f32)], [HB],
        [pltpu.VMEM((ndp, 4, capacity * 8, 128), bf16), pltpu.SemaphoreType.DMA], 1 << 20, 4 << 20, 12,
    )(held_state)

    bits = [bit_of(me, core, s).astype(jnp.int32).reshape(1) for s in range(2)]

    def halve(own, got, s):
        shape = own.shape[:-1] + (own.shape[-1] // 2,)
        return call(
            halve_body, [(shape, bf16), (shape, f32)], [SM, VM, VM], [], 1 << 20, 4 << 20, 16,
        )(bits[s], own, got)

    def rest_of(keep, got):
        for s in range(2, nbits - 1):
            tot = (keep + got.astype(f32)).astype(bf16)
            keep, got = tot.astype(f32), swap(tot, s)
        return keep, got

    def to_groups(part):
        return [part[0]] + [swap_mp(part[m], m) for m in range(1, groups)]

    def total_m(keep, got):
        return call(
            total_body, [((1,) + keep.shape[1:], bf16)] * groups, [SM, VM, VM], [], 1 << 20, 2 << 20, 12,
        )(meta, *rest_of(keep, got))

    def total_q(keep, got, extra):
        keep, got = rest_of(keep, got)
        for s in range(2, nbits - 1):
            extra = extra + swap(extra, s)
        shape = (1, keep.shape[1] + 2 * extra.shape[0], keep.shape[2])
        return call(
            total_q_body, [(shape, bf16)] * groups, [SM, VM, VM, VM], [], 1 << 20, 2 << 20, 12,
        )(meta, keep, got, extra)

    give_m, keep_m = halve(grad_m, after(swap_core(give_m), dstates[1], dstates[3], slot_state), 0)
    got_m = swap(give_m, 0)
    dq, dkn, dvn = call(
        near_back_body,
        [((rows, width), bf16), ((rows, width), f32), ((rows, width), f32)],
        [SM, HB, HB] + [VM] * 2 + [HB] * 2,
        [
            pltpu.VMEM((rows + 2 * EDGE, width), bf16), pltpu.VMEM((rows + 2 * EDGE, width), f32),
            pltpu.VMEM((ext, width), f32), pltpu.VMEM((ext, width), f32),
            pltpu.VMEM(wout.shape, bf16), big, all_qkv, pltpu.SemaphoreType.DMA((4,)),
        ],
        mm * 2048, 24 << 20, 20,
    )(meta, qkv, after(dctx, give_m), dstates[1], dstates[3], wout, dqf)
    n_q = w_qkv.size // width // 2
    n_ng = 4 * width // 128
    dproj, grad_q, give_q = call(
        proj_body,
        [((groups, rows, 3 * PAIR), bf16), ((groups, n_q, width), f32), ((groups, n_q, width), f32)],
        [SM, HB] + [VM] * 7 + [HB],
        [
            pltpu.VMEM((groups, rows, 3 * PAIR), bf16), pltpu.VMEM((3 * width, 128), f32),
            pltpu.VMEM((2 * n_q, width), f32), all_qkv, low,
            pltpu.SemaphoreType.DMA, pltpu.SemaphoreType.DMA((2,)),
        ],
        mm * 3 * width, 24 << 20, 20, (HB, VM, VM),
    )(meta, qkv, dq, dkn, dvn, *dstates, a1e)
    got_q = swap_core(after(give_q, got_m))
    give_m, keep_m = halve(keep_m, after(got_m, give_q), 1)
    got_m = swap(give_m, 1)
    give_q, keep_q = halve(grad_q, got_q, 0)
    got_q = swap(give_q, 0)
    tokens_grad, ng = call(
        last_body,
        [((rows, width), f32), ((n_ng, 128), f32)],
        [SM, HB, VM, HB, VM, VM] + [HB] * 4,
        [
            big, pltpu.VMEM((n_ng, 128), f32), proj_w, pltpu.VMEM((groups, rows, 3 * PAIR), bf16), big,
            pltpu.SemaphoreType.DMA, pltpu.SemaphoreType.DMA((2,)),
        ],
        mm * 3 * width, 8 << 20, 16,
    )(meta, after(dproj, give_q), tok, dx2, norm_gains, ng2, *qkv_bufs)
    give_q, keep_q = halve(keep_q, after(got_q, ng), 1)
    z_m = to_groups(total_m(keep_m, after(got_m, give_q)))
    got_q = swap(give_q, 1)
    nb_q = n_q * 2 // 16

    def updated(z, n, first, extra):
        return call(
            functools.partial(pieces_body, first, len(z)),
            [((2 * n + extra, 128), bf16)],
            [SM, SM] + [VM] * (len(z) + 1), [pltpu.VMEM((n, 128), f32)], 1 << 20, 4 << 20, 20,
        )(owners, slot, *z, slot_state)[0]

    def everywhere(piece, *first):
        x, y = swap(piece, 0), swap(piece, 1)
        return both_cores([piece, x, y, swap(after(x, *first), 1)])

    part_q = total_q(keep_q, got_q, ng)
    z_q = to_groups(part_q)
    z_m[0] = after(z_m[0], part_q[0])
    fresh_m = updated(z_m, n_m, nb_q, 0)
    m_x, m_y = swap(fresh_m, 0), swap(fresh_m, 1)
    z_q[0] = after(z_q[0], m_x, m_y)
    fresh_q = updated(z_q, n_q, 0, n_q + 2 * n_ng)
    q_x, q_y = swap(fresh_q, 0), swap(fresh_q, 1)
    m_bufs = both_cores([fresh_m, m_x, m_y, swap(after(m_x, fresh_q), 1)])
    part_shape = (4, capacity, 2, 8, 128)
    new_out, new_in, new_down, later = call(
        functools.partial(place_body, nb_q),
        [(w_out.shape, bf16), (w_in.shape, bf16), (w_down.shape, bf16), (part_shape, f32)],
        [SM, SM] + [HB] * 8,
        [
            pltpu.VMEM((8, 2 * n_m, 128), bf16), pltpu.VMEM((8, n_m, 128), f32), pltpu.VMEM(part_shape, f32),
            pltpu.SemaphoreType.DMA,
        ],
        1 << 20, 4 << 20, 16, (VM, VM, VM, HB),
    )(meta, held, *m_bufs)
    q_z = swap(after(q_x, q_y, m_bufs[3]), 1)
    q_bufs = [fresh_q, q_x, q_y, q_z]
    q_bufs += [swap_core(b) for b in q_bufs[:3]] + [swap_core(after(q_z, new_down))]
    state_shape = (capacity, block_rows, 128)
    norm_shape = (4, width)
    n_held = fresh_q.shape[0]
    (first_new, second_new, master_new, new_qkv, norm_first_new, norm_second_new, norm_new) = call(
        owner_body,
        [(state_shape, f32)] * 3 + [(w_qkv.shape, bf16)] + [(norm_shape, f32)] * 3,
        [SM] * 3 + [HB] * 4 + [VM] * 4 + [HB] * 8,
        [
            pltpu.VMEM((8, n_held, 128), bf16), pltpu.VMEM((8, n_q, 128), f32), pltpu.VMEM(part_shape, f32),
            pltpu.VMEM((capacity * block_rows, 128), f32), pltpu.VMEM((w_qkv.size // 128, 128), f32),
            pltpu.VMEM((n_ng, 128), f32),
            pltpu.VMEM(state_shape, f32), pltpu.VMEM(state_shape, f32), pltpu.VMEM(state_shape, f32),
            pltpu.SemaphoreType.DMA, pltpu.SemaphoreType.DMA,
        ],
        1 << 20, 8 << 20, 24,
    )(
        meta, counts, held, later, master, first_moment, second_moment,
        norm_gains, norm_biases, norm_first, norm_second, *q_bufs,
    )
    return (
        outputs[None], tokens_grad[None], first_new, second_new, master_new,
        new_qkv, new_out, new_in, new_down, norm_first_new, norm_second_new, norm_new,
    )


def solution(mesh):
    sharded = P("dp", "mp", None)
    return jax.shard_map(
        per_device,
        mesh=mesh,
        in_specs=(
            sharded, sharded, P("dp"), P(), P(None, "mp"), P("mp", None), P(None, "mp"), P("mp", None),
            sharded, sharded, sharded, P(), P(), P(), P(),
        ),
        out_specs=(
            sharded, sharded, sharded, sharded, sharded,
            P(None, "mp"), P("mp", None), P(None, "mp"), P("mp", None), P(), P(), P(),
        ),
        check_vma=False,
    )
```

```python
import functools

import jax
import jax.numpy as jnp
from jax import lax
from jax.experimental import pallas as pl
from jax.experimental.pallas import tpu as pltpu
from jax.sharding import PartitionSpec as P

HEAD = 64
BAND = 30
STEP = 10
HALO = 64
EDGE = 32
QB = 64
WIN = 128
PAIR = 128
COST = 1
STATE = 144

learn_rate = 0.1
norm_rate = 0.3
decay_rate = 0.1
beta_one = 0.9
beta_two = 0.95
adam_epsilon = 1e-08
norm_epsilon = 1e-05
GELU_C = 0.7978845608028654
GELU_A = 0.044715

f32 = jnp.float32
bf16 = jnp.bfloat16

VM = pl.BlockSpec(memory_space=pltpu.VMEM)
HB = pl.BlockSpec(memory_space=pltpu.HBM)
SM = pl.BlockSpec(memory_space=pltpu.SMEM)
ANY = pl.BlockSpec(memory_space=pl.ANY)


def call(body, outs, in_specs, scratch, flops, moved, vmem=48, out_specs=None):
    specs = out_specs or tuple(VM for _ in outs)
    run = pl.pallas_call(
        body,
        out_shape=tuple(
            pltpu.HBM(s, d) if spec is HB else jax.ShapeDtypeStruct(s, d) for (s, d), spec in zip(outs, specs)
        ),
        in_specs=in_specs,
        out_specs=specs,
        scratch_shapes=scratch,
        compiler_params=pltpu.CompilerParams(vmem_limit_bytes=vmem << 20),
        cost_estimate=pl.CostEstimate(flops=flops // COST, bytes_accessed=moved // COST, transcendentals=0),
    )

    def fixed(*args):
        return run(
            *[
                pltpu.with_memory_space_constraint(x, pltpu.HBM) if spec is HB else x
                for x, spec in zip(args, in_specs)
            ]
        )

    return fixed


def load(pairs, sem):
    copies = [pltpu.make_async_copy(a, b, sem) for a, b in pairs]
    for c in copies:
        c.start()
    return copies


def dot(a, b):
    return jnp.dot(a, b, preferred_element_type=f32)


def turned(a):
    return a.astype(f32).T.astype(bf16)


def dot_nt(a, b):
    return dot(a, turned(b))


def dot_tn(a, b):
    return lax.dot_general(a, b, (((0,), (0,)), ((), ())), preferred_element_type=f32)


def normalize(x):
    mean = jnp.mean(x, axis=-1, keepdims=True)
    cen = x - mean
    var = jnp.mean(cen * cen, axis=-1, keepdims=True)
    rstd = lax.rsqrt(var + norm_epsilon)
    return cen * rstd, rstd


def same_head(n=PAIR):
    r = lax.broadcasted_iota(jnp.int32, (n, n), 0)
    c = lax.broadcasted_iota(jnp.int32, (n, n), 1)
    return (r < HEAD) == (c < HEAD)


def pack_state(s1, s2, z):
    both = jnp.where(same_head(), s1, pltpu.roll(s2, HEAD, 1))
    hi = z.astype(bf16).astype(f32)
    row = lax.broadcasted_iota(jnp.int32, (16, PAIR), 0)
    tail = jnp.where(row == 0, hi, jnp.where(row == 1, z - hi, 0.0))
    return both.astype(bf16), tail.astype(bf16)


def unpack_state(refs, g):
    tot = refs[0][g].astype(f32)
    for r in refs[1:]:
        tot = tot + r[g].astype(f32)
    both = tot[:PAIR]
    diag = same_head()
    s1 = jnp.where(diag, both, 0.0)
    s2 = jnp.where(diag, pltpu.roll(both, HEAD, 1), 0.0)
    z = tot[PAIR : PAIR + 1] + tot[PAIR + 1 : PAIR + 2]
    return s1, s2, z


def split_dot(a, ones):
    hi, lo = two(a)
    return dot(hi, ones) + dot(lo, ones)


def two(a):
    hi = a.astype(bf16)
    return hi, (a - hi.astype(f32)).astype(bf16)


def phi(v):
    low = jnp.exp(jnp.minimum(v, 0.0))
    return jnp.where(v > 0, v + 1.0, low), jnp.where(v > 0, 1.0, low)


def band_parts():
    c = lax.broadcasted_iota(jnp.int32, (WIN, 2 * QB), 0)
    r = lax.broadcasted_iota(jnp.int32, (WIN, 2 * QB), 1) % QB
    off = r + EDGE - c
    return (jnp.abs(off) <= BAND), off == 0, c


def stacked(rows):
    lane = lax.broadcasted_iota(jnp.int32, (1, PAIR), 1)
    first = (lane < HEAD).astype(f32).astype(bf16)
    second = (lane >= HEAD).astype(f32).astype(bf16)
    return jnp.concatenate([rows * first, rows * second], axis=0)


def unstack(both):
    lane = lax.broadcasted_iota(jnp.int32, (QB, PAIR), 1)
    return jnp.where(lane < HEAD, both[:QB], both[QB:])


def softmax_of(raw, mask):
    scores = jnp.where(mask, raw * 0.125, -1e30)
    ex = jnp.exp(scores - jnp.max(scores, axis=0, keepdims=True))
    return ex * (1.0 / jnp.sum(ex, axis=0, keepdims=True))


def piece_at(meta, r, bits, other):
    b0, b1 = (meta[6], meta[7]) if other else (meta[4], meta[5])
    core = 1 - meta[2] if other else meta[2]
    if bits == 1:
        return core * 2 + (b0 ^ r)
    return core * 4 + (b0 ^ (r & 1)) * 2 + (b1 ^ (r >> 1))


def fetch_pieces(meta, bufs, lo, rows, weight, sem):
    n = len(bufs) // 2
    copies = []
    for k, buf in enumerate(bufs):
        p = piece_at(meta, k % n, n // 2, k >= n)
        at = pl.ds(pl.multiple_of(p * rows, rows), rows)
        for m in range(buf.shape[0]):
            src = buf.at[m, pl.ds(lo, rows), :]
            copies.append(pltpu.make_async_copy(src, weight.at[meta[3] ^ m, at, :], sem))
    for c in copies:
        c.start()
    return copies


def norm_body(tok, left, right, gains, biases, a1e_h, a1e_o, sem):
    rows = tok.shape[0]
    gain, bias = gains[0:1, :], biases[0:1, :]

    def ln(x):
        return (normalize(x.astype(f32))[0] * gain + bias).astype(bf16)

    a1e_o[0:HALO, :] = ln(left[...])
    a1e_o[HALO + rows :, :] = ln(right[...])

    def chunk(i, _):
        at = pl.ds(pl.multiple_of(i * 128, 128), 128)
        a1e_o[pl.ds(pl.multiple_of(i * 128 + HALO, 64), 128), :] = ln(tok[at, :])
        return 0

    lax.fori_loop(0, rows // 128, chunk, 0)
    out = pltpu.make_async_copy(a1e_o, a1e_h, sem)
    out.start()
    out.wait()


def qkv_body(meta, a1e_h, *refs):
    bufs, (qkv_h, st_o, w, qkv_o, a1e, sem, out_sem) = refs[:4], refs[4:]
    pull = pltpu.make_async_copy(a1e_h, a1e, out_sem)
    pull.start()
    ext = a1e.shape[0]
    rows = ext - 2 * HALO
    groups = bufs[0].shape[0]
    for c in fetch_pieces(meta, bufs, 0, bufs[0].shape[1], w, sem):
        c.wait()
    pull.wait()
    length, base = meta[0], meta[1]
    pos = base + lax.broadcasted_iota(jnp.int32, (rows, 1), 0)
    valid = (pos < length).astype(f32)
    gs = range(groups)
    for g in gs:
        qkv_o[g] = dot(a1e[...], w[g]).astype(bf16)
    own_rows = slice(HALO, HALO + rows)
    out = pltpu.make_async_copy(qkv_o, qkv_h, out_sem)
    out.start()
    parts = []
    for g in gs:
        keys = qkv_o[g, own_rows, PAIR : 2 * PAIR].astype(f32)
        feat = phi(keys)[0] * valid
        parts.append((jnp.sum(feat, axis=0, keepdims=True), two(feat), two(jnp.tanh(keys) * valid)))
    for g in gs:
        z, (fhi, flo), (thi, tlo) = parts[g]
        vals = qkv_o[g, own_rows, 2 * PAIR :]
        s1 = dot_tn(fhi, vals) + dot_tn(flo, vals)
        s2 = dot_tn(thi, vals) + dot_tn(tlo, vals)
        st_o[g, :PAIR, :], st_o[g, PAIR:, :] = pack_state(s1, s2, z)
    out.wait()


def near_body(meta, qkv_h, near_h, qkv, near_o, sem):
    pull = pltpu.make_async_copy(qkv_h, qkv, sem)
    pull.start()
    groups = qkv.shape[0]
    rows = near_o.shape[0]
    length, base = meta[0], meta[1]
    band, diag, lane = band_parts()
    pull.wait()

    def block(b, _):
        at = b * QB
        kpos = base + at - EDGE + lane
        mask = band & (((kpos >= 0) & (kpos < length)) | diag)
        q_at = pl.ds(pl.multiple_of(at + HALO, QB), QB)
        w_at = pl.ds(pl.multiple_of(at + HALO - EDGE, EDGE), WIN)
        gs = range(groups)
        sc = [dot_nt(qkv[g, w_at, PAIR : 2 * PAIR], stacked(qkv[g, q_at, 0:PAIR])) for g in gs]
        p = [softmax_of(sc[g], mask).astype(bf16) for g in gs]
        res = [dot_tn(p[g], qkv[g, w_at, 2 * PAIR :]) for g in gs]
        for g in gs:
            near_o[pl.ds(pl.multiple_of(at, QB), QB), g * PAIR : (g + 1) * PAIR] = unstack(res[g])
        return 0

    lax.fori_loop(0, rows // QB, block, 0, unroll=4)
    out = pltpu.make_async_copy(near_o, near_h, sem)
    out.start()
    out.wait()


def put_halves(core, keep, give, g, lo, grad):
    n, width = grad.shape
    tiles = grad.reshape(n // 16, 2, 8, width)
    even, odd = tiles[:, 0].reshape(n // 2, width), tiles[:, 1].reshape(n // 2, width)
    first = jnp.full(even.shape, core, jnp.int32) == 0
    at = slice(lo, lo + n // 2)
    keep[g, at, :] = jnp.where(first, even, odd).astype(keep.dtype)
    give[g, at, :] = jnp.where(first, odd, even).astype(give.dtype)


def main_body(meta, near_h, qkv_h, h0, h1, h2, h3, tok_h, cot_h, gains, biases, *refs):
    bufs, refs = refs[:8], refs[8:]
    out_h, dst_o, far_o, dx2_h, dctx_h, dqf_h, ng_o, wout_h, keep_h, give_h = refs[:10]
    refs = refs[10:]
    do_o, dctx_o, wout_o, near, tok, cot, st = refs[:7]
    refs = (None,) * 5 + refs
    w_in, w_down, x2, xhat, rs, u, dh, acc, da2, far1, inv, dnum, phq, thq = refs[12:26]
    ctx_o, a2_o, dm_o, hid_o, du_o, out_o, keep, give, query, sem, out_sem = refs[26:]
    rows, width = tok.shape
    groups, hw = hid_o.shape[0], hid_o.shape[2]
    s0, s1, s2, s3 = [st.at[k] for k in range(4)]
    moved = load([(near_h, near), (tok_h, tok), (cot_h, cot)] + [(h, st.at[k]) for k, h in enumerate((h0, h1, h2, h3))], sem.at[4])
    pr = hw // 8
    orow = bufs[0].shape[1] - 2 * pr
    core = meta[2]
    sent = []

    def send(src, dst):
        sent.append(pltpu.make_async_copy(src, dst, out_sem))
        sent[-1].start()

    length, base = meta[0], meta[1]
    pull = pltpu.make_async_copy(qkv_h.at[:, pl.ds(HALO, rows), pl.ds(0, PAIR)], query, sem.at[3])
    pull.start()
    copies = fetch_pieces(meta, bufs, 2 * pr, orow, wout_o, sem.at[0])
    later = fetch_pieces(meta, bufs, 0, pr, w_in, sem.at[1])
    last = fetch_pieces(meta, bufs, pr, pr, w_down, sem.at[2])
    rlen = 1.0 / length.astype(f32)
    gain, bias = gains[1:2, :], biases[1:2, :]
    ones = same_head().astype(f32).astype(bf16)
    gs = range(groups)
    cols = [slice(g * PAIR, (g + 1) * PAIR) for g in gs]
    for c in moved:
        c.wait()
    states = [unpack_state((s0, s1, s2, s3), g) for g in gs]
    s1b, s2b = [two(st[0]) for st in states], [two(st[1]) for st in states]
    cr = 128

    def far_chunk(i, _):
        at = pl.ds(pl.multiple_of(i * cr, cr), cr)
        q = [query[g, at, :].astype(f32) for g in gs]
        ph = [phi(q[g])[0] for g in gs]
        ph2 = [two(ph[g]) for g in gs]
        th2 = [two(jnp.tanh(q[g])) for g in gs]
        den = [split_dot(ph[g] * states[g][2], ones) for g in gs]
        num = [dot(ph2[g][0], s1b[g][0]) + dot(ph2[g][0], s1b[g][1]) + dot(ph2[g][1], s1b[g][0]) for g in gs]
        sec = [dot(th2[g][0], s2b[g][0]) + dot(th2[g][0], s2b[g][1]) + dot(th2[g][1], s2b[g][0]) for g in gs]
        for g in gs:
            phq[at, cols[g]] = ph2[g][0]
            thq[at, cols[g]] = th2[g][0]
        rec = [1.0 / den[g] for g in gs]
        for g in gs:
            part = num[g] * rec[g]
            inv[at, cols[g]] = rec[g]
            far1[at, cols[g]] = part
            ctx_o[at, cols[g]] = (near[at, cols[g]] + (part + sec[g] * rlen)).astype(bf16)
        pos = base + i * cr + lax.broadcasted_iota(jnp.int32, (cr, 1), 0)
        dm_o[at, :] = (cot[at, :].astype(f32) * (pos < length).astype(f32)).astype(bf16)
        return 0

    pull.wait()
    lax.fori_loop(0, rows // cr, far_chunk, 0)
    for c in copies:
        c.wait()
    wout = wout_o[...].reshape(width, width)
    x2[...] = dot(ctx_o[...], wout)

    def norm_chunk(i, _):
        at = pl.ds(pl.multiple_of(i * 128, 128), 128)
        val = x2[at, :] + tok[at, :].astype(f32)
        x2[at, :] = val
        xh, rstd = normalize(val)
        xhat[at, :] = xh
        rs[at, :] = jnp.broadcast_to(rstd, (128, 128))
        a2_o[at, :] = (xh * gain + bias).astype(bf16)
        return 0

    lax.fori_loop(0, rows // 128, norm_chunk, 0)
    for c in later + last:
        c.wait()
    for g in gs:
        u[g] = dot(a2_o[...], w_in[g])
        dh[g] = dot_nt(dm_o[...], w_down[g])

    def act(i, _):
        at = pl.ds(pl.multiple_of(i * 16, 16), 16)
        for g in gs:
            v = u[g, at, :]
            sq = v * v
            half = 0.5 + 0.5 * jnp.tanh(v * (GELU_C + GELU_C * GELU_A * sq))
            hid = v * half
            hid_o[g, at, :] = hid.astype(bf16)
            slope = half + (hid * (1.0 - half)) * (2.0 * GELU_C + 6.0 * GELU_C * GELU_A * sq)
            du_o[g, at, :] = (dh[g, at, :] * slope).astype(bf16)
        return 0

    lax.fori_loop(0, rows // 16, act, 0)
    acc[...] = sum(dot(hid_o[g], w_down[g]) for g in gs)
    da2[...] = sum(dot_nt(du_o[g], w_in[g]) for g in gs)

    def back_chunk(i, carry):
        dg, db = carry
        at = pl.ds(pl.multiple_of(i * 128, 128), 128)
        out_o[at, :] = (x2[at, :] + acc[at, :]).astype(bf16)
        xh = xhat[at, :]
        rstd = rs[at, 0:1]
        d = da2[at, :]
        dg = dg + jnp.sum(d * xh, axis=0, keepdims=True)
        db = db + jnp.sum(d, axis=0, keepdims=True)
        e = d * gain
        m1 = jnp.mean(e, axis=-1, keepdims=True)
        m2 = jnp.mean(e * xh, axis=-1, keepdims=True)
        dx = dm_o[at, :].astype(f32) + rstd * (e - m1 - xh * m2)
        acc[at, :] = dx
        do_o[at, :] = dx.astype(bf16)
        return dg, db

    zero = jnp.zeros((1, width), f32)
    dg, db = lax.fori_loop(0, rows // 128, back_chunk, (zero, zero))
    even = jnp.full((EDGE, width), meta[3] & 1, jnp.int32) == 0
    head, tail = do_o[0:EDGE, :].astype(f32), do_o[rows - EDGE :, :].astype(f32)
    near_edge, far_edge = jnp.where(even, tail, head).astype(bf16), jnp.where(even, head, tail).astype(bf16)
    for g in gs:
        dst_o[g, STATE:, :] = near_edge[:, cols[g]]
        far_o[g, STATE:, :] = far_edge[:, cols[g]]
    send(out_o, out_h)
    send(wout_o, wout_h)
    send(acc, dx2_h)
    ng_o[0:1, :] = dg
    ng_o[1:2, :] = db
    dctx_o[...] = dot_nt(do_o[...], wout).astype(bf16)
    send(dctx_o, dctx_h)

    def far_back(i, carry):
        at = pl.ds(pl.multiple_of(i * cr, cr), cr)
        dc = [dctx_o[at, cols[g]] for g in gs]
        dcf = [dc[g].astype(f32) for g in gs]
        rec = [inv[at, cols[g]] for g in gs]
        dn = [(dcf[g] * rec[g]).astype(bf16) for g in gs]
        dots = [split_dot(dcf[g] * far1[at, cols[g]], ones) for g in gs]
        dph = [dot_nt(dn[g], s1b[g][0]) for g in gs]
        dth = [dot_nt(dc[g], s2b[g][0]) for g in gs]
        out = []
        for g in gs:
            dnum[at, cols[g]] = dn[g]
            dden = -dots[g] * rec[g]
            out.append(carry[g] + jnp.sum(phq[at, cols[g]].astype(f32) * dden, axis=0, keepdims=True))
            slope = phi(query[g, at, :].astype(f32))[1]
            th = thq[at, cols[g]].astype(f32)
            da2[at, cols[g]] = (dph[g] + dden * states[g][2]) * slope + dth[g] * rlen * (1.0 - th * th)
        return tuple(out)

    none = jnp.zeros((1, PAIR), f32)
    dz = lax.fori_loop(0, rows // cr, far_back, (none,) * groups)
    for g in gs:
        d1 = dot_tn(phq[:, cols[g]], dnum[:, cols[g]])
        d2 = dot_tn(thq[:, cols[g]], dctx_o[:, cols[g]]) * rlen
        both, low = pack_state(d1, d2, dz[g])
        for ref in (dst_o, far_o):
            ref[g, :PAIR, :] = both
            ref[g, PAIR:STATE, :] = low
    send(da2, dqf_h)
    n_out = ctx_o.shape[1] // groups

    def finish(g, lo, n, grad):
        put_halves(core, keep, give, g, lo, grad)
        part = pl.ds(lo, n)
        send(keep.at[g, part, :], keep_h.at[g, part, :])
        send(give.at[g, part, :], give_h.at[g, part, :])

    for g in gs:
        finish(g, n_out // 2, width // 2, dot_tn(a2_o[...], du_o[g]))
    for g in gs:
        finish(g, 0, n_out // 2, dot_tn(ctx_o[:, g * n_out : (g + 1) * n_out], do_o[...]))
    for g in gs:
        finish(g, n_out // 2 + width // 2, hw // 2, dot_tn(hid_o[g], dm_o[...]))
    for c in sent:
        c.wait()


def near_back_body(
    meta, qkv_h, dctx_h, one, three, wout_h, dqf_h, dq_o, dk_o, dv_o, dce, dqe, dke, dve, wout, dqf, qkv, sem,
):
    pull = pltpu.make_async_copy(qkv_h, qkv, sem.at[2])
    pull.start()
    groups = qkv.shape[0]
    rows, width = dctx_h.shape
    third = pltpu.make_async_copy(dctx_h, dce.at[pl.ds(EDGE, rows), :], sem.at[3])
    third.start()
    length, base = meta[0], meta[1]
    band, diag, lane = band_parts()
    first = pltpu.make_async_copy(wout_h, wout, sem.at[0])
    first.start()
    second = pltpu.make_async_copy(dqf_h, dqf, sem.at[1])
    second.start()
    first.wait()
    w = wout[...].reshape(width, -1)
    z = meta[3]
    odd = jnp.full((EDGE, width), z & 1, jnp.int32) == 1
    side = [
        jnp.concatenate([ref[g, STATE:, :] for g in range(groups)], axis=1).astype(f32) for ref in (one, three)
    ]
    last_z = meta[17] - 1
    do_l = jnp.where(odd, side[0], side[1]) * (z > 0).astype(f32)
    do_r = jnp.where(odd, side[1], side[0]) * (z < last_z).astype(f32)
    dce[0:EDGE, :] = dot_nt(do_l.astype(bf16), w).astype(bf16)
    dce[EDGE + rows :, :] = dot_nt(do_r.astype(bf16), w).astype(bf16)
    dke[...] = jnp.zeros(dke.shape, f32)
    dve[...] = jnp.zeros(dve.shape, f32)
    pull.wait()
    third.wait()

    def block(b, _):
        at = b * QB
        kpos = base + at - HALO + lane
        mask = band & (((kpos >= 0) & (kpos < length)) | diag)
        c_at = pl.ds(pl.multiple_of(at, QB), QB)
        q_at = pl.ds(pl.multiple_of(at + EDGE, EDGE), QB)
        w_at = pl.ds(pl.multiple_of(at, QB), WIN)
        gs = range(groups)
        cols = [slice(g * PAIR, (g + 1) * PAIR) for g in gs]
        qs = [stacked(qkv[g, q_at, 0:PAIR]) for g in gs]
        cs = [stacked(dce[c_at, cols[g]]) for g in gs]
        kw = [qkv[g, w_at, PAIR : 2 * PAIR] for g in gs]
        sc = [dot_nt(kw[g], qs[g]) for g in gs]
        dp = [dot_nt(qkv[g, w_at, 2 * PAIR :], cs[g]) for g in gs]
        p = [softmax_of(sc[g], mask) for g in gs]
        row = [jnp.sum(p[g] * dp[g], axis=0, keepdims=True) for g in gs]
        ds = [(p[g] * (dp[g] - row[g])).astype(bf16) for g in gs]
        pb = [p[g].astype(bf16) for g in gs]
        for g in gs:
            dke[w_at, cols[g]] += dot(ds[g], qs[g])
            dve[w_at, cols[g]] += dot(pb[g], cs[g])
        dq = [dot_tn(ds[g], kw[g]) for g in gs]
        for g in gs:
            dqe[c_at, cols[g]] = unstack(dq[g])
        return 0

    lax.fori_loop(0, rows // QB + 1, block, 0, unroll=9)
    second.wait()
    dq_o[...] = (dqe[EDGE : EDGE + rows, :] * 0.125 + dqf[...]).astype(bf16)
    dk_o[...] = dke[HALO : HALO + rows, :] * 0.125
    dv_o[...] = dve[HALO : HALO + rows, :]


def proj_body(
    meta, qkv_h, dq, dkn, dvn, s0, s1, s2, s3, a1e_h, dproj_h, keep_o, give_o, dproj, flat, pseudo, qkv, a1e, sem, in_sem,
):
    rows = dq.shape[0]
    other = pltpu.make_async_copy(a1e_h.at[pl.ds(HALO, rows), :], a1e, in_sem.at[1])
    other.start()
    pull = pltpu.make_async_copy(qkv_h, qkv, in_sem.at[0])
    pull.start()
    groups = qkv.shape[0]
    rows, width = dq.shape
    length, base, core = meta[0], meta[1], meta[2]
    cr = 128
    gs = range(groups)
    cols = [slice(g * PAIR, (g + 1) * PAIR) for g in gs]
    states = [unpack_state((s0, s1, s2, s3), g) for g in gs]
    s1b, s2b = [st[0].astype(bf16) for st in states], [st[1].astype(bf16) for st in states]

    def far_chunk(i, _):
        at = pl.ds(pl.multiple_of(i * cr, cr), cr)
        e_at = pl.ds(pl.multiple_of(i * cr + HALO, HALO), cr)
        pos = base + i * cr + lax.broadcasted_iota(jnp.int32, (cr, 1), 0)
        valid = (pos < length).astype(f32)
        k = [qkv[g, e_at, PAIR : 2 * PAIR].astype(f32) for g in gs]
        v = [qkv[g, e_at, 2 * PAIR :] for g in gs]
        feat = [phi(k[g]) for g in gs]
        th = [jnp.tanh(k[g]) for g in gs]
        vd1 = [dot_nt(v[g], s1b[g]) for g in gs]
        vd2 = [dot_nt(v[g], s2b[g]) for g in gs]
        dv = [
            dot((feat[g][0] * valid).astype(bf16), s1b[g]) + dot((th[g] * valid).astype(bf16), s2b[g]) for g in gs
        ]
        for g in gs:
            dk = (vd1[g] + states[g][2]) * feat[g][1] + vd2[g] * (1.0 - th[g] * th[g])
            dproj[g, at, 0:PAIR] = dq[at, cols[g]]
            dproj[g, at, PAIR : 2 * PAIR] = (dkn[at, cols[g]] + dk * valid).astype(bf16)
            dproj[g, at, 2 * PAIR :] = (dvn[at, cols[g]] + dv[g]).astype(bf16)
        return 0

    pull.wait()
    lax.fori_loop(0, rows // cr, far_chunk, 0)
    out = pltpu.make_async_copy(dproj, dproj_h, sem)
    out.start()
    other.wait()
    n_flat = 3 * width
    for g in gs:
        grad = dot_tn(a1e[...], dproj[g])
        for part in range(3):
            flat[pl.ds(part, width, stride=3), :] = grad[:, part * PAIR : (part + 1) * PAIR]
        for j in range(4):
            pseudo[:, j * 128 : (j + 1) * 128] = flat[pl.ds(j, n_flat // 4, stride=4), :]
        put_halves(core, keep_o, give_o, g, 0, pseudo[...])
    out.wait()


def last_body(meta, dproj_h, tok, dx2_h, gains, ng2, *refs):
    bufs, (tg_o, ng_o, da1, ngs, wqkv, dproj, dx2, sem, sems) = refs[:4], refs[4:]
    groups = dproj.shape[0]
    rows, width = tok.shape
    gain = gains[0:1, :]
    copies = fetch_pieces(meta, bufs, 0, bufs[0].shape[1], wqkv, sem)
    copies.append(pltpu.make_async_copy(dproj_h, dproj, sems.at[0]))
    copies[-1].start()
    late = pltpu.make_async_copy(dx2_h, dx2, sems.at[1])
    late.start()
    for c in copies:
        c.wait()
    da1[...] = sum(dot_nt(dproj[g], wqkv[g]) for g in range(groups))

    late.wait()

    def back_chunk(i, carry):
        dg, db = carry
        at = pl.ds(pl.multiple_of(i * 64, 64), 64)
        xh, rstd = normalize(tok[at, :].astype(f32))
        d = da1[at, :]
        dg = dg + jnp.sum(d * xh, axis=0, keepdims=True)
        db = db + jnp.sum(d, axis=0, keepdims=True)
        e = d * gain
        m1 = jnp.mean(e, axis=-1, keepdims=True)
        m2 = jnp.mean(e * xh, axis=-1, keepdims=True)
        tg_o[at, :] = dx2[at, :] + rstd * (e - m1 - xh * m2)
        return dg, db

    zero = jnp.zeros((1, width), f32)
    dg, db = lax.fori_loop(0, rows // 64, back_chunk, (zero, zero))
    for k, val in enumerate((dg, db, ng2[0:1, :], ng2[1:2, :])):
        for j in range(width // 128):
            at = k * (width // 128) + j
            ngs[at : at + 1, :] = val[:, j * 128 : (j + 1) * 128]
    ng_o[...] = ngs[...]


def halve_body(bit, own, got, give_o, keep_o):
    groups, _, n = give_o.shape
    out = pl.ds(pl.multiple_of((1 - bit[0]) * n, 128), n)
    stay = pl.ds(pl.multiple_of(bit[0] * n, 128), n)
    for g in range(groups):
        give_o[g] = (own[g, :, out].astype(f32) + got[g, :, out].astype(f32)).astype(bf16)
    for g in range(groups):
        keep_o[g] = own[g, :, stay].astype(f32) + got[g, :, stay].astype(f32)


def total_body(meta, keep, got, *outs):
    for m, out in enumerate(outs):
        g = meta[3] ^ m
        out[0] = (keep[g] + got[g].astype(f32)).astype(bf16)


def total_q_body(meta, keep, got, ng, *outs):
    n, k = keep.shape[1], ng.shape[0]
    hi, lo = two(ng[...])
    for m, out in enumerate(outs):
        g = meta[3] ^ m
        out[0, 0:n, :] = (keep[g] + got[g].astype(f32)).astype(bf16)
        out[0, n : n + k, :], out[0, n + k :, :] = hi, lo


def slices_body(where, master, first, second, out_h, held, parts, sem, out_sem):
    caps = held.shape[1] // 64
    copies = [pltpu.make_async_copy(ref, held.at[t], sem.at[t]) for t, ref in enumerate((master, first, second))]
    for c in copies:
        c.start()
    sent = []
    for t in range(3):
        copies[t].wait()
        for j in range(4):
            val = held[t, pl.ds(j, caps * 16, stride=4), :].reshape(caps, 2, 8, 128)
            for c in range(2):
                hi, lo = two(val[:, c].reshape(caps * 8, 128))
                for k, part in ((0, hi), (1, lo)) if t == 0 else ((t + 1, hi),):
                    parts[k, c, j] = part
                    for d in where[c][j]:
                        sent.append(pltpu.make_async_copy(parts.at[k, c, j], out_h.at[d, k], out_sem))
                        sent[-1].start()
    for c in sent:
        c.wait()


def widen_body(recv_h, st_o, recv, sem):
    copies = load([(recv_h.at[d], recv.at[d]) for d in range(recv.shape[0])], sem)
    for c in copies:
        c.wait()

    def owner(d, _):
        st_o[d, 0] = recv[d, 0].astype(f32) + recv[d, 1].astype(f32)
        st_o[d, 1] = recv[d, 2].astype(f32)
        st_o[d, 2] = recv[d, 3].astype(f32)
        return 0

    lax.fori_loop(0, recv.shape[0], owner, 0)


def adam(g, m_old, f_old, s_old):
    corr_one = 1.0 - beta_one**STEP
    corr_two = 1.0 - beta_two**STEP
    fn = beta_one * f_old + (1.0 - beta_one) * g
    sn = beta_two * s_old + (1.0 - beta_two) * g * g
    step = fn / corr_one / (jnp.sqrt(sn / corr_two) + adam_epsilon)
    return fn, sn, m_old - learn_rate * (step + decay_rate * m_old)


def pieces_body(first, count, owners, slots, *refs):
    parts, (st, w_o, piece_o) = refs[:count], refs[count:]
    n = piece_o.shape[0]
    src = [(r, s) for r in parts for s in range(r.shape[0])]
    piece_o[...] = sum(r[s, 0:n, :].astype(f32) for r, s in src)
    w_o[n : 2 * n, :] = piece_o[...].astype(bf16)
    if w_o.shape[0] > 2 * n:
        k = (parts[0].shape[1] - n) // 2
        w_o[2 * n : 3 * n, :] = two(piece_o[...])[1]
        norms = sum(r[s, n : n + k, :].astype(f32) + r[s, n + k :, :].astype(f32) for r, s in src)
        w_o[3 * n : 3 * n + k, :], w_o[3 * n + k :, :] = two(norms)

    def pair(i, _):
        new = []
        for k in range(2):
            b = i * 2 + k
            at = pl.ds(pl.multiple_of(slots[first + b] * 8, 8), 8)
            own = owners[first + b]
            g = piece_o[pl.ds(pl.multiple_of(b * 8, 8), 8), :]
            new.append(adam(g, st[own, 0, at, :], st[own, 1, at, :], st[own, 2, at, :])[2])
        w_o[pl.ds(pl.multiple_of(i * 16, 16), 16), :] = jnp.concatenate(new, axis=0).astype(bf16)
        return 0

    lax.fori_loop(0, n // 16, pair, 0, unroll=4)


def owner_body(
    meta, counts, blocks, later_h, master_h, first_h, second_h, gains, biases, n_first, n_second, *refs
):
    bufs, (f_o, s_o, m_o, q_o, nf_o, ns_o, np_o) = refs[:8], refs[8:15]
    held, early, parts, grad, flat, total, master, first, second, sem, sems = refs[15:]
    moved = load([(later_h, parts), (master_h, master), (first_h, first), (second_h, second)], sems)
    collect(meta, bufs, held, sem)
    for c in moved:
        c.wait()
    caps, br, _ = master.shape
    n = q_o.shape[0] * q_o.shape[1] // (128 * 64)
    k_ng = total.shape[0]
    for p in range(8):
        early[p] = held[p, n * 8 : n * 16, :].astype(f32) + held[p, n * 16 : n * 24, :].astype(f32)
    total[...] = sum(
        held[p, n * 24 : n * 24 + k_ng, :].astype(f32) + held[p, n * 24 + k_ng :, :].astype(f32) for p in range(8)
    )
    start = meta[8] * caps

    def pick(r, _):
        b = blocks[start + r]
        old = pl.ds(pl.multiple_of(jnp.minimum(b, n - 1) * 8, 8), 8)
        is_q = jnp.full((8, 128), b, jnp.int32) < n
        for p in range(8):
            parts[p % 4, r, p // 4] = jnp.where(is_q, early[p, old, :], parts[p % 4, r, p // 4])
        return 0

    lax.fori_loop(0, caps, pick, 0, unroll=2)
    for j in range(4):
        grad[pl.ds(j, caps * 16, stride=4), :] = parts[j].reshape(caps * 16, 128)

    def slot(r, _):
        g = grad[pl.ds(pl.multiple_of(r * br, br), br), :]
        m_old, f_old, s_old = master[r], first[r], second[r]
        fn, sn, mn = adam(g, m_old, f_old, s_old)
        keep = jnp.full(g.shape, counts[start + r], jnp.int32) > 0
        f_o[r] = jnp.where(keep, fn, f_old)
        s_o[r] = jnp.where(keep, sn, s_old)
        m_o[r] = jnp.where(keep, mn, m_old)
        return 0

    lax.fori_loop(0, caps, slot, 0, unroll=2)
    rows = q_o.shape[0]
    for j in range(4):
        flat[pl.ds(j, n * 16, stride=4), :] = columns(held, j, 0, n * 8)
    for part in range(3):
        q_o[:, part * 128 : (part + 1) * 128] = flat[pl.ds(part, rows, stride=3), :].astype(bf16)
    corr_one = 1.0 - beta_one**STEP
    corr_two = 1.0 - beta_two**STEP
    per = n_first.shape[1] // 128
    for k in range(4):
        old = (biases if k % 2 else gains)[k // 2 : k // 2 + 1, :]
        g = jnp.concatenate([total[k * per + j : k * per + j + 1, :] for j in range(per)], axis=1)
        fn = beta_one * n_first[k : k + 1, :] + (1.0 - beta_one) * g
        sn = beta_two * n_second[k : k + 1, :] + (1.0 - beta_two) * g * g
        nf_o[k : k + 1, :] = fn
        ns_o[k : k + 1, :] = sn
        np_o[k : k + 1, :] = old - norm_rate * (fn / corr_one / (jnp.sqrt(sn / corr_two) + adam_epsilon))


def collect(meta, bufs, held, sem):
    copies = []
    for k, buf in enumerate(bufs):
        copies.append(pltpu.make_async_copy(buf, held.at[piece_at(meta, k % 4, 2, k >= 4)], sem))
        copies[-1].start()
    for c in copies:
        c.wait()


def columns(held, j, lo, n):
    even, odd = [held[c * 4 + j, lo : lo + n, :].astype(f32).reshape(n // 8, 1, 8, 128) for c in range(2)]
    return jnp.concatenate([even, odd], axis=1).reshape(2 * n, 128)


def place_body(first, meta, blocks, *refs):
    bufs, outs, (parts_h, held, grads, parts, sem) = refs[:8], refs[8:11], refs[11:]
    collect(meta, bufs, held, sem)
    half = held.shape[1] // 2
    for p in range(8):
        grads[p] = held[p, half:, :].astype(f32)
    caps = parts.shape[1]

    def pick(r, _):
        b = jnp.maximum(blocks[meta[8] * caps + r] - first, 0)
        at = pl.ds(pl.multiple_of(b * 8, 8), 8)
        for p in range(8):
            parts[p % 4, r, p // 4] = grads[p, at, :]
        return 0

    lax.fori_loop(0, caps, pick, 0, unroll=2)
    out = pltpu.make_async_copy(parts, parts_h, sem)
    out.start()
    lo = 0
    for ref in outs:
        n = ref.shape[0] // 2
        for j in range(4):
            ref[:, j * 128 : (j + 1) * 128] = columns(held, j, lo, n).astype(bf16)
        lo += n
    out.wait()


def per_device(
    tokens, cotangent, lengths, owners, w_qkv, w_out, w_in, w_down,
    master, first_moment, second_moment, norm_gains, norm_biases, norm_first, norm_second,
):
    rows, width = tokens.shape[1], tokens.shape[2]
    groups = lax.axis_size("mp")
    ndp = lax.axis_size("dp")
    nbits = ndp.bit_length() - 1
    rest = list(range(1, nbits))
    order = (rest, rest[:2][::-1] + rest[2:][::-1])
    me, zi = lax.axis_index("dp"), lax.axis_index("mp")
    core = me & 1

    def bit_of(who, at, s):
        return (who >> jnp.where(at == 0, order[0][s], order[1][s])) & 1

    def swap(x, s):
        return lax.ppermute(x, "dp", [(i, i ^ (1 << order[i & 1][s])) for i in range(ndp)])

    def swap_core(x):
        return lax.ppermute(x, "dp", [(i, i ^ 1) for i in range(ndp)])

    def from_mp(x, step):
        return lax.ppermute(x, "mp", [(i, i + step) for i in range(groups) if 0 <= i + step < groups])

    def swap_mp(x, mask):
        return lax.ppermute(x, "mp", [(i, i ^ mask) for i in range(groups)])

    def exchange(x, axis):
        return lax.all_to_all(x, axis, 0, 0, tiled=True)

    def all_states(x):
        return [x] + [swap_mp(x, m) for m in range(1, groups)]

    q0, q1 = bit_of(me, core, 0), bit_of(me, core, 1)
    o0, o1 = bit_of(me, 1 - core, 0), bit_of(me, 1 - core, 1)
    length = lengths[0]
    base = zi * rows
    ids = [length, base, core, zi, q0, q1, o0, o1, me]
    ids += [
        me - (me & 7) + c + ((j >> 1) << order[c][0]) + ((j & 1) << order[c][1]) for c in range(2) for j in range(4)
    ]
    ids.append(jnp.int32(groups))
    meta = jnp.stack(ids).astype(jnp.int32)

    def after(x, *deps):
        return lax.optimization_barrier((x,) + deps)[0]

    def over_mp(piece):
        return [piece] + [swap_mp(piece, m) for m in range(1, groups)]

    def both_cores(bufs):
        return bufs + [swap_core(b) for b in bufs]

    def part_of(w, n, at):
        return lax.dynamic_slice_in_dim(w, at * (w.shape[0] // n), w.shape[0] // n, 0)

    mine = core * 4 + q0 * 2 + q1
    tok, cot = tokens[0], cotangent[0]
    ext = rows + 2 * HALO
    mm = 2 * rows * width
    qkv_z = over_mp(part_of(w_qkv, 4, core * 2 + q0))
    left, right = from_mp(tok[rows - HALO :], 1), from_mp(tok[:HALO], -1)
    ffn_piece = jnp.concatenate([part_of(w, 8, mine) for w in (w_in, w_down, w_out)], axis=0)
    qkv_z = after(jnp.stack(qkv_z), left, right, ffn_piece)
    ffn_z = jnp.stack(over_mp(after(ffn_piece, qkv_z)))
    qkv_bufs = [qkv_z, swap(qkv_z, 0)]
    capacity, block_rows = master.shape[0], master.shape[1]
    where = [[[] for _ in range(4)] for _ in range(2)]
    for d in range(ndp):
        b = order[d & 1]
        where[d & 1][2 * ((d >> b[0]) & 1) + ((d >> b[1]) & 1)].append(d)
    flat_state = [x.reshape(capacity * block_rows, 128) for x in (master, first_moment, second_moment)]
    [parts] = call(
        functools.partial(slices_body, where), [((ndp, 4, capacity * 8, 128), bf16)], [HB] * 3,
        [
            pltpu.VMEM((3, capacity * block_rows, 128), f32), pltpu.VMEM((4, 2, 4, capacity * 8, 128), bf16),
            pltpu.SemaphoreType.DMA((3,)), pltpu.SemaphoreType.DMA,
        ],
        1 << 20, 4 << 20, 12, (HB,),
    )(*flat_state)
    [a1e] = call(norm_body, [((ext, width), bf16)], [VM] * 5,
        [pltpu.VMEM((ext, width), bf16), pltpu.SemaphoreType.DMA], 4 * mm, 1 << 20, 16, (HB,),
    )(
        after(tok, parts), left, right, norm_gains, norm_biases
    )
    qkv_bufs = both_cores([qkv_bufs[0], after(qkv_bufs[1], a1e)])
    all_qkv = pltpu.VMEM((groups, ext, 3 * PAIR), bf16)
    proj_w = pltpu.VMEM((groups, width, 3 * PAIR), bf16)
    qkv, state = call(
        qkv_body,
        [((groups, ext, 3 * PAIR), bf16), ((groups, STATE, PAIR), bf16)],
        [SM, HB] + [ANY] * 4,
        [proj_w, all_qkv, pltpu.VMEM((ext, width), bf16), pltpu.SemaphoreType.DMA, pltpu.SemaphoreType.DMA],
        2 * ext * width * 3 * width, 6 << 20, 20, (HB, VM),
    )(meta, after(a1e, ffn_z), *qkv_bufs)
    states = all_states(state)
    ffn_z = after(ffn_z, a1e, qkv_bufs[1])
    ffn_x, ffn_y = swap(ffn_z, 0), swap(ffn_z, 1)
    ffn_oth = [swap_core(b) for b in (ffn_z, ffn_x, ffn_y)]
    ffn_bufs = [ffn_z, ffn_x, ffn_y, swap(after(ffn_x, ffn_y, *states), 1)]
    blocks = owners.shape[0]
    earlier = jnp.arange(blocks)[None, :] < jnp.arange(blocks)[:, None]
    alike = owners[None, :] == owners[:, None]
    slot = jnp.sum((earlier & alike).astype(jnp.int32), axis=1)
    slot_rows = owners * capacity + slot
    hit = slot_rows[None, :] == jnp.arange(ndp * capacity, dtype=jnp.int32)[:, None]
    held = jnp.sum(jnp.where(hit, jnp.arange(blocks, dtype=jnp.int32)[None, :], 0), axis=1)
    counts = jnp.sum(hit.astype(jnp.int32), axis=1)
    [near] = call(
        near_body, [((rows, width), f32)], [SM, HB],
        [all_qkv, pltpu.VMEM((rows, width), f32), pltpu.SemaphoreType.DMA], mm * 1024, 12 << 20, 16, (HB,),
    )(meta, after(qkv, slot, held, counts, *ffn_oth, *states))
    ffn_bufs = ffn_bufs + ffn_oth + [swap_core(ffn_bufs[3])]
    held_state = exchange(after(parts, ffn_bufs[3], near), "dp")

    hid_w = w_in.shape[1]
    big = pltpu.VMEM((rows, width), f32)
    low = pltpu.VMEM((rows, width), bf16)
    n_m = (w_out.shape[0] + w_in.shape[0] + w_down.shape[0]) // 2
    wide = pltpu.VMEM((groups, rows, hid_w), f32)
    half = pltpu.VMEM((groups, n_m, width), bf16)
    four = pltpu.VMEM((groups, rows, hid_w), bf16)
    (outputs, dstate, dfar, dx2, dctx, dqf, ng2, wout, grad_m, give_m) = call(
        main_body,
        [
            ((rows, width), bf16), ((groups, STATE + EDGE, PAIR), bf16), ((groups, STATE + EDGE, PAIR), bf16),
            ((rows, width), f32), ((rows, width), bf16), ((rows, width), f32), ((2, width), f32),
            ((groups,) + w_out.shape, bf16), ((groups, n_m, width), bf16), ((groups, n_m, width), bf16),
        ],
        [SM] + [HB] * 8 + [VM] * 2 + [HB] * 7 + [ANY],
        [
            low, low, pltpu.VMEM((groups,) + w_out.shape, bf16), big, low, low,
            pltpu.VMEM((4, groups, STATE, PAIR), bf16),
            pltpu.VMEM((groups, width, hid_w), bf16), pltpu.VMEM((groups, hid_w, width), bf16),
            big, big, pltpu.VMEM((rows, 128), f32), wide, wide, big, big, big, big,
            low, low, low, low, low, low, four, four, low, half, half,
            pltpu.VMEM((groups, rows, PAIR), bf16), pltpu.SemaphoreType.DMA((5,)), pltpu.SemaphoreType.DMA,
        ],
        mm * hid_w * groups * 6, 24 << 20, 44,
        (HB, VM, VM, HB, HB, HB, VM, HB, HB, HB),
    )(meta, near, qkv, *states, tok, cot, norm_gains, norm_biases, *ffn_bufs)

    dstate, dfar, give_m, _ = lax.optimization_barrier((dstate, dfar, give_m, held_state))
    dstates = [dstate, swap_mp(dstate, 1), swap_mp(dstate, 2), swap_mp(dfar, 3)]

    [slot_state] = call(
        widen_body, [((ndp, 3, capacity * 8, 128), f32)], [HB],
        [pltpu.VMEM((ndp, 4, capacity * 8, 128), bf16), pltpu.SemaphoreType.DMA], 1 << 20, 4 << 20, 12,
    )(held_state)

    bits = [bit_of(me, core, s).astype(jnp.int32).reshape(1) for s in range(2)]

    def halve(own, got, s):
        shape = own.shape[:-1] + (own.shape[-1] // 2,)
        return call(
            halve_body, [(shape, bf16), (shape, f32)], [SM, VM, VM], [], 1 << 20, 4 << 20, 16,
        )(bits[s], own, got)

    def rest_of(keep, got):
        for s in range(2, nbits - 1):
            tot = (keep + got.astype(f32)).astype(bf16)
            keep, got = tot.astype(f32), swap(tot, s)
        return keep, got

    def to_groups(part):
        return [part[0]] + [swap_mp(part[m], m) for m in range(1, groups)]

    def total_m(keep, got):
        return call(
            total_body, [((1,) + keep.shape[1:], bf16)] * groups, [SM, VM, VM], [], 1 << 20, 2 << 20, 12,
        )(meta, *rest_of(keep, got))

    def total_q(keep, got, extra):
        keep, got = rest_of(keep, got)
        for s in range(2, nbits - 1):
            extra = extra + swap(extra, s)
        shape = (1, keep.shape[1] + 2 * extra.shape[0], keep.shape[2])
        return call(
            total_q_body, [(shape, bf16)] * groups, [SM, VM, VM, VM], [], 1 << 20, 2 << 20, 12,
        )(meta, keep, got, extra)

    give_m, keep_m = halve(grad_m, after(swap_core(give_m), dstates[1], dstates[3], slot_state), 0)
    got_m = swap(give_m, 0)
    dq, dkn, dvn = call(
        near_back_body,
        [((rows, width), bf16), ((rows, width), f32), ((rows, width), f32)],
        [SM, HB, HB] + [VM] * 2 + [HB] * 2,
        [
            pltpu.VMEM((rows + 2 * EDGE, width), bf16), pltpu.VMEM((rows + 2 * EDGE, width), f32),
            pltpu.VMEM((ext, width), f32), pltpu.VMEM((ext, width), f32),
            pltpu.VMEM(wout.shape, bf16), big, all_qkv, pltpu.SemaphoreType.DMA((4,)),
        ],
        mm * 2048, 24 << 20, 20,
    )(meta, qkv, after(dctx, give_m), dstates[1], dstates[3], wout, dqf)
    n_q = w_qkv.size // width // 2
    n_ng = 4 * width // 128
    dproj, grad_q, give_q = call(
        proj_body,
        [((groups, rows, 3 * PAIR), bf16), ((groups, n_q, width), f32), ((groups, n_q, width), f32)],
        [SM, HB] + [VM] * 7 + [HB],
        [
            pltpu.VMEM((groups, rows, 3 * PAIR), bf16), pltpu.VMEM((3 * width, 128), f32),
            pltpu.VMEM((2 * n_q, width), f32), all_qkv, low,
            pltpu.SemaphoreType.DMA, pltpu.SemaphoreType.DMA((2,)),
        ],
        mm * 3 * width, 24 << 20, 20, (HB, VM, VM),
    )(meta, qkv, dq, dkn, dvn, *dstates, a1e)
    got_q = swap_core(after(give_q, got_m))
    give_m, keep_m = halve(keep_m, after(got_m, give_q), 1)
    got_m = swap(give_m, 1)
    give_q, keep_q = halve(grad_q, got_q, 0)
    got_q = swap(give_q, 0)
    tokens_grad, ng = call(
        last_body,
        [((rows, width), f32), ((n_ng, 128), f32)],
        [SM, HB, VM, HB, VM, VM] + [HB] * 4,
        [
            big, pltpu.VMEM((n_ng, 128), f32), proj_w, pltpu.VMEM((groups, rows, 3 * PAIR), bf16), big,
            pltpu.SemaphoreType.DMA, pltpu.SemaphoreType.DMA((2,)),
        ],
        mm * 3 * width, 8 << 20, 16,
    )(meta, after(dproj, give_q), tok, dx2, norm_gains, ng2, *qkv_bufs)
    give_q, keep_q = halve(keep_q, after(got_q, ng), 1)
    z_m = to_groups(total_m(keep_m, after(got_m, give_q)))
    got_q = swap(give_q, 1)
    nb_q = n_q * 2 // 16

    def updated(z, n, first, extra):
        return call(
            functools.partial(pieces_body, first, len(z)),
            [((2 * n + extra, 128), bf16)],
            [SM, SM] + [VM] * (len(z) + 1), [pltpu.VMEM((n, 128), f32)], 1 << 20, 4 << 20, 20,
        )(owners, slot, *z, slot_state)[0]

    def everywhere(piece, *first):
        x, y = swap(piece, 0), swap(piece, 1)
        return both_cores([piece, x, y, swap(after(x, *first), 1)])

    part_q = total_q(keep_q, got_q, ng)
    z_q = to_groups(part_q)
    z_m[0] = after(z_m[0], part_q[0])
    fresh_m = updated(z_m, n_m, nb_q, 0)
    m_x, m_y = swap(fresh_m, 0), swap(fresh_m, 1)
    z_q[0] = after(z_q[0], m_x, m_y)
    fresh_q = updated(z_q, n_q, 0, n_q + 2 * n_ng)
    q_x, q_y = swap(fresh_q, 0), swap(fresh_q, 1)
    m_bufs = both_cores([fresh_m, m_x, m_y, swap(after(m_x, fresh_q), 1)])
    part_shape = (4, capacity, 2, 8, 128)
    new_out, new_in, new_down, later = call(
        functools.partial(place_body, nb_q),
        [(w_out.shape, bf16), (w_in.shape, bf16), (w_down.shape, bf16), (part_shape, f32)],
        [SM, SM] + [ANY] * 8,
        [
            pltpu.VMEM((8, 2 * n_m, 128), bf16), pltpu.VMEM((8, n_m, 128), f32), pltpu.VMEM(part_shape, f32),
            pltpu.SemaphoreType.DMA,
        ],
        1 << 20, 4 << 20, 16, (VM, VM, VM, HB),
    )(meta, held, *m_bufs)
    q_z = swap(after(q_x, q_y, m_bufs[3]), 1)
    q_bufs = [fresh_q, q_x, q_y, q_z]
    q_bufs += [swap_core(b) for b in q_bufs[:3]] + [swap_core(after(q_z, new_down))]
    state_shape = (capacity, block_rows, 128)
    norm_shape = (4, width)
    n_held = fresh_q.shape[0]
    (first_new, second_new, master_new, new_qkv, norm_first_new, norm_second_new, norm_new) = call(
        owner_body,
        [(state_shape, f32)] * 3 + [(w_qkv.shape, bf16)] + [(norm_shape, f32)] * 3,
        [SM] * 3 + [HB] * 4 + [VM] * 4 + [ANY] * 8,
        [
            pltpu.VMEM((8, n_held, 128), bf16), pltpu.VMEM((8, n_q, 128), f32), pltpu.VMEM(part_shape, f32),
            pltpu.VMEM((capacity * block_rows, 128), f32), pltpu.VMEM((w_qkv.size // 128, 128), f32),
            pltpu.VMEM((n_ng, 128), f32),
            pltpu.VMEM(state_shape, f32), pltpu.VMEM(state_shape, f32), pltpu.VMEM(state_shape, f32),
            pltpu.SemaphoreType.DMA, pltpu.SemaphoreType.DMA,
        ],
        1 << 20, 8 << 20, 24,
    )(
        meta, counts, held, later, master, first_moment, second_moment,
        norm_gains, norm_biases, norm_first, norm_second, *q_bufs,
    )
    return (
        outputs[None], tokens_grad[None], first_new, second_new, master_new,
        new_qkv, new_out, new_in, new_down, norm_first_new, norm_second_new, norm_new,
    )


def solution(mesh):
    sharded = P("dp", "mp", None)
    return jax.shard_map(
        per_device,
        mesh=mesh,
        in_specs=(
            sharded, sharded, P("dp"), P(), P(None, "mp"), P("mp", None), P(None, "mp"), P("mp", None),
            sharded, sharded, sharded, P(), P(), P(), P(),
        ),
        out_specs=(
            sharded, sharded, sharded, sharded, sharded,
            P(None, "mp"), P("mp", None), P(None, "mp"), P("mp", None), P(), P(), P(),
        ),
        check_vma=False,
    )
```

```python
import functools

import jax
import jax.numpy as jnp
from jax import lax
from jax.experimental import pallas as pl
from jax.experimental.pallas import tpu as pltpu
from jax.sharding import PartitionSpec as P

HEAD = 64
BAND = 30
STEP = 10
HALO = 64
EDGE = 32
QB = 64
WIN = 128
PAIR = 128
COST = 1
STATE = 144

learn_rate = 0.1
norm_rate = 0.3
decay_rate = 0.1
beta_one = 0.9
beta_two = 0.95
adam_epsilon = 1e-08
norm_epsilon = 1e-05
GELU_C = 0.7978845608028654
GELU_A = 0.044715

f32 = jnp.float32
bf16 = jnp.bfloat16

VM = pl.BlockSpec(memory_space=pltpu.VMEM)
HB = pl.BlockSpec(memory_space=pltpu.HBM)
SM = pl.BlockSpec(memory_space=pltpu.SMEM)
ANY = pl.BlockSpec(memory_space=pl.ANY)


def call(body, outs, in_specs, scratch, flops, moved, vmem=48, out_specs=None):
    specs = out_specs or tuple(VM for _ in outs)
    run = pl.pallas_call(
        body,
        out_shape=tuple(
            pltpu.HBM(s, d) if spec is HB else jax.ShapeDtypeStruct(s, d) for (s, d), spec in zip(outs, specs)
        ),
        in_specs=in_specs,
        out_specs=specs,
        scratch_shapes=scratch,
        compiler_params=pltpu.CompilerParams(vmem_limit_bytes=vmem << 20),
        cost_estimate=pl.CostEstimate(flops=flops // COST, bytes_accessed=moved // COST, transcendentals=0),
    )

    def fixed(*args):
        return run(
            *[
                pltpu.with_memory_space_constraint(x, pltpu.HBM) if spec is HB else x
                for x, spec in zip(args, in_specs)
            ]
        )

    return fixed


def load(pairs, sem):
    copies = [pltpu.make_async_copy(a, b, sem) for a, b in pairs]
    for c in copies:
        c.start()
    return copies


def dot(a, b):
    return jnp.dot(a, b, preferred_element_type=f32)


def turned(a):
    return a.astype(f32).T.astype(bf16)


def dot_nt(a, b):
    return dot(a, turned(b))


def dot_tn(a, b):
    return lax.dot_general(a, b, (((0,), (0,)), ((), ())), preferred_element_type=f32)


def normalize(x):
    mean = jnp.mean(x, axis=-1, keepdims=True)
    cen = x - mean
    var = jnp.mean(cen * cen, axis=-1, keepdims=True)
    rstd = lax.rsqrt(var + norm_epsilon)
    return cen * rstd, rstd


def same_head(n=PAIR):
    r = lax.broadcasted_iota(jnp.int32, (n, n), 0)
    c = lax.broadcasted_iota(jnp.int32, (n, n), 1)
    return (r < HEAD) == (c < HEAD)


def pack_state(s1, s2, z):
    both = jnp.where(same_head(), s1, pltpu.roll(s2, HEAD, 1))
    hi = z.astype(bf16).astype(f32)
    row = lax.broadcasted_iota(jnp.int32, (16, PAIR), 0)
    tail = jnp.where(row == 0, hi, jnp.where(row == 1, z - hi, 0.0))
    return both.astype(bf16), tail.astype(bf16)


def unpack_state(refs, g):
    tot = refs[0][g].astype(f32)
    for r in refs[1:]:
        tot = tot + r[g].astype(f32)
    both = tot[:PAIR]
    diag = same_head()
    s1 = jnp.where(diag, both, 0.0)
    s2 = jnp.where(diag, pltpu.roll(both, HEAD, 1), 0.0)
    z = tot[PAIR : PAIR + 1] + tot[PAIR + 1 : PAIR + 2]
    return s1, s2, z


def split_dot(a, ones):
    hi, lo = two(a)
    return dot(hi, ones) + dot(lo, ones)


def two(a):
    hi = a.astype(bf16)
    return hi, (a - hi.astype(f32)).astype(bf16)


def phi(v):
    low = jnp.exp(jnp.minimum(v, 0.0))
    return jnp.where(v > 0, v + 1.0, low), jnp.where(v > 0, 1.0, low)


def band_parts():
    c = lax.broadcasted_iota(jnp.int32, (WIN, 2 * QB), 0)
    r = lax.broadcasted_iota(jnp.int32, (WIN, 2 * QB), 1) % QB
    off = r + EDGE - c
    return (jnp.abs(off) <= BAND), off == 0, c


def stacked(rows):
    lane = lax.broadcasted_iota(jnp.int32, (1, PAIR), 1)
    first = (lane < HEAD).astype(f32).astype(bf16)
    second = (lane >= HEAD).astype(f32).astype(bf16)
    return jnp.concatenate([rows * first, rows * second], axis=0)


def unstack(both):
    lane = lax.broadcasted_iota(jnp.int32, (QB, PAIR), 1)
    return jnp.where(lane < HEAD, both[:QB], both[QB:])


def softmax_of(raw, mask):
    scores = jnp.where(mask, raw * 0.125, -1e30)
    ex = jnp.exp(scores - jnp.max(scores, axis=0, keepdims=True))
    return ex * (1.0 / jnp.sum(ex, axis=0, keepdims=True))


def piece_at(meta, r, bits, other):
    b0, b1 = (meta[6], meta[7]) if other else (meta[4], meta[5])
    core = 1 - meta[2] if other else meta[2]
    if bits == 1:
        return core * 2 + (b0 ^ r)
    return core * 4 + (b0 ^ (r & 1)) * 2 + (b1 ^ (r >> 1))


def fetch_pieces(meta, bufs, lo, rows, weight, sem):
    n = len(bufs) // 2
    copies = []
    for k, buf in enumerate(bufs):
        p = piece_at(meta, k % n, n // 2, k >= n)
        at = pl.ds(pl.multiple_of(p * rows, rows), rows)
        for m in range(buf.shape[0]):
            src = buf.at[m, pl.ds(lo, rows), :]
            copies.append(pltpu.make_async_copy(src, weight.at[meta[3] ^ m, at, :], sem))
    for c in copies:
        c.start()
    return copies


def norm_body(tok, left, right, gains, biases, a1e_h, a1e_o, sem):
    rows = tok.shape[0]
    gain, bias = gains[0:1, :], biases[0:1, :]

    def ln(x):
        return (normalize(x.astype(f32))[0] * gain + bias).astype(bf16)

    a1e_o[0:HALO, :] = ln(left[...])
    a1e_o[HALO + rows :, :] = ln(right[...])

    def chunk(i, _):
        at = pl.ds(pl.multiple_of(i * 128, 128), 128)
        a1e_o[pl.ds(pl.multiple_of(i * 128 + HALO, 64), 128), :] = ln(tok[at, :])
        return 0

    lax.fori_loop(0, rows // 128, chunk, 0)
    out = pltpu.make_async_copy(a1e_o, a1e_h, sem)
    out.start()
    out.wait()


def qkv_body(meta, a1e_h, *refs):
    bufs, (qkv_h, st_o, w, qkv_o, a1e, sem, out_sem) = refs[:4], refs[4:]
    pull = pltpu.make_async_copy(a1e_h, a1e, out_sem)
    pull.start()
    ext = a1e.shape[0]
    rows = ext - 2 * HALO
    groups = bufs[0].shape[0]
    for c in fetch_pieces(meta, bufs, 0, bufs[0].shape[1], w, sem):
        c.wait()
    pull.wait()
    length, base = meta[0], meta[1]
    pos = base + lax.broadcasted_iota(jnp.int32, (rows, 1), 0)
    valid = (pos < length).astype(f32)
    gs = range(groups)
    for g in gs:
        qkv_o[g] = dot(a1e[...], w[g]).astype(bf16)
    own_rows = slice(HALO, HALO + rows)
    out = pltpu.make_async_copy(qkv_o, qkv_h, out_sem)
    out.start()
    parts = []
    for g in gs:
        keys = qkv_o[g, own_rows, PAIR : 2 * PAIR].astype(f32)
        feat = phi(keys)[0] * valid
        parts.append((jnp.sum(feat, axis=0, keepdims=True), two(feat), two(jnp.tanh(keys) * valid)))
    for g in gs:
        z, (fhi, flo), (thi, tlo) = parts[g]
        vals = qkv_o[g, own_rows, 2 * PAIR :]
        s1 = dot_tn(fhi, vals) + dot_tn(flo, vals)
        s2 = dot_tn(thi, vals) + dot_tn(tlo, vals)
        st_o[g, :PAIR, :], st_o[g, PAIR:, :] = pack_state(s1, s2, z)
    out.wait()


def near_body(meta, qkv_h, near_h, qkv, near_o, sem):
    pull = pltpu.make_async_copy(qkv_h, qkv, sem)
    pull.start()
    groups = qkv.shape[0]
    rows = near_o.shape[0]
    length, base = meta[0], meta[1]
    band, diag, lane = band_parts()
    pull.wait()

    def block(b, _):
        at = b * QB
        kpos = base + at - EDGE + lane
        mask = band & (((kpos >= 0) & (kpos < length)) | diag)
        q_at = pl.ds(pl.multiple_of(at + HALO, QB), QB)
        w_at = pl.ds(pl.multiple_of(at + HALO - EDGE, EDGE), WIN)
        gs = range(groups)
        sc = [dot_nt(qkv[g, w_at, PAIR : 2 * PAIR], stacked(qkv[g, q_at, 0:PAIR])) for g in gs]
        p = [softmax_of(sc[g], mask).astype(bf16) for g in gs]
        res = [dot_tn(p[g], qkv[g, w_at, 2 * PAIR :]) for g in gs]
        for g in gs:
            near_o[pl.ds(pl.multiple_of(at, QB), QB), g * PAIR : (g + 1) * PAIR] = unstack(res[g])
        return 0

    lax.fori_loop(0, rows // QB, block, 0, unroll=4)
    out = pltpu.make_async_copy(near_o, near_h, sem)
    out.start()
    out.wait()


def put_halves(core, keep, give, g, lo, grad):
    n, width = grad.shape
    tiles = grad.reshape(n // 16, 2, 8, width)
    even, odd = tiles[:, 0].reshape(n // 2, width), tiles[:, 1].reshape(n // 2, width)
    first = jnp.full(even.shape, core, jnp.int32) == 0
    at = slice(lo, lo + n // 2)
    keep[g, at, :] = jnp.where(first, even, odd).astype(keep.dtype)
    give[g, at, :] = jnp.where(first, odd, even).astype(give.dtype)


def main_body(meta, near_h, qkv_h, h0, h1, h2, h3, tok_h, cot_h, gains, biases, *refs):
    bufs, refs = refs[:8], refs[8:]
    out_h, dst_o, far_o, dx2_h, dctx_h, dqf_h, ng_o, wout_h, keep_h, give_h = refs[:10]
    refs = refs[10:]
    do_o, dctx_o, wout_o, near, tok, cot, st = refs[:7]
    refs = (None,) * 5 + refs
    w_in, w_down, x2, xhat, rs, u, dh, acc, da2, far1, inv, dnum, phq, thq = refs[12:26]
    ctx_o, a2_o, dm_o, hid_o, du_o, out_o, keep, give, query, sem, out_sem = refs[26:]
    rows, width = tok.shape
    groups, hw = hid_o.shape[0], hid_o.shape[2]
    s0, s1, s2, s3 = [st.at[k] for k in range(4)]
    moved = load([(near_h, near), (tok_h, tok), (cot_h, cot)] + [(h, st.at[k]) for k, h in enumerate((h0, h1, h2, h3))], sem.at[4])
    pr = hw // 8
    orow = bufs[0].shape[1] - 2 * pr
    core = meta[2]
    sent = []

    def send(src, dst):
        sent.append(pltpu.make_async_copy(src, dst, out_sem))
        sent[-1].start()

    length, base = meta[0], meta[1]
    pull = pltpu.make_async_copy(qkv_h.at[:, pl.ds(HALO, rows), pl.ds(0, PAIR)], query, sem.at[3])
    pull.start()
    copies = fetch_pieces(meta, bufs, 2 * pr, orow, wout_o, sem.at[0])
    later = fetch_pieces(meta, bufs, 0, pr, w_in, sem.at[1])
    last = fetch_pieces(meta, bufs, pr, pr, w_down, sem.at[2])
    rlen = 1.0 / length.astype(f32)
    gain, bias = gains[1:2, :], biases[1:2, :]
    ones = same_head().astype(f32).astype(bf16)
    gs = range(groups)
    cols = [slice(g * PAIR, (g + 1) * PAIR) for g in gs]
    for c in moved:
        c.wait()
    states = [unpack_state((s0, s1, s2, s3), g) for g in gs]
    s1b, s2b = [two(st[0]) for st in states], [two(st[1]) for st in states]
    cr = 128

    def far_chunk(i, _):
        at = pl.ds(pl.multiple_of(i * cr, cr), cr)
        q = [query[g, at, :].astype(f32) for g in gs]
        ph = [phi(q[g])[0] for g in gs]
        ph2 = [two(ph[g]) for g in gs]
        th2 = [two(jnp.tanh(q[g])) for g in gs]
        den = [split_dot(ph[g] * states[g][2], ones) for g in gs]
        num = [dot(ph2[g][0], s1b[g][0]) + dot(ph2[g][0], s1b[g][1]) + dot(ph2[g][1], s1b[g][0]) for g in gs]
        sec = [dot(th2[g][0], s2b[g][0]) + dot(th2[g][0], s2b[g][1]) + dot(th2[g][1], s2b[g][0]) for g in gs]
        for g in gs:
            phq[at, cols[g]] = ph2[g][0]
            thq[at, cols[g]] = th2[g][0]
        rec = [1.0 / den[g] for g in gs]
        for g in gs:
            part = num[g] * rec[g]
            inv[at, cols[g]] = rec[g]
            far1[at, cols[g]] = part
            ctx_o[at, cols[g]] = (near[at, cols[g]] + (part + sec[g] * rlen)).astype(bf16)
        pos = base + i * cr + lax.broadcasted_iota(jnp.int32, (cr, 1), 0)
        dm_o[at, :] = (cot[at, :].astype(f32) * (pos < length).astype(f32)).astype(bf16)
        return 0

    pull.wait()
    lax.fori_loop(0, rows // cr, far_chunk, 0)
    for c in copies:
        c.wait()
    wout = wout_o[...].reshape(width, width)
    x2[...] = dot(ctx_o[...], wout)

    def norm_chunk(i, _):
        at = pl.ds(pl.multiple_of(i * 128, 128), 128)
        val = x2[at, :] + tok[at, :].astype(f32)
        x2[at, :] = val
        xh, rstd = normalize(val)
        xhat[at, :] = xh
        rs[at, :] = jnp.broadcast_to(rstd, (128, 128))
        a2_o[at, :] = (xh * gain + bias).astype(bf16)
        return 0

    lax.fori_loop(0, rows // 128, norm_chunk, 0)
    for c in later + last:
        c.wait()
    for g in gs:
        u[g] = dot(a2_o[...], w_in[g])
        dh[g] = dot_nt(dm_o[...], w_down[g])

    def act(i, _):
        at = pl.ds(pl.multiple_of(i * 16, 16), 16)
        for g in gs:
            v = u[g, at, :]
            sq = v * v
            half = 0.5 + 0.5 * jnp.tanh(v * (GELU_C + GELU_C * GELU_A * sq))
            hid = v * half
            hid_o[g, at, :] = hid.astype(bf16)
            slope = half + (hid * (1.0 - half)) * (2.0 * GELU_C + 6.0 * GELU_C * GELU_A * sq)
            du_o[g, at, :] = (dh[g, at, :] * slope).astype(bf16)
        return 0

    lax.fori_loop(0, rows // 16, act, 0)
    acc[...] = sum(dot(hid_o[g], w_down[g]) for g in gs)
    da2[...] = sum(dot_nt(du_o[g], w_in[g]) for g in gs)

    def back_chunk(i, carry):
        dg, db = carry
        at = pl.ds(pl.multiple_of(i * 128, 128), 128)
        out_o[at, :] = (x2[at, :] + acc[at, :]).astype(bf16)
        xh = xhat[at, :]
        rstd = rs[at, 0:1]
        d = da2[at, :]
        dg = dg + jnp.sum(d * xh, axis=0, keepdims=True)
        db = db + jnp.sum(d, axis=0, keepdims=True)
        e = d * gain
        m1 = jnp.mean(e, axis=-1, keepdims=True)
        m2 = jnp.mean(e * xh, axis=-1, keepdims=True)
        dx = dm_o[at, :].astype(f32) + rstd * (e - m1 - xh * m2)
        acc[at, :] = dx
        do_o[at, :] = dx.astype(bf16)
        return dg, db

    zero = jnp.zeros((1, width), f32)
    dg, db = lax.fori_loop(0, rows // 128, back_chunk, (zero, zero))
    even = jnp.full((EDGE, width), meta[3] & 1, jnp.int32) == 0
    head, tail = do_o[0:EDGE, :].astype(f32), do_o[rows - EDGE :, :].astype(f32)
    near_edge, far_edge = jnp.where(even, tail, head).astype(bf16), jnp.where(even, head, tail).astype(bf16)
    for g in gs:
        dst_o[g, STATE:, :] = near_edge[:, cols[g]]
        far_o[g, STATE:, :] = far_edge[:, cols[g]]
    send(out_o, out_h)
    send(wout_o, wout_h)
    send(acc, dx2_h)
    ng_o[0:1, :] = dg
    ng_o[1:2, :] = db
    dctx_o[...] = dot_nt(do_o[...], wout).astype(bf16)
    send(dctx_o, dctx_h)

    def far_back(i, carry):
        at = pl.ds(pl.multiple_of(i * cr, cr), cr)
        dc = [dctx_o[at, cols[g]] for g in gs]
        dcf = [dc[g].astype(f32) for g in gs]
        rec = [inv[at, cols[g]] for g in gs]
        dn = [(dcf[g] * rec[g]).astype(bf16) for g in gs]
        dots = [split_dot(dcf[g] * far1[at, cols[g]], ones) for g in gs]
        dph = [dot_nt(dn[g], s1b[g][0]) for g in gs]
        dth = [dot_nt(dc[g], s2b[g][0]) for g in gs]
        out = []
        for g in gs:
            dnum[at, cols[g]] = dn[g]
            dden = -dots[g] * rec[g]
            out.append(carry[g] + jnp.sum(phq[at, cols[g]].astype(f32) * dden, axis=0, keepdims=True))
            slope = phi(query[g, at, :].astype(f32))[1]
            th = thq[at, cols[g]].astype(f32)
            da2[at, cols[g]] = (dph[g] + dden * states[g][2]) * slope + dth[g] * rlen * (1.0 - th * th)
        return tuple(out)

    none = jnp.zeros((1, PAIR), f32)
    dz = lax.fori_loop(0, rows // cr, far_back, (none,) * groups)
    for g in gs:
        d1 = dot_tn(phq[:, cols[g]], dnum[:, cols[g]])
        d2 = dot_tn(thq[:, cols[g]], dctx_o[:, cols[g]]) * rlen
        both, low = pack_state(d1, d2, dz[g])
        for ref in (dst_o, far_o):
            ref[g, :PAIR, :] = both
            ref[g, PAIR:STATE, :] = low
    send(da2, dqf_h)
    n_out = ctx_o.shape[1] // groups

    def finish(g, lo, n, grad):
        put_halves(core, keep, give, g, lo, grad)
        part = pl.ds(lo, n)
        send(keep.at[g, part, :], keep_h.at[g, part, :])
        send(give.at[g, part, :], give_h.at[g, part, :])

    for g in gs:
        finish(g, n_out // 2, width // 2, dot_tn(a2_o[...], du_o[g]))
    for g in gs:
        finish(g, 0, n_out // 2, dot_tn(ctx_o[:, g * n_out : (g + 1) * n_out], do_o[...]))
    for g in gs:
        finish(g, n_out // 2 + width // 2, hw // 2, dot_tn(hid_o[g], dm_o[...]))
    for c in sent:
        c.wait()


def near_back_body(
    meta, qkv_h, dctx_h, one, three, wout_h, dqf_h, dq_o, dk_o, dv_o, dce, dqe, dke, dve, wout, dqf, qkv, sem,
):
    pull = pltpu.make_async_copy(qkv_h, qkv, sem.at[2])
    pull.start()
    groups = qkv.shape[0]
    rows, width = dctx_h.shape
    third = pltpu.make_async_copy(dctx_h, dce.at[pl.ds(EDGE, rows), :], sem.at[3])
    third.start()
    length, base = meta[0], meta[1]
    band, diag, lane = band_parts()
    first = pltpu.make_async_copy(wout_h, wout, sem.at[0])
    first.start()
    second = pltpu.make_async_copy(dqf_h, dqf, sem.at[1])
    second.start()
    first.wait()
    w = wout[...].reshape(width, -1)
    z = meta[3]
    odd = jnp.full((EDGE, width), z & 1, jnp.int32) == 1
    side = [
        jnp.concatenate([ref[g, STATE:, :] for g in range(groups)], axis=1).astype(f32) for ref in (one, three)
    ]
    last_z = meta[17] - 1
    do_l = jnp.where(odd, side[0], side[1]) * (z > 0).astype(f32)
    do_r = jnp.where(odd, side[1], side[0]) * (z < last_z).astype(f32)
    dce[0:EDGE, :] = dot_nt(do_l.astype(bf16), w).astype(bf16)
    dce[EDGE + rows :, :] = dot_nt(do_r.astype(bf16), w).astype(bf16)
    dke[...] = jnp.zeros(dke.shape, f32)
    dve[...] = jnp.zeros(dve.shape, f32)
    pull.wait()
    third.wait()

    def block(b, _):
        at = b * QB
        kpos = base + at - HALO + lane
        mask = band & (((kpos >= 0) & (kpos < length)) | diag)
        c_at = pl.ds(pl.multiple_of(at, QB), QB)
        q_at = pl.ds(pl.multiple_of(at + EDGE, EDGE), QB)
        w_at = pl.ds(pl.multiple_of(at, QB), WIN)
        gs = range(groups)
        cols = [slice(g * PAIR, (g + 1) * PAIR) for g in gs]
        qs = [stacked(qkv[g, q_at, 0:PAIR]) for g in gs]
        cs = [stacked(dce[c_at, cols[g]]) for g in gs]
        kw = [qkv[g, w_at, PAIR : 2 * PAIR] for g in gs]
        sc = [dot_nt(kw[g], qs[g]) for g in gs]
        dp = [dot_nt(qkv[g, w_at, 2 * PAIR :], cs[g]) for g in gs]
        p = [softmax_of(sc[g], mask) for g in gs]
        row = [jnp.sum(p[g] * dp[g], axis=0, keepdims=True) for g in gs]
        ds = [(p[g] * (dp[g] - row[g])).astype(bf16) for g in gs]
        pb = [p[g].astype(bf16) for g in gs]
        for g in gs:
            dke[w_at, cols[g]] += dot(ds[g], qs[g])
            dve[w_at, cols[g]] += dot(pb[g], cs[g])
        dq = [dot_tn(ds[g], kw[g]) for g in gs]
        for g in gs:
            dqe[c_at, cols[g]] = unstack(dq[g])
        return 0

    lax.fori_loop(0, rows // QB + 1, block, 0, unroll=9)
    second.wait()
    dq_o[...] = (dqe[EDGE : EDGE + rows, :] * 0.125 + dqf[...]).astype(bf16)
    dk_o[...] = dke[HALO : HALO + rows, :] * 0.125
    dv_o[...] = dve[HALO : HALO + rows, :]


def proj_body(
    meta, qkv_h, dq, dkn, dvn, s0, s1, s2, s3, a1e_h, dproj_h, keep_o, give_o, dproj, flat, pseudo, qkv, a1e, sem, in_sem,
):
    rows = dq.shape[0]
    other = pltpu.make_async_copy(a1e_h.at[pl.ds(HALO, rows), :], a1e, in_sem.at[1])
    other.start()
    pull = pltpu.make_async_copy(qkv_h, qkv, in_sem.at[0])
    pull.start()
    groups = qkv.shape[0]
    rows, width = dq.shape
    length, base, core = meta[0], meta[1], meta[2]
    cr = 128
    gs = range(groups)
    cols = [slice(g * PAIR, (g + 1) * PAIR) for g in gs]
    states = [unpack_state((s0, s1, s2, s3), g) for g in gs]
    s1b, s2b = [st[0].astype(bf16) for st in states], [st[1].astype(bf16) for st in states]

    def far_chunk(i, _):
        at = pl.ds(pl.multiple_of(i * cr, cr), cr)
        e_at = pl.ds(pl.multiple_of(i * cr + HALO, HALO), cr)
        pos = base + i * cr + lax.broadcasted_iota(jnp.int32, (cr, 1), 0)
        valid = (pos < length).astype(f32)
        k = [qkv[g, e_at, PAIR : 2 * PAIR].astype(f32) for g in gs]
        v = [qkv[g, e_at, 2 * PAIR :] for g in gs]
        feat = [phi(k[g]) for g in gs]
        th = [jnp.tanh(k[g]) for g in gs]
        vd1 = [dot_nt(v[g], s1b[g]) for g in gs]
        vd2 = [dot_nt(v[g], s2b[g]) for g in gs]
        dv = [
            dot((feat[g][0] * valid).astype(bf16), s1b[g]) + dot((th[g] * valid).astype(bf16), s2b[g]) for g in gs
        ]
        for g in gs:
            dk = (vd1[g] + states[g][2]) * feat[g][1] + vd2[g] * (1.0 - th[g] * th[g])
            dproj[g, at, 0:PAIR] = dq[at, cols[g]]
            dproj[g, at, PAIR : 2 * PAIR] = (dkn[at, cols[g]] + dk * valid).astype(bf16)
            dproj[g, at, 2 * PAIR :] = (dvn[at, cols[g]] + dv[g]).astype(bf16)
        return 0

    pull.wait()
    lax.fori_loop(0, rows // cr, far_chunk, 0)
    out = pltpu.make_async_copy(dproj, dproj_h, sem)
    out.start()
    other.wait()
    n_flat = 3 * width
    for g in gs:
        grad = dot_tn(a1e[...], dproj[g])
        for part in range(3):
            flat[pl.ds(part, width, stride=3), :] = grad[:, part * PAIR : (part + 1) * PAIR]
        for j in range(4):
            pseudo[:, j * 128 : (j + 1) * 128] = flat[pl.ds(j, n_flat // 4, stride=4), :]
        put_halves(core, keep_o, give_o, g, 0, pseudo[...])
    out.wait()


def last_body(meta, dproj_h, tok, dx2_h, gains, ng2, *refs):
    bufs, (tg_o, ng_o, da1, ngs, wqkv, dproj, dx2, sem, sems) = refs[:4], refs[4:]
    groups = dproj.shape[0]
    rows, width = tok.shape
    gain = gains[0:1, :]
    copies = fetch_pieces(meta, bufs, 0, bufs[0].shape[1], wqkv, sem)
    copies.append(pltpu.make_async_copy(dproj_h, dproj, sems.at[0]))
    copies[-1].start()
    late = pltpu.make_async_copy(dx2_h, dx2, sems.at[1])
    late.start()
    for c in copies:
        c.wait()
    da1[...] = sum(dot_nt(dproj[g], wqkv[g]) for g in range(groups))

    late.wait()

    def back_chunk(i, carry):
        dg, db = carry
        at = pl.ds(pl.multiple_of(i * 64, 64), 64)
        xh, rstd = normalize(tok[at, :].astype(f32))
        d = da1[at, :]
        dg = dg + jnp.sum(d * xh, axis=0, keepdims=True)
        db = db + jnp.sum(d, axis=0, keepdims=True)
        e = d * gain
        m1 = jnp.mean(e, axis=-1, keepdims=True)
        m2 = jnp.mean(e * xh, axis=-1, keepdims=True)
        tg_o[at, :] = dx2[at, :] + rstd * (e - m1 - xh * m2)
        return dg, db

    zero = jnp.zeros((1, width), f32)
    dg, db = lax.fori_loop(0, rows // 64, back_chunk, (zero, zero))
    for k, val in enumerate((dg, db, ng2[0:1, :], ng2[1:2, :])):
        for j in range(width // 128):
            at = k * (width // 128) + j
            ngs[at : at + 1, :] = val[:, j * 128 : (j + 1) * 128]
    ng_o[...] = ngs[...]


def halve_body(bit, own, got, give_o, keep_o):
    groups, _, n = give_o.shape
    out = pl.ds(pl.multiple_of((1 - bit[0]) * n, 128), n)
    stay = pl.ds(pl.multiple_of(bit[0] * n, 128), n)
    for g in range(groups):
        give_o[g] = (own[g, :, out].astype(f32) + got[g, :, out].astype(f32)).astype(bf16)
    for g in range(groups):
        keep_o[g] = own[g, :, stay].astype(f32) + got[g, :, stay].astype(f32)


def total_body(meta, keep, got, *outs):
    for m, out in enumerate(outs):
        g = meta[3] ^ m
        out[0] = (keep[g] + got[g].astype(f32)).astype(bf16)


def total_q_body(meta, keep, got, ng, *outs):
    n, k = keep.shape[1], ng.shape[0]
    hi, lo = two(ng[...])
    for m, out in enumerate(outs):
        g = meta[3] ^ m
        out[0, 0:n, :] = (keep[g] + got[g].astype(f32)).astype(bf16)
        out[0, n : n + k, :], out[0, n + k :, :] = hi, lo


def slices_body(where, master, first, second, out_h, held, parts, sem, out_sem):
    caps = held.shape[1] // 64
    copies = [pltpu.make_async_copy(ref, held.at[t], sem.at[t]) for t, ref in enumerate((master, first, second))]
    for c in copies:
        c.start()
    sent = []
    for t in range(3):
        copies[t].wait()
        for j in range(4):
            val = held[t, pl.ds(j, caps * 16, stride=4), :].reshape(caps, 2, 8, 128)
            for c in range(2):
                hi, lo = two(val[:, c].reshape(caps * 8, 128))
                for k, part in ((0, hi), (1, lo)) if t == 0 else ((t + 1, hi),):
                    parts[k, c, j] = part
                    for d in where[c][j]:
                        sent.append(pltpu.make_async_copy(parts.at[k, c, j], out_h.at[d, k], out_sem))
                        sent[-1].start()
    for c in sent:
        c.wait()


def widen_body(recv_h, st_o, recv, sem):
    copies = load([(recv_h.at[d], recv.at[d]) for d in range(recv.shape[0])], sem)
    for c in copies:
        c.wait()

    def owner(d, _):
        st_o[d, 0] = recv[d, 0].astype(f32) + recv[d, 1].astype(f32)
        st_o[d, 1] = recv[d, 2].astype(f32)
        st_o[d, 2] = recv[d, 3].astype(f32)
        return 0

    lax.fori_loop(0, recv.shape[0], owner, 0)


def adam(g, m_old, f_old, s_old):
    corr_one = 1.0 - beta_one**STEP
    corr_two = 1.0 - beta_two**STEP
    fn = beta_one * f_old + (1.0 - beta_one) * g
    sn = beta_two * s_old + (1.0 - beta_two) * g * g
    step = fn / corr_one / (jnp.sqrt(sn / corr_two) + adam_epsilon)
    return fn, sn, m_old - learn_rate * (step + decay_rate * m_old)


def pieces_body(first, count, owners, slots, *refs):
    parts, (st, w_o, piece_o) = refs[:count], refs[count:]
    n = piece_o.shape[0]
    src = [(r, s) for r in parts for s in range(r.shape[0])]
    piece_o[...] = sum(r[s, 0:n, :].astype(f32) for r, s in src)
    w_o[n : 2 * n, :] = piece_o[...].astype(bf16)
    if w_o.shape[0] > 2 * n:
        k = (parts[0].shape[1] - n) // 2
        w_o[2 * n : 3 * n, :] = two(piece_o[...])[1]
        norms = sum(r[s, n : n + k, :].astype(f32) + r[s, n + k :, :].astype(f32) for r, s in src)
        w_o[3 * n : 3 * n + k, :], w_o[3 * n + k :, :] = two(norms)

    def pair(i, _):
        new = []
        for k in range(2):
            b = i * 2 + k
            at = pl.ds(pl.multiple_of(slots[first + b] * 8, 8), 8)
            own = owners[first + b]
            g = piece_o[pl.ds(pl.multiple_of(b * 8, 8), 8), :]
            new.append(adam(g, st[own, 0, at, :], st[own, 1, at, :], st[own, 2, at, :])[2])
        w_o[pl.ds(pl.multiple_of(i * 16, 16), 16), :] = jnp.concatenate(new, axis=0).astype(bf16)
        return 0

    lax.fori_loop(0, n // 16, pair, 0, unroll=4)


def owner_body(
    meta, counts, blocks, later_h, master_h, first_h, second_h, gains, biases, n_first, n_second, *refs
):
    bufs, (f_o, s_o, m_o, q_o, nf_o, ns_o, np_o) = refs[:8], refs[8:15]
    held, early, parts, grad, flat, total, master, first, second, sem, sems = refs[15:]
    moved = load([(later_h, parts), (master_h, master), (first_h, first), (second_h, second)], sems)
    collect(meta, bufs, held, sem)
    for c in moved:
        c.wait()
    caps, br, _ = master.shape
    n = q_o.shape[0] * q_o.shape[1] // (128 * 64)
    k_ng = total.shape[0]
    for p in range(8):
        early[p] = held[p, n * 8 : n * 16, :].astype(f32) + held[p, n * 16 : n * 24, :].astype(f32)
    total[...] = sum(
        held[p, n * 24 : n * 24 + k_ng, :].astype(f32) + held[p, n * 24 + k_ng :, :].astype(f32) for p in range(8)
    )
    start = meta[8] * caps

    def pick(r, _):
        b = blocks[start + r]
        old = pl.ds(pl.multiple_of(jnp.minimum(b, n - 1) * 8, 8), 8)
        is_q = jnp.full((8, 128), b, jnp.int32) < n
        for p in range(8):
            parts[p % 4, r, p // 4] = jnp.where(is_q, early[p, old, :], parts[p % 4, r, p // 4])
        return 0

    lax.fori_loop(0, caps, pick, 0, unroll=2)
    for j in range(4):
        grad[pl.ds(j, caps * 16, stride=4), :] = parts[j].reshape(caps * 16, 128)

    def slot(r, _):
        g = grad[pl.ds(pl.multiple_of(r * br, br), br), :]
        m_old, f_old, s_old = master[r], first[r], second[r]
        fn, sn, mn = adam(g, m_old, f_old, s_old)
        keep = jnp.full(g.shape, counts[start + r], jnp.int32) > 0
        f_o[r] = jnp.where(keep, fn, f_old)
        s_o[r] = jnp.where(keep, sn, s_old)
        m_o[r] = jnp.where(keep, mn, m_old)
        return 0

    lax.fori_loop(0, caps, slot, 0, unroll=2)
    rows = q_o.shape[0]
    for j in range(4):
        flat[pl.ds(j, n * 16, stride=4), :] = columns(held, j, 0, n * 8)
    for part in range(3):
        q_o[:, part * 128 : (part + 1) * 128] = flat[pl.ds(part, rows, stride=3), :].astype(bf16)
    corr_one = 1.0 - beta_one**STEP
    corr_two = 1.0 - beta_two**STEP
    per = n_first.shape[1] // 128
    for k in range(4):
        old = (biases if k % 2 else gains)[k // 2 : k // 2 + 1, :]
        g = jnp.concatenate([total[k * per + j : k * per + j + 1, :] for j in range(per)], axis=1)
        fn = beta_one * n_first[k : k + 1, :] + (1.0 - beta_one) * g
        sn = beta_two * n_second[k : k + 1, :] + (1.0 - beta_two) * g * g
        nf_o[k : k + 1, :] = fn
        ns_o[k : k + 1, :] = sn
        np_o[k : k + 1, :] = old - norm_rate * (fn / corr_one / (jnp.sqrt(sn / corr_two) + adam_epsilon))


def collect(meta, bufs, held, sem):
    copies = []
    for k, buf in enumerate(bufs):
        copies.append(pltpu.make_async_copy(buf, held.at[piece_at(meta, k % 4, 2, k >= 4)], sem))
        copies[-1].start()
    for c in copies:
        c.wait()


def columns(held, j, lo, n):
    even, odd = [held[c * 4 + j, lo : lo + n, :].astype(f32).reshape(n // 8, 1, 8, 128) for c in range(2)]
    return jnp.concatenate([even, odd], axis=1).reshape(2 * n, 128)


def place_body(first, meta, blocks, *refs):
    bufs, outs, (parts_h, held, grads, parts, sem) = refs[:8], refs[8:11], refs[11:]
    collect(meta, bufs, held, sem)
    half = held.shape[1] // 2
    for p in range(8):
        grads[p] = held[p, half:, :].astype(f32)
    caps = parts.shape[1]

    def pick(r, _):
        b = jnp.maximum(blocks[meta[8] * caps + r] - first, 0)
        at = pl.ds(pl.multiple_of(b * 8, 8), 8)
        for p in range(8):
            parts[p % 4, r, p // 4] = grads[p, at, :]
        return 0

    lax.fori_loop(0, caps, pick, 0, unroll=2)
    out = pltpu.make_async_copy(parts, parts_h, sem)
    out.start()
    lo = 0
    for ref in outs:
        n = ref.shape[0] // 2
        for j in range(4):
            ref[:, j * 128 : (j + 1) * 128] = columns(held, j, lo, n).astype(bf16)
        lo += n
    out.wait()


def per_device(
    tokens, cotangent, lengths, owners, w_qkv, w_out, w_in, w_down,
    master, first_moment, second_moment, norm_gains, norm_biases, norm_first, norm_second,
):
    rows, width = tokens.shape[1], tokens.shape[2]
    groups = lax.axis_size("mp")
    ndp = lax.axis_size("dp")
    nbits = ndp.bit_length() - 1
    rest = list(range(1, nbits))
    order = (rest, rest[:2][::-1] + rest[2:][::-1])
    me, zi = lax.axis_index("dp"), lax.axis_index("mp")
    core = me & 1

    def bit_of(who, at, s):
        return (who >> jnp.where(at == 0, order[0][s], order[1][s])) & 1

    def swap(x, s):
        return lax.ppermute(x, "dp", [(i, i ^ (1 << order[i & 1][s])) for i in range(ndp)])

    def swap_core(x):
        return lax.ppermute(x, "dp", [(i, i ^ 1) for i in range(ndp)])

    def from_mp(x, step):
        return lax.ppermute(x, "mp", [(i, i + step) for i in range(groups) if 0 <= i + step < groups])

    def swap_mp(x, mask):
        return lax.ppermute(x, "mp", [(i, i ^ mask) for i in range(groups)])

    def exchange(x, axis):
        return lax.all_to_all(x, axis, 0, 0, tiled=True)

    def all_states(x):
        return [x] + [swap_mp(x, m) for m in range(1, groups)]

    q0, q1 = bit_of(me, core, 0), bit_of(me, core, 1)
    o0, o1 = bit_of(me, 1 - core, 0), bit_of(me, 1 - core, 1)
    length = lengths[0]
    base = zi * rows
    ids = [length, base, core, zi, q0, q1, o0, o1, me]
    ids += [
        me - (me & 7) + c + ((j >> 1) << order[c][0]) + ((j & 1) << order[c][1]) for c in range(2) for j in range(4)
    ]
    ids.append(jnp.int32(groups))
    meta = jnp.stack(ids).astype(jnp.int32)

    def after(x, *deps):
        return lax.optimization_barrier((x,) + deps)[0]

    def over_mp(piece):
        return [piece] + [swap_mp(piece, m) for m in range(1, groups)]

    def both_cores(bufs):
        return bufs + [swap_core(b) for b in bufs]

    def part_of(w, n, at):
        return lax.dynamic_slice_in_dim(w, at * (w.shape[0] // n), w.shape[0] // n, 0)

    mine = core * 4 + q0 * 2 + q1
    tok, cot = tokens[0], cotangent[0]
    ext = rows + 2 * HALO
    mm = 2 * rows * width
    qkv_z = over_mp(part_of(w_qkv, 4, core * 2 + q0))
    left, right = from_mp(tok[rows - HALO :], 1), from_mp(tok[:HALO], -1)
    ffn_piece = jnp.concatenate([part_of(w, 8, mine) for w in (w_in, w_down, w_out)], axis=0)
    qkv_z = after(jnp.stack(qkv_z), left, right, ffn_piece)
    ffn_z = jnp.stack(over_mp(after(ffn_piece, qkv_z)))
    qkv_bufs = [qkv_z, swap(qkv_z, 0)]
    capacity, block_rows = master.shape[0], master.shape[1]
    where = [[[] for _ in range(4)] for _ in range(2)]
    for d in range(ndp):
        b = order[d & 1]
        where[d & 1][2 * ((d >> b[0]) & 1) + ((d >> b[1]) & 1)].append(d)
    flat_state = [x.reshape(capacity * block_rows, 128) for x in (master, first_moment, second_moment)]
    [parts] = call(
        functools.partial(slices_body, where), [((ndp, 4, capacity * 8, 128), bf16)], [HB] * 3,
        [
            pltpu.VMEM((3, capacity * block_rows, 128), f32), pltpu.VMEM((4, 2, 4, capacity * 8, 128), bf16),
            pltpu.SemaphoreType.DMA((3,)), pltpu.SemaphoreType.DMA,
        ],
        1 << 20, 4 << 20, 12, (HB,),
    )(*flat_state)
    [a1e] = call(norm_body, [((ext, width), bf16)], [VM] * 5,
        [pltpu.VMEM((ext, width), bf16), pltpu.SemaphoreType.DMA], 4 * mm, 1 << 20, 16, (HB,),
    )(
        after(tok, parts), left, right, norm_gains, norm_biases
    )
    qkv_bufs = both_cores([qkv_bufs[0], after(qkv_bufs[1], a1e)])
    all_qkv = pltpu.VMEM((groups, ext, 3 * PAIR), bf16)
    proj_w = pltpu.VMEM((groups, width, 3 * PAIR), bf16)
    qkv, state = call(
        qkv_body,
        [((groups, ext, 3 * PAIR), bf16), ((groups, STATE, PAIR), bf16)],
        [SM, HB] + [ANY] * 4,
        [proj_w, all_qkv, pltpu.VMEM((ext, width), bf16), pltpu.SemaphoreType.DMA, pltpu.SemaphoreType.DMA],
        2 * ext * width * 3 * width, 6 << 20, 20, (HB, VM),
    )(meta, after(a1e, ffn_z), *qkv_bufs)
    states = all_states(state)
    ffn_z = after(ffn_z, a1e, qkv_bufs[1])
    ffn_x, ffn_y = swap(ffn_z, 0), swap(ffn_z, 1)
    ffn_oth = [swap_core(b) for b in (ffn_z, ffn_x, ffn_y)]
    ffn_bufs = [ffn_z, ffn_x, ffn_y, swap(after(ffn_x, ffn_y, *states), 1)]
    blocks = owners.shape[0]
    earlier = jnp.arange(blocks)[None, :] < jnp.arange(blocks)[:, None]
    alike = owners[None, :] == owners[:, None]
    slot = jnp.sum((earlier & alike).astype(jnp.int32), axis=1)
    slot_rows = owners * capacity + slot
    hit = slot_rows[None, :] == jnp.arange(ndp * capacity, dtype=jnp.int32)[:, None]
    held = jnp.sum(jnp.where(hit, jnp.arange(blocks, dtype=jnp.int32)[None, :], 0), axis=1)
    counts = jnp.sum(hit.astype(jnp.int32), axis=1)
    [near] = call(
        near_body, [((rows, width), f32)], [SM, HB],
        [all_qkv, pltpu.VMEM((rows, width), f32), pltpu.SemaphoreType.DMA], mm * 1024, 12 << 20, 16, (HB,),
    )(meta, after(qkv, slot, held, counts, *ffn_oth, *states))
    ffn_bufs = ffn_bufs + ffn_oth + [swap_core(ffn_bufs[3])]
    held_state = exchange(after(parts, near), "dp")

    hid_w = w_in.shape[1]
    big = pltpu.VMEM((rows, width), f32)
    low = pltpu.VMEM((rows, width), bf16)
    n_m = (w_out.shape[0] + w_in.shape[0] + w_down.shape[0]) // 2
    wide = pltpu.VMEM((groups, rows, hid_w), f32)
    half = pltpu.VMEM((groups, n_m, width), bf16)
    four = pltpu.VMEM((groups, rows, hid_w), bf16)
    (outputs, dstate, dfar, dx2, dctx, dqf, ng2, wout, grad_m, give_m) = call(
        main_body,
        [
            ((rows, width), bf16), ((groups, STATE + EDGE, PAIR), bf16), ((groups, STATE + EDGE, PAIR), bf16),
            ((rows, width), f32), ((rows, width), bf16), ((rows, width), f32), ((2, width), f32),
            ((groups,) + w_out.shape, bf16), ((groups, n_m, width), bf16), ((groups, n_m, width), bf16),
        ],
        [SM] + [HB] * 8 + [VM] * 2 + [HB] * 7 + [ANY],
        [
            low, low, pltpu.VMEM((groups,) + w_out.shape, bf16), big, low, low,
            pltpu.VMEM((4, groups, STATE, PAIR), bf16),
            pltpu.VMEM((groups, width, hid_w), bf16), pltpu.VMEM((groups, hid_w, width), bf16),
            big, big, pltpu.VMEM((rows, 128), f32), wide, wide, big, big, big, big,
            low, low, low, low, low, low, four, four, low, half, half,
            pltpu.VMEM((groups, rows, PAIR), bf16), pltpu.SemaphoreType.DMA((5,)), pltpu.SemaphoreType.DMA,
        ],
        mm * hid_w * groups * 6, 24 << 20, 44,
        (HB, VM, VM, HB, HB, HB, VM, HB, HB, HB),
    )(meta, near, qkv, *states, tok, cot, norm_gains, norm_biases, *ffn_bufs)

    dstate, dfar, give_m, _ = lax.optimization_barrier((dstate, dfar, give_m, held_state))
    dstates = [dstate, swap_mp(dstate, 1), swap_mp(dstate, 2), swap_mp(dfar, 3)]

    [slot_state] = call(
        widen_body, [((ndp, 3, capacity * 8, 128), f32)], [HB],
        [pltpu.VMEM((ndp, 4, capacity * 8, 128), bf16), pltpu.SemaphoreType.DMA], 1 << 20, 4 << 20, 12,
    )(held_state)

    bits = [bit_of(me, core, s).astype(jnp.int32).reshape(1) for s in range(2)]

    def halve(own, got, s):
        shape = own.shape[:-1] + (own.shape[-1] // 2,)
        return call(
            halve_body, [(shape, bf16), (shape, f32)], [SM, VM, VM], [], 1 << 20, 4 << 20, 16,
        )(bits[s], own, got)

    def rest_of(keep, got):
        for s in range(2, nbits - 1):
            tot = (keep + got.astype(f32)).astype(bf16)
            keep, got = tot.astype(f32), swap(tot, s)
        return keep, got

    def to_groups(part):
        return [part[0]] + [swap_mp(part[m], m) for m in range(1, groups)]

    def total_m(keep, got):
        return call(
            total_body, [((1,) + keep.shape[1:], bf16)] * groups, [SM, VM, VM], [], 1 << 20, 2 << 20, 12,
        )(meta, *rest_of(keep, got))

    def total_q(keep, got, extra):
        keep, got = rest_of(keep, got)
        for s in range(2, nbits - 1):
            extra = extra + swap(extra, s)
        shape = (1, keep.shape[1] + 2 * extra.shape[0], keep.shape[2])
        return call(
            total_q_body, [(shape, bf16)] * groups, [SM, VM, VM, VM], [], 1 << 20, 2 << 20, 12,
        )(meta, keep, got, extra)

    give_m, keep_m = halve(grad_m, after(swap_core(give_m), dstates[1], dstates[3], slot_state), 0)
    got_m = swap(give_m, 0)
    dq, dkn, dvn = call(
        near_back_body,
        [((rows, width), bf16), ((rows, width), f32), ((rows, width), f32)],
        [SM, HB, HB] + [VM] * 2 + [HB] * 2,
        [
            pltpu.VMEM((rows + 2 * EDGE, width), bf16), pltpu.VMEM((rows + 2 * EDGE, width), f32),
            pltpu.VMEM((ext, width), f32), pltpu.VMEM((ext, width), f32),
            pltpu.VMEM(wout.shape, bf16), big, all_qkv, pltpu.SemaphoreType.DMA((4,)),
        ],
        mm * 2048, 24 << 20, 20,
    )(meta, qkv, after(dctx, give_m), dstates[1], dstates[3], wout, dqf)
    n_q = w_qkv.size // width // 2
    n_ng = 4 * width // 128
    dproj, grad_q, give_q = call(
        proj_body,
        [((groups, rows, 3 * PAIR), bf16), ((groups, n_q, width), f32), ((groups, n_q, width), f32)],
        [SM, HB] + [VM] * 7 + [HB],
        [
            pltpu.VMEM((groups, rows, 3 * PAIR), bf16), pltpu.VMEM((3 * width, 128), f32),
            pltpu.VMEM((2 * n_q, width), f32), all_qkv, low,
            pltpu.SemaphoreType.DMA, pltpu.SemaphoreType.DMA((2,)),
        ],
        mm * 3 * width, 24 << 20, 20, (HB, VM, VM),
    )(meta, qkv, dq, dkn, dvn, *dstates, a1e)
    got_q = swap_core(after(give_q, got_m))
    give_m, keep_m = halve(keep_m, after(got_m, give_q), 1)
    got_m = swap(give_m, 1)
    give_q, keep_q = halve(grad_q, got_q, 0)
    got_q = swap(give_q, 0)
    tokens_grad, ng = call(
        last_body,
        [((rows, width), f32), ((n_ng, 128), f32)],
        [SM, HB, VM, HB, VM, VM] + [HB] * 4,
        [
            big, pltpu.VMEM((n_ng, 128), f32), proj_w, pltpu.VMEM((groups, rows, 3 * PAIR), bf16), big,
            pltpu.SemaphoreType.DMA, pltpu.SemaphoreType.DMA((2,)),
        ],
        mm * 3 * width, 8 << 20, 16,
    )(meta, after(dproj, give_q), tok, dx2, norm_gains, ng2, *qkv_bufs)
    give_q, keep_q = halve(keep_q, after(got_q, ng), 1)
    z_m = to_groups(total_m(keep_m, after(got_m, give_q)))
    got_q = swap(give_q, 1)
    nb_q = n_q * 2 // 16

    def updated(z, n, first, extra):
        return call(
            functools.partial(pieces_body, first, len(z)),
            [((2 * n + extra, 128), bf16)],
            [SM, SM] + [VM] * (len(z) + 1), [pltpu.VMEM((n, 128), f32)], 1 << 20, 4 << 20, 20,
        )(owners, slot, *z, slot_state)[0]

    def everywhere(piece, *first):
        x, y = swap(piece, 0), swap(piece, 1)
        return both_cores([piece, x, y, swap(after(x, *first), 1)])

    part_q = total_q(keep_q, got_q, ng)
    z_q = to_groups(part_q)
    z_m[0] = after(z_m[0], part_q[0])
    fresh_m = updated(z_m, n_m, nb_q, 0)
    m_x, m_y = swap(fresh_m, 0), swap(fresh_m, 1)
    z_q[0] = after(z_q[0], m_x, m_y)
    fresh_q = updated(z_q, n_q, 0, n_q + 2 * n_ng)
    q_x, q_y = swap(fresh_q, 0), swap(fresh_q, 1)
    m_bufs = both_cores([fresh_m, m_x, m_y, swap(after(m_x, fresh_q), 1)])
    part_shape = (4, capacity, 2, 8, 128)
    new_out, new_in, new_down, later = call(
        functools.partial(place_body, nb_q),
        [(w_out.shape, bf16), (w_in.shape, bf16), (w_down.shape, bf16), (part_shape, f32)],
        [SM, SM] + [ANY] * 8,
        [
            pltpu.VMEM((8, 2 * n_m, 128), bf16), pltpu.VMEM((8, n_m, 128), f32), pltpu.VMEM(part_shape, f32),
            pltpu.SemaphoreType.DMA,
        ],
        1 << 20, 4 << 20, 16, (VM, VM, VM, HB),
    )(meta, held, *m_bufs)
    q_z = swap(after(q_x, q_y, m_bufs[3]), 1)
    q_bufs = [fresh_q, q_x, q_y, q_z]
    q_bufs += [swap_core(b) for b in q_bufs[:3]] + [swap_core(after(q_z, new_down))]
    state_shape = (capacity, block_rows, 128)
    norm_shape = (4, width)
    n_held = fresh_q.shape[0]
    (first_new, second_new, master_new, new_qkv, norm_first_new, norm_second_new, norm_new) = call(
        owner_body,
        [(state_shape, f32)] * 3 + [(w_qkv.shape, bf16)] + [(norm_shape, f32)] * 3,
        [SM] * 3 + [HB] * 4 + [VM] * 4 + [ANY] * 8,
        [
            pltpu.VMEM((8, n_held, 128), bf16), pltpu.VMEM((8, n_q, 128), f32), pltpu.VMEM(part_shape, f32),
            pltpu.VMEM((capacity * block_rows, 128), f32), pltpu.VMEM((w_qkv.size // 128, 128), f32),
            pltpu.VMEM((n_ng, 128), f32),
            pltpu.VMEM(state_shape, f32), pltpu.VMEM(state_shape, f32), pltpu.VMEM(state_shape, f32),
            pltpu.SemaphoreType.DMA, pltpu.SemaphoreType.DMA,
        ],
        1 << 20, 8 << 20, 24,
    )(
        meta, counts, held, later, master, first_moment, second_moment,
        norm_gains, norm_biases, norm_first, norm_second, *q_bufs,
    )
    return (
        outputs[None], tokens_grad[None], first_new, second_new, master_new,
        new_qkv, new_out, new_in, new_down, norm_first_new, norm_second_new, norm_new,
    )


def solution(mesh):
    sharded = P("dp", "mp", None)
    return jax.shard_map(
        per_device,
        mesh=mesh,
        in_specs=(
            sharded, sharded, P("dp"), P(), P(None, "mp"), P("mp", None), P(None, "mp"), P("mp", None),
            sharded, sharded, sharded, P(), P(), P(), P(),
        ),
        out_specs=(
            sharded, sharded, sharded, sharded, sharded,
            P(None, "mp"), P("mp", None), P(None, "mp"), P("mp", None), P(), P(), P(),
        ),
        check_vma=False,
    )
```

```python
import functools

import jax
import jax.numpy as jnp
from jax import lax
from jax.experimental import pallas as pl
from jax.experimental.pallas import tpu as pltpu
from jax.sharding import PartitionSpec as P

HEAD = 64
BAND = 30
STEP = 10
HALO = 64
EDGE = 32
QB = 64
WIN = 128
PAIR = 128
COST = 1
STATE = 144

learn_rate = 0.1
norm_rate = 0.3
decay_rate = 0.1
beta_one = 0.9
beta_two = 0.95
adam_epsilon = 1e-08
norm_epsilon = 1e-05
GELU_C = 0.7978845608028654
GELU_A = 0.044715

f32 = jnp.float32
bf16 = jnp.bfloat16

VM = pl.BlockSpec(memory_space=pltpu.VMEM)
HB = pl.BlockSpec(memory_space=pltpu.HBM)
SM = pl.BlockSpec(memory_space=pltpu.SMEM)
ANY = pl.BlockSpec(memory_space=pl.ANY)


def call(body, outs, in_specs, scratch, flops, moved, vmem=48, out_specs=None):
    specs = out_specs or tuple(VM for _ in outs)
    run = pl.pallas_call(
        body,
        out_shape=tuple(
            pltpu.HBM(s, d) if spec is HB else jax.ShapeDtypeStruct(s, d) for (s, d), spec in zip(outs, specs)
        ),
        in_specs=in_specs,
        out_specs=specs,
        scratch_shapes=scratch,
        compiler_params=pltpu.CompilerParams(vmem_limit_bytes=vmem << 20),
        cost_estimate=pl.CostEstimate(flops=flops // COST, bytes_accessed=moved // COST, transcendentals=0),
    )

    def fixed(*args):
        return run(
            *[
                pltpu.with_memory_space_constraint(x, pltpu.HBM) if spec is HB else x
                for x, spec in zip(args, in_specs)
            ]
        )

    return fixed


def load(pairs, sem):
    copies = [pltpu.make_async_copy(a, b, sem) for a, b in pairs]
    for c in copies:
        c.start()
    return copies


def dot(a, b):
    return jnp.dot(a, b, preferred_element_type=f32)


def turned(a):
    return a.astype(f32).T.astype(bf16)


def dot_nt(a, b):
    return dot(a, turned(b))


def dot_tn(a, b):
    return lax.dot_general(a, b, (((0,), (0,)), ((), ())), preferred_element_type=f32)


def normalize(x):
    mean = jnp.mean(x, axis=-1, keepdims=True)
    cen = x - mean
    var = jnp.mean(cen * cen, axis=-1, keepdims=True)
    rstd = lax.rsqrt(var + norm_epsilon)
    return cen * rstd, rstd


def same_head(n=PAIR):
    r = lax.broadcasted_iota(jnp.int32, (n, n), 0)
    c = lax.broadcasted_iota(jnp.int32, (n, n), 1)
    return (r < HEAD) == (c < HEAD)


def pack_state(s1, s2, z):
    both = jnp.where(same_head(), s1, pltpu.roll(s2, HEAD, 1))
    hi = z.astype(bf16).astype(f32)
    row = lax.broadcasted_iota(jnp.int32, (16, PAIR), 0)
    tail = jnp.where(row == 0, hi, jnp.where(row == 1, z - hi, 0.0))
    return both.astype(bf16), tail.astype(bf16)


def unpack_state(refs, g):
    tot = refs[0][g].astype(f32)
    for r in refs[1:]:
        tot = tot + r[g].astype(f32)
    both = tot[:PAIR]
    diag = same_head()
    s1 = jnp.where(diag, both, 0.0)
    s2 = jnp.where(diag, pltpu.roll(both, HEAD, 1), 0.0)
    z = tot[PAIR : PAIR + 1] + tot[PAIR + 1 : PAIR + 2]
    return s1, s2, z


def split_dot(a, ones):
    hi, lo = two(a)
    return dot(hi, ones) + dot(lo, ones)


def two(a):
    hi = a.astype(bf16)
    return hi, (a - hi.astype(f32)).astype(bf16)


def phi(v):
    low = jnp.exp(jnp.minimum(v, 0.0))
    return jnp.where(v > 0, v + 1.0, low), jnp.where(v > 0, 1.0, low)


def band_parts():
    c = lax.broadcasted_iota(jnp.int32, (WIN, 2 * QB), 0)
    r = lax.broadcasted_iota(jnp.int32, (WIN, 2 * QB), 1) % QB
    off = r + EDGE - c
    return (jnp.abs(off) <= BAND), off == 0, c


def stacked(rows):
    lane = lax.broadcasted_iota(jnp.int32, (1, PAIR), 1)
    first = (lane < HEAD).astype(f32).astype(bf16)
    second = (lane >= HEAD).astype(f32).astype(bf16)
    return jnp.concatenate([rows * first, rows * second], axis=0)


def unstack(both):
    lane = lax.broadcasted_iota(jnp.int32, (QB, PAIR), 1)
    return jnp.where(lane < HEAD, both[:QB], both[QB:])


def softmax_of(raw, mask):
    scores = jnp.where(mask, raw * 0.125, -1e30)
    ex = jnp.exp(scores - jnp.max(scores, axis=0, keepdims=True))
    return ex * (1.0 / jnp.sum(ex, axis=0, keepdims=True))


def piece_at(meta, r, bits, other):
    b0, b1 = (meta[6], meta[7]) if other else (meta[4], meta[5])
    core = 1 - meta[2] if other else meta[2]
    if bits == 1:
        return core * 2 + (b0 ^ r)
    return core * 4 + (b0 ^ (r & 1)) * 2 + (b1 ^ (r >> 1))


def fetch_pieces(meta, bufs, lo, rows, weight, sem):
    n = len(bufs) // 2
    copies = []
    for k, buf in enumerate(bufs):
        p = piece_at(meta, k % n, n // 2, k >= n)
        at = pl.ds(pl.multiple_of(p * rows, rows), rows)
        for m in range(buf.shape[0]):
            src = buf.at[m, pl.ds(lo, rows), :]
            copies.append(pltpu.make_async_copy(src, weight.at[meta[3] ^ m, at, :], sem))
    for c in copies:
        c.start()
    return copies


def norm_body(tok, left, right, gains, biases, a1e_h, a1e_o, sem):
    rows = tok.shape[0]
    gain, bias = gains[0:1, :], biases[0:1, :]

    def ln(x):
        return (normalize(x.astype(f32))[0] * gain + bias).astype(bf16)

    a1e_o[0:HALO, :] = ln(left[...])
    a1e_o[HALO + rows :, :] = ln(right[...])

    def chunk(i, _):
        at = pl.ds(pl.multiple_of(i * 128, 128), 128)
        a1e_o[pl.ds(pl.multiple_of(i * 128 + HALO, 64), 128), :] = ln(tok[at, :])
        return 0

    lax.fori_loop(0, rows // 128, chunk, 0)
    out = pltpu.make_async_copy(a1e_o, a1e_h, sem)
    out.start()
    out.wait()


def qkv_body(meta, a1e_h, *refs):
    bufs, (qkv_h, st_o, w, qkv_o, a1e, sem, out_sem) = refs[:4], refs[4:]
    pull = pltpu.make_async_copy(a1e_h, a1e, out_sem)
    pull.start()
    ext = a1e.shape[0]
    rows = ext - 2 * HALO
    groups = bufs[0].shape[0]
    for c in fetch_pieces(meta, bufs, 0, bufs[0].shape[1], w, sem):
        c.wait()
    pull.wait()
    length, base = meta[0], meta[1]
    pos = base + lax.broadcasted_iota(jnp.int32, (rows, 1), 0)
    valid = (pos < length).astype(f32)
    gs = range(groups)
    for g in gs:
        qkv_o[g] = dot(a1e[...], w[g]).astype(bf16)
    own_rows = slice(HALO, HALO + rows)
    out = pltpu.make_async_copy(qkv_o, qkv_h, out_sem)
    out.start()
    parts = []
    for g in gs:
        keys = qkv_o[g, own_rows, PAIR : 2 * PAIR].astype(f32)
        feat = phi(keys)[0] * valid
        parts.append((jnp.sum(feat, axis=0, keepdims=True), two(feat), two(jnp.tanh(keys) * valid)))
    for g in gs:
        z, (fhi, flo), (thi, tlo) = parts[g]
        vals = qkv_o[g, own_rows, 2 * PAIR :]
        s1 = dot_tn(fhi, vals) + dot_tn(flo, vals)
        s2 = dot_tn(thi, vals) + dot_tn(tlo, vals)
        st_o[g, :PAIR, :], st_o[g, PAIR:, :] = pack_state(s1, s2, z)
    out.wait()


def near_body(meta, qkv_h, near_h, qkv, near_o, sem):
    pull = pltpu.make_async_copy(qkv_h, qkv, sem)
    pull.start()
    groups = qkv.shape[0]
    rows = near_o.shape[0]
    length, base = meta[0], meta[1]
    band, diag, lane = band_parts()
    pull.wait()

    def block(b, _):
        at = b * QB
        kpos = base + at - EDGE + lane
        mask = band & (((kpos >= 0) & (kpos < length)) | diag)
        q_at = pl.ds(pl.multiple_of(at + HALO, QB), QB)
        w_at = pl.ds(pl.multiple_of(at + HALO - EDGE, EDGE), WIN)
        gs = range(groups)
        sc = [dot_nt(qkv[g, w_at, PAIR : 2 * PAIR], stacked(qkv[g, q_at, 0:PAIR])) for g in gs]
        p = [softmax_of(sc[g], mask).astype(bf16) for g in gs]
        res = [dot_tn(p[g], qkv[g, w_at, 2 * PAIR :]) for g in gs]
        for g in gs:
            near_o[pl.ds(pl.multiple_of(at, QB), QB), g * PAIR : (g + 1) * PAIR] = unstack(res[g])
        return 0

    lax.fori_loop(0, rows // QB, block, 0, unroll=4)
    out = pltpu.make_async_copy(near_o, near_h, sem)
    out.start()
    out.wait()


def put_halves(core, keep, give, g, lo, grad):
    n, width = grad.shape
    tiles = grad.reshape(n // 16, 2, 8, width)
    even, odd = tiles[:, 0].reshape(n // 2, width), tiles[:, 1].reshape(n // 2, width)
    first = jnp.full(even.shape, core, jnp.int32) == 0
    at = slice(lo, lo + n // 2)
    keep[g, at, :] = jnp.where(first, even, odd).astype(keep.dtype)
    give[g, at, :] = jnp.where(first, odd, even).astype(give.dtype)


def main_body(meta, near_h, qkv_h, h0, h1, h2, h3, tok_h, cot_h, gains, biases, *refs):
    bufs, refs = refs[:8], refs[8:]
    out_h, dst_o, far_o, dx2_h, dctx_h, dqf_h, ng_o, wout_h, keep_h, give_h = refs[:10]
    refs = refs[10:]
    do_o, dctx_o, wout_o, near, tok, cot, st = refs[:7]
    refs = (None,) * 5 + refs
    w_in, w_down, x2, xhat, rs, u, dh, acc, da2, far1, inv, dnum, phq, thq = refs[12:26]
    ctx_o, a2_o, dm_o, hid_o, du_o, out_o, keep, give, query, sem, out_sem = refs[26:]
    rows, width = tok.shape
    groups, hw = hid_o.shape[0], hid_o.shape[2]
    s0, s1, s2, s3 = [st.at[k] for k in range(4)]
    moved = load([(near_h, near), (tok_h, tok), (cot_h, cot)] + [(h, st.at[k]) for k, h in enumerate((h0, h1, h2, h3))], sem.at[4])
    pr = hw // 8
    orow = bufs[0].shape[1] - 2 * pr
    core = meta[2]
    sent = []

    def send(src, dst):
        sent.append(pltpu.make_async_copy(src, dst, out_sem))
        sent[-1].start()

    length, base = meta[0], meta[1]
    pull = pltpu.make_async_copy(qkv_h.at[:, pl.ds(HALO, rows), pl.ds(0, PAIR)], query, sem.at[3])
    pull.start()
    copies = fetch_pieces(meta, bufs, 2 * pr, orow, wout_o, sem.at[0])
    later = fetch_pieces(meta, bufs, 0, pr, w_in, sem.at[1])
    last = fetch_pieces(meta, bufs, pr, pr, w_down, sem.at[2])
    rlen = 1.0 / length.astype(f32)
    gain, bias = gains[1:2, :], biases[1:2, :]
    ones = same_head().astype(f32).astype(bf16)
    gs = range(groups)
    cols = [slice(g * PAIR, (g + 1) * PAIR) for g in gs]
    for c in moved:
        c.wait()
    states = [unpack_state((s0, s1, s2, s3), g) for g in gs]
    s1b, s2b = [two(st[0]) for st in states], [two(st[1]) for st in states]
    cr = 128

    def far_chunk(i, _):
        at = pl.ds(pl.multiple_of(i * cr, cr), cr)
        q = [query[g, at, :].astype(f32) for g in gs]
        ph = [phi(q[g])[0] for g in gs]
        ph2 = [two(ph[g]) for g in gs]
        th2 = [two(jnp.tanh(q[g])) for g in gs]
        den = [split_dot(ph[g] * states[g][2], ones) for g in gs]
        num = [dot(ph2[g][0], s1b[g][0]) + dot(ph2[g][0], s1b[g][1]) + dot(ph2[g][1], s1b[g][0]) for g in gs]
        sec = [dot(th2[g][0], s2b[g][0]) + dot(th2[g][0], s2b[g][1]) + dot(th2[g][1], s2b[g][0]) for g in gs]
        for g in gs:
            phq[at, cols[g]] = ph2[g][0]
            thq[at, cols[g]] = th2[g][0]
        rec = [1.0 / den[g] for g in gs]
        for g in gs:
            part = num[g] * rec[g]
            inv[at, cols[g]] = rec[g]
            far1[at, cols[g]] = part
            ctx_o[at, cols[g]] = (near[at, cols[g]] + (part + sec[g] * rlen)).astype(bf16)
        pos = base + i * cr + lax.broadcasted_iota(jnp.int32, (cr, 1), 0)
        dm_o[at, :] = (cot[at, :].astype(f32) * (pos < length).astype(f32)).astype(bf16)
        return 0

    pull.wait()
    lax.fori_loop(0, rows // cr, far_chunk, 0)
    for c in copies:
        c.wait()
    wout = wout_o[...].reshape(width, width)
    x2[...] = dot(ctx_o[...], wout)

    def norm_chunk(i, _):
        at = pl.ds(pl.multiple_of(i * 128, 128), 128)
        val = x2[at, :] + tok[at, :].astype(f32)
        x2[at, :] = val
        xh, rstd = normalize(val)
        xhat[at, :] = xh
        rs[at, :] = jnp.broadcast_to(rstd, (128, 128))
        a2_o[at, :] = (xh * gain + bias).astype(bf16)
        return 0

    lax.fori_loop(0, rows // 128, norm_chunk, 0)
    for c in later + last:
        c.wait()
    for g in gs:
        u[g] = dot(a2_o[...], w_in[g])
        dh[g] = dot_nt(dm_o[...], w_down[g])

    def act(i, _):
        at = pl.ds(pl.multiple_of(i * 16, 16), 16)
        for g in gs:
            v = u[g, at, :]
            sq = v * v
            half = 0.5 + 0.5 * jnp.tanh(v * (GELU_C + GELU_C * GELU_A * sq))
            hid = v * half
            hid_o[g, at, :] = hid.astype(bf16)
            slope = half + (hid * (1.0 - half)) * (2.0 * GELU_C + 6.0 * GELU_C * GELU_A * sq)
            du_o[g, at, :] = (dh[g, at, :] * slope).astype(bf16)
        return 0

    lax.fori_loop(0, rows // 16, act, 0)
    acc[...] = sum(dot(hid_o[g], w_down[g]) for g in gs)
    da2[...] = sum(dot_nt(du_o[g], w_in[g]) for g in gs)

    def back_chunk(i, carry):
        dg, db = carry
        at = pl.ds(pl.multiple_of(i * 128, 128), 128)
        out_o[at, :] = (x2[at, :] + acc[at, :]).astype(bf16)
        xh = xhat[at, :]
        rstd = rs[at, 0:1]
        d = da2[at, :]
        dg = dg + jnp.sum(d * xh, axis=0, keepdims=True)
        db = db + jnp.sum(d, axis=0, keepdims=True)
        e = d * gain
        m1 = jnp.mean(e, axis=-1, keepdims=True)
        m2 = jnp.mean(e * xh, axis=-1, keepdims=True)
        dx = dm_o[at, :].astype(f32) + rstd * (e - m1 - xh * m2)
        acc[at, :] = dx
        do_o[at, :] = dx.astype(bf16)
        return dg, db

    zero = jnp.zeros((1, width), f32)
    dg, db = lax.fori_loop(0, rows // 128, back_chunk, (zero, zero))
    even = jnp.full((EDGE, width), meta[3] & 1, jnp.int32) == 0
    head, tail = do_o[0:EDGE, :].astype(f32), do_o[rows - EDGE :, :].astype(f32)
    near_edge, far_edge = jnp.where(even, tail, head).astype(bf16), jnp.where(even, head, tail).astype(bf16)
    for g in gs:
        dst_o[g, STATE:, :] = near_edge[:, cols[g]]
        far_o[g, STATE:, :] = far_edge[:, cols[g]]
    send(out_o, out_h)
    send(wout_o, wout_h)
    send(acc, dx2_h)
    ng_o[0:1, :] = dg
    ng_o[1:2, :] = db
    dctx_o[...] = dot_nt(do_o[...], wout).astype(bf16)
    send(dctx_o, dctx_h)

    def far_back(i, carry):
        at = pl.ds(pl.multiple_of(i * cr, cr), cr)
        dc = [dctx_o[at, cols[g]] for g in gs]
        dcf = [dc[g].astype(f32) for g in gs]
        rec = [inv[at, cols[g]] for g in gs]
        dn = [(dcf[g] * rec[g]).astype(bf16) for g in gs]
        dots = [split_dot(dcf[g] * far1[at, cols[g]], ones) for g in gs]
        dph = [dot_nt(dn[g], s1b[g][0]) for g in gs]
        dth = [dot_nt(dc[g], s2b[g][0]) for g in gs]
        out = []
        for g in gs:
            dnum[at, cols[g]] = dn[g]
            dden = -dots[g] * rec[g]
            out.append(carry[g] + jnp.sum(phq[at, cols[g]].astype(f32) * dden, axis=0, keepdims=True))
            slope = phi(query[g, at, :].astype(f32))[1]
            th = thq[at, cols[g]].astype(f32)
            da2[at, cols[g]] = (dph[g] + dden * states[g][2]) * slope + dth[g] * rlen * (1.0 - th * th)
        return tuple(out)

    none = jnp.zeros((1, PAIR), f32)
    dz = lax.fori_loop(0, rows // cr, far_back, (none,) * groups)
    for g in gs:
        d1 = dot_tn(phq[:, cols[g]], dnum[:, cols[g]])
        d2 = dot_tn(thq[:, cols[g]], dctx_o[:, cols[g]]) * rlen
        both, low = pack_state(d1, d2, dz[g])
        for ref in (dst_o, far_o):
            ref[g, :PAIR, :] = both
            ref[g, PAIR:STATE, :] = low
    send(da2, dqf_h)
    n_out = ctx_o.shape[1] // groups

    def finish(g, lo, n, grad):
        put_halves(core, keep, give, g, lo, grad)
        part = pl.ds(lo, n)
        send(keep.at[g, part, :], keep_h.at[g, part, :])
        send(give.at[g, part, :], give_h.at[g, part, :])

    for g in gs:
        finish(g, n_out // 2, width // 2, dot_tn(a2_o[...], du_o[g]))
    for g in gs:
        finish(g, 0, n_out // 2, dot_tn(ctx_o[:, g * n_out : (g + 1) * n_out], do_o[...]))
    for g in gs:
        finish(g, n_out // 2 + width // 2, hw // 2, dot_tn(hid_o[g], dm_o[...]))
    for c in sent:
        c.wait()


def near_back_body(
    meta, qkv_h, dctx_h, one, three, wout_h, dqf_h, dq_o, dk_o, dv_o, dce, dqe, dke, dve, wout, dqf, qkv, sem,
):
    pull = pltpu.make_async_copy(qkv_h, qkv, sem.at[2])
    pull.start()
    groups = qkv.shape[0]
    rows, width = dctx_h.shape
    third = pltpu.make_async_copy(dctx_h, dce.at[pl.ds(EDGE, rows), :], sem.at[3])
    third.start()
    length, base = meta[0], meta[1]
    band, diag, lane = band_parts()
    first = pltpu.make_async_copy(wout_h, wout, sem.at[0])
    first.start()
    second = pltpu.make_async_copy(dqf_h, dqf, sem.at[1])
    second.start()
    first.wait()
    w = wout[...].reshape(width, -1)
    z = meta[3]
    odd = jnp.full((EDGE, width), z & 1, jnp.int32) == 1
    side = [
        jnp.concatenate([ref[g, STATE:, :] for g in range(groups)], axis=1).astype(f32) for ref in (one, three)
    ]
    last_z = meta[17] - 1
    do_l = jnp.where(odd, side[0], side[1]) * (z > 0).astype(f32)
    do_r = jnp.where(odd, side[1], side[0]) * (z < last_z).astype(f32)
    dce[0:EDGE, :] = dot_nt(do_l.astype(bf16), w).astype(bf16)
    dce[EDGE + rows :, :] = dot_nt(do_r.astype(bf16), w).astype(bf16)
    dke[...] = jnp.zeros(dke.shape, f32)
    dve[...] = jnp.zeros(dve.shape, f32)
    pull.wait()
    third.wait()

    def block(b, _):
        at = b * QB
        kpos = base + at - HALO + lane
        mask = band & (((kpos >= 0) & (kpos < length)) | diag)
        c_at = pl.ds(pl.multiple_of(at, QB), QB)
        q_at = pl.ds(pl.multiple_of(at + EDGE, EDGE), QB)
        w_at = pl.ds(pl.multiple_of(at, QB), WIN)
        gs = range(groups)
        cols = [slice(g * PAIR, (g + 1) * PAIR) for g in gs]
        qs = [stacked(qkv[g, q_at, 0:PAIR]) for g in gs]
        cs = [stacked(dce[c_at, cols[g]]) for g in gs]
        kw = [qkv[g, w_at, PAIR : 2 * PAIR] for g in gs]
        sc = [dot_nt(kw[g], qs[g]) for g in gs]
        dp = [dot_nt(qkv[g, w_at, 2 * PAIR :], cs[g]) for g in gs]
        p = [softmax_of(sc[g], mask) for g in gs]
        row = [jnp.sum(p[g] * dp[g], axis=0, keepdims=True) for g in gs]
        ds = [(p[g] * (dp[g] - row[g])).astype(bf16) for g in gs]
        pb = [p[g].astype(bf16) for g in gs]
        for g in gs:
            dke[w_at, cols[g]] += dot(ds[g], qs[g])
            dve[w_at, cols[g]] += dot(pb[g], cs[g])
        dq = [dot_tn(ds[g], kw[g]) for g in gs]
        for g in gs:
            dqe[c_at, cols[g]] = unstack(dq[g])
        return 0

    lax.fori_loop(0, rows // QB + 1, block, 0, unroll=9)
    second.wait()
    dq_o[...] = (dqe[EDGE : EDGE + rows, :] * 0.125 + dqf[...]).astype(bf16)
    dk_o[...] = dke[HALO : HALO + rows, :] * 0.125
    dv_o[...] = dve[HALO : HALO + rows, :]


def proj_body(
    meta, qkv_h, dq, dkn, dvn, s0, s1, s2, s3, a1e_h, dproj_h, keep_o, give_o, dproj, flat, pseudo, qkv, a1e, sem, in_sem,
):
    rows = dq.shape[0]
    other = pltpu.make_async_copy(a1e_h.at[pl.ds(HALO, rows), :], a1e, in_sem.at[1])
    other.start()
    pull = pltpu.make_async_copy(qkv_h, qkv, in_sem.at[0])
    pull.start()
    groups = qkv.shape[0]
    rows, width = dq.shape
    length, base, core = meta[0], meta[1], meta[2]
    cr = 128
    gs = range(groups)
    cols = [slice(g * PAIR, (g + 1) * PAIR) for g in gs]
    states = [unpack_state((s0, s1, s2, s3), g) for g in gs]
    s1b, s2b = [st[0].astype(bf16) for st in states], [st[1].astype(bf16) for st in states]

    def far_chunk(i, _):
        at = pl.ds(pl.multiple_of(i * cr, cr), cr)
        e_at = pl.ds(pl.multiple_of(i * cr + HALO, HALO), cr)
        pos = base + i * cr + lax.broadcasted_iota(jnp.int32, (cr, 1), 0)
        valid = (pos < length).astype(f32)
        k = [qkv[g, e_at, PAIR : 2 * PAIR].astype(f32) for g in gs]
        v = [qkv[g, e_at, 2 * PAIR :] for g in gs]
        feat = [phi(k[g]) for g in gs]
        th = [jnp.tanh(k[g]) for g in gs]
        vd1 = [dot_nt(v[g], s1b[g]) for g in gs]
        vd2 = [dot_nt(v[g], s2b[g]) for g in gs]
        dv = [
            dot((feat[g][0] * valid).astype(bf16), s1b[g]) + dot((th[g] * valid).astype(bf16), s2b[g]) for g in gs
        ]
        for g in gs:
            dk = (vd1[g] + states[g][2]) * feat[g][1] + vd2[g] * (1.0 - th[g] * th[g])
            dproj[g, at, 0:PAIR] = dq[at, cols[g]]
            dproj[g, at, PAIR : 2 * PAIR] = (dkn[at, cols[g]] + dk * valid).astype(bf16)
            dproj[g, at, 2 * PAIR :] = (dvn[at, cols[g]] + dv[g]).astype(bf16)
        return 0

    pull.wait()
    lax.fori_loop(0, rows // cr, far_chunk, 0)
    out = pltpu.make_async_copy(dproj, dproj_h, sem)
    out.start()
    other.wait()
    n_flat = 3 * width
    for g in gs:
        grad = dot_tn(a1e[...], dproj[g])
        for part in range(3):
            flat[pl.ds(part, width, stride=3), :] = grad[:, part * PAIR : (part + 1) * PAIR]
        for j in range(4):
            pseudo[:, j * 128 : (j + 1) * 128] = flat[pl.ds(j, n_flat // 4, stride=4), :]
        put_halves(core, keep_o, give_o, g, 0, pseudo[...])
    out.wait()


def last_body(meta, dproj_h, tok, dx2_h, gains, ng2, *refs):
    bufs, (tg_o, ng_o, da1, ngs, wqkv, dproj, dx2, sem, sems) = refs[:4], refs[4:]
    groups = dproj.shape[0]
    rows, width = tok.shape
    gain = gains[0:1, :]
    copies = fetch_pieces(meta, bufs, 0, bufs[0].shape[1], wqkv, sem)
    copies.append(pltpu.make_async_copy(dproj_h, dproj, sems.at[0]))
    copies[-1].start()
    late = pltpu.make_async_copy(dx2_h, dx2, sems.at[1])
    late.start()
    for c in copies:
        c.wait()
    da1[...] = sum(dot_nt(dproj[g], wqkv[g]) for g in range(groups))

    late.wait()

    def back_chunk(i, carry):
        dg, db = carry
        at = pl.ds(pl.multiple_of(i * 64, 64), 64)
        xh, rstd = normalize(tok[at, :].astype(f32))
        d = da1[at, :]
        dg = dg + jnp.sum(d * xh, axis=0, keepdims=True)
        db = db + jnp.sum(d, axis=0, keepdims=True)
        e = d * gain
        m1 = jnp.mean(e, axis=-1, keepdims=True)
        m2 = jnp.mean(e * xh, axis=-1, keepdims=True)
        tg_o[at, :] = dx2[at, :] + rstd * (e - m1 - xh * m2)
        return dg, db

    zero = jnp.zeros((1, width), f32)
    dg, db = lax.fori_loop(0, rows // 64, back_chunk, (zero, zero))
    for k, val in enumerate((dg, db, ng2[0:1, :], ng2[1:2, :])):
        for j in range(width // 128):
            at = k * (width // 128) + j
            ngs[at : at + 1, :] = val[:, j * 128 : (j + 1) * 128]
    ng_o[...] = ngs[...]


def halve_body(bit, own, got, give_o, keep_o):
    groups, _, n = give_o.shape
    out = pl.ds(pl.multiple_of((1 - bit[0]) * n, 128), n)
    stay = pl.ds(pl.multiple_of(bit[0] * n, 128), n)
    for g in range(groups):
        give_o[g] = (own[g, :, out].astype(f32) + got[g, :, out].astype(f32)).astype(bf16)
    for g in range(groups):
        keep_o[g] = own[g, :, stay].astype(f32) + got[g, :, stay].astype(f32)


def total_body(meta, keep, got, *outs):
    for m, out in enumerate(outs):
        g = meta[3] ^ m
        out[0] = (keep[g] + got[g].astype(f32)).astype(bf16)


def total_q_body(meta, keep, got, ng, *outs):
    n, k = keep.shape[1], ng.shape[0]
    hi, lo = two(ng[...])
    for m, out in enumerate(outs):
        g = meta[3] ^ m
        out[0, 0:n, :] = (keep[g] + got[g].astype(f32)).astype(bf16)
        out[0, n : n + k, :], out[0, n + k :, :] = hi, lo


def slices_body(where, master, first, second, out_h, held, parts, sem, out_sem):
    caps = held.shape[1] // 64
    copies = [pltpu.make_async_copy(ref, held.at[t], sem.at[t]) for t, ref in enumerate((master, first, second))]
    for c in copies:
        c.start()
    sent = []
    for t in range(3):
        copies[t].wait()
        for j in range(4):
            val = held[t, pl.ds(j, caps * 16, stride=4), :].reshape(caps, 2, 8, 128)
            for c in range(2):
                hi, lo = two(val[:, c].reshape(caps * 8, 128))
                for k, part in ((0, hi), (1, lo)) if t == 0 else ((t + 1, hi),):
                    parts[k, c, j] = part
                    for d in where[c][j]:
                        sent.append(pltpu.make_async_copy(parts.at[k, c, j], out_h.at[d, k], out_sem))
                        sent[-1].start()
    for c in sent:
        c.wait()


def widen_body(recv_h, st_o, recv, sem):
    copies = load([(recv_h.at[d], recv.at[d]) for d in range(recv.shape[0])], sem)
    for c in copies:
        c.wait()

    def owner(d, _):
        st_o[d, 0] = recv[d, 0].astype(f32) + recv[d, 1].astype(f32)
        st_o[d, 1] = recv[d, 2].astype(f32)
        st_o[d, 2] = recv[d, 3].astype(f32)
        return 0

    lax.fori_loop(0, recv.shape[0], owner, 0)


def adam(g, m_old, f_old, s_old):
    corr_one = 1.0 - beta_one**STEP
    corr_two = 1.0 - beta_two**STEP
    fn = beta_one * f_old + (1.0 - beta_one) * g
    sn = beta_two * s_old + (1.0 - beta_two) * g * g
    step = fn / corr_one / (jnp.sqrt(sn / corr_two) + adam_epsilon)
    return fn, sn, m_old - learn_rate * (step + decay_rate * m_old)


def pieces_body(first, count, owners, slots, *refs):
    parts, (st, w_o, piece_o) = refs[:count], refs[count:]
    n = piece_o.shape[0]
    src = [(r, s) for r in parts for s in range(r.shape[0])]
    piece_o[...] = sum(r[s, 0:n, :].astype(f32) for r, s in src)
    w_o[n : 2 * n, :] = piece_o[...].astype(bf16)
    if w_o.shape[0] > 2 * n:
        k = (parts[0].shape[1] - n) // 2
        w_o[2 * n : 3 * n, :] = two(piece_o[...])[1]
        norms = sum(r[s, n : n + k, :].astype(f32) + r[s, n + k :, :].astype(f32) for r, s in src)
        w_o[3 * n : 3 * n + k, :], w_o[3 * n + k :, :] = two(norms)

    def pair(i, _):
        new = []
        for k in range(2):
            b = i * 2 + k
            at = pl.ds(pl.multiple_of(slots[first + b] * 8, 8), 8)
            own = owners[first + b]
            g = piece_o[pl.ds(pl.multiple_of(b * 8, 8), 8), :]
            new.append(adam(g, st[own, 0, at, :], st[own, 1, at, :], st[own, 2, at, :])[2])
        w_o[pl.ds(pl.multiple_of(i * 16, 16), 16), :] = jnp.concatenate(new, axis=0).astype(bf16)
        return 0

    lax.fori_loop(0, n // 16, pair, 0, unroll=4)


def owner_body(
    meta, counts, blocks, later_h, master_h, first_h, second_h, gains, biases, n_first, n_second, *refs
):
    bufs, (f_o, s_o, m_o, q_o, nf_o, ns_o, np_o) = refs[:8], refs[8:15]
    held, early, parts, grad, flat, total, master, first, second, sem, sems = refs[15:]
    moved = load([(later_h, parts), (master_h, master), (first_h, first), (second_h, second)], sems)
    collect(meta, bufs, held, sem)
    for c in moved:
        c.wait()
    caps, br, _ = master.shape
    n = q_o.shape[0] * q_o.shape[1] // (128 * 64)
    k_ng = total.shape[0]
    for p in range(8):
        early[p] = held[p, n * 8 : n * 16, :].astype(f32) + held[p, n * 16 : n * 24, :].astype(f32)
    total[...] = sum(
        held[p, n * 24 : n * 24 + k_ng, :].astype(f32) + held[p, n * 24 + k_ng :, :].astype(f32) for p in range(8)
    )
    start = meta[8] * caps

    def pick(r, _):
        b = blocks[start + r]
        old = pl.ds(pl.multiple_of(jnp.minimum(b, n - 1) * 8, 8), 8)
        is_q = jnp.full((8, 128), b, jnp.int32) < n
        for p in range(8):
            parts[p % 4, r, p // 4] = jnp.where(is_q, early[p, old, :], parts[p % 4, r, p // 4])
        return 0

    lax.fori_loop(0, caps, pick, 0, unroll=2)
    for j in range(4):
        grad[pl.ds(j, caps * 16, stride=4), :] = parts[j].reshape(caps * 16, 128)

    def slot(r, _):
        g = grad[pl.ds(pl.multiple_of(r * br, br), br), :]
        m_old, f_old, s_old = master[r], first[r], second[r]
        fn, sn, mn = adam(g, m_old, f_old, s_old)
        keep = jnp.full(g.shape, counts[start + r], jnp.int32) > 0
        f_o[r] = jnp.where(keep, fn, f_old)
        s_o[r] = jnp.where(keep, sn, s_old)
        m_o[r] = jnp.where(keep, mn, m_old)
        return 0

    lax.fori_loop(0, caps, slot, 0, unroll=2)
    rows = q_o.shape[0]
    for j in range(4):
        flat[pl.ds(j, n * 16, stride=4), :] = columns(held, j, 0, n * 8)
    for part in range(3):
        q_o[:, part * 128 : (part + 1) * 128] = flat[pl.ds(part, rows, stride=3), :].astype(bf16)
    corr_one = 1.0 - beta_one**STEP
    corr_two = 1.0 - beta_two**STEP
    per = n_first.shape[1] // 128
    for k in range(4):
        old = (biases if k % 2 else gains)[k // 2 : k // 2 + 1, :]
        g = jnp.concatenate([total[k * per + j : k * per + j + 1, :] for j in range(per)], axis=1)
        fn = beta_one * n_first[k : k + 1, :] + (1.0 - beta_one) * g
        sn = beta_two * n_second[k : k + 1, :] + (1.0 - beta_two) * g * g
        nf_o[k : k + 1, :] = fn
        ns_o[k : k + 1, :] = sn
        np_o[k : k + 1, :] = old - norm_rate * (fn / corr_one / (jnp.sqrt(sn / corr_two) + adam_epsilon))


def collect(meta, bufs, held, sem):
    copies = []
    for k, buf in enumerate(bufs):
        copies.append(pltpu.make_async_copy(buf, held.at[piece_at(meta, k % 4, 2, k >= 4)], sem))
        copies[-1].start()
    for c in copies:
        c.wait()


def columns(held, j, lo, n):
    even, odd = [held[c * 4 + j, lo : lo + n, :].astype(f32).reshape(n // 8, 1, 8, 128) for c in range(2)]
    return jnp.concatenate([even, odd], axis=1).reshape(2 * n, 128)


def place_body(first, meta, blocks, *refs):
    bufs, outs, (parts_h, held, grads, parts, sem) = refs[:8], refs[8:11], refs[11:]
    collect(meta, bufs, held, sem)
    half = held.shape[1] // 2
    for p in range(8):
        grads[p] = held[p, half:, :].astype(f32)
    caps = parts.shape[1]

    def pick(r, _):
        b = jnp.maximum(blocks[meta[8] * caps + r] - first, 0)
        at = pl.ds(pl.multiple_of(b * 8, 8), 8)
        for p in range(8):
            parts[p % 4, r, p // 4] = grads[p, at, :]
        return 0

    lax.fori_loop(0, caps, pick, 0, unroll=2)
    out = pltpu.make_async_copy(parts, parts_h, sem)
    out.start()
    lo = 0
    for ref in outs:
        n = ref.shape[0] // 2
        for j in range(4):
            ref[:, j * 128 : (j + 1) * 128] = columns(held, j, lo, n).astype(bf16)
        lo += n
    out.wait()


def per_device(
    tokens, cotangent, lengths, owners, w_qkv, w_out, w_in, w_down,
    master, first_moment, second_moment, norm_gains, norm_biases, norm_first, norm_second,
):
    rows, width = tokens.shape[1], tokens.shape[2]
    groups = lax.axis_size("mp")
    ndp = lax.axis_size("dp")
    nbits = ndp.bit_length() - 1
    rest = list(range(1, nbits))
    order = (rest, rest[:2][::-1] + rest[2:][::-1])
    me, zi = lax.axis_index("dp"), lax.axis_index("mp")
    core = me & 1

    def bit_of(who, at, s):
        return (who >> jnp.where(at == 0, order[0][s], order[1][s])) & 1

    def swap(x, s):
        return lax.ppermute(x, "dp", [(i, i ^ (1 << order[i & 1][s])) for i in range(ndp)])

    def swap_core(x):
        return lax.ppermute(x, "dp", [(i, i ^ 1) for i in range(ndp)])

    def from_mp(x, step):
        return lax.ppermute(x, "mp", [(i, i + step) for i in range(groups) if 0 <= i + step < groups])

    def swap_mp(x, mask):
        return lax.ppermute(x, "mp", [(i, i ^ mask) for i in range(groups)])

    def exchange(x, axis):
        return lax.all_to_all(x, axis, 0, 0, tiled=True)

    def all_states(x):
        return [x] + [swap_mp(x, m) for m in range(1, groups)]

    q0, q1 = bit_of(me, core, 0), bit_of(me, core, 1)
    o0, o1 = bit_of(me, 1 - core, 0), bit_of(me, 1 - core, 1)
    length = lengths[0]
    base = zi * rows
    ids = [length, base, core, zi, q0, q1, o0, o1, me]
    ids += [
        me - (me & 7) + c + ((j >> 1) << order[c][0]) + ((j & 1) << order[c][1]) for c in range(2) for j in range(4)
    ]
    ids.append(jnp.int32(groups))
    meta = jnp.stack(ids).astype(jnp.int32)

    def after(x, *deps):
        return lax.optimization_barrier((x,) + deps)[0]

    def over_mp(piece):
        return [piece] + [swap_mp(piece, m) for m in range(1, groups)]

    def both_cores(bufs):
        return bufs + [swap_core(b) for b in bufs]

    def part_of(w, n, at):
        return lax.dynamic_slice_in_dim(w, at * (w.shape[0] // n), w.shape[0] // n, 0)

    mine = core * 4 + q0 * 2 + q1
    tok, cot = tokens[0], cotangent[0]
    ext = rows + 2 * HALO
    mm = 2 * rows * width
    qkv_z = over_mp(part_of(w_qkv, 4, core * 2 + q0))
    left, right = from_mp(tok[rows - HALO :], 1), from_mp(tok[:HALO], -1)
    ffn_piece = jnp.concatenate([part_of(w, 8, mine) for w in (w_in, w_down, w_out)], axis=0)
    qkv_z = after(jnp.stack(qkv_z), left, right, ffn_piece)
    ffn_z = jnp.stack(over_mp(after(ffn_piece, qkv_z)))
    qkv_bufs = [qkv_z, swap(qkv_z, 0)]
    capacity, block_rows = master.shape[0], master.shape[1]
    where = [[[] for _ in range(4)] for _ in range(2)]
    for d in range(ndp):
        b = order[d & 1]
        where[d & 1][2 * ((d >> b[0]) & 1) + ((d >> b[1]) & 1)].append(d)
    flat_state = [x.reshape(capacity * block_rows, 128) for x in (master, first_moment, second_moment)]
    [parts] = call(
        functools.partial(slices_body, where), [((ndp, 4, capacity * 8, 128), bf16)], [HB] * 3,
        [
            pltpu.VMEM((3, capacity * block_rows, 128), f32), pltpu.VMEM((4, 2, 4, capacity * 8, 128), bf16),
            pltpu.SemaphoreType.DMA((3,)), pltpu.SemaphoreType.DMA,
        ],
        1 << 20, 4 << 20, 12, (HB,),
    )(*flat_state)
    [a1e] = call(norm_body, [((ext, width), bf16)], [VM] * 5,
        [pltpu.VMEM((ext, width), bf16), pltpu.SemaphoreType.DMA], 4 * mm, 1 << 20, 16, (HB,),
    )(
        after(tok, parts), left, right, norm_gains, norm_biases
    )
    qkv_bufs = both_cores([qkv_bufs[0], after(qkv_bufs[1], a1e)])
    all_qkv = pltpu.VMEM((groups, ext, 3 * PAIR), bf16)
    proj_w = pltpu.VMEM((groups, width, 3 * PAIR), bf16)
    qkv, state = call(
        qkv_body,
        [((groups, ext, 3 * PAIR), bf16), ((groups, STATE, PAIR), bf16)],
        [SM, HB] + [ANY] * 4,
        [proj_w, all_qkv, pltpu.VMEM((ext, width), bf16), pltpu.SemaphoreType.DMA, pltpu.SemaphoreType.DMA],
        2 * ext * width * 3 * width, 6 << 20, 20, (HB, VM),
    )(meta, after(a1e, ffn_z), *qkv_bufs)
    states = all_states(state)
    ffn_z = after(ffn_z, a1e, qkv_bufs[1])
    ffn_x, ffn_y = swap(ffn_z, 0), swap(ffn_z, 1)
    ffn_oth = [swap_core(b) for b in (ffn_z, ffn_x, ffn_y)]
    ffn_bufs = [ffn_z, ffn_x, ffn_y, swap(after(ffn_x, ffn_y, *states), 1)]
    blocks = owners.shape[0]
    earlier = jnp.arange(blocks)[None, :] < jnp.arange(blocks)[:, None]
    alike = owners[None, :] == owners[:, None]
    slot = jnp.sum((earlier & alike).astype(jnp.int32), axis=1)
    slot_rows = owners * capacity + slot
    hit = slot_rows[None, :] == jnp.arange(ndp * capacity, dtype=jnp.int32)[:, None]
    held = jnp.sum(jnp.where(hit, jnp.arange(blocks, dtype=jnp.int32)[None, :], 0), axis=1)
    counts = jnp.sum(hit.astype(jnp.int32), axis=1)
    [near] = call(
        near_body, [((rows, width), f32)], [SM, HB],
        [all_qkv, pltpu.VMEM((rows, width), f32), pltpu.SemaphoreType.DMA], mm * 1024, 12 << 20, 16, (HB,),
    )(meta, after(qkv, slot, held, counts, *ffn_oth, *states))
    ffn_bufs = ffn_bufs + ffn_oth + [swap_core(ffn_bufs[3])]
    held_state = exchange(after(parts, near), "dp")

    hid_w = w_in.shape[1]
    big = pltpu.VMEM((rows, width), f32)
    low = pltpu.VMEM((rows, width), bf16)
    n_m = (w_out.shape[0] + w_in.shape[0] + w_down.shape[0]) // 2
    wide = pltpu.VMEM((groups, rows, hid_w), f32)
    half = pltpu.VMEM((groups, n_m, width), bf16)
    four = pltpu.VMEM((groups, rows, hid_w), bf16)
    (outputs, dstate, dfar, dx2, dctx, dqf, ng2, wout, grad_m, give_m) = call(
        main_body,
        [
            ((rows, width), bf16), ((groups, STATE + EDGE, PAIR), bf16), ((groups, STATE + EDGE, PAIR), bf16),
            ((rows, width), f32), ((rows, width), bf16), ((rows, width), f32), ((2, width), f32),
            ((groups,) + w_out.shape, bf16), ((groups, n_m, width), bf16), ((groups, n_m, width), bf16),
        ],
        [SM] + [HB] * 8 + [VM] * 2 + [HB] * 7 + [ANY],
        [
            low, low, pltpu.VMEM((groups,) + w_out.shape, bf16), big, low, low,
            pltpu.VMEM((4, groups, STATE, PAIR), bf16),
            pltpu.VMEM((groups, width, hid_w), bf16), pltpu.VMEM((groups, hid_w, width), bf16),
            big, big, pltpu.VMEM((rows, 128), f32), wide, wide, big, big, big, big,
            low, low, low, low, low, low, four, four, low, half, half,
            pltpu.VMEM((groups, rows, PAIR), bf16), pltpu.SemaphoreType.DMA((5,)), pltpu.SemaphoreType.DMA,
        ],
        mm * hid_w * groups * 6, 24 << 20, 44,
        (HB, VM, VM, HB, HB, HB, VM, HB, HB, HB),
    )(meta, near, qkv, *states, tok, cot, norm_gains, norm_biases, *ffn_bufs)

    dstate, dfar, give_m, _ = lax.optimization_barrier((dstate, dfar, give_m, held_state))
    dstates = [dstate, swap_mp(dstate, 1), swap_mp(dstate, 2), swap_mp(dfar, 3)]

    [slot_state] = call(
        widen_body, [((ndp, 3, capacity * 8, 128), f32)], [HB],
        [pltpu.VMEM((ndp, 4, capacity * 8, 128), bf16), pltpu.SemaphoreType.DMA], 1 << 20, 4 << 20, 12,
    )(held_state)

    bits = [bit_of(me, core, s).astype(jnp.int32).reshape(1) for s in range(2)]

    def halve(own, got, s):
        shape = own.shape[:-1] + (own.shape[-1] // 2,)
        return call(
            halve_body, [(shape, bf16), (shape, f32)], [SM, VM, VM], [], 1 << 20, 4 << 20, 16,
        )(bits[s], own, got)

    def rest_of(keep, got):
        for s in range(2, nbits - 1):
            tot = (keep + got.astype(f32)).astype(bf16)
            keep, got = tot.astype(f32), swap(tot, s)
        return keep, got

    def to_groups(part):
        return [part[0]] + [swap_mp(part[m], m) for m in range(1, groups)]

    def total_m(keep, got):
        return call(
            total_body, [((1,) + keep.shape[1:], bf16)] * groups, [SM, VM, VM], [], 1 << 20, 2 << 20, 12,
        )(meta, *rest_of(keep, got))

    def total_q(keep, got, extra):
        keep, got = rest_of(keep, got)
        for s in range(2, nbits - 1):
            extra = extra + swap(extra, s)
        shape = (1, keep.shape[1] + 2 * extra.shape[0], keep.shape[2])
        return call(
            total_q_body, [(shape, bf16)] * groups, [SM, VM, VM, VM], [], 1 << 20, 2 << 20, 12,
        )(meta, keep, got, extra)

    give_m, keep_m = halve(grad_m, after(swap_core(give_m), dstates[1], dstates[3], slot_state), 0)
    got_m = swap(give_m, 0)
    dq, dkn, dvn = call(
        near_back_body,
        [((rows, width), bf16), ((rows, width), f32), ((rows, width), f32)],
        [SM, HB, HB] + [VM] * 2 + [HB] * 2,
        [
            pltpu.VMEM((rows + 2 * EDGE, width), bf16), pltpu.VMEM((rows + 2 * EDGE, width), f32),
            pltpu.VMEM((ext, width), f32), pltpu.VMEM((ext, width), f32),
            pltpu.VMEM(wout.shape, bf16), big, all_qkv, pltpu.SemaphoreType.DMA((4,)),
        ],
        mm * 2048, 24 << 20, 20,
    )(meta, qkv, after(dctx, give_m), dstates[1], dstates[3], wout, dqf)
    n_q = w_qkv.size // width // 2
    n_ng = 4 * width // 128
    dproj, grad_q, give_q = call(
        proj_body,
        [((groups, rows, 3 * PAIR), bf16), ((groups, n_q, width), f32), ((groups, n_q, width), f32)],
        [SM, HB] + [VM] * 7 + [HB],
        [
            pltpu.VMEM((groups, rows, 3 * PAIR), bf16), pltpu.VMEM((3 * width, 128), f32),
            pltpu.VMEM((2 * n_q, width), f32), all_qkv, low,
            pltpu.SemaphoreType.DMA, pltpu.SemaphoreType.DMA((2,)),
        ],
        mm * 3 * width, 24 << 20, 20, (HB, VM, VM),
    )(meta, qkv, dq, dkn, dvn, *dstates, a1e)
    got_q = swap_core(after(give_q, got_m))
    give_m, keep_m = halve(keep_m, after(got_m, give_q), 1)
    got_m = swap(give_m, 1)
    give_q, keep_q = halve(grad_q, got_q, 0)
    got_q = swap(give_q, 0)
    tokens_grad, ng = call(
        last_body,
        [((rows, width), f32), ((n_ng, 128), f32)],
        [SM, HB, VM, HB, VM, VM] + [HB] * 4,
        [
            big, pltpu.VMEM((n_ng, 128), f32), proj_w, pltpu.VMEM((groups, rows, 3 * PAIR), bf16), big,
            pltpu.SemaphoreType.DMA, pltpu.SemaphoreType.DMA((2,)),
        ],
        mm * 3 * width, 8 << 20, 16,
    )(meta, after(dproj, give_q), tok, dx2, norm_gains, ng2, *qkv_bufs)
    give_q, keep_q = halve(keep_q, after(got_q, ng), 1)
    z_m = to_groups(total_m(keep_m, after(got_m, give_q)))
    got_q = swap(give_q, 1)
    nb_q = n_q * 2 // 16

    def updated(z, n, first, extra):
        return call(
            functools.partial(pieces_body, first, len(z)),
            [((2 * n + extra, 128), bf16)],
            [SM, SM] + [VM] * (len(z) + 1), [pltpu.VMEM((n, 128), f32)], 1 << 20, 4 << 20, 20,
        )(owners, slot, *z, slot_state)[0]

    def everywhere(piece, *first):
        x, y = swap(piece, 0), swap(piece, 1)
        return both_cores([piece, x, y, swap(after(x, *first), 1)])

    part_q = total_q(keep_q, got_q, ng)
    z_q = to_groups(part_q)
    z_m[0] = after(z_m[0], part_q[0])
    fresh_m = updated(z_m, n_m, nb_q, 0)
    m_x, m_y = swap(fresh_m, 0), swap(fresh_m, 1)
    fresh_q = updated(z_q, n_q, 0, n_q + 2 * n_ng)
    q_x, q_y = swap(fresh_q, 0), swap(fresh_q, 1)
    m_bufs = both_cores([fresh_m, m_x, m_y, swap(after(m_x, fresh_q), 1)])
    part_shape = (4, capacity, 2, 8, 128)
    new_out, new_in, new_down, later = call(
        functools.partial(place_body, nb_q),
        [(w_out.shape, bf16), (w_in.shape, bf16), (w_down.shape, bf16), (part_shape, f32)],
        [SM, SM] + [ANY] * 8,
        [
            pltpu.VMEM((8, 2 * n_m, 128), bf16), pltpu.VMEM((8, n_m, 128), f32), pltpu.VMEM(part_shape, f32),
            pltpu.SemaphoreType.DMA,
        ],
        1 << 20, 4 << 20, 16, (VM, VM, VM, HB),
    )(meta, held, *m_bufs)
    q_z = swap(after(q_x, q_y, m_bufs[3]), 1)
    q_bufs = [fresh_q, q_x, q_y, q_z]
    q_bufs += [swap_core(b) for b in q_bufs[:3]] + [swap_core(after(q_z, new_down))]
    state_shape = (capacity, block_rows, 128)
    norm_shape = (4, width)
    n_held = fresh_q.shape[0]
    (first_new, second_new, master_new, new_qkv, norm_first_new, norm_second_new, norm_new) = call(
        owner_body,
        [(state_shape, f32)] * 3 + [(w_qkv.shape, bf16)] + [(norm_shape, f32)] * 3,
        [SM] * 3 + [HB] * 4 + [VM] * 4 + [ANY] * 8,
        [
            pltpu.VMEM((8, n_held, 128), bf16), pltpu.VMEM((8, n_q, 128), f32), pltpu.VMEM(part_shape, f32),
            pltpu.VMEM((capacity * block_rows, 128), f32), pltpu.VMEM((w_qkv.size // 128, 128), f32),
            pltpu.VMEM((n_ng, 128), f32),
            pltpu.VMEM(state_shape, f32), pltpu.VMEM(state_shape, f32), pltpu.VMEM(state_shape, f32),
            pltpu.SemaphoreType.DMA, pltpu.SemaphoreType.DMA,
        ],
        1 << 20, 8 << 20, 24,
    )(
        meta, counts, held, later, master, first_moment, second_moment,
        norm_gains, norm_biases, norm_first, norm_second, *q_bufs,
    )
    return (
        outputs[None], tokens_grad[None], first_new, second_new, master_new,
        new_qkv, new_out, new_in, new_down, norm_first_new, norm_second_new, norm_new,
    )


def solution(mesh):
    sharded = P("dp", "mp", None)
    return jax.shard_map(
        per_device,
        mesh=mesh,
        in_specs=(
            sharded, sharded, P("dp"), P(), P(None, "mp"), P("mp", None), P(None, "mp"), P("mp", None),
            sharded, sharded, sharded, P(), P(), P(), P(),
        ),
        out_specs=(
            sharded, sharded, sharded, sharded, sharded,
            P(None, "mp"), P("mp", None), P(None, "mp"), P("mp", None), P(), P(), P(),
        ),
        check_vma=False,
    )
```
